32 devices in a mesh: pass: 8 (over z, x), head: 4 (over y, core).
Axes of the slice: x: 2, y: 2, z: 4, core: 2. Of those that a mesh axis runs over, the one named last changes fastest.
Arguments:
- queries: bfloat16 [3072, 8192], P('pass', 'head'), may hold values from -4.5 to 4.5
- own_kv: bfloat16 [3072, 8, 256], P('pass', 'head'), may hold values from -4.5 to 4.5
- passage_cache: bfloat16 [128, 512, 8, 256], P('pass', None, 'head'), may hold values from -4.5 to 4.5
- out_weight: bfloat16 [8192, 4096], P('head', 'pass'), may hold values from -3.5 to 3.5
- lists: int32 [24, 8], replicated, may hold values from 0 to 127, as said below
- passage_slot: int32 [128], replicated, may hold values from 0 to 127, as said below
- question_slot: int32 [24], replicated, may hold values from 0 to 23, as said below
Outputs:
- attended: bfloat16 [3072, 4096], P('pass', 'head')
The draws below stay inside these ranges and needn't reach their ends.
Inputs may be any that keep to these rules, and one draw needn't show every extreme that they name: Each question lists 8 different passages. The listed passages of the 3 questions at slots d * 3 to d * 3 + 2 are all different, and at most 3 of them have their cache rows in one aligned block of 16 rows; some block holds exactly 3 of them. `passage_slot`: A permutation. `question_slot`: A permutation.
All inputs are finite; a program needn't handle non-finite values.
Results may differ from the reference program's by a relative error of at most 0.014.
Values may be sent and summed in bfloat16 or wider, within the bound.
A program may use at most 192 MiB of HBM per device.

```python
import jax
import jax.numpy as jnp
from jax import lax

H = 64
KVH = 8
HD = 128
DOUT = 4096
LQ = 128
PLEN = 512
TOPP = 8
Q_DEV = 3
PASS_DEV = 16
NQ = 24
NPASS = 128
TOKENS = 3072
GROUP_ROWS = 2048


def request_layout(key):
    shard_count = NPASS // PASS_DEV
    device_count = NQ // Q_DEV
    entries = Q_DEV * TOPP
    question_slot = jax.random.permutation(jax.random.fold_in(key, 101), NQ).astype(jnp.int32)
    passage_slot = jax.random.permutation(jax.random.fold_in(key, 102), NPASS).astype(jnp.int32)

    def shuffle(subkey):
        return jax.random.permutation(subkey, shard_count).astype(jnp.int32)
    orders = jax.vmap(shuffle)(jax.random.split(jax.random.fold_in(key, 103), device_count))
    first = jax.random.randint(jax.random.fold_in(key, 104), (device_count, shard_count), 0, PASS_DEV)
    second = jax.random.randint(jax.random.fold_in(key, 105), (device_count, shard_count), 0, PASS_DEV)
    base = jnp.minimum(first, second).astype(jnp.int32)
    position = jnp.arange(entries, dtype=jnp.int32) % shard_count
    layer = jnp.arange(entries, dtype=jnp.int32) // shard_count
    shard = orders[:, position]
    local_row = (base[:, position] + layer[None, :]) % PASS_DEV
    cache_row = shard * PASS_DEV + local_row
    passage_of_row = jnp.zeros((NPASS,), jnp.int32).at[passage_slot].set(jnp.arange(NPASS, dtype=jnp.int32))
    by_slot = passage_of_row[cache_row].reshape(NQ, TOPP)
    lists = by_slot[question_slot]
    return (question_slot, passage_slot, lists)


def draw_lists(key, part):
    return request_layout(key)[2]


def draw_passage_slot(key, part):
    return request_layout(key)[1]


def draw_question_slot(key, part):
    return request_layout(key)[0]


def draw_queries(key, part):
    shape = (TOKENS, H, HD)
    values = jnp.clip(jax.random.normal(key, shape, jnp.float32), -4.5, 4.5)
    return values.reshape(TOKENS, H * HD).astype(jnp.bfloat16)


def draw_own_kv(key, part):
    shape = (TOKENS, KVH, 2 * HD)
    values = jnp.clip(jax.random.normal(key, shape, jnp.float32), -4.5, 4.5)
    return values.astype(jnp.bfloat16)


def draw_passage_cache(key, part):
    shape = (NPASS, PLEN, KVH, 2 * HD)
    values = jnp.clip(jax.random.normal(key, shape, jnp.float32), -4.5, 4.5)
    return values.astype(jnp.bfloat16)


def level_of(key, dims, cuts, least, top_value):
    def one(dim, blocks):
        draws = jax.random.uniform(jax.random.fold_in(jax.random.fold_in(key, 6), dim), (blocks,), jnp.float32, least / len(cuts), top_value / len(cuts))
        return jnp.repeat(jnp.exp(draws), dims[dim] // blocks).reshape((-1,) + (1,) * (len(dims) - dim - 1))

    factor_of = one(*cuts[0])
    for cut in cuts[1:]:
        factor_of = factor_of * one(*cut)
    return factor_of


def normal_values(own_key, shape, deviation, limit, pieces=(), kind=jnp.bfloat16):
    level = level_of(own_key, shape, pieces, -0.22, 0.18) if pieces else 1.0
    values = jax.random.normal(own_key, shape, jnp.float32) * deviation * level
    return jnp.minimum(jnp.maximum(values, -limit), limit).astype(kind)


def setup_inputs(seed: int = 0) -> dict:
    streams_of = jax.random.split(jax.random.key(seed), 8)
    queries = draw_queries(jax.random.fold_in(streams_of[7], 71), 0)
    own_kv = draw_own_kv(jax.random.fold_in(streams_of[7], 71), 0)
    passage_cache = draw_passage_cache(jax.random.fold_in(streams_of[7], 71), 0)
    out_weight = normal_values(streams_of[3], (H * HD, DOUT), (20.0 / (H * HD) ** 0.5), 3.5, ((0, 4), (1, 8)))
    lists = draw_lists(jax.random.fold_in(streams_of[7], 71), 0)
    passage_slot = draw_passage_slot(jax.random.fold_in(streams_of[7], 71), 0)
    question_slot = draw_question_slot(jax.random.fold_in(streams_of[7], 71), 0)
    return dict(queries=queries, own_kv=own_kv, passage_cache=passage_cache, out_weight=out_weight, lists=lists, passage_slot=passage_slot, question_slot=question_slot)


def attend(query, keys, values, causal):
    heads = query.shape[1]
    rows = query.shape[0] * heads
    flat = query.reshape(rows, query.shape[2])
    scores = lax.dot_general(flat, keys, (((1,), (1,)), ((), ())), preferred_element_type=jnp.float32)
    scores = scores * (query.shape[2] ** -0.5)
    if causal:
        token = lax.broadcasted_iota(jnp.int32, scores.shape, 0) // heads
        column = lax.broadcasted_iota(jnp.int32, scores.shape, 1)
        scores = jnp.where(column <= token, scores, -1e30)
    row_max = jnp.max(scores, axis=1, keepdims=True)
    weights = jnp.exp(scores - row_max)
    row_total = jnp.sum(weights, axis=1, keepdims=True)
    mixed = jnp.dot(weights.astype(jnp.bfloat16), values, preferred_element_type=jnp.float32) / row_total
    level = row_max + jnp.log(row_total)
    return mixed.astype(jnp.bfloat16).reshape(query.shape[0], heads * query.shape[2]), level.reshape(query.shape[0], heads)


def combine(outputs, levels, heads):
    stacked = jnp.stack(outputs)
    level_stack = jnp.stack(levels)
    peak = jnp.max(level_stack, axis=0, keepdims=True)
    overall = peak + jnp.log(jnp.sum(jnp.exp(level_stack - peak), axis=0, keepdims=True))
    share = jnp.exp(level_stack - overall)
    shaped = stacked.reshape(stacked.shape[0], stacked.shape[1], heads, -1).astype(jnp.float32)
    context = jnp.sum(shaped * share[..., None], axis=0)
    return context.reshape(stacked.shape[1], -1).astype(jnp.bfloat16)


def reference(queries, own_kv, passage_cache, out_weight, lists, passage_slot, question_slot):
    group = H // KVH
    slots = jnp.arange(NQ, dtype=jnp.int32)
    holder = (question_slot[None, :] == slots[:, None]).astype(jnp.int32)
    chosen = jnp.sum(holder[:, :, None] * lists[None, :, :], axis=1).astype(jnp.int32)
    catalog = jnp.arange(NPASS, dtype=jnp.int32)
    picked = (chosen[:, :, None] == catalog[None, None, :]).astype(jnp.int32)
    cache_rows = jnp.sum(picked * passage_slot[None, None, :], axis=2).astype(jnp.int32)
    blocks = queries.reshape(NQ, LQ, KVH, group, HD)
    own_blocks = own_kv.reshape(NQ, LQ, KVH, 2 * HD)

    def per_slot(item):
        query_block, own_block, row_list = item
        head_contexts = []
        for head in range(KVH):
            outputs, levels = [], []
            for index in range(TOPP):
                cache_block = lax.dynamic_index_in_dim(passage_cache, row_list[index], 0, keepdims=False)[:, head]
                mixed, level = attend(query_block[:, head], cache_block[:, :HD], cache_block[:, HD:], False)
                outputs.append(mixed)
                levels.append(level)
            mixed, level = attend(query_block[:, head], own_block[:, head, :HD], own_block[:, head, HD:], True)
            outputs.append(mixed)
            levels.append(level)
            head_contexts.append(combine(outputs, levels, group))
        return jnp.concatenate(head_contexts, axis=1)

    context = lax.map(per_slot, (blocks, own_blocks, cache_rows)).reshape(TOKENS, H * HD)
    result = jnp.zeros((TOKENS, DOUT), jnp.float32)
    for index in range(H * HD // GROUP_ROWS):
        lower = index * GROUP_ROWS
        piece = jnp.dot(context[:, lower:lower + GROUP_ROWS], out_weight[lower:lower + GROUP_ROWS], preferred_element_type=jnp.float32)
        rounded = lax.optimization_barrier(piece.astype(jnp.bfloat16))
        result = result + rounded.astype(jnp.float32)
    return result.astype(jnp.bfloat16)
```

```python
import functools
import math

import jax
import jax.numpy as jnp
from jax import lax
from jax.experimental import pallas as pl
from jax.experimental.pallas import tpu as pltpu
from jax.sharding import PartitionSpec as P

H = 64
KVH = 8
HD = 128
LQ = 128
GROUP = H // KVH
COEF = HD ** (-0.5) * math.log2(math.e)
NEG = -1e30
ROWS = 256


def round_of(a, b, n):
    if n & (n - 1) == 0:
        return a ^ b
    return lax.rem(b - a + n, n)


def pairs_of(k, n):
    if n & (n - 1) == 0:
        return [(p, p ^ k) for p in range(n)]
    return [(p, (p + k) % n) for p in range(n)]


def order_of(n):
    rest = range(1, n)
    return sorted(rest, key=lambda k: (bin(k).count("1"), k))


def gather_kernel(n, most, per_device, order, lists_ref, pslot_ref, qslot_ref, cache_ref, *refs):
    recv_ref, own_row_ref = refs[0], refs[1]
    outs = refs[2 : 2 + len(order)]
    send_row, send_cnt, recv_cnt, buf, in_sem, out_sem = refs[2 + len(order) :]
    me = lax.axis_index("pass")
    pass_dev = cache_ref.shape[0]
    topp, nq = lists_ref.shape
    for k in range(n):
        send_cnt[k] = 0
        recv_cnt[k] = 0
    for i in range(n * most):
        recv_ref[i] = -1
        send_row[i] = 0

    def question(q, carry):
        slot = qslot_ref[q]
        dest = slot // per_device
        local = slot - dest * per_device
        k_send = round_of(me, dest, n)
        for t in range(topp):
            row = pslot_ref[lists_ref[t, q]]
            owner = row // pass_dev

            @pl.when(owner == me)
            def _():
                count = send_cnt[k_send]
                send_row[k_send * most + count] = row - owner * pass_dev
                send_cnt[k_send] = count + 1

            @pl.when(dest == me)
            def _():
                k = round_of(owner, me, n)
                count = recv_cnt[k]
                recv_ref[k * most + count] = local
                recv_cnt[k] = count + 1

        return carry

    lax.fori_loop(0, nq, question, 0)
    for r in range(most):
        own_row_ref[r] = send_row[r]
    copies = []
    for j, k in enumerate(order):
        for r in range(most):
            i = j * most + r
            get = pltpu.make_async_copy(
                cache_ref.at[send_row[k * most + r]], buf.at[i], in_sem.at[i]
            )
            get.start()
            copies.append((get, pltpu.make_async_copy(buf.at[i], outs[j].at[r], out_sem.at[i])))
    for get, put in copies:
        get.wait()
        put.start()
    for get, put in copies:
        put.wait()


def gather(lists, passage_slot, question_slot, cache, n, most, per_device, order):
    item = cache.shape[1:]
    slots = (n - 1) * most
    smem = pl.BlockSpec(memory_space=pltpu.SMEM)
    anyspace = pl.BlockSpec(memory_space=pl.ANY)
    return pl.pallas_call(
        functools.partial(gather_kernel, n, most, per_device, order),
        out_shape=[
            jax.ShapeDtypeStruct((n * most,), jnp.int32),
            jax.ShapeDtypeStruct((most,), jnp.int32),
        ]
        + [jax.ShapeDtypeStruct((most,) + item, cache.dtype)] * len(order),
        in_specs=[smem, smem, smem, anyspace],
        out_specs=[smem, smem] + [anyspace] * len(order),
        scratch_shapes=[
            pltpu.SMEM((n * most,), jnp.int32),
            pltpu.SMEM((n,), jnp.int32),
            pltpu.SMEM((n,), jnp.int32),
            pltpu.VMEM((slots,) + item, cache.dtype),
            pltpu.SemaphoreType.DMA((slots,)),
            pltpu.SemaphoreType.DMA((slots,)),
        ],
        name="gather_items",
        cost_estimate=pl.CostEstimate(
            flops=0, bytes_accessed=2 * slots * math.prod(item) * 2, transcendentals=0
        ),
    )(lists.T, passage_slot, question_slot, cache)


def block_step(q_ref, m_ref, l_ref, acc_ref, question, head, keys, values, causal):
    rows = q_ref.shape[2]
    step = min(ROWS, rows)
    width = keys.shape[0]
    ones = jnp.ones(values.shape, values.dtype)
    extended = jnp.concatenate([values, ones], axis=1)
    for start in range(0, rows, step):
        part = pl.ds(start, step)
        q = q_ref[question, head, part, :]
        scores = (
            lax.dot_general(q, keys, (((1,), (1,)), ((), ())), preferred_element_type=jnp.float32)
            * COEF
        )
        if causal:
            token = lax.broadcasted_iota(jnp.int32, scores.shape, 0) % LQ
            column = lax.broadcasted_iota(jnp.int32, scores.shape, 1)
            scores = jnp.where(column <= token, scores, NEG)
        old = m_ref[question, head, part, :]
        new = jnp.maximum(old, jnp.max(scores, axis=1, keepdims=True))
        weights = jnp.exp2(scores - jnp.concatenate([new] * (width // HD), axis=1))
        mixed = jnp.dot(
            weights.astype(jnp.bfloat16), extended, preferred_element_type=jnp.float32
        )
        alpha = jnp.exp2(old - new)
        m_ref[question, head, part, :] = new
        l_ref[question, head, part, :] = l_ref[question, head, part, :] * alpha + mixed[:, HD:]
        acc_ref[question, head, part, :] = (
            acc_ref[question, head, part, :] * alpha + mixed[:, :HD]
        )


def attend_kernel(first, last, rounds, most, *refs):
    refs = list(refs)
    recv_ref, q_ref = refs.pop(0), refs.pop(0)
    if first:
        row_ref, own_ref, cache_ref = refs.pop(0), refs.pop(0), refs.pop(0)
        sources = None
        entries = most
    else:
        state_in = [refs.pop(0) for _ in range(3)]
        sources = [refs.pop(0) for _ in rounds]
        entries = len(rounds) * most
    if last:
        out_ref = refs.pop(0)
        m_ref, l_ref, acc_ref = [refs.pop(0) for _ in range(3)]
    else:
        m_ref, l_ref, acc_ref = [refs.pop(0) for _ in range(3)]
    buf, sem = refs
    per_device, heads = q_ref.shape[0], q_ref.shape[1]

    def fetch(i, slot):
        if first:
            pltpu.make_async_copy(cache_ref.at[row_ref[i]], buf.at[slot], sem.at[slot]).start()
            return
        for j in range(len(rounds)):

            @pl.when(i // most == j)
            def _():
                pltpu.make_async_copy(
                    sources[j].at[i - j * most], buf.at[slot], sem.at[slot]
                ).start()

    def tag_of(i):
        if first:
            return recv_ref[i]
        k = jnp.int32(0)
        for j, value in enumerate(rounds):
            k = jnp.where(i // most == j, value, k)
        return recv_ref[k * most + lax.rem(i, most)]

    fetch(jnp.int32(0), 0)
    if first:
        m_ref[...] = jnp.full(m_ref.shape, NEG, jnp.float32)
        l_ref[...] = jnp.zeros(l_ref.shape, jnp.float32)
        acc_ref[...] = jnp.zeros(acc_ref.shape, jnp.float32)

        def own_block(question, carry):
            for head in range(heads):
                block = own_ref[question, head]
                block_step(
                    q_ref, m_ref, l_ref, acc_ref, question, head, block[:, :HD], block[:, HD:], True
                )
            return carry

        lax.fori_loop(0, per_device, own_block, 0)
    else:
        m_ref[...] = state_in[0][...]
        l_ref[...] = state_in[1][...]
        acc_ref[...] = state_in[2][...]

    def item(i, carry):
        slot = lax.rem(i, 2)
        pltpu.make_async_copy(buf.at[slot], buf.at[slot], sem.at[slot]).wait()

        @pl.when(i + 1 < entries)
        def _():
            fetch(i + 1, lax.rem(i + 1, 2))

        tag = tag_of(i)

        @pl.when(tag >= 0)
        def _():
            for head in range(heads):
                block_step(
                    q_ref,
                    m_ref,
                    l_ref,
                    acc_ref,
                    tag,
                    head,
                    buf[slot, head, :, :HD],
                    buf[slot, head, :, HD:],
                    False,
                )

        return carry

    lax.fori_loop(0, entries, item, 0)
    if last:
        for question in range(per_device):
            for head in range(heads):
                for g in range(GROUP):
                    part = pl.ds(g * LQ, LQ)
                    column = (head * GROUP + g) * HD
                    out_ref[pl.ds(question * LQ, LQ), pl.ds(column, HD)] = (
                        acc_ref[question, head, part, :] / l_ref[question, head, part, :]
                    ).astype(out_ref.dtype)


def attend_call(first, last, rounds, most, recv, q, rest, item):
    per_device, heads, rows, _ = q.shape
    state = jax.ShapeDtypeStruct(q.shape, jnp.float32)
    smem = pl.BlockSpec(memory_space=pltpu.SMEM)
    vmem = pl.BlockSpec(memory_space=pltpu.VMEM)
    anyspace = pl.BlockSpec(memory_space=pl.ANY)
    if first:
        in_specs = [smem, vmem, smem, vmem, anyspace]
        entries = most
    else:
        in_specs = [smem, vmem] + [vmem] * 3 + [anyspace] * len(rounds)
        entries = most * len(rounds)
    scratch = [pltpu.VMEM((2,) + item, q.dtype), pltpu.SemaphoreType.DMA((2,))]
    if last:
        out_shape = jax.ShapeDtypeStruct((per_device * LQ, heads * GROUP * HD), q.dtype)
        out_specs = vmem
        scratch = [pltpu.VMEM(q.shape, jnp.float32)] * 3 + scratch
    else:
        out_shape = [state] * 3
        out_specs = [vmem] * 3
    weights = entries * heads * rows * item[1]
    return pl.pallas_call(
        functools.partial(attend_kernel, first, last, rounds, most),
        out_shape=out_shape,
        in_specs=in_specs,
        out_specs=out_specs,
        scratch_shapes=scratch,
        name="attend_first" if first else ("attend_last" if last else "attend_more"),
        cost_estimate=pl.CostEstimate(
            flops=weights * HD * 4,
            bytes_accessed=entries * math.prod(item) * 2,
            transcendentals=weights,
        ),
    )(recv, q, *rest)


def weight_blocks(own, n):
    if n & (n - 1):
        return [lax.all_gather(own, "pass", axis=1, tiled=True)]
    have = {0: own}
    bit = n // 2
    while bit:
        for k in list(have):
            have[k ^ bit] = lax.ppermute(have[k], "pass", pairs_of(bit, n))
        bit //= 2
    return [have[k] for k in range(n)]


def project(context, weights, n):
    parts = [
        jnp.dot(context, weight, preferred_element_type=jnp.float32).astype(jnp.bfloat16)
        for weight in weights
    ]
    me = lax.axis_index("pass")
    bit = len(parts) // 2
    while bit:
        swap = (me & bit) != 0
        parts = [jnp.where(swap, parts[k ^ bit], parts[k]) for k in range(len(parts))]
        bit //= 2
    return jnp.concatenate(parts, axis=1)


def body(queries, own_kv, passage_cache, out_weight, lists, passage_slot, question_slot):
    n = lax.axis_size("pass")
    per_device = queries.shape[0] // LQ
    heads = own_kv.shape[1]
    entries = per_device * lists.shape[1]
    most = (entries + n - 1) // n
    order = order_of(n)
    cache = jnp.transpose(passage_cache, (0, 2, 1, 3))
    recv, own_row, *items = gather(
        lists, passage_slot, question_slot, cache, n, most, per_device, order
    )
    arrived = [
        lax.ppermute(item, "pass", pairs_of(k, n)) for k, item in zip(order, items)
    ]
    weights = weight_blocks(out_weight, n)
    q = (
        queries.reshape(per_device, LQ, heads, GROUP, HD)
        .transpose(0, 2, 3, 1, 4)
        .reshape(per_device, heads, GROUP * LQ, HD)
    )
    own = own_kv.reshape(per_device, LQ, heads, 2 * HD).transpose(0, 2, 1, 3)
    item = cache.shape[1:]
    state = attend_call(True, False, (0,), most, recv, q, (own_row, own, cache), item)
    calls = 3
    bounds = [len(order) * i // calls for i in range(calls + 1)]
    for i in range(calls):
        rounds = tuple(order[bounds[i] : bounds[i + 1]])
        rest = tuple(state) + tuple(arrived[bounds[i] : bounds[i + 1]])
        state = attend_call(False, i == calls - 1, rounds, most, recv, q, rest, item)
    context = state
    return lax.psum_scatter(
        project(context, weights, n), "head", scatter_dimension=1, tiled=True
    )


LINE = 4
EXTRA = 16


def mirror(k, ends=None):
    pairs = [(p, p ^ int(2 * k)) for p in range(2 * LINE)]
    if ends is None:
        return pairs
    return [(p, d) for p, d in pairs if (p // 2 in (0, LINE - 1)) == (ends == "outer")]


def is_inner():
    z = lax.axis_index("pass") // 2
    return jnp.logical_and(z > 0, z < LINE - 1)


def sort_kernel(most, per_device, lists_ref, pslot_ref, qslot_ref, cache_ref, *refs):
    row_ref, tag_ref, far_tag_ref = refs[:3]
    outs = refs[3 : 3 + LINE]
    send_row, near_cnt, send_cnt, far_cnt, buf, in_sem, out_sem = refs[3 + LINE :]
    me = lax.axis_index("pass")
    z, x = me // 2, me % 2
    pass_dev = cache_ref.shape[0]
    topp, nq = lists_ref.shape
    for k in range(LINE):
        near_cnt[k] = 0
        send_cnt[k] = 0
        far_cnt[k] = 0

    def question(q, carry):
        slot = qslot_ref[q]
        dest = slot // per_device
        local = slot - dest * per_device
        k = (dest // 2) ^ z
        same = dest % 2 == x
        for t in range(topp):
            row = pslot_ref[lists_ref[t, q]]
            owner = row // pass_dev
            mine = owner == me

            @pl.when(jnp.logical_and(mine, same))
            def _():
                at = k * most + near_cnt[k]
                row_ref[at] = row - owner * pass_dev
                tag_ref[at] = local
                near_cnt[k] = near_cnt[k] + 1

            @pl.when(jnp.logical_and(mine, jnp.logical_not(same)))
            def _():
                send_row[k * most + send_cnt[k]] = row - owner * pass_dev
                send_cnt[k] = send_cnt[k] + 1

            @pl.when(jnp.logical_and(owner == (me ^ 1), same))
            def _():
                far_tag_ref[k * most + far_cnt[k]] = local
                far_cnt[k] = far_cnt[k] + 1

        return carry

    lax.fori_loop(0, nq, question, 0)
    copies = []
    for k in (1, 2, 3, 0):
        for r in range(most):
            i = k * most + r
            get = pltpu.make_async_copy(cache_ref.at[send_row[i]], buf.at[i], in_sem.at[i])
            get.start()
            copies.append((get, pltpu.make_async_copy(buf.at[i], outs[k].at[r], out_sem.at[i])))
    for get, put in copies:
        get.wait()
        put.start()
    for get, put in copies:
        put.wait()


def sort_items(lists, passage_slot, question_slot, cache, most, per_device):
    item = cache.shape[1:]
    slots = LINE * most
    smem = pl.BlockSpec(memory_space=pltpu.SMEM)
    anyspace = pl.BlockSpec(memory_space=pl.ANY)
    return pl.pallas_call(
        functools.partial(sort_kernel, most, per_device),
        out_shape=[jax.ShapeDtypeStruct((slots,), jnp.int32)] * 3
        + [jax.ShapeDtypeStruct((most,) + item, cache.dtype)] * LINE,
        in_specs=[smem, smem, smem, anyspace],
        out_specs=[smem] * 3 + [anyspace] * LINE,
        scratch_shapes=[
            pltpu.SMEM((slots,), jnp.int32),
            pltpu.SMEM((LINE,), jnp.int32),
            pltpu.SMEM((LINE,), jnp.int32),
            pltpu.SMEM((LINE,), jnp.int32),
            pltpu.VMEM((slots,) + item, cache.dtype),
            pltpu.SemaphoreType.DMA((slots,)),
            pltpu.SemaphoreType.DMA((slots,)),
        ],
        name="sort_items",
        cost_estimate=pl.CostEstimate(
            flops=0, bytes_accessed=2 * slots * math.prod(item) * 2, transcendentals=0
        ),
    )(lists.T, passage_slot, question_slot, cache)


def unit():
    r = lax.broadcasted_iota(jnp.int32, (LQ, LQ), 0)
    c = lax.broadcasted_iota(jnp.int32, (LQ, LQ), 1)
    return r == c


def part_step(q_ref, m_ref, l_ref, acc_ref, question, head, keys, values, causal):
    rows = GROUP * LQ
    width = keys.shape[0]
    ones = jnp.ones(values.shape, values.dtype)
    extended = jnp.concatenate([values, ones], axis=1)
    tokens = pl.ds(pl.multiple_of(question * LQ, LQ), LQ)
    for start in range(0, rows, ROWS):
        part = pl.ds(start, ROWS)
        q = jnp.concatenate(
            [
                q_ref[tokens, pl.ds((head * GROUP + g) * HD, HD)]
                for g in range(start // LQ, (start + ROWS) // LQ)
            ],
            axis=0,
        )
        scores = (
            lax.dot_general(q, keys, (((1,), (1,)), ((), ())), preferred_element_type=jnp.float32)
            * COEF
        )
        if causal:
            token = lax.broadcasted_iota(jnp.int32, scores.shape, 0) % LQ
            column = lax.broadcasted_iota(jnp.int32, scores.shape, 1)
            scores = jnp.where(column <= token, scores, NEG)
        old = m_ref[question, head, part, :]
        new = jnp.maximum(old, jnp.max(scores, axis=1, keepdims=True))
        weights = jnp.exp2(scores - jnp.concatenate([new] * (width // HD), axis=1))
        mixed = jnp.dot(
            weights.astype(jnp.bfloat16), extended, preferred_element_type=jnp.float32
        )
        alpha = jnp.exp2(old - new)
        m_ref[question, head, part, :] = new
        l_ref[question, head, part, :] = l_ref[question, head, part, :] * alpha + mixed[:, HD:]
        acc_ref[question, head, part, :] = (
            acc_ref[question, head, part, :] * alpha + mixed[:, :HD]
        )


def part_kernel(k, most, heads, *refs):
    refs = list(refs)
    row_ref, tag_ref, far_tag_ref = refs.pop(0), refs.pop(0), refs.pop(0)
    own_ref = refs.pop(0) if k == 0 else None
    questions = [refs.pop(0) for _ in range(2 if k > 1 else 1)]
    cache_ref, items_ref, out_ref, q_ref, m_ref, l_ref, acc_ref, buf, sem, q_sem = refs
    per_device = q_ref.shape[0] // LQ
    entries = 2 * most

    def fetch(i, slot):
        @pl.when(i < most)
        def _():
            row = row_ref[k * most + jnp.minimum(i, most - 1)]
            pltpu.make_async_copy(cache_ref.at[row], buf.at[slot], sem.at[slot]).start()

        @pl.when(i >= most)
        def _():
            pltpu.make_async_copy(
                items_ref.at[jnp.maximum(i - most, 0)], buf.at[slot], sem.at[slot]
            ).start()

    if len(questions) == 1:
        pltpu.make_async_copy(questions[0], q_ref, q_sem).start()
    else:
        inner = is_inner()

        @pl.when(inner)
        def _():
            pltpu.make_async_copy(questions[0], q_ref, q_sem).start()

        @pl.when(jnp.logical_not(inner))
        def _():
            pltpu.make_async_copy(questions[1], q_ref, q_sem).start()

    fetch(jnp.int32(0), 0)
    m_ref[...] = jnp.full(m_ref.shape, NEG, jnp.float32)
    l_ref[...] = jnp.zeros(l_ref.shape, jnp.float32)
    acc_ref[...] = jnp.zeros(acc_ref.shape, jnp.float32)
    pltpu.make_async_copy(q_ref, q_ref, q_sem).wait()
    if k == 0:

        def own_block(question, carry):
            for head in range(heads):
                block = own_ref[question, head]
                part_step(
                    q_ref, m_ref, l_ref, acc_ref, question, head, block[:, :HD], block[:, HD:], True
                )
            return carry

        lax.fori_loop(0, per_device, own_block, 0)

    def item(i, carry):
        slot = lax.rem(i, 2)
        pltpu.make_async_copy(buf.at[slot], buf.at[slot], sem.at[slot]).wait()

        @pl.when(i + 1 < entries)
        def _():
            fetch(i + 1, lax.rem(i + 1, 2))

        at = k * most + lax.rem(i, most)
        tag = jnp.where(i < most, tag_ref[at], far_tag_ref[at])
        for head in range(heads):
            part_step(
                q_ref,
                m_ref,
                l_ref,
                acc_ref,
                tag,
                head,
                buf[slot, head, :, :HD],
                buf[slot, head, :, HD:],
                False,
            )
        return carry

    lax.fori_loop(0, entries, item, 0)
    eye = unit()
    row_of = lax.broadcasted_iota(jnp.int32, (8, LQ), 0)
    for head in range(heads):
        for g in range(GROUP):
            columns = pl.ds((head * GROUP + g) * HD, HD)
            tile = jnp.full((8, LQ), NEG, jnp.float32)
            for question in range(per_device):
                part = pl.ds(g * LQ, LQ)
                total = l_ref[question, head, part, :]
                some = total > 0.0
                safe = jnp.where(some, total, 1.0)
                out_ref[pl.ds(question * LQ, LQ), columns] = (
                    acc_ref[question, head, part, :] / safe
                ).astype(out_ref.dtype)
                level = jnp.where(some, m_ref[question, head, part, :] + jnp.log2(safe), NEG)
                line = jnp.sum(jnp.where(eye, level, 0.0), axis=0, keepdims=True)
                tile = jnp.where(row_of == question, line, tile)
            store_level(out_ref, columns, tile)


def store_level(out_ref, columns, tile):
    high = tile.astype(jnp.bfloat16).astype(jnp.float32)
    both = jnp.concatenate([high, tile - high], axis=0)
    out_ref[pl.ds(out_ref.shape[0] - EXTRA, EXTRA), columns] = both.astype(out_ref.dtype)


def load_level(ref, columns):
    both = ref[pl.ds(ref.shape[0] - EXTRA, EXTRA), columns].astype(jnp.float32)
    return both[:8] + both[8:]


def part_call(k, most, tables, own, questions, cache, items):
    tokens, columns = questions[0].shape
    heads, item = cache.shape[1], cache.shape[1:]
    state = (tokens // LQ, heads, GROUP * LQ, HD)
    smem = pl.BlockSpec(memory_space=pltpu.SMEM)
    vmem = pl.BlockSpec(memory_space=pltpu.VMEM)
    anyspace = pl.BlockSpec(memory_space=pl.ANY)
    owned = [own] if k == 0 else []
    weights = 2 * most * heads * GROUP * LQ * item[1]
    return pl.pallas_call(
        functools.partial(part_kernel, k, most, heads),
        out_shape=jax.ShapeDtypeStruct((tokens + EXTRA, columns), cache.dtype),
        in_specs=[smem] * 3 + [vmem] * len(owned) + [anyspace] * (len(questions) + 2),
        out_specs=vmem,
        scratch_shapes=[
            pltpu.VMEM((tokens, columns), cache.dtype),
            pltpu.VMEM(state, jnp.float32),
            pltpu.VMEM(state, jnp.float32),
            pltpu.VMEM(state, jnp.float32),
            pltpu.VMEM((2,) + item, cache.dtype),
            pltpu.SemaphoreType.DMA((2,)),
            pltpu.SemaphoreType.DMA,
        ],
        name=f"attend_part{k}",
        cost_estimate=pl.CostEstimate(
            flops=weights * HD * 4,
            bytes_accessed=2 * most * math.prod(item) * 2,
            transcendentals=weights,
        ),
    )(*tables, *owned, *questions, cache, items)


def merge_into(a_ref, b_ref, out_ref, out_rows, leveled):
    rows = a_ref.shape[0] - EXTRA
    eye = unit()

    def tile(c, carry):
        columns = pl.ds(pl.multiple_of(c * HD, HD), HD)
        one, two = load_level(a_ref, columns), load_level(b_ref, columns)
        top = jnp.maximum(one, two)
        first, second = jnp.exp2(one - top), jnp.exp2(two - top)
        total = first + second
        share = first / total
        for question in range(rows // LQ):
            line = jnp.broadcast_to(share[question : question + 1, :], (LQ, LQ))
            column = jnp.sum(jnp.where(eye, line, 0.0), axis=1, keepdims=True)
            tokens = pl.ds(question * LQ, LQ)
            a = a_ref[tokens, columns].astype(jnp.float32)
            b = b_ref[tokens, columns].astype(jnp.float32)
            out_ref[pl.ds(out_rows + question * LQ, LQ), columns] = (
                a * column + b * (1.0 - column)
            ).astype(out_ref.dtype)
        if leveled:
            store_level(out_ref, columns, top + jnp.log2(total))
        return carry

    lax.fori_loop(0, a_ref.shape[1] // HD, tile, 0)


def merge_kernel(a_ref, b_ref, out_ref):
    inner = is_inner()

    @pl.when(inner)
    def _():
        merge_into(a_ref, b_ref, out_ref, 0, True)

    @pl.when(jnp.logical_not(inner))
    def _():
        out_ref[...] = a_ref[...]


def merge(a, b, name):
    vmem = pl.BlockSpec(memory_space=pltpu.VMEM)
    return pl.pallas_call(
        merge_kernel,
        out_shape=jax.ShapeDtypeStruct(a.shape, a.dtype),
        in_specs=[vmem, vmem],
        out_specs=vmem,
        name=name,
        cost_estimate=pl.CostEstimate(
            flops=a.size * 8, bytes_accessed=a.size * 6, transcendentals=0
        ),
    )(a, b)


def finish_kernel(a_ref, b_ref, c_ref, d_ref, out_ref):
    rows = a_ref.shape[0] - EXTRA
    merge_into(a_ref, b_ref, out_ref, 0, False)
    merge_into(c_ref, d_ref, out_ref, rows, False)


def finish(a, b, c, d):
    vmem = pl.BlockSpec(memory_space=pltpu.VMEM)
    return pl.pallas_call(
        finish_kernel,
        out_shape=jax.ShapeDtypeStruct((2 * (a.shape[0] - EXTRA), a.shape[1]), a.dtype),
        in_specs=[vmem] * 4,
        out_specs=vmem,
        name="finish_context",
        cost_estimate=pl.CostEstimate(
            flops=a.size * 16, bytes_accessed=a.size * 12, transcendentals=0
        ),
    )(a, b, c, d)


def line_body(queries, own_kv, passage_cache, out_weight, lists, passage_slot, question_slot):
    per_device = queries.shape[0] // LQ
    heads = own_kv.shape[1]
    most = per_device * lists.shape[1] // (2 * LINE)

    def send(value, pairs):
        return lax.ppermute(value, "pass", pairs)

    near, middle = mirror(1), mirror(3, "inner")
    inward, outward = mirror(1, "outer"), mirror(1, "inner")
    q_near = send(queries, near)
    q_mid = send(queries, middle)
    cache = jnp.transpose(passage_cache, (0, 2, 1, 3))
    row, tag, far_tag, *items = sort_items(
        lists, passage_slot, question_slot, cache, most, per_device
    )
    tables = (row, tag, far_tag)
    q_out = send(q_mid, outward)
    q_cross = send(q_near, middle)
    q_end = send(q_cross, outward)
    across = mirror(0.5)
    far = {k: send(items[k], across) for k in (1, 2, 3, 0)}
    own = own_kv.reshape(per_device, LQ, heads, 2 * HD).transpose(0, 2, 1, 3)
    part1 = part_call(1, most, tables, None, [q_near], cache, far[1])
    part2 = part_call(2, most, tables, None, [q_cross, q_out], cache, far[2])
    part3 = part_call(3, most, tables, None, [q_mid, q_end], cache, far[3])
    back3 = send(part3, inward)
    back2 = send(part2, inward)
    w_own = out_weight
    w_line = send(out_weight, mirror(2))
    w_across = send(out_weight, across)
    w_both = send(w_line, across)
    part0 = part_call(0, most, tables, own, [queries], cache, far[0])
    cross2 = send(merge(part2, back3, "merge2"), middle)
    cross3 = send(merge(part3, back2, "merge3"), middle)
    near1 = merge(part1, cross2, "merge1")
    near0 = merge(part0, cross3, "merge0")
    back1 = send(near1, near)
    beside = send(near0, near)
    context = finish(near0, back1, near1, beside)
    return line_project(context, (w_own, w_across), (w_line, w_both))


def line_project(context, here, there):
    me = lax.axis_index("pass")
    z, x = me // 2, me % 2
    rows = context.shape[0] // 2

    def columns(pair):
        parts = [
            jnp.dot(context, w, preferred_element_type=jnp.float32).astype(jnp.bfloat16)
            for w in pair
        ]
        first = jnp.where(x == 0, parts[0], parts[1])
        second = jnp.where(x == 0, parts[1], parts[0])
        return jnp.concatenate([first, second], axis=1)

    mine, other = columns(here), columns(there)
    pieces = []
    for h in range(LINE):
        own_rows = (h % 2) == (z % 2)
        block = jnp.where(own_rows, h, h ^ 1)
        value = jnp.where(block == z, mine, other)
        pieces.append(jnp.where(own_rows, value[:rows], value[rows:]))
    summed = lax.psum_scatter(
        jnp.concatenate(pieces, axis=1), "head", scatter_dimension=1, tiled=True
    )
    pairs = []
    for p in range(2 * LINE):
        for h in range(LINE):
            if (p // 2) % 2 != h % 2:
                pairs.append((p * LINE + h, (p ^ 2) * LINE + (h ^ 1)))
    moved = lax.ppermute(summed, ("pass", "head"), pairs)
    return jnp.where(lax.axis_index("head") % 2 == z % 2, summed, moved)


def suits_line(mesh, queries, lists):
    passes, heads = mesh.shape["pass"], mesh.shape["head"]
    entries = queries.shape[0] // LQ // passes * lists.shape[1]
    return passes == 2 * LINE and heads == LINE and entries % passes == 0


def solution(mesh):
    in_specs = (
        P("pass", "head"),
        P("pass", "head", None),
        P("pass", None, "head", None),
        P("head", "pass"),
        P(),
        P(),
        P(),
    )
    out_specs = P("pass", "head")

    def run(*args):
        chosen = line_body if suits_line(mesh, args[0], args[4]) else body
        return jax.shard_map(
            chosen, mesh=mesh, in_specs=in_specs, out_specs=out_specs, check_vma=False
        )(*args)

    return run
```

```python
import functools
import math

import jax
import jax.numpy as jnp
from jax import lax
from jax.experimental import pallas as pl
from jax.experimental.pallas import tpu as pltpu
from jax.sharding import PartitionSpec as P


H = 64
KVH = 8
HD = 128
LQ = 128
GROUP = H // KVH
COEF = HD ** (-0.5) * math.log2(math.e)
NEG = -1e30
ROWS = 256


def round_of(a, b, n):
    if n & (n - 1) == 0:
        return a ^ b
    return lax.rem(b - a + n, n)


def pairs_of(k, n):
    if n & (n - 1) == 0:
        return [(p, p ^ k) for p in range(n)]
    return [(p, (p + k) % n) for p in range(n)]


def order_of(n):
    rest = range(1, n)
    return sorted(rest, key=lambda k: (bin(k).count("1"), k))


def gather_kernel(n, most, per_device, order, lists_ref, pslot_ref, qslot_ref, cache_ref, *refs):
    recv_ref, own_row_ref = refs[0], refs[1]
    outs = refs[2 : 2 + len(order)]
    send_row, send_cnt, recv_cnt, buf, in_sem, out_sem = refs[2 + len(order) :]
    me = lax.axis_index("pass")
    pass_dev = cache_ref.shape[0]
    topp, nq = lists_ref.shape
    for k in range(n):
        send_cnt[k] = 0
        recv_cnt[k] = 0
    for i in range(n * most):
        recv_ref[i] = -1
        send_row[i] = 0

    def question(q, carry):
        slot = qslot_ref[q]
        dest = slot // per_device
        local = slot - dest * per_device
        k_send = round_of(me, dest, n)
        for t in range(topp):
            row = pslot_ref[lists_ref[t, q]]
            owner = row // pass_dev

            @pl.when(owner == me)
            def _():
                count = send_cnt[k_send]
                send_row[k_send * most + count] = row - owner * pass_dev
                send_cnt[k_send] = count + 1

            @pl.when(dest == me)
            def _():
                k = round_of(owner, me, n)
                count = recv_cnt[k]
                recv_ref[k * most + count] = local
                recv_cnt[k] = count + 1

        return carry

    lax.fori_loop(0, nq, question, 0)
    for r in range(most):
        own_row_ref[r] = send_row[r]
    copies = []
    for j, k in enumerate(order):
        for r in range(most):
            i = j * most + r
            get = pltpu.make_async_copy(
                cache_ref.at[send_row[k * most + r]], buf.at[i], in_sem.at[i]
            )
            get.start()
            copies.append((get, pltpu.make_async_copy(buf.at[i], outs[j].at[r], out_sem.at[i])))
    for get, put in copies:
        get.wait()
        put.start()
    for get, put in copies:
        put.wait()


def gather(lists, passage_slot, question_slot, cache, n, most, per_device, order):
    item = cache.shape[1:]
    slots = (n - 1) * most
    smem = pl.BlockSpec(memory_space=pltpu.SMEM)
    anyspace = pl.BlockSpec(memory_space=pl.ANY)
    return pl.pallas_call(
        functools.partial(gather_kernel, n, most, per_device, order),
        out_shape=[
            jax.ShapeDtypeStruct((n * most,), jnp.int32),
            jax.ShapeDtypeStruct((most,), jnp.int32),
        ]
        + [jax.ShapeDtypeStruct((most,) + item, cache.dtype)] * len(order),
        in_specs=[smem, smem, smem, anyspace],
        out_specs=[smem, smem] + [anyspace] * len(order),
        scratch_shapes=[
            pltpu.SMEM((n * most,), jnp.int32),
            pltpu.SMEM((n,), jnp.int32),
            pltpu.SMEM((n,), jnp.int32),
            pltpu.VMEM((slots,) + item, cache.dtype),
            pltpu.SemaphoreType.DMA((slots,)),
            pltpu.SemaphoreType.DMA((slots,)),
        ],
        name="gather_items",
        cost_estimate=pl.CostEstimate(
            flops=0, bytes_accessed=2 * slots * math.prod(item) * 2, transcendentals=0
        ),
    )(lists.T, passage_slot, question_slot, cache)


def block_step(q_ref, m_ref, l_ref, acc_ref, question, head, keys, values, causal):
    rows = q_ref.shape[2]
    step = min(ROWS, rows)
    width = keys.shape[0]
    ones = jnp.ones(values.shape, values.dtype)
    extended = jnp.concatenate([values, ones], axis=1)
    for start in range(0, rows, step):
        part = pl.ds(start, step)
        q = q_ref[question, head, part, :]
        scores = (
            lax.dot_general(q, keys, (((1,), (1,)), ((), ())), preferred_element_type=jnp.float32)
            * COEF
        )
        if causal:
            token = lax.broadcasted_iota(jnp.int32, scores.shape, 0) % LQ
            column = lax.broadcasted_iota(jnp.int32, scores.shape, 1)
            scores = jnp.where(column <= token, scores, NEG)
        old = m_ref[question, head, part, :]
        new = jnp.maximum(old, jnp.max(scores, axis=1, keepdims=True))
        weights = jnp.exp2(scores - jnp.concatenate([new] * (width // HD), axis=1))
        mixed = jnp.dot(
            weights.astype(jnp.bfloat16), extended, preferred_element_type=jnp.float32
        )
        alpha = jnp.exp2(old - new)
        m_ref[question, head, part, :] = new
        l_ref[question, head, part, :] = l_ref[question, head, part, :] * alpha + mixed[:, HD:]
        acc_ref[question, head, part, :] = (
            acc_ref[question, head, part, :] * alpha + mixed[:, :HD]
        )


def attend_kernel(first, last, rounds, most, *refs):
    refs = list(refs)
    recv_ref, q_ref = refs.pop(0), refs.pop(0)
    if first:
        row_ref, own_ref, cache_ref = refs.pop(0), refs.pop(0), refs.pop(0)
        sources = None
        entries = most
    else:
        state_in = [refs.pop(0) for _ in range(3)]
        sources = [refs.pop(0) for _ in rounds]
        entries = len(rounds) * most
    if last:
        out_ref = refs.pop(0)
        m_ref, l_ref, acc_ref = [refs.pop(0) for _ in range(3)]
    else:
        m_ref, l_ref, acc_ref = [refs.pop(0) for _ in range(3)]
    buf, sem = refs
    per_device, heads = q_ref.shape[0], q_ref.shape[1]

    def fetch(i, slot):
        if first:
            pltpu.make_async_copy(cache_ref.at[row_ref[i]], buf.at[slot], sem.at[slot]).start()
            return
        for j in range(len(rounds)):

            @pl.when(i // most == j)
            def _():
                pltpu.make_async_copy(
                    sources[j].at[i - j * most], buf.at[slot], sem.at[slot]
                ).start()

    def tag_of(i):
        if first:
            return recv_ref[i]
        k = jnp.int32(0)
        for j, value in enumerate(rounds):
            k = jnp.where(i // most == j, value, k)
        return recv_ref[k * most + lax.rem(i, most)]

    fetch(jnp.int32(0), 0)
    if first:
        m_ref[...] = jnp.full(m_ref.shape, NEG, jnp.float32)
        l_ref[...] = jnp.zeros(l_ref.shape, jnp.float32)
        acc_ref[...] = jnp.zeros(acc_ref.shape, jnp.float32)

        def own_block(question, carry):
            for head in range(heads):
                block = own_ref[question, head]
                block_step(
                    q_ref, m_ref, l_ref, acc_ref, question, head, block[:, :HD], block[:, HD:], True
                )
            return carry

        lax.fori_loop(0, per_device, own_block, 0)
    else:
        m_ref[...] = state_in[0][...]
        l_ref[...] = state_in[1][...]
        acc_ref[...] = state_in[2][...]

    def item(i, carry):
        slot = lax.rem(i, 2)
        pltpu.make_async_copy(buf.at[slot], buf.at[slot], sem.at[slot]).wait()

        @pl.when(i + 1 < entries)
        def _():
            fetch(i + 1, lax.rem(i + 1, 2))

        tag = tag_of(i)

        @pl.when(tag >= 0)
        def _():
            for head in range(heads):
                block_step(
                    q_ref,
                    m_ref,
                    l_ref,
                    acc_ref,
                    tag,
                    head,
                    buf[slot, head, :, :HD],
                    buf[slot, head, :, HD:],
                    False,
                )

        return carry

    lax.fori_loop(0, entries, item, 0)
    if last:
        for question in range(per_device):
            for head in range(heads):
                for g in range(GROUP):
                    part = pl.ds(g * LQ, LQ)
                    column = (head * GROUP + g) * HD
                    out_ref[pl.ds(question * LQ, LQ), pl.ds(column, HD)] = (
                        acc_ref[question, head, part, :] / l_ref[question, head, part, :]
                    ).astype(out_ref.dtype)


def attend_call(first, last, rounds, most, recv, q, rest, item):
    per_device, heads, rows, _ = q.shape
    state = jax.ShapeDtypeStruct(q.shape, jnp.float32)
    smem = pl.BlockSpec(memory_space=pltpu.SMEM)
    vmem = pl.BlockSpec(memory_space=pltpu.VMEM)
    anyspace = pl.BlockSpec(memory_space=pl.ANY)
    if first:
        in_specs = [smem, vmem, smem, vmem, anyspace]
        entries = most
    else:
        in_specs = [smem, vmem] + [vmem] * 3 + [anyspace] * len(rounds)
        entries = most * len(rounds)
    scratch = [pltpu.VMEM((2,) + item, q.dtype), pltpu.SemaphoreType.DMA((2,))]
    if last:
        out_shape = jax.ShapeDtypeStruct((per_device * LQ, heads * GROUP * HD), q.dtype)
        out_specs = vmem
        scratch = [pltpu.VMEM(q.shape, jnp.float32)] * 3 + scratch
    else:
        out_shape = [state] * 3
        out_specs = [vmem] * 3
    weights = entries * heads * rows * item[1]
    return pl.pallas_call(
        functools.partial(attend_kernel, first, last, rounds, most),
        out_shape=out_shape,
        in_specs=in_specs,
        out_specs=out_specs,
        scratch_shapes=scratch,
        name="attend_first" if first else ("attend_last" if last else "attend_more"),
        cost_estimate=pl.CostEstimate(
            flops=weights * HD * 4,
            bytes_accessed=entries * math.prod(item) * 2,
            transcendentals=weights,
        ),
    )(recv, q, *rest)


def weight_blocks(own, n):
    if n & (n - 1):
        return [lax.all_gather(own, "pass", axis=1, tiled=True)]
    have = {0: own}
    bit = n // 2
    while bit:
        for k in list(have):
            have[k ^ bit] = lax.ppermute(have[k], "pass", pairs_of(bit, n))
        bit //= 2
    return [have[k] for k in range(n)]


def project(context, weights):
    parts = [
        jnp.dot(context, weight, preferred_element_type=jnp.float32).astype(jnp.bfloat16)
        for weight in weights
    ]
    me = lax.axis_index("pass")
    bit = len(parts) // 2
    while bit:
        swap = (me & bit) != 0
        parts = [jnp.where(swap, parts[k ^ bit], parts[k]) for k in range(len(parts))]
        bit //= 2
    return jnp.concatenate(parts, axis=1)


def body(queries, own_kv, passage_cache, out_weight, lists, passage_slot, question_slot):
    n = lax.axis_size("pass")
    per_device = queries.shape[0] // LQ
    heads = own_kv.shape[1]
    entries = per_device * lists.shape[1]
    most = (entries + n - 1) // n
    order = order_of(n)
    cache = jnp.transpose(passage_cache, (0, 2, 1, 3))
    recv, own_row, *items = gather(
        lists, passage_slot, question_slot, cache, n, most, per_device, order
    )
    arrived = [
        lax.ppermute(item, "pass", pairs_of(k, n)) for k, item in zip(order, items)
    ]
    weights = weight_blocks(out_weight, n)
    q = (
        queries.reshape(per_device, LQ, heads, GROUP, HD)
        .transpose(0, 2, 3, 1, 4)
        .reshape(per_device, heads, GROUP * LQ, HD)
    )
    own = own_kv.reshape(per_device, LQ, heads, 2 * HD).transpose(0, 2, 1, 3)
    item = cache.shape[1:]
    state = attend_call(True, False, (0,), most, recv, q, (own_row, own, cache), item)
    calls = 3
    bounds = [len(order) * i // calls for i in range(calls + 1)]
    for i in range(calls):
        rounds = tuple(order[bounds[i] : bounds[i + 1]])
        rest = tuple(state) + tuple(arrived[bounds[i] : bounds[i + 1]])
        state = attend_call(False, i == calls - 1, rounds, most, recv, q, rest, item)
    context = state
    return lax.psum_scatter(project(context, weights), "head", scatter_dimension=1, tiled=True)


LINE = 4
EXTRA = 16


def mirror(k, ends=None):
    pairs = [(p, p ^ int(2 * k)) for p in range(2 * LINE)]
    if ends is None:
        return pairs
    return [(p, d) for p, d in pairs if (p // 2 in (0, LINE - 1)) == (ends == "outer")]


def is_inner():
    z = lax.axis_index("pass") // 2
    return jnp.logical_and(z > 0, z < LINE - 1)


def sort_kernel(most, per_device, lists_ref, pslot_ref, qslot_ref, cache_ref, *refs):
    row_ref, tag_ref, far_tag_ref = refs[:3]
    outs = refs[3 : 3 + LINE]
    send_row, near_cnt, send_cnt, far_cnt, buf, in_sem, out_sem = refs[3 + LINE :]
    me = lax.axis_index("pass")
    z, x = me // 2, me % 2
    pass_dev = cache_ref.shape[0]
    topp, nq = lists_ref.shape
    for k in range(LINE):
        near_cnt[k] = 0
        send_cnt[k] = 0
        far_cnt[k] = 0

    def question(q, carry):
        slot = qslot_ref[q]
        dest = slot // per_device
        local = slot - dest * per_device
        k = (dest // 2) ^ z
        same = dest % 2 == x
        for t in range(topp):
            row = pslot_ref[lists_ref[t, q]]
            owner = row // pass_dev
            mine = owner == me

            @pl.when(jnp.logical_and(mine, same))
            def _():
                at = k * most + near_cnt[k]
                row_ref[at] = row - owner * pass_dev
                tag_ref[at] = local
                near_cnt[k] = near_cnt[k] + 1

            @pl.when(jnp.logical_and(mine, jnp.logical_not(same)))
            def _():
                send_row[k * most + send_cnt[k]] = row - owner * pass_dev
                send_cnt[k] = send_cnt[k] + 1

            @pl.when(jnp.logical_and(owner == (me ^ 1), same))
            def _():
                far_tag_ref[k * most + far_cnt[k]] = local
                far_cnt[k] = far_cnt[k] + 1

        return carry

    lax.fori_loop(0, nq, question, 0)
    copies = []
    for k in (1, 2, 3, 0):
        for r in range(most):
            i = k * most + r
            get = pltpu.make_async_copy(cache_ref.at[send_row[i]], buf.at[i], in_sem.at[i])
            get.start()
            copies.append((get, pltpu.make_async_copy(buf.at[i], outs[k].at[r], out_sem.at[i])))
    for get, put in copies:
        get.wait()
        put.start()
    for get, put in copies:
        put.wait()


def sort_items(lists, passage_slot, question_slot, cache, most, per_device):
    item = cache.shape[1:]
    slots = LINE * most
    smem = pl.BlockSpec(memory_space=pltpu.SMEM)
    anyspace = pl.BlockSpec(memory_space=pl.ANY)
    return pl.pallas_call(
        functools.partial(sort_kernel, most, per_device),
        out_shape=[jax.ShapeDtypeStruct((slots,), jnp.int32)] * 3
        + [jax.ShapeDtypeStruct((most,) + item, cache.dtype)] * LINE,
        in_specs=[smem, smem, smem, anyspace],
        out_specs=[smem] * 3 + [anyspace] * LINE,
        scratch_shapes=[
            pltpu.SMEM((slots,), jnp.int32),
            pltpu.SMEM((LINE,), jnp.int32),
            pltpu.SMEM((LINE,), jnp.int32),
            pltpu.SMEM((LINE,), jnp.int32),
            pltpu.VMEM((slots,) + item, cache.dtype),
            pltpu.SemaphoreType.DMA((slots,)),
            pltpu.SemaphoreType.DMA((slots,)),
        ],
        name="sort_items",
        cost_estimate=pl.CostEstimate(
            flops=0, bytes_accessed=2 * slots * math.prod(item) * 2, transcendentals=0
        ),
    )(lists.T, passage_slot, question_slot, cache)


def unit():
    r = lax.broadcasted_iota(jnp.int32, (LQ, LQ), 0)
    c = lax.broadcasted_iota(jnp.int32, (LQ, LQ), 1)
    return r == c


def part_step(q_ref, m_ref, l_ref, acc_ref, question, head, keys, values, causal):
    rows = GROUP * LQ
    width = keys.shape[0]
    ones = jnp.ones(values.shape, values.dtype)
    extended = jnp.concatenate([values, ones], axis=1)
    tokens = pl.ds(pl.multiple_of(question * LQ, LQ), LQ)
    for start in range(0, rows, ROWS):
        part = pl.ds(start, ROWS)
        q = jnp.concatenate(
            [
                q_ref[tokens, pl.ds(pl.multiple_of((head * GROUP + g) * HD, HD), HD)]
                for g in range(start // LQ, (start + ROWS) // LQ)
            ],
            axis=0,
        )
        scores = (
            lax.dot_general(q, keys, (((1,), (1,)), ((), ())), preferred_element_type=jnp.float32)
            * COEF
        )
        if causal:
            token = lax.broadcasted_iota(jnp.int32, scores.shape, 0) % LQ
            column = lax.broadcasted_iota(jnp.int32, scores.shape, 1)
            scores = jnp.where(column <= token, scores, NEG)
        old = m_ref[question, head, part, :]
        new = jnp.maximum(old, jnp.max(scores, axis=1, keepdims=True))
        weights = jnp.exp2(scores - jnp.concatenate([new] * (width // HD), axis=1))
        mixed = jnp.dot(
            weights.astype(jnp.bfloat16), extended, preferred_element_type=jnp.float32
        )
        alpha = jnp.exp2(old - new)
        m_ref[question, head, part, :] = new
        l_ref[question, head, part, :] = l_ref[question, head, part, :] * alpha + mixed[:, HD:]
        acc_ref[question, head, part, :] = (
            acc_ref[question, head, part, :] * alpha + mixed[:, :HD]
        )


def part_kernel(k, most, heads, *refs):
    refs = list(refs)
    row_ref, tag_ref, far_tag_ref = refs.pop(0), refs.pop(0), refs.pop(0)
    own_ref = refs.pop(0) if k == 0 else None
    questions = [refs.pop(0) for _ in range(2 if k > 1 else 1)]
    cache_ref, items_ref, out_ref, q_ref, m_ref, l_ref, acc_ref, buf, sem, q_sem = refs
    per_device = q_ref.shape[0] // LQ
    entries = 2 * most

    def fetch(i, slot):
        @pl.when(i < most)
        def _():
            row = row_ref[k * most + jnp.minimum(i, most - 1)]
            pltpu.make_async_copy(cache_ref.at[row], buf.at[slot], sem.at[slot]).start()

        @pl.when(i >= most)
        def _():
            pltpu.make_async_copy(
                items_ref.at[jnp.maximum(i - most, 0)], buf.at[slot], sem.at[slot]
            ).start()

    if len(questions) == 1:
        pltpu.make_async_copy(questions[0], q_ref, q_sem).start()
    else:
        inner = is_inner()

        @pl.when(inner)
        def _():
            pltpu.make_async_copy(questions[0], q_ref, q_sem).start()

        @pl.when(jnp.logical_not(inner))
        def _():
            pltpu.make_async_copy(questions[1], q_ref, q_sem).start()

    fetch(jnp.int32(0), 0)
    m_ref[...] = jnp.full(m_ref.shape, NEG, jnp.float32)
    l_ref[...] = jnp.zeros(l_ref.shape, jnp.float32)
    acc_ref[...] = jnp.zeros(acc_ref.shape, jnp.float32)
    pltpu.make_async_copy(q_ref, q_ref, q_sem).wait()
    if k == 0:

        def own_block(i, carry):
            question, head = i // heads, lax.rem(i, heads)
            part_step(
                q_ref,
                m_ref,
                l_ref,
                acc_ref,
                question,
                head,
                own_ref[question, head, :, :HD],
                own_ref[question, head, :, HD:],
                True,
            )
            return carry

        lax.fori_loop(0, per_device * heads, own_block, 0)

    def item(i, carry):
        slot = lax.rem(i, 2)
        pltpu.make_async_copy(buf.at[slot], buf.at[slot], sem.at[slot]).wait()

        @pl.when(i + 1 < entries)
        def _():
            fetch(i + 1, lax.rem(i + 1, 2))

        at = k * most + lax.rem(i, most)
        tag = jnp.where(i < most, tag_ref[at], far_tag_ref[at])

        def one_head(head, carry):
            part_step(
                q_ref,
                m_ref,
                l_ref,
                acc_ref,
                tag,
                head,
                buf[slot, head, :, :HD],
                buf[slot, head, :, HD:],
                False,
            )
            return carry

        return lax.fori_loop(0, heads, one_head, carry)

    lax.fori_loop(0, entries, item, 0)
    eye = unit()
    row_of = lax.broadcasted_iota(jnp.int32, (8, LQ), 0)

    def close(c, carry):
        head, g = c // GROUP, lax.rem(c, GROUP)
        columns = pl.ds(pl.multiple_of(c * HD, HD), HD)
        part = pl.ds(pl.multiple_of(g * LQ, LQ), LQ)
        tile = jnp.full((8, LQ), NEG, jnp.float32)
        for question in range(per_device):
            total = l_ref[question, head, part, :]
            some = total > 0.0
            safe = jnp.where(some, total, 1.0)
            out_ref[pl.ds(question * LQ, LQ), columns] = (
                acc_ref[question, head, part, :] / safe
            ).astype(out_ref.dtype)
            level = jnp.where(some, m_ref[question, head, part, :] + jnp.log2(safe), NEG)
            line = jnp.sum(jnp.where(eye, level, 0.0), axis=0, keepdims=True)
            tile = jnp.where(row_of == question, line, tile)
        store_level(out_ref, columns, tile)
        return carry

    lax.fori_loop(0, heads * GROUP, close, 0)


def store_level(out_ref, columns, tile):
    high = tile.astype(jnp.bfloat16).astype(jnp.float32)
    both = jnp.concatenate([high, tile - high], axis=0)
    out_ref[pl.ds(out_ref.shape[0] - EXTRA, EXTRA), columns] = both.astype(out_ref.dtype)


def load_level(ref, columns):
    both = ref[pl.ds(ref.shape[0] - EXTRA, EXTRA), columns].astype(jnp.float32)
    return both[:8] + both[8:]


def part_call(k, most, tables, own, questions, cache, items):
    tokens, columns = questions[0].shape
    heads, item = cache.shape[1], cache.shape[1:]
    state = (tokens // LQ, heads, GROUP * LQ, HD)
    smem = pl.BlockSpec(memory_space=pltpu.SMEM)
    vmem = pl.BlockSpec(memory_space=pltpu.VMEM)
    anyspace = pl.BlockSpec(memory_space=pl.ANY)
    owned = [own] if k == 0 else []
    weights = 2 * most * heads * GROUP * LQ * item[1]
    return pl.pallas_call(
        functools.partial(part_kernel, k, most, heads),
        out_shape=jax.ShapeDtypeStruct((tokens + EXTRA, columns), cache.dtype),
        in_specs=[smem] * 3 + [vmem] * len(owned) + [anyspace] * (len(questions) + 2),
        out_specs=vmem,
        scratch_shapes=[
            pltpu.VMEM((tokens, columns), cache.dtype),
            pltpu.VMEM(state, jnp.float32),
            pltpu.VMEM(state, jnp.float32),
            pltpu.VMEM(state, jnp.float32),
            pltpu.VMEM((2,) + item, cache.dtype),
            pltpu.SemaphoreType.DMA((2,)),
            pltpu.SemaphoreType.DMA,
        ],
        cost_estimate=pl.CostEstimate(
            flops=weights * HD * 4,
            bytes_accessed=2 * most * math.prod(item) * 2,
            transcendentals=weights,
        ),
    )(*tables, *owned, *questions, cache, items)


def merge_into(a_ref, b_ref, out_ref, out_rows, leveled):
    rows = a_ref.shape[0] - EXTRA
    eye = unit()
    ones = jnp.ones((2 * LQ, LQ), jnp.bfloat16)

    def tile(c, carry):
        columns = pl.ds(pl.multiple_of(c * HD, HD), HD)
        one, two = load_level(a_ref, columns), load_level(b_ref, columns)
        top = jnp.maximum(one, two)
        first, second = jnp.exp2(one - top), jnp.exp2(two - top)
        total = first + second
        share = first / total
        high = share.astype(jnp.bfloat16).astype(jnp.float32)
        low = share - high
        for question in range(rows // LQ):
            at = slice(question, question + 1)
            spread = jnp.concatenate(
                [
                    jnp.where(eye, jnp.broadcast_to(v[at, :], (LQ, LQ)), 0.0).astype(jnp.bfloat16)
                    for v in (high, low)
                ],
                axis=1,
            )
            column = jnp.dot(spread, ones, preferred_element_type=jnp.float32)
            tokens = pl.ds(question * LQ, LQ)
            a = a_ref[tokens, columns].astype(jnp.float32)
            b = b_ref[tokens, columns].astype(jnp.float32)
            out_ref[pl.ds(out_rows + question * LQ, LQ), columns] = (
                b + (a - b) * column
            ).astype(out_ref.dtype)
        if leveled:
            store_level(out_ref, columns, top + jnp.log2(total))
        return carry

    lax.fori_loop(0, a_ref.shape[1] // HD, tile, 0)


def merge_kernel(a_ref, b_ref, out_ref):
    inner = is_inner()

    @pl.when(inner)
    def _():
        merge_into(a_ref, b_ref, out_ref, 0, True)

    @pl.when(jnp.logical_not(inner))
    def _():
        out_ref[...] = a_ref[...]


def merge(a, b):
    vmem = pl.BlockSpec(memory_space=pltpu.VMEM)
    return pl.pallas_call(
        merge_kernel,
        out_shape=jax.ShapeDtypeStruct(a.shape, a.dtype),
        in_specs=[vmem, vmem],
        out_specs=vmem,
        cost_estimate=pl.CostEstimate(
            flops=a.size * 8, bytes_accessed=a.size * 6, transcendentals=0
        ),
    )(a, b)


def finish_kernel(a_ref, b_ref, c_ref, d_ref, out_ref):
    rows = a_ref.shape[0] - EXTRA
    merge_into(a_ref, b_ref, out_ref, 0, False)
    merge_into(c_ref, d_ref, out_ref, rows, False)


def finish(a, b, c, d):
    vmem = pl.BlockSpec(memory_space=pltpu.VMEM)
    return pl.pallas_call(
        finish_kernel,
        out_shape=jax.ShapeDtypeStruct((2 * (a.shape[0] - EXTRA), a.shape[1]), a.dtype),
        in_specs=[vmem] * 4,
        out_specs=vmem,
        name="finish_context",
        cost_estimate=pl.CostEstimate(
            flops=a.size * 16, bytes_accessed=a.size * 12, transcendentals=0
        ),
    )(a, b, c, d)


def line_steps(queries, own_kv, passage_cache, out_weight, lists, passage_slot, question_slot):
    per_device = queries.shape[0] // LQ
    heads = own_kv.shape[1]
    most = per_device * lists.shape[1] // (2 * LINE)
    half = out_weight.shape[0] // 2

    def send(value, pairs):
        return lax.ppermute(value, "pass", pairs)

    def part(k, *args):
        return part_call(k, most, tables, own if k == 0 else None, *args)

    across = [(p, p ^ 1) for p in range(2 * LINE)]
    inner_across = [(p, d) for p, d in across if p // 2 in (1, 2)]
    outer_across = [(p, d) for p, d in across if p // 2 not in (1, 2)]
    near, middle = mirror(1), mirror(3, "inner")
    inward, outward = mirror(1, "outer"), mirror(1, "inner")
    q_near = send(queries, near)
    q_mid = send(queries, middle)
    w_across0 = send(out_weight[:half], across)
    w_across1 = send(out_weight[half:], across)
    cache = jnp.transpose(passage_cache, (0, 2, 1, 3))
    row, tag, far_tag, *items = sort_items(
        lists, passage_slot, question_slot, cache, most, per_device
    )
    tables = (row, tag, far_tag)
    q_out = send(q_mid, outward)
    q_cross = send(q_near, middle)
    q_end = send(q_cross, outward)
    far = [send(items[k], across) for k in range(LINE)]
    own = own_kv.reshape(per_device, LQ, heads, 2 * HD).transpose(0, 2, 1, 3)
    part2 = part(2, [q_cross, q_out], cache, far[2])
    part3 = part(3, [q_mid, q_end], cache, far[3])
    part0 = part(0, [queries], cache, far[0])
    part1 = part(1, [q_near], cache, far[1])
    back2 = send(part2, inward)
    back3 = send(part3, inward)
    w_in = send(out_weight, mirror(2, "outer"))
    w_out = send(out_weight, mirror(2, "inner"))
    w_in_both = send(w_in, inner_across)
    w_out_both = send(w_out, outer_across)
    cross3 = send(merge(part3, back2), middle)
    cross2 = send(merge(part2, back3), middle)
    near0 = merge(part0, cross3)
    near1 = merge(part1, cross2)
    beside = send(near0, near)
    back1 = send(near1, near)
    context = finish(near0, back1, near1, beside)
    return project_call(
        context, out_weight, w_across0, w_across1, w_in, w_in_both, w_out, w_out_both
    )


MESH = pl.DeviceIdType.MESH


def project_kernel(context_ref, own_ref, a0_ref, a1_ref, *refs):
    in_ref, in2_ref, out1_ref, out2_ref = refs[:4]
    out_ref, w_ref, part_ref, core_ref, y_ref, ysend_ref, zsend_ref = refs[4:11]
    w_sem, send_sem, recv_sem = refs[11:]
    me, head = lax.axis_index("pass"), lax.axis_index("head")
    z, x, y, core = me // 2, me % 2, head // 2, head % 2
    rows, wide = out_ref.shape[0], w_ref.shape[3]
    half = a0_ref.shape[0]
    inner = is_inner()
    core_peer = (me, head ^ 1)
    y_peer = (me, head ^ 2)
    z_peer = (me ^ 2, head ^ 1)
    stays = core == z % 2

    loads = [
        pltpu.make_async_copy(own_ref, w_ref.at[0, x], w_sem.at[0]),
        pltpu.make_async_copy(a0_ref, w_ref.at[0, 1 - x, pl.ds(0, half)], w_sem.at[1]),
        pltpu.make_async_copy(a1_ref, w_ref.at[0, 1 - x, pl.ds(half, half)], w_sem.at[2]),
    ]
    for load in loads:
        load.start()
    inner_loads = [
        pltpu.make_async_copy(in_ref, w_ref.at[1, x], w_sem.at[3]),
        pltpu.make_async_copy(in2_ref, w_ref.at[1, 1 - x], w_sem.at[4]),
    ]
    outer_loads = [
        pltpu.make_async_copy(out1_ref, w_ref.at[1, x], w_sem.at[3]),
        pltpu.make_async_copy(out2_ref, w_ref.at[1, 1 - x], w_sem.at[4]),
    ]

    @pl.when(inner)
    def _():
        for load in inner_loads:
            load.start()

    @pl.when(jnp.logical_not(inner))
    def _():
        for load in outer_loads:
            load.start()

    barrier = pltpu.get_barrier_semaphore()
    for peer in (core_peer, y_peer, z_peer):
        pl.semaphore_signal(barrier, inc=1, device_id=peer, device_id_type=MESH)
    pl.semaphore_wait(barrier, 3)

    def remote(src, dst, i, peer):
        return pltpu.make_async_remote_copy(
            src_ref=src,
            dst_ref=dst,
            send_sem=send_sem.at[i],
            recv_sem=recv_sem.at[i],
            device_id=peer,
            device_id_type=MESH,
        )

    def columns(j):
        return pl.ds(j * wide, wide)

    core_copies = [
        [remote(part_ref.at[s, j], core_ref.at[s, j], s * 2 + j, core_peer) for j in range(2)]
        for s in range(2)
    ]
    y_copies = [remote(ysend_ref.at[j], y_ref.at[j], 4 + j, y_peer) for j in range(2)]
    z_copies = [remote(zsend_ref.at[j], out_ref.at[:, columns(j)], 6 + j, z_peer) for j in range(2)]

    for load in loads + inner_loads:
        load.wait()

    def product(to_y, to_core, j):
        start = pl.multiple_of(jnp.where(to_core == z % 2, 0, rows), LQ)
        here = jnp.where(to_y == z // 2, 0, 1)
        return jnp.dot(
            context_ref[pl.ds(start, rows), :],
            w_ref[here, j],
            preferred_element_type=jnp.float32,
        ).astype(jnp.bfloat16)

    for s, to_y in enumerate((1 - y, y)):
        for j in range(2):
            part_ref[s, j] = product(to_y, 1 - core, j)
            core_copies[s][j].start()
        for j in range(2):
            value = product(to_y, core, j).astype(jnp.float32)
            core_copies[s][j].wait_recv()
            value = value + core_ref[s, j].astype(jnp.float32)
            if s == 0:
                ysend_ref[j] = value.astype(jnp.bfloat16)
                y_copies[j].start()
            else:
                y_copies[j].wait_recv()
                total = (value + y_ref[j].astype(jnp.float32)).astype(jnp.bfloat16)

                @pl.when(stays)
                def _():
                    out_ref[:, columns(j)] = total

                @pl.when(jnp.logical_not(stays))
                def _():
                    zsend_ref[j] = total
                    z_copies[j].start()

    @pl.when(jnp.logical_not(stays))
    def _():
        for copy in z_copies:
            copy.wait()

    for copies in core_copies + [y_copies]:
        for copy in copies:
            copy.wait_send()


def project_call(context, own, a0, a1, *lines):
    rows, depth = context.shape[0] // 2, context.shape[1]
    wide = own.shape[1]
    dtype = context.dtype
    vmem = pl.BlockSpec(memory_space=pltpu.VMEM)
    anyspace = pl.BlockSpec(memory_space=pl.ANY)
    return pl.pallas_call(
        project_kernel,
        out_shape=jax.ShapeDtypeStruct((rows, 2 * wide), dtype),
        in_specs=[vmem] + [anyspace] * 7,
        out_specs=vmem,
        scratch_shapes=[
            pltpu.VMEM((2, 2, depth, wide), dtype),
            pltpu.VMEM((2, 2, rows, wide), dtype),
            pltpu.VMEM((2, 2, rows, wide), dtype),
            pltpu.VMEM((2, rows, wide), dtype),
            pltpu.VMEM((2, rows, wide), dtype),
            pltpu.VMEM((2, rows, wide), dtype),
            pltpu.SemaphoreType.DMA((5,)),
            pltpu.SemaphoreType.DMA((8,)),
            pltpu.SemaphoreType.DMA((8,)),
        ],
        compiler_params=pltpu.CompilerParams(collective_id=0, has_side_effects=True),
        name="project_sum",
        cost_estimate=pl.CostEstimate(
            flops=2 * 4 * 2 * rows * depth * wide,
            bytes_accessed=4 * depth * wide * 2,
            transcendentals=0,
        ),
    )(context, own, a0, a1, *lines)


def suits_line(mesh, queries, lists):
    passes, heads = mesh.shape["pass"], mesh.shape["head"]
    entries = queries.shape[0] // LQ // passes * lists.shape[1]
    return passes == 2 * LINE and heads == LINE and entries % passes == 0


def solution(mesh):
    in_specs = (
        P("pass", "head"),
        P("pass", "head", None),
        P("pass", None, "head", None),
        P("head", "pass"),
        P(),
        P(),
        P(),
    )
    out_specs = P("pass", "head")

    def run(*args):
        if not suits_line(mesh, args[0], args[4]):
            return jax.shard_map(
                body, mesh=mesh, in_specs=in_specs, out_specs=out_specs, check_vma=False
            )(*args)
        step = jax.shard_map(
            line_steps, mesh=mesh, in_specs=in_specs, out_specs=out_specs, check_vma=False
        )
        return step(*args)

    return run
```

```python
import functools
import math

import jax
import jax.numpy as jnp
from jax import lax
from jax.experimental import pallas as pl
from jax.experimental.pallas import tpu as pltpu
from jax.sharding import PartitionSpec as P


H = 64
KVH = 8
HD = 128
LQ = 128
GROUP = H // KVH
COEF = HD ** (-0.5) * math.log2(math.e)
NEG = -1e30
ROWS = 256


def round_of(a, b, n):
    if n & (n - 1) == 0:
        return a ^ b
    return lax.rem(b - a + n, n)


def pairs_of(k, n):
    if n & (n - 1) == 0:
        return [(p, p ^ k) for p in range(n)]
    return [(p, (p + k) % n) for p in range(n)]


def order_of(n):
    rest = range(1, n)
    return sorted(rest, key=lambda k: (bin(k).count("1"), k))


def gather_kernel(n, most, per_device, order, lists_ref, pslot_ref, qslot_ref, cache_ref, *refs):
    recv_ref, own_row_ref = refs[0], refs[1]
    outs = refs[2 : 2 + len(order)]
    send_row, send_cnt, recv_cnt, buf, in_sem, out_sem = refs[2 + len(order) :]
    me = lax.axis_index("pass")
    pass_dev = cache_ref.shape[0]
    topp, nq = lists_ref.shape
    for k in range(n):
        send_cnt[k] = 0
        recv_cnt[k] = 0
    for i in range(n * most):
        recv_ref[i] = -1
        send_row[i] = 0

    def question(q, carry):
        slot = qslot_ref[q]
        dest = slot // per_device
        local = slot - dest * per_device
        k_send = round_of(me, dest, n)
        for t in range(topp):
            row = pslot_ref[lists_ref[t, q]]
            owner = row // pass_dev

            @pl.when(owner == me)
            def _():
                count = send_cnt[k_send]
                send_row[k_send * most + count] = row - owner * pass_dev
                send_cnt[k_send] = count + 1

            @pl.when(dest == me)
            def _():
                k = round_of(owner, me, n)
                count = recv_cnt[k]
                recv_ref[k * most + count] = local
                recv_cnt[k] = count + 1

        return carry

    lax.fori_loop(0, nq, question, 0)
    for r in range(most):
        own_row_ref[r] = send_row[r]
    copies = []
    for j, k in enumerate(order):
        for r in range(most):
            i = j * most + r
            get = pltpu.make_async_copy(
                cache_ref.at[send_row[k * most + r]], buf.at[i], in_sem.at[i]
            )
            get.start()
            copies.append((get, pltpu.make_async_copy(buf.at[i], outs[j].at[r], out_sem.at[i])))
    for get, put in copies:
        get.wait()
        put.start()
    for get, put in copies:
        put.wait()


def gather(lists, passage_slot, question_slot, cache, n, most, per_device, order):
    item = cache.shape[1:]
    slots = (n - 1) * most
    smem = pl.BlockSpec(memory_space=pltpu.SMEM)
    anyspace = pl.BlockSpec(memory_space=pl.ANY)
    return pl.pallas_call(
        functools.partial(gather_kernel, n, most, per_device, order),
        out_shape=[
            jax.ShapeDtypeStruct((n * most,), jnp.int32),
            jax.ShapeDtypeStruct((most,), jnp.int32),
        ]
        + [jax.ShapeDtypeStruct((most,) + item, cache.dtype)] * len(order),
        in_specs=[smem, smem, smem, anyspace],
        out_specs=[smem, smem] + [anyspace] * len(order),
        scratch_shapes=[
            pltpu.SMEM((n * most,), jnp.int32),
            pltpu.SMEM((n,), jnp.int32),
            pltpu.SMEM((n,), jnp.int32),
            pltpu.VMEM((slots,) + item, cache.dtype),
            pltpu.SemaphoreType.DMA((slots,)),
            pltpu.SemaphoreType.DMA((slots,)),
        ],
        name="gather_items",
        cost_estimate=pl.CostEstimate(
            flops=0, bytes_accessed=2 * slots * math.prod(item) * 2, transcendentals=0
        ),
    )(lists.T, passage_slot, question_slot, cache)


def block_step(q_ref, m_ref, l_ref, acc_ref, question, head, keys, values, causal):
    rows = q_ref.shape[2]
    step = min(ROWS, rows)
    width = keys.shape[0]
    ones = jnp.ones(values.shape, values.dtype)
    extended = jnp.concatenate([values, ones], axis=1)
    for start in range(0, rows, step):
        part = pl.ds(start, step)
        q = q_ref[question, head, part, :]
        scores = (
            lax.dot_general(q, keys, (((1,), (1,)), ((), ())), preferred_element_type=jnp.float32)
            * COEF
        )
        if causal:
            token = lax.broadcasted_iota(jnp.int32, scores.shape, 0) % LQ
            column = lax.broadcasted_iota(jnp.int32, scores.shape, 1)
            scores = jnp.where(column <= token, scores, NEG)
        old = m_ref[question, head, part, :]
        new = jnp.maximum(old, jnp.max(scores, axis=1, keepdims=True))
        weights = jnp.exp2(scores - jnp.concatenate([new] * (width // HD), axis=1))
        mixed = jnp.dot(
            weights.astype(jnp.bfloat16), extended, preferred_element_type=jnp.float32
        )
        alpha = jnp.exp2(old - new)
        m_ref[question, head, part, :] = new
        l_ref[question, head, part, :] = l_ref[question, head, part, :] * alpha + mixed[:, HD:]
        acc_ref[question, head, part, :] = (
            acc_ref[question, head, part, :] * alpha + mixed[:, :HD]
        )


def attend_kernel(first, last, rounds, most, *refs):
    refs = list(refs)
    recv_ref, q_ref = refs.pop(0), refs.pop(0)
    if first:
        row_ref, own_ref, cache_ref = refs.pop(0), refs.pop(0), refs.pop(0)
        sources = None
        entries = most
    else:
        state_in = [refs.pop(0) for _ in range(3)]
        sources = [refs.pop(0) for _ in rounds]
        entries = len(rounds) * most
    if last:
        out_ref = refs.pop(0)
        m_ref, l_ref, acc_ref = [refs.pop(0) for _ in range(3)]
    else:
        m_ref, l_ref, acc_ref = [refs.pop(0) for _ in range(3)]
    buf, sem = refs
    per_device, heads = q_ref.shape[0], q_ref.shape[1]

    def fetch(i, slot):
        if first:
            pltpu.make_async_copy(cache_ref.at[row_ref[i]], buf.at[slot], sem.at[slot]).start()
            return
        for j in range(len(rounds)):

            @pl.when(i // most == j)
            def _():
                pltpu.make_async_copy(
                    sources[j].at[i - j * most], buf.at[slot], sem.at[slot]
                ).start()

    def tag_of(i):
        if first:
            return recv_ref[i]
        k = jnp.int32(0)
        for j, value in enumerate(rounds):
            k = jnp.where(i // most == j, value, k)
        return recv_ref[k * most + lax.rem(i, most)]

    fetch(jnp.int32(0), 0)
    if first:
        m_ref[...] = jnp.full(m_ref.shape, NEG, jnp.float32)
        l_ref[...] = jnp.zeros(l_ref.shape, jnp.float32)
        acc_ref[...] = jnp.zeros(acc_ref.shape, jnp.float32)

        def own_block(question, carry):
            for head in range(heads):
                block = own_ref[question, head]
                block_step(
                    q_ref, m_ref, l_ref, acc_ref, question, head, block[:, :HD], block[:, HD:], True
                )
            return carry

        lax.fori_loop(0, per_device, own_block, 0)
    else:
        m_ref[...] = state_in[0][...]
        l_ref[...] = state_in[1][...]
        acc_ref[...] = state_in[2][...]

    def item(i, carry):
        slot = lax.rem(i, 2)
        pltpu.make_async_copy(buf.at[slot], buf.at[slot], sem.at[slot]).wait()

        @pl.when(i + 1 < entries)
        def _():
            fetch(i + 1, lax.rem(i + 1, 2))

        tag = tag_of(i)

        @pl.when(tag >= 0)
        def _():
            for head in range(heads):
                block_step(
                    q_ref,
                    m_ref,
                    l_ref,
                    acc_ref,
                    tag,
                    head,
                    buf[slot, head, :, :HD],
                    buf[slot, head, :, HD:],
                    False,
                )

        return carry

    lax.fori_loop(0, entries, item, 0)
    if last:
        for question in range(per_device):
            for head in range(heads):
                for g in range(GROUP):
                    part = pl.ds(g * LQ, LQ)
                    column = (head * GROUP + g) * HD
                    out_ref[pl.ds(question * LQ, LQ), pl.ds(column, HD)] = (
                        acc_ref[question, head, part, :] / l_ref[question, head, part, :]
                    ).astype(out_ref.dtype)


def attend_call(first, last, rounds, most, recv, q, rest, item):
    per_device, heads, rows, _ = q.shape
    state = jax.ShapeDtypeStruct(q.shape, jnp.float32)
    smem = pl.BlockSpec(memory_space=pltpu.SMEM)
    vmem = pl.BlockSpec(memory_space=pltpu.VMEM)
    anyspace = pl.BlockSpec(memory_space=pl.ANY)
    if first:
        in_specs = [smem, vmem, smem, vmem, anyspace]
        entries = most
    else:
        in_specs = [smem, vmem] + [vmem] * 3 + [anyspace] * len(rounds)
        entries = most * len(rounds)
    scratch = [pltpu.VMEM((2,) + item, q.dtype), pltpu.SemaphoreType.DMA((2,))]
    if last:
        out_shape = jax.ShapeDtypeStruct((per_device * LQ, heads * GROUP * HD), q.dtype)
        out_specs = vmem
        scratch = [pltpu.VMEM(q.shape, jnp.float32)] * 3 + scratch
    else:
        out_shape = [state] * 3
        out_specs = [vmem] * 3
    weights = entries * heads * rows * item[1]
    return pl.pallas_call(
        functools.partial(attend_kernel, first, last, rounds, most),
        out_shape=out_shape,
        in_specs=in_specs,
        out_specs=out_specs,
        scratch_shapes=scratch,
        name="attend_first" if first else ("attend_last" if last else "attend_more"),
        cost_estimate=pl.CostEstimate(
            flops=weights * HD * 4,
            bytes_accessed=entries * math.prod(item) * 2,
            transcendentals=weights,
        ),
    )(recv, q, *rest)


def weight_blocks(own, n):
    if n & (n - 1):
        return [lax.all_gather(own, "pass", axis=1, tiled=True)]
    have = {0: own}
    bit = n // 2
    while bit:
        for k in list(have):
            have[k ^ bit] = lax.ppermute(have[k], "pass", pairs_of(bit, n))
        bit //= 2
    return [have[k] for k in range(n)]


def project(context, weights):
    parts = [
        jnp.dot(context, weight, preferred_element_type=jnp.float32).astype(jnp.bfloat16)
        for weight in weights
    ]
    me = lax.axis_index("pass")
    bit = len(parts) // 2
    while bit:
        swap = (me & bit) != 0
        parts = [jnp.where(swap, parts[k ^ bit], parts[k]) for k in range(len(parts))]
        bit //= 2
    return jnp.concatenate(parts, axis=1)


def body(queries, own_kv, passage_cache, out_weight, lists, passage_slot, question_slot):
    n = lax.axis_size("pass")
    per_device = queries.shape[0] // LQ
    heads = own_kv.shape[1]
    entries = per_device * lists.shape[1]
    most = (entries + n - 1) // n
    order = order_of(n)
    cache = jnp.transpose(passage_cache, (0, 2, 1, 3))
    recv, own_row, *items = gather(
        lists, passage_slot, question_slot, cache, n, most, per_device, order
    )
    arrived = [
        lax.ppermute(item, "pass", pairs_of(k, n)) for k, item in zip(order, items)
    ]
    weights = weight_blocks(out_weight, n)
    q = (
        queries.reshape(per_device, LQ, heads, GROUP, HD)
        .transpose(0, 2, 3, 1, 4)
        .reshape(per_device, heads, GROUP * LQ, HD)
    )
    own = own_kv.reshape(per_device, LQ, heads, 2 * HD).transpose(0, 2, 1, 3)
    item = cache.shape[1:]
    state = attend_call(True, False, (0,), most, recv, q, (own_row, own, cache), item)
    calls = 3
    bounds = [len(order) * i // calls for i in range(calls + 1)]
    for i in range(calls):
        rounds = tuple(order[bounds[i] : bounds[i + 1]])
        rest = tuple(state) + tuple(arrived[bounds[i] : bounds[i + 1]])
        state = attend_call(False, i == calls - 1, rounds, most, recv, q, rest, item)
    context = state
    return lax.psum_scatter(project(context, weights), "head", scatter_dimension=1, tiled=True)


LINE = 4
EXTRA = 16


def mirror(k, ends=None):
    pairs = [(p, p ^ int(2 * k)) for p in range(2 * LINE)]
    if ends is None:
        return pairs
    return [(p, d) for p, d in pairs if (p // 2 in (0, LINE - 1)) == (ends == "outer")]


def is_inner():
    z = lax.axis_index("pass") // 2
    return jnp.logical_and(z > 0, z < LINE - 1)


def sort_kernel(most, per_device, lists_ref, pslot_ref, qslot_ref, cache_ref, *refs):
    row_ref, tag_ref, far_tag_ref = refs[:3]
    outs = refs[3 : 3 + LINE]
    send_row, near_cnt, send_cnt, far_cnt, buf, in_sem, out_sem = refs[3 + LINE :]
    me = lax.axis_index("pass")
    z, x = me // 2, me % 2
    pass_dev = cache_ref.shape[0]
    topp, nq = lists_ref.shape
    for k in range(LINE):
        near_cnt[k] = 0
        send_cnt[k] = 0
        far_cnt[k] = 0

    def question(q, carry):
        slot = qslot_ref[q]
        dest = slot // per_device
        local = slot - dest * per_device
        k = (dest // 2) ^ z
        same = dest % 2 == x
        for t in range(topp):
            row = pslot_ref[lists_ref[t, q]]
            owner = row // pass_dev
            mine = owner == me

            @pl.when(jnp.logical_and(mine, same))
            def _():
                at = k * most + near_cnt[k]
                row_ref[at] = row - owner * pass_dev
                tag_ref[at] = local
                near_cnt[k] = near_cnt[k] + 1

            @pl.when(jnp.logical_and(mine, jnp.logical_not(same)))
            def _():
                send_row[k * most + send_cnt[k]] = row - owner * pass_dev
                send_cnt[k] = send_cnt[k] + 1

            @pl.when(jnp.logical_and(owner == (me ^ 1), same))
            def _():
                far_tag_ref[k * most + far_cnt[k]] = local
                far_cnt[k] = far_cnt[k] + 1

        return carry

    lax.fori_loop(0, nq, question, 0)
    copies = []
    for k in (1, 2, 3, 0):
        for r in range(most):
            i = k * most + r
            get = pltpu.make_async_copy(cache_ref.at[send_row[i]], buf.at[i], in_sem.at[i])
            get.start()
            copies.append((get, pltpu.make_async_copy(buf.at[i], outs[k].at[r], out_sem.at[i])))
    for get, put in copies:
        get.wait()
        put.start()
    for get, put in copies:
        put.wait()


def sort_items(lists, passage_slot, question_slot, cache, most, per_device):
    item = cache.shape[1:]
    slots = LINE * most
    smem = pl.BlockSpec(memory_space=pltpu.SMEM)
    anyspace = pl.BlockSpec(memory_space=pl.ANY)
    return pl.pallas_call(
        functools.partial(sort_kernel, most, per_device),
        out_shape=[jax.ShapeDtypeStruct((slots,), jnp.int32)] * 3
        + [jax.ShapeDtypeStruct((most,) + item, cache.dtype)] * LINE,
        in_specs=[smem, smem, smem, anyspace],
        out_specs=[smem] * 3 + [anyspace] * LINE,
        scratch_shapes=[
            pltpu.SMEM((slots,), jnp.int32),
            pltpu.SMEM((LINE,), jnp.int32),
            pltpu.SMEM((LINE,), jnp.int32),
            pltpu.SMEM((LINE,), jnp.int32),
            pltpu.VMEM((slots,) + item, cache.dtype),
            pltpu.SemaphoreType.DMA((slots,)),
            pltpu.SemaphoreType.DMA((slots,)),
        ],
        name="sort_items",
        cost_estimate=pl.CostEstimate(
            flops=0, bytes_accessed=2 * slots * math.prod(item) * 2, transcendentals=0
        ),
    )(lists.T, passage_slot, question_slot, cache)


def unit():
    r = lax.broadcasted_iota(jnp.int32, (LQ, LQ), 0)
    c = lax.broadcasted_iota(jnp.int32, (LQ, LQ), 1)
    return r == c


def part_step(q_ref, m_ref, l_ref, acc_ref, question, head, keys, values, causal):
    rows = GROUP * LQ
    width = keys.shape[0]
    ones = jnp.ones(values.shape, values.dtype)
    extended = jnp.concatenate([values, ones], axis=1)
    tokens = pl.ds(pl.multiple_of(question * LQ, LQ), LQ)
    for start in range(0, rows, ROWS):
        part = pl.ds(start, ROWS)
        q = jnp.concatenate(
            [
                q_ref[tokens, pl.ds(pl.multiple_of((head * GROUP + g) * HD, HD), HD)]
                for g in range(start // LQ, (start + ROWS) // LQ)
            ],
            axis=0,
        )
        scores = (
            lax.dot_general(q, keys, (((1,), (1,)), ((), ())), preferred_element_type=jnp.float32)
            * COEF
        )
        if causal:
            token = lax.broadcasted_iota(jnp.int32, scores.shape, 0) % LQ
            column = lax.broadcasted_iota(jnp.int32, scores.shape, 1)
            scores = jnp.where(column <= token, scores, NEG)
        old = m_ref[question, head, part, :]
        new = jnp.maximum(old, jnp.max(scores, axis=1, keepdims=True))
        weights = jnp.exp2(scores - jnp.concatenate([new] * (width // HD), axis=1))
        mixed = jnp.dot(
            weights.astype(jnp.bfloat16), extended, preferred_element_type=jnp.float32
        )
        alpha = jnp.exp2(old - new)
        m_ref[question, head, part, :] = new
        l_ref[question, head, part, :] = l_ref[question, head, part, :] * alpha + mixed[:, HD:]
        acc_ref[question, head, part, :] = (
            acc_ref[question, head, part, :] * alpha + mixed[:, :HD]
        )


def part_kernel(k, most, heads, *refs):
    refs = list(refs)
    row_ref, tag_ref, far_tag_ref = refs.pop(0), refs.pop(0), refs.pop(0)
    own_ref = refs.pop(0) if k == 0 else None
    questions = [refs.pop(0) for _ in range(2 if k > 1 else 1)]
    cache_ref, items_ref, out_ref, q_ref, m_ref, l_ref, acc_ref, buf, sem, q_sem = refs
    per_device = q_ref.shape[0] // LQ
    entries = 2 * most

    def fetch(i, slot):
        @pl.when(i < most)
        def _():
            row = row_ref[k * most + jnp.minimum(i, most - 1)]
            pltpu.make_async_copy(cache_ref.at[row], buf.at[slot], sem.at[slot]).start()

        @pl.when(i >= most)
        def _():
            pltpu.make_async_copy(
                items_ref.at[jnp.maximum(i - most, 0)], buf.at[slot], sem.at[slot]
            ).start()

    if len(questions) == 1:
        pltpu.make_async_copy(questions[0], q_ref, q_sem).start()
    else:
        inner = is_inner()

        @pl.when(inner)
        def _():
            pltpu.make_async_copy(questions[0], q_ref, q_sem).start()

        @pl.when(jnp.logical_not(inner))
        def _():
            pltpu.make_async_copy(questions[1], q_ref, q_sem).start()

    fetch(jnp.int32(0), 0)
    m_ref[...] = jnp.full(m_ref.shape, NEG, jnp.float32)
    l_ref[...] = jnp.zeros(l_ref.shape, jnp.float32)
    acc_ref[...] = jnp.zeros(acc_ref.shape, jnp.float32)
    pltpu.make_async_copy(q_ref, q_ref, q_sem).wait()
    if k == 0:

        def own_block(i, carry):
            question, head = i // heads, lax.rem(i, heads)
            part_step(
                q_ref,
                m_ref,
                l_ref,
                acc_ref,
                question,
                head,
                own_ref[question, head, :, :HD],
                own_ref[question, head, :, HD:],
                True,
            )
            return carry

        lax.fori_loop(0, per_device * heads, own_block, 0)

    def item(i, carry):
        slot = lax.rem(i, 2)
        pltpu.make_async_copy(buf.at[slot], buf.at[slot], sem.at[slot]).wait()

        @pl.when(i + 1 < entries)
        def _():
            fetch(i + 1, lax.rem(i + 1, 2))

        at = k * most + lax.rem(i, most)
        tag = jnp.where(i < most, tag_ref[at], far_tag_ref[at])

        for head in range(heads):
            part_step(
                q_ref,
                m_ref,
                l_ref,
                acc_ref,
                tag,
                head,
                buf[slot, head, :, :HD],
                buf[slot, head, :, HD:],
                False,
            )
        return carry

    lax.fori_loop(0, entries, item, 0)
    eye = unit()

    def close(c, carry):
        head, g = c // GROUP, lax.rem(c, GROUP)
        columns = pl.ds(pl.multiple_of(c * HD, HD), HD)
        part = pl.ds(pl.multiple_of(g * LQ, LQ), LQ)
        for question in range(per_device):
            total = l_ref[question, head, part, :]
            some = total > 0.0
            safe = jnp.where(some, total, 1.0)
            out_ref[question, :LQ, columns] = (
                acc_ref[question, head, part, :] / safe
            ).astype(out_ref.dtype)
            level = jnp.where(some, m_ref[question, head, part, :] + jnp.log2(safe), NEG)
            line = jnp.sum(jnp.where(eye, level, 0.0), axis=0, keepdims=True)
            store_level(out_ref, question, columns, line)
        return carry

    lax.fori_loop(0, heads * GROUP, close, 0)


def store_level(out_ref, question, columns, line):
    row_of = lax.broadcasted_iota(jnp.int32, (EXTRA, line.shape[1]), 0)
    high = line.astype(jnp.bfloat16).astype(jnp.float32)
    both = jnp.where(row_of == 0, high, jnp.where(row_of == EXTRA // 2, line - high, 0.0))
    out_ref[question, LQ:, columns] = both.astype(out_ref.dtype)


def part_call(k, most, tables, own, questions, cache, items):
    tokens, columns = questions[0].shape
    heads, item = cache.shape[1], cache.shape[1:]
    state = (tokens // LQ, heads, GROUP * LQ, HD)
    smem = pl.BlockSpec(memory_space=pltpu.SMEM)
    vmem = pl.BlockSpec(memory_space=pltpu.VMEM)
    anyspace = pl.BlockSpec(memory_space=pl.ANY)
    owned = [own] if k == 0 else []
    weights = 2 * most * heads * GROUP * LQ * item[1]
    return pl.pallas_call(
        functools.partial(part_kernel, k, most, heads),
        out_shape=jax.ShapeDtypeStruct((tokens // LQ, LQ + EXTRA, columns), cache.dtype),
        in_specs=[smem] * 3 + [vmem] * len(owned) + [anyspace] * (len(questions) + 2),
        out_specs=vmem,
        scratch_shapes=[
            pltpu.VMEM((tokens, columns), cache.dtype),
            pltpu.VMEM(state, jnp.float32),
            pltpu.VMEM(state, jnp.float32),
            pltpu.VMEM(state, jnp.float32),
            pltpu.VMEM((2,) + item, cache.dtype),
            pltpu.SemaphoreType.DMA((2,)),
            pltpu.SemaphoreType.DMA,
        ],
        cost_estimate=pl.CostEstimate(
            flops=weights * HD * 4,
            bytes_accessed=2 * most * math.prod(item) * 2,
            transcendentals=weights,
        ),
    )(*tables, *owned, *questions, cache, items)


def blend(a_ref, b_ref, out_ref, leveled):
    eye = unit()
    ones = jnp.ones((2 * LQ, LQ), jnp.bfloat16)

    def level_of(ref):
        both = ref[0, LQ:, :].astype(jnp.float32)
        return both[:1] + both[EXTRA // 2 : EXTRA // 2 + 1]

    one, two = level_of(a_ref), level_of(b_ref)
    top = jnp.maximum(one, two)
    first, second = jnp.exp2(one - top), jnp.exp2(two - top)
    total = first + second
    share = first / total
    high = share.astype(jnp.bfloat16).astype(jnp.float32)
    low = share - high
    for c in range(share.shape[1] // HD):
        columns = slice(c * HD, (c + 1) * HD)
        spread = jnp.concatenate(
            [
                jnp.where(eye, jnp.broadcast_to(v[:, columns], (LQ, LQ)), 0.0).astype(jnp.bfloat16)
                for v in (high, low)
            ],
            axis=1,
        )
        column = jnp.dot(spread, ones, preferred_element_type=jnp.float32)
        a = a_ref[0, :LQ, columns].astype(jnp.float32)
        b = b_ref[0, :LQ, columns].astype(jnp.float32)
        value = (b + (a - b) * column).astype(out_ref.dtype)
        if leveled:
            out_ref[0, :LQ, columns] = value
        else:
            out_ref[:, columns] = value
    if leveled:
        store_level(out_ref, 0, slice(None), top + jnp.log2(total))


def merge_kernel(a_ref, b_ref, out_ref):
    inner = is_inner()

    @pl.when(inner)
    def _():
        blend(a_ref, b_ref, out_ref, True)

    @pl.when(jnp.logical_not(inner))
    def _():
        out_ref[...] = a_ref[...]


def finish_kernel(a_ref, b_ref, out_ref):
    blend(a_ref, b_ref, out_ref, False)


def question_spec(value, at):
    shape = (1,) + value.shape[1:]
    if value.shape[0] == 1:
        return pl.BlockSpec(shape, lambda q: (0, 0, 0))
    if at is None:
        return pl.BlockSpec(shape, lambda q: (q, 0, 0))
    return pl.BlockSpec(shape, lambda q: (at, 0, 0))


def join_call(a, b, at, leveled):
    questions = a.shape[0] if at is None else 1
    columns = a.shape[2]
    if leveled:
        shape, block = (questions,) + a.shape[1:], (1,) + a.shape[1:]
        out_spec = pl.BlockSpec(block, lambda q: (q, 0, 0))
    else:
        shape = (questions * LQ, columns)
        out_spec = pl.BlockSpec((LQ, columns), lambda q: (q, 0))
    size = questions * LQ * columns
    return pl.pallas_call(
        merge_kernel if leveled else finish_kernel,
        out_shape=jax.ShapeDtypeStruct(shape, a.dtype),
        grid=(questions,),
        in_specs=[question_spec(a, at), question_spec(b, at)],
        out_specs=out_spec,
        cost_estimate=pl.CostEstimate(flops=size * 8, bytes_accessed=size * 6, transcendentals=0),
    )(a, b)


def line_steps(queries, own_kv, passage_cache, out_weight, lists, passage_slot, question_slot):
    per_device = queries.shape[0] // LQ
    heads = own_kv.shape[1]
    most = per_device * lists.shape[1] // (2 * LINE)
    half = out_weight.shape[0] // 2

    def send(value, pairs):
        return lax.ppermute(value, "pass", pairs)

    def part(k, *args):
        return part_call(k, most, tables, own if k == 0 else None, *args)

    def join(a, b, at=None, leveled=True):
        return join_call(a, b, at, leveled)

    across = [(p, p ^ 1) for p in range(2 * LINE)]
    inner_across = [(p, d) for p, d in across if p // 2 in (1, 2)]
    outer_across = [(p, d) for p, d in across if p // 2 not in (1, 2)]
    near, middle = mirror(1), mirror(3, "inner")
    inward, outward = mirror(1, "outer"), mirror(1, "inner")
    q_near = send(queries, near)
    q_mid = send(queries, middle)
    w_across0 = send(out_weight[:half], across)
    w_across1 = send(out_weight[half:], across)
    cache = jnp.transpose(passage_cache, (0, 2, 1, 3))
    row, tag, far_tag, *items = sort_items(
        lists, passage_slot, question_slot, cache, most, per_device
    )
    tables = (row, tag, far_tag)
    q_out = send(q_mid, outward)
    q_cross = send(q_near, middle)
    q_end = send(q_cross, outward)
    far = [send(items[k], across) for k in range(LINE)]
    own = own_kv.reshape(per_device, LQ, heads, 2 * HD).transpose(0, 2, 1, 3)
    part2 = part(2, [q_cross, q_out], cache, far[2])
    part3 = part(3, [q_mid, q_end], cache, far[3])
    part0 = part(0, [queries], cache, far[0])
    part1 = part(1, [q_near], cache, far[1])
    back2 = send(part2, inward)
    w_in = send(out_weight, mirror(2, "outer"))
    w_out = send(out_weight, mirror(2, "inner"))
    back3 = send(part3, inward)
    w_in_both = send(w_in, inner_across)
    w_out_both = send(w_out, outer_across)
    cross3 = send(join(part3, back2), middle)
    near0 = join(part0, cross3)
    beside = send(near0, near)
    own_rows, near_rows = [], []
    for q in range(per_device):
        cross2 = send(join(part2, back3, q), middle)
        near1 = join(part1, cross2, q)
        back1 = send(near1, near)
        near_rows.append(join(near1, beside, q, False))
        own_rows.append(join(near0, back1, q, False))
    return project_call(
        own_rows + near_rows,
        out_weight,
        w_across0,
        w_across1,
        w_in,
        w_in_both,
        w_out,
        w_out_both,
    )


MESH = pl.DeviceIdType.MESH


def project_kernel(pieces, *refs):
    rows_refs = refs[:pieces]
    own_ref, a0_ref, a1_ref, in_ref, in2_ref, out1_ref, out2_ref = refs[pieces : pieces + 7]
    refs = refs[pieces + 7 :]
    out_ref, context_ref, w_ref, part_ref, core_ref, y_ref, ysend_ref, zsend_ref = refs[:8]
    row_sem, w_sem, send_sem, recv_sem = refs[8:]
    me, head = lax.axis_index("pass"), lax.axis_index("head")
    z, x, y, core = me // 2, me % 2, head // 2, head % 2
    rows, wide = out_ref.shape[0], w_ref.shape[3]
    half = a0_ref.shape[0]
    inner = is_inner()
    core_peer = (me, head ^ 1)
    y_peer = (me, head ^ 2)
    z_peer = (me ^ 2, head ^ 1)
    stays = core == z % 2

    row_loads = [
        pltpu.make_async_copy(ref, context_ref.at[pl.ds(i * LQ, LQ)], row_sem.at[i])
        for i, ref in enumerate(rows_refs)
    ]
    for load in row_loads:
        load.start()

    def load_here():
        pltpu.make_async_copy(own_ref, w_ref.at[0, x], w_sem.at[0, x]).start()
        low, high = w_ref.at[0, 1 - x, pl.ds(0, half)], w_ref.at[0, 1 - x, pl.ds(half, half)]
        pltpu.make_async_copy(a0_ref, low, w_sem.at[0, 1 - x]).start()
        pltpu.make_async_copy(a1_ref, high, w_sem.at[0, 1 - x]).start()

    def load_there():
        for which, (one, two) in (
            (inner, (in_ref, in2_ref)),
            (jnp.logical_not(inner), (out1_ref, out2_ref)),
        ):

            @pl.when(which)
            def _():
                pltpu.make_async_copy(one, w_ref.at[1, x], w_sem.at[1, x]).start()
                pltpu.make_async_copy(two, w_ref.at[1, 1 - x], w_sem.at[1, 1 - x]).start()

    load_here()
    load_there()
    barrier = pltpu.get_barrier_semaphore()
    for peer in (core_peer, y_peer, z_peer):
        pl.semaphore_signal(barrier, inc=1, device_id=peer, device_id_type=MESH)
    pl.semaphore_wait(barrier, 3)

    def remote(src, dst, i, peer):
        return pltpu.make_async_remote_copy(
            src_ref=src,
            dst_ref=dst,
            send_sem=send_sem.at[i],
            recv_sem=recv_sem.at[i],
            device_id=peer,
            device_id_type=MESH,
        )

    def columns(j):
        return pl.ds(j * wide, wide)

    core_copies = [
        [remote(part_ref.at[s, j], core_ref.at[s, j], s * 2 + j, core_peer) for j in range(2)]
        for s in range(2)
    ]
    y_copies = [remote(ysend_ref.at[j], y_ref.at[j], 4 + j, y_peer) for j in range(2)]
    z_copies = [remote(zsend_ref.at[j], out_ref.at[:, columns(j)], 6 + j, z_peer) for j in range(2)]

    for load in row_loads:
        load.wait()

    def product(to_y, to_core, j):
        start = pl.multiple_of(jnp.where(to_core == z % 2, 0, rows), LQ)
        here = jnp.where(to_y == z // 2, 0, 1)
        return jnp.dot(
            context_ref[pl.ds(start, rows), :],
            w_ref[here, j],
            preferred_element_type=jnp.float32,
        ).astype(jnp.bfloat16)

    for s, to_y in enumerate((1 - y, y)):
        here = jnp.where(to_y == z // 2, 0, 1)
        for j in range(2):
            block = w_ref.at[here, j]
            pltpu.make_async_copy(block, block, w_sem.at[here, j]).wait()
            part_ref[s, j] = product(to_y, 1 - core, j)
            core_copies[s][j].start()
            value = product(to_y, core, j).astype(jnp.float32)
            core_copies[s][j].wait_recv()
            value = value + core_ref[s, j].astype(jnp.float32)
            if s == 0:
                ysend_ref[j] = value.astype(jnp.bfloat16)
                y_copies[j].start()
            else:
                y_copies[j].wait_recv()
                total = (value + y_ref[j].astype(jnp.float32)).astype(jnp.bfloat16)

                @pl.when(stays)
                def _():
                    out_ref[:, columns(j)] = total

                @pl.when(jnp.logical_not(stays))
                def _():
                    zsend_ref[j] = total
                    z_copies[j].start()

    @pl.when(jnp.logical_not(stays))
    def _():
        for copy in z_copies:
            copy.wait()

    for copies in core_copies + [y_copies]:
        for copy in copies:
            copy.wait_send()


def project_call(pieces, own, a0, a1, *lines):
    rows, depth = len(pieces) // 2 * LQ, own.shape[0]
    wide = own.shape[1]
    dtype = own.dtype
    anyspace = pl.BlockSpec(memory_space=pl.ANY)
    return pl.pallas_call(
        functools.partial(project_kernel, len(pieces)),
        out_shape=jax.ShapeDtypeStruct((rows, 2 * wide), dtype),
        in_specs=[anyspace] * (len(pieces) + 7),
        out_specs=pl.BlockSpec(memory_space=pltpu.VMEM),
        scratch_shapes=[
            pltpu.VMEM((2 * rows, depth), dtype),
            pltpu.VMEM((2, 2, depth, wide), dtype),
            pltpu.VMEM((2, 2, rows, wide), dtype),
            pltpu.VMEM((2, 2, rows, wide), dtype),
            pltpu.VMEM((2, rows, wide), dtype),
            pltpu.VMEM((2, rows, wide), dtype),
            pltpu.VMEM((2, rows, wide), dtype),
            pltpu.SemaphoreType.DMA((len(pieces),)),
            pltpu.SemaphoreType.DMA((2, 2)),
            pltpu.SemaphoreType.DMA((8,)),
            pltpu.SemaphoreType.DMA((8,)),
        ],
        compiler_params=pltpu.CompilerParams(collective_id=0, has_side_effects=True),
        name="project_sum",
        cost_estimate=pl.CostEstimate(
            flops=2 * 4 * 2 * rows * depth * wide,
            bytes_accessed=4 * depth * wide * 2,
            transcendentals=0,
        ),
    )(*pieces, own, a0, a1, *lines)


def suits_line(mesh, queries, lists):
    passes, heads = mesh.shape["pass"], mesh.shape["head"]
    entries = queries.shape[0] // LQ // passes * lists.shape[1]
    return passes == 2 * LINE and heads == LINE and entries % passes == 0


def solution(mesh):
    in_specs = (
        P("pass", "head"),
        P("pass", "head", None),
        P("pass", None, "head", None),
        P("head", "pass"),
        P(),
        P(),
        P(),
    )
    out_specs = P("pass", "head")

    def run(*args):
        if not suits_line(mesh, args[0], args[4]):
            return jax.shard_map(
                body, mesh=mesh, in_specs=in_specs, out_specs=out_specs, check_vma=False
            )(*args)
        step = jax.shard_map(
            line_steps, mesh=mesh, in_specs=in_specs, out_specs=out_specs, check_vma=False
        )
        return step(*args)

    return run
```

```python
import functools
import math

import jax
import jax.numpy as jnp
from jax import lax
from jax.experimental import pallas as pl
from jax.experimental.pallas import tpu as pltpu
from jax.sharding import PartitionSpec as P


H = 64
KVH = 8
HD = 128
LQ = 128
GROUP = H // KVH
COEF = HD ** (-0.5) * math.log2(math.e)
NEG = -1e30
ROWS = 256


def round_of(a, b, n):
    if n & (n - 1) == 0:
        return a ^ b
    return lax.rem(b - a + n, n)


def pairs_of(k, n):
    if n & (n - 1) == 0:
        return [(p, p ^ k) for p in range(n)]
    return [(p, (p + k) % n) for p in range(n)]


def order_of(n):
    rest = range(1, n)
    return sorted(rest, key=lambda k: (bin(k).count("1"), k))


def gather_kernel(n, most, per_device, order, lists_ref, pslot_ref, qslot_ref, cache_ref, *refs):
    recv_ref, own_row_ref = refs[0], refs[1]
    outs = refs[2 : 2 + len(order)]
    send_row, send_cnt, recv_cnt, buf, in_sem, out_sem = refs[2 + len(order) :]
    me = lax.axis_index("pass")
    pass_dev = cache_ref.shape[0]
    topp, nq = lists_ref.shape
    for k in range(n):
        send_cnt[k] = 0
        recv_cnt[k] = 0
    for i in range(n * most):
        recv_ref[i] = -1
        send_row[i] = 0

    def question(q, carry):
        slot = qslot_ref[q]
        dest = slot // per_device
        local = slot - dest * per_device
        k_send = round_of(me, dest, n)
        for t in range(topp):
            row = pslot_ref[lists_ref[t, q]]
            owner = row // pass_dev

            @pl.when(owner == me)
            def _():
                count = send_cnt[k_send]
                send_row[k_send * most + count] = row - owner * pass_dev
                send_cnt[k_send] = count + 1

            @pl.when(dest == me)
            def _():
                k = round_of(owner, me, n)
                count = recv_cnt[k]
                recv_ref[k * most + count] = local
                recv_cnt[k] = count + 1

        return carry

    lax.fori_loop(0, nq, question, 0)
    for r in range(most):
        own_row_ref[r] = send_row[r]
    copies = []
    for j, k in enumerate(order):
        for r in range(most):
            i = j * most + r
            get = pltpu.make_async_copy(
                cache_ref.at[send_row[k * most + r]], buf.at[i], in_sem.at[i]
            )
            get.start()
            copies.append((get, pltpu.make_async_copy(buf.at[i], outs[j].at[r], out_sem.at[i])))
    for get, put in copies:
        get.wait()
        put.start()
    for get, put in copies:
        put.wait()


def gather(lists, passage_slot, question_slot, cache, n, most, per_device, order):
    item = cache.shape[1:]
    slots = (n - 1) * most
    smem = pl.BlockSpec(memory_space=pltpu.SMEM)
    anyspace = pl.BlockSpec(memory_space=pl.ANY)
    return pl.pallas_call(
        functools.partial(gather_kernel, n, most, per_device, order),
        out_shape=[
            jax.ShapeDtypeStruct((n * most,), jnp.int32),
            jax.ShapeDtypeStruct((most,), jnp.int32),
        ]
        + [jax.ShapeDtypeStruct((most,) + item, cache.dtype)] * len(order),
        in_specs=[smem, smem, smem, anyspace],
        out_specs=[smem, smem] + [anyspace] * len(order),
        scratch_shapes=[
            pltpu.SMEM((n * most,), jnp.int32),
            pltpu.SMEM((n,), jnp.int32),
            pltpu.SMEM((n,), jnp.int32),
            pltpu.VMEM((slots,) + item, cache.dtype),
            pltpu.SemaphoreType.DMA((slots,)),
            pltpu.SemaphoreType.DMA((slots,)),
        ],
        name="gather_items",
        cost_estimate=pl.CostEstimate(
            flops=0, bytes_accessed=2 * slots * math.prod(item) * 2, transcendentals=0
        ),
    )(lists.T, passage_slot, question_slot, cache)


def block_step(q_ref, m_ref, l_ref, acc_ref, question, head, keys, values, causal):
    rows = q_ref.shape[2]
    step = min(ROWS, rows)
    width = keys.shape[0]
    ones = jnp.ones(values.shape, values.dtype)
    extended = jnp.concatenate([values, ones], axis=1)
    for start in range(0, rows, step):
        part = pl.ds(start, step)
        q = q_ref[question, head, part, :]
        scores = (
            lax.dot_general(q, keys, (((1,), (1,)), ((), ())), preferred_element_type=jnp.float32)
            * COEF
        )
        if causal:
            token = lax.broadcasted_iota(jnp.int32, scores.shape, 0) % LQ
            column = lax.broadcasted_iota(jnp.int32, scores.shape, 1)
            scores = jnp.where(column <= token, scores, NEG)
        old = m_ref[question, head, part, :]
        new = jnp.maximum(old, jnp.max(scores, axis=1, keepdims=True))
        weights = jnp.exp2(scores - jnp.concatenate([new] * (width // HD), axis=1))
        mixed = jnp.dot(
            weights.astype(jnp.bfloat16), extended, preferred_element_type=jnp.float32
        )
        alpha = jnp.exp2(old - new)
        m_ref[question, head, part, :] = new
        l_ref[question, head, part, :] = l_ref[question, head, part, :] * alpha + mixed[:, HD:]
        acc_ref[question, head, part, :] = (
            acc_ref[question, head, part, :] * alpha + mixed[:, :HD]
        )


def attend_kernel(first, last, rounds, most, *refs):
    refs = list(refs)
    recv_ref, q_ref = refs.pop(0), refs.pop(0)
    if first:
        row_ref, own_ref, cache_ref = refs.pop(0), refs.pop(0), refs.pop(0)
        sources = None
        entries = most
    else:
        state_in = [refs.pop(0) for _ in range(3)]
        sources = [refs.pop(0) for _ in rounds]
        entries = len(rounds) * most
    if last:
        out_ref = refs.pop(0)
        m_ref, l_ref, acc_ref = [refs.pop(0) for _ in range(3)]
    else:
        m_ref, l_ref, acc_ref = [refs.pop(0) for _ in range(3)]
    buf, sem = refs
    per_device, heads = q_ref.shape[0], q_ref.shape[1]

    def fetch(i, slot):
        if first:
            pltpu.make_async_copy(cache_ref.at[row_ref[i]], buf.at[slot], sem.at[slot]).start()
            return
        for j in range(len(rounds)):

            @pl.when(i // most == j)
            def _():
                pltpu.make_async_copy(
                    sources[j].at[i - j * most], buf.at[slot], sem.at[slot]
                ).start()

    def tag_of(i):
        if first:
            return recv_ref[i]
        k = jnp.int32(0)
        for j, value in enumerate(rounds):
            k = jnp.where(i // most == j, value, k)
        return recv_ref[k * most + lax.rem(i, most)]

    fetch(jnp.int32(0), 0)
    if first:
        m_ref[...] = jnp.full(m_ref.shape, NEG, jnp.float32)
        l_ref[...] = jnp.zeros(l_ref.shape, jnp.float32)
        acc_ref[...] = jnp.zeros(acc_ref.shape, jnp.float32)

        def own_block(question, carry):
            for head in range(heads):
                block = own_ref[question, head]
                block_step(
                    q_ref, m_ref, l_ref, acc_ref, question, head, block[:, :HD], block[:, HD:], True
                )
            return carry

        lax.fori_loop(0, per_device, own_block, 0)
    else:
        m_ref[...] = state_in[0][...]
        l_ref[...] = state_in[1][...]
        acc_ref[...] = state_in[2][...]

    def item(i, carry):
        slot = lax.rem(i, 2)
        pltpu.make_async_copy(buf.at[slot], buf.at[slot], sem.at[slot]).wait()

        @pl.when(i + 1 < entries)
        def _():
            fetch(i + 1, lax.rem(i + 1, 2))

        tag = tag_of(i)

        @pl.when(tag >= 0)
        def _():
            for head in range(heads):
                block_step(
                    q_ref,
                    m_ref,
                    l_ref,
                    acc_ref,
                    tag,
                    head,
                    buf[slot, head, :, :HD],
                    buf[slot, head, :, HD:],
                    False,
                )

        return carry

    lax.fori_loop(0, entries, item, 0)
    if last:
        for question in range(per_device):
            for head in range(heads):
                for g in range(GROUP):
                    part = pl.ds(g * LQ, LQ)
                    column = (head * GROUP + g) * HD
                    out_ref[pl.ds(question * LQ, LQ), pl.ds(column, HD)] = (
                        acc_ref[question, head, part, :] / l_ref[question, head, part, :]
                    ).astype(out_ref.dtype)


def attend_call(first, last, rounds, most, recv, q, rest, item):
    per_device, heads, rows, _ = q.shape
    state = jax.ShapeDtypeStruct(q.shape, jnp.float32)
    smem = pl.BlockSpec(memory_space=pltpu.SMEM)
    vmem = pl.BlockSpec(memory_space=pltpu.VMEM)
    anyspace = pl.BlockSpec(memory_space=pl.ANY)
    if first:
        in_specs = [smem, vmem, smem, vmem, anyspace]
        entries = most
    else:
        in_specs = [smem, vmem] + [vmem] * 3 + [anyspace] * len(rounds)
        entries = most * len(rounds)
    scratch = [pltpu.VMEM((2,) + item, q.dtype), pltpu.SemaphoreType.DMA((2,))]
    if last:
        out_shape = jax.ShapeDtypeStruct((per_device * LQ, heads * GROUP * HD), q.dtype)
        out_specs = vmem
        scratch = [pltpu.VMEM(q.shape, jnp.float32)] * 3 + scratch
    else:
        out_shape = [state] * 3
        out_specs = [vmem] * 3
    weights = entries * heads * rows * item[1]
    return pl.pallas_call(
        functools.partial(attend_kernel, first, last, rounds, most),
        out_shape=out_shape,
        in_specs=in_specs,
        out_specs=out_specs,
        scratch_shapes=scratch,
        name="attend_first" if first else ("attend_last" if last else "attend_more"),
        cost_estimate=pl.CostEstimate(
            flops=weights * HD * 4,
            bytes_accessed=entries * math.prod(item) * 2,
            transcendentals=weights,
        ),
    )(recv, q, *rest)


def weight_blocks(own, n):
    if n & (n - 1):
        return [lax.all_gather(own, "pass", axis=1, tiled=True)]
    have = {0: own}
    bit = n // 2
    while bit:
        for k in list(have):
            have[k ^ bit] = lax.ppermute(have[k], "pass", pairs_of(bit, n))
        bit //= 2
    return [have[k] for k in range(n)]


def project(context, weights):
    parts = [
        jnp.dot(context, weight, preferred_element_type=jnp.float32).astype(jnp.bfloat16)
        for weight in weights
    ]
    me = lax.axis_index("pass")
    bit = len(parts) // 2
    while bit:
        swap = (me & bit) != 0
        parts = [jnp.where(swap, parts[k ^ bit], parts[k]) for k in range(len(parts))]
        bit //= 2
    return jnp.concatenate(parts, axis=1)


def body(queries, own_kv, passage_cache, out_weight, lists, passage_slot, question_slot):
    n = lax.axis_size("pass")
    per_device = queries.shape[0] // LQ
    heads = own_kv.shape[1]
    entries = per_device * lists.shape[1]
    most = (entries + n - 1) // n
    order = order_of(n)
    cache = jnp.transpose(passage_cache, (0, 2, 1, 3))
    recv, own_row, *items = gather(
        lists, passage_slot, question_slot, cache, n, most, per_device, order
    )
    arrived = [
        lax.ppermute(item, "pass", pairs_of(k, n)) for k, item in zip(order, items)
    ]
    weights = weight_blocks(out_weight, n)
    q = (
        queries.reshape(per_device, LQ, heads, GROUP, HD)
        .transpose(0, 2, 3, 1, 4)
        .reshape(per_device, heads, GROUP * LQ, HD)
    )
    own = own_kv.reshape(per_device, LQ, heads, 2 * HD).transpose(0, 2, 1, 3)
    item = cache.shape[1:]
    state = attend_call(True, False, (0,), most, recv, q, (own_row, own, cache), item)
    calls = 3
    bounds = [len(order) * i // calls for i in range(calls + 1)]
    for i in range(calls):
        rounds = tuple(order[bounds[i] : bounds[i + 1]])
        rest = tuple(state) + tuple(arrived[bounds[i] : bounds[i + 1]])
        state = attend_call(False, i == calls - 1, rounds, most, recv, q, rest, item)
    context = state
    return lax.psum_scatter(project(context, weights), "head", scatter_dimension=1, tiled=True)


LINE = 4
EXTRA = 8
VMEM_BYTES = 67043328


def mirror(k, ends=None):
    pairs = [(p, p ^ int(2 * k)) for p in range(2 * LINE)]
    if ends is None:
        return pairs
    return [(p, d) for p, d in pairs if (p // 2 in (0, LINE - 1)) == (ends == "outer")]


def is_inner():
    z = lax.axis_index("pass") // 2
    return jnp.logical_and(z > 0, z < LINE - 1)


def sort_kernel(most, per_device, lists_ref, pslot_ref, qslot_ref, cache_ref, *refs):
    row_ref, tag_ref, far_tag_ref = refs[:3]
    outs = refs[3 : 3 + LINE]
    send_row, near_cnt, send_cnt, far_cnt, buf, in_sem, out_sem = refs[3 + LINE :]
    me = lax.axis_index("pass")
    z, x = me // 2, me % 2
    pass_dev = cache_ref.shape[0]
    topp, nq = lists_ref.shape
    for k in range(LINE):
        near_cnt[k] = 0
        send_cnt[k] = 0
        far_cnt[k] = 0

    def question(q, carry):
        slot = qslot_ref[q]
        dest = slot // per_device
        local = slot - dest * per_device
        k = (dest // 2) ^ z
        same = dest % 2 == x
        for t in range(topp):
            row = pslot_ref[lists_ref[t, q]]
            owner = row // pass_dev
            mine = owner == me

            @pl.when(jnp.logical_and(mine, same))
            def _():
                at = k * most + near_cnt[k]
                row_ref[at] = row - owner * pass_dev
                tag_ref[at] = local
                near_cnt[k] = near_cnt[k] + 1

            @pl.when(jnp.logical_and(mine, jnp.logical_not(same)))
            def _():
                send_row[k * most + send_cnt[k]] = row - owner * pass_dev
                send_cnt[k] = send_cnt[k] + 1

            @pl.when(jnp.logical_and(owner == (me ^ 1), same))
            def _():
                far_tag_ref[k * most + far_cnt[k]] = local
                far_cnt[k] = far_cnt[k] + 1

        return carry

    lax.fori_loop(0, nq, question, 0)
    copies = []
    for k in (1, 2, 3, 0):
        for r in range(most):
            i = k * most + r
            get = pltpu.make_async_copy(cache_ref.at[send_row[i]], buf.at[i], in_sem.at[i])
            get.start()
            copies.append((get, pltpu.make_async_copy(buf.at[i], outs[k].at[r], out_sem.at[i])))
    for get, put in copies:
        get.wait()
        put.start()
    for get, put in copies:
        put.wait()


def sort_items(lists, passage_slot, question_slot, cache, most, per_device):
    item = cache.shape[1:]
    slots = LINE * most
    smem = pl.BlockSpec(memory_space=pltpu.SMEM)
    anyspace = pl.BlockSpec(memory_space=pl.ANY)
    return pl.pallas_call(
        functools.partial(sort_kernel, most, per_device),
        out_shape=[jax.ShapeDtypeStruct((slots,), jnp.int32)] * 3
        + [jax.ShapeDtypeStruct((most,) + item, cache.dtype)] * LINE,
        in_specs=[smem, smem, smem, anyspace],
        out_specs=[smem] * 3 + [anyspace] * LINE,
        scratch_shapes=[
            pltpu.SMEM((slots,), jnp.int32),
            pltpu.SMEM((LINE,), jnp.int32),
            pltpu.SMEM((LINE,), jnp.int32),
            pltpu.SMEM((LINE,), jnp.int32),
            pltpu.VMEM((slots,) + item, cache.dtype),
            pltpu.SemaphoreType.DMA((slots,)),
            pltpu.SemaphoreType.DMA((slots,)),
        ],
        compiler_params=pltpu.CompilerParams(vmem_limit_bytes=VMEM_BYTES),
        name="sort_items",
        cost_estimate=pl.CostEstimate(
            flops=0, bytes_accessed=2 * slots * math.prod(item) * 2, transcendentals=0
        ),
    )(lists.T, passage_slot, question_slot, cache)


def unit():
    r = lax.broadcasted_iota(jnp.int32, (LQ, LQ), 0)
    c = lax.broadcasted_iota(jnp.int32, (LQ, LQ), 1)
    return r == c


def part_step(q_ref, m_ref, l_ref, acc_ref, question, head, keys, values, causal):
    rows = GROUP * LQ
    width = keys.shape[0]
    ones = jnp.ones(values.shape, values.dtype)
    extended = jnp.concatenate([values, ones], axis=1)
    tokens = pl.ds(pl.multiple_of(question * LQ, LQ), LQ)
    for start in range(0, rows, ROWS):
        part = pl.ds(start, ROWS)
        q = jnp.concatenate(
            [
                q_ref[tokens, pl.ds(pl.multiple_of((head * GROUP + g) * HD, HD), HD)]
                for g in range(start // LQ, (start + ROWS) // LQ)
            ],
            axis=0,
        )
        scores = (
            lax.dot_general(q, keys, (((1,), (1,)), ((), ())), preferred_element_type=jnp.float32)
            * COEF
        )
        if causal:
            token = lax.broadcasted_iota(jnp.int32, scores.shape, 0) % LQ
            column = lax.broadcasted_iota(jnp.int32, scores.shape, 1)
            scores = jnp.where(column <= token, scores, NEG)
        old = m_ref[question, head, part, :]
        new = jnp.maximum(old, jnp.max(scores, axis=1, keepdims=True))
        weights = jnp.exp2(scores - jnp.concatenate([new] * (width // HD), axis=1))
        mixed = jnp.dot(
            weights.astype(jnp.bfloat16), extended, preferred_element_type=jnp.float32
        )
        alpha = jnp.exp2(old - new)
        m_ref[question, head, part, :] = new
        l_ref[question, head, part, :] = l_ref[question, head, part, :] * alpha + mixed[:, HD:]
        acc_ref[question, head, part, :] = (
            acc_ref[question, head, part, :] * alpha + mixed[:, :HD]
        )


def part_kernel(k, most, heads, *refs):
    refs = list(refs)
    row_ref, tag_ref, far_tag_ref = refs.pop(0), refs.pop(0), refs.pop(0)
    own_ref = refs.pop(0) if k == 0 else None
    questions = [refs.pop(0) for _ in range(2 if k > 1 else 1)]
    cache_ref, items_ref, out_ref, q_ref, m_ref, l_ref, acc_ref, buf, sem, q_sem = refs
    per_device = q_ref.shape[0] // LQ
    entries = 2 * most

    def fetch(i, slot):
        @pl.when(i < most)
        def _():
            row = row_ref[k * most + jnp.minimum(i, most - 1)]
            pltpu.make_async_copy(cache_ref.at[row], buf.at[slot], sem.at[slot]).start()

        @pl.when(i >= most)
        def _():
            pltpu.make_async_copy(
                items_ref.at[jnp.maximum(i - most, 0)], buf.at[slot], sem.at[slot]
            ).start()

    if len(questions) == 1:
        pltpu.make_async_copy(questions[0], q_ref, q_sem).start()
    else:
        inner = is_inner()

        @pl.when(inner)
        def _():
            pltpu.make_async_copy(questions[0], q_ref, q_sem).start()

        @pl.when(jnp.logical_not(inner))
        def _():
            pltpu.make_async_copy(questions[1], q_ref, q_sem).start()

    fetch(jnp.int32(0), 0)
    m_ref[...] = jnp.full(m_ref.shape, NEG, jnp.float32)
    l_ref[...] = jnp.zeros(l_ref.shape, jnp.float32)
    acc_ref[...] = jnp.zeros(acc_ref.shape, jnp.float32)
    pltpu.make_async_copy(q_ref, q_ref, q_sem).wait()
    if k == 0:

        def own_block(i, carry):
            question, head = i // heads, lax.rem(i, heads)
            part_step(
                q_ref,
                m_ref,
                l_ref,
                acc_ref,
                question,
                head,
                own_ref[question, head, :, :HD],
                own_ref[question, head, :, HD:],
                True,
            )
            return carry

        lax.fori_loop(0, per_device * heads, own_block, 0)

    def item(i, carry):
        slot = lax.rem(i, 2)
        pltpu.make_async_copy(buf.at[slot], buf.at[slot], sem.at[slot]).wait()

        @pl.when(i + 1 < entries)
        def _():
            fetch(i + 1, lax.rem(i + 1, 2))

        at = k * most + lax.rem(i, most)
        tag = jnp.where(i < most, tag_ref[at], far_tag_ref[at])

        for head in range(heads):
            part_step(
                q_ref,
                m_ref,
                l_ref,
                acc_ref,
                tag,
                head,
                buf[slot, head, :, :HD],
                buf[slot, head, :, HD:],
                False,
            )
        return carry

    lax.fori_loop(0, entries, item, 0)
    eye = unit()

    def close(c, carry):
        head, g = c // GROUP, lax.rem(c, GROUP)
        columns = pl.ds(pl.multiple_of(c * HD, HD), HD)
        part = pl.ds(pl.multiple_of(g * LQ, LQ), LQ)
        for question in range(per_device):
            total = l_ref[question, head, part, :]
            some = total > 0.0
            safe = jnp.where(some, total, 1.0)
            out_ref[question, :LQ, columns] = (
                acc_ref[question, head, part, :] / safe
            ).astype(out_ref.dtype)
            level = jnp.where(some, m_ref[question, head, part, :] + jnp.log2(safe), NEG)
            line = jnp.sum(jnp.where(eye, level, 0.0), axis=0, keepdims=True)
            store_level(out_ref, question, columns, line)
        return carry

    lax.fori_loop(0, heads * GROUP, close, 0)


def store_level(out_ref, question, columns, line):
    row_of = lax.broadcasted_iota(jnp.int32, (EXTRA, line.shape[1]), 0)
    high = line.astype(jnp.bfloat16).astype(jnp.float32)
    both = jnp.where(row_of == 0, high, jnp.where(row_of == 1, line - high, 0.0))
    out_ref[question, LQ:, columns] = both.astype(out_ref.dtype)


def part_call(k, most, tables, own, questions, cache, items):
    tokens, columns = questions[0].shape
    heads, item = cache.shape[1], cache.shape[1:]
    state = (tokens // LQ, heads, GROUP * LQ, HD)
    smem = pl.BlockSpec(memory_space=pltpu.SMEM)
    vmem = pl.BlockSpec(memory_space=pltpu.VMEM)
    anyspace = pl.BlockSpec(memory_space=pl.ANY)
    owned = [own] if k == 0 else []
    weights = 2 * most * heads * GROUP * LQ * item[1]
    return pl.pallas_call(
        functools.partial(part_kernel, k, most, heads),
        out_shape=jax.ShapeDtypeStruct((tokens // LQ, LQ + EXTRA, columns), cache.dtype),
        in_specs=[smem] * 3 + [vmem] * len(owned) + [anyspace] * (len(questions) + 2),
        out_specs=vmem,
        scratch_shapes=[
            pltpu.VMEM((tokens, columns), cache.dtype),
            pltpu.VMEM(state, jnp.float32),
            pltpu.VMEM(state, jnp.float32),
            pltpu.VMEM(state, jnp.float32),
            pltpu.VMEM((2,) + item, cache.dtype),
            pltpu.SemaphoreType.DMA((2,)),
            pltpu.SemaphoreType.DMA,
        ],
        compiler_params=pltpu.CompilerParams(vmem_limit_bytes=VMEM_BYTES),
        cost_estimate=pl.CostEstimate(
            flops=weights * HD * 4,
            bytes_accessed=2 * most * math.prod(item) * 2,
            transcendentals=weights,
        ),
    )(*tables, *owned, *questions, cache, items)


def blend(a_ref, b_ref, out_ref, leveled):
    eye = unit()
    ones = jnp.ones((2 * LQ, LQ), jnp.bfloat16)

    def level_of(ref):
        both = ref[0, LQ:, :].astype(jnp.float32)
        return both[:1] + both[1:2]

    one, two = level_of(a_ref), level_of(b_ref)
    top = jnp.maximum(one, two)
    first, second = jnp.exp2(one - top), jnp.exp2(two - top)
    total = first + second
    share = first / total
    high = share.astype(jnp.bfloat16).astype(jnp.float32)
    low = share - high
    for c in range(share.shape[1] // HD):
        columns = slice(c * HD, (c + 1) * HD)
        spread = jnp.concatenate(
            [
                jnp.where(eye, jnp.broadcast_to(v[:, columns], (LQ, LQ)), 0.0).astype(jnp.bfloat16)
                for v in (high, low)
            ],
            axis=1,
        )
        column = jnp.dot(spread, ones, preferred_element_type=jnp.float32)
        a = a_ref[0, :LQ, columns].astype(jnp.float32)
        b = b_ref[0, :LQ, columns].astype(jnp.float32)
        value = (b + (a - b) * column).astype(out_ref.dtype)
        if leveled:
            out_ref[0, :LQ, columns] = value
        else:
            out_ref[:, columns] = value
    if leveled:
        store_level(out_ref, 0, slice(None), top + jnp.log2(total))


def merge_kernel(a_ref, b_ref, out_ref):
    inner = is_inner()

    @pl.when(inner)
    def _():
        blend(a_ref, b_ref, out_ref, True)

    @pl.when(jnp.logical_not(inner))
    def _():
        out_ref[...] = a_ref[...]


def finish_kernel(a_ref, b_ref, out_ref):
    blend(a_ref, b_ref, out_ref, False)


def question_spec(value, at):
    shape = (1,) + value.shape[1:]
    if value.shape[0] == 1:
        return pl.BlockSpec(shape, lambda q: (0, 0, 0))
    if at is None:
        return pl.BlockSpec(shape, lambda q: (q, 0, 0))
    return pl.BlockSpec(shape, lambda q: (at, 0, 0))


def join_call(a, b, at, leveled):
    questions = a.shape[0] if at is None else 1
    columns = a.shape[2]
    if leveled:
        shape, block = (questions,) + a.shape[1:], (1,) + a.shape[1:]
        out_spec = pl.BlockSpec(block, lambda q: (q, 0, 0))
    else:
        shape = (questions * LQ, columns)
        out_spec = pl.BlockSpec((LQ, columns), lambda q: (q, 0))
    size = questions * LQ * columns
    return pl.pallas_call(
        merge_kernel if leveled else finish_kernel,
        out_shape=jax.ShapeDtypeStruct(shape, a.dtype),
        grid=(questions,),
        in_specs=[question_spec(a, at), question_spec(b, at)],
        out_specs=out_spec,
        compiler_params=pltpu.CompilerParams(vmem_limit_bytes=VMEM_BYTES),
        cost_estimate=pl.CostEstimate(flops=size * 8, bytes_accessed=size * 6, transcendentals=0),
    )(a, b)


def line_steps(queries, own_kv, passage_cache, out_weight, lists, passage_slot, question_slot):
    per_device = queries.shape[0] // LQ
    heads = own_kv.shape[1]
    most = per_device * lists.shape[1] // (2 * LINE)
    half = out_weight.shape[0] // 2

    def send(value, pairs):
        return lax.ppermute(value, "pass", pairs)

    def part(k, *args):
        return part_call(k, most, tables, own if k == 0 else None, *args)

    def join(a, b, at=None, leveled=True):
        return join_call(a, b, at, leveled)

    across = [(p, p ^ 1) for p in range(2 * LINE)]
    inner_across = [(p, d) for p, d in across if p // 2 in (1, 2)]
    outer_across = [(p, d) for p, d in across if p // 2 not in (1, 2)]
    near, middle = mirror(1), mirror(3, "inner")
    inward, outward = mirror(1, "outer"), mirror(1, "inner")
    q_near = send(queries, near)
    q_mid = send(queries, middle)
    w_across0 = send(out_weight[:half], across)
    w_across1 = send(out_weight[half:], across)
    cache = jnp.transpose(passage_cache, (0, 2, 1, 3))
    row, tag, far_tag, *items = sort_items(
        lists, passage_slot, question_slot, cache, most, per_device
    )
    tables = (row, tag, far_tag)
    q_out = send(q_mid, outward)
    q_cross = send(q_near, middle)
    q_end = send(q_cross, outward)
    far = [send(items[k], across) for k in range(LINE)]
    own = own_kv.reshape(per_device, LQ, heads, 2 * HD).transpose(0, 2, 1, 3)
    part2 = part(2, [q_cross, q_out], cache, far[2])
    part3 = part(3, [q_mid, q_end], cache, far[3])
    part0 = part(0, [queries], cache, far[0])
    part1 = part(1, [q_near], cache, far[1])
    back2 = send(part2, inward)
    w_in = send(out_weight, mirror(2, "outer"))
    w_out = send(out_weight, mirror(2, "inner"))
    back3 = send(part3, inward)
    w_in_both = send(w_in, inner_across)
    w_out_both = send(w_out, outer_across)
    own_rows, near_rows = [], []
    for q in range(per_device):
        cross3 = send(join(part3, back2, q), middle)
        near0 = join(part0, cross3, q)
        beside = send(near0, near)
        cross2 = send(join(part2, back3, q), middle)
        near1 = join(part1, cross2, q)
        back1 = send(near1, near)
        near_rows.append(join(near1, beside, q, False))
        own_rows.append(join(near0, back1, q, False))
    return project_call(
        own_rows + near_rows,
        out_weight,
        w_across0,
        w_across1,
        w_in,
        w_in_both,
        w_out,
        w_out_both,
    )


MESH = pl.DeviceIdType.MESH


def project_kernel(pieces, *refs):
    rows_refs = refs[:pieces]
    own_ref, a0_ref, a1_ref, in_ref, in2_ref, out1_ref, out2_ref = refs[pieces : pieces + 7]
    refs = refs[pieces + 7 :]
    out_ref, context_ref, w_ref, part_ref, core_ref, y_ref, ysend_ref, zsend_ref = refs[:8]
    row_sem, w_sem, send_sem, recv_sem = refs[8:]
    me, head = lax.axis_index("pass"), lax.axis_index("head")
    z, x, y, core = me // 2, me % 2, head // 2, head % 2
    rows, wide = out_ref.shape[0], w_ref.shape[3]
    half = a0_ref.shape[0]
    inner = is_inner()
    core_peer = (me, head ^ 1)
    y_peer = (me, head ^ 2)
    z_peer = (me ^ 2, head ^ 1)
    stays = core == z % 2

    row_loads = [
        pltpu.make_async_copy(ref, context_ref.at[pl.ds(i * LQ, LQ)], row_sem.at[i])
        for i, ref in enumerate(rows_refs)
    ]
    for load in row_loads:
        load.start()

    def load_here():
        pltpu.make_async_copy(own_ref, w_ref.at[0, x], w_sem.at[0, x]).start()
        low, high = w_ref.at[0, 1 - x, pl.ds(0, half)], w_ref.at[0, 1 - x, pl.ds(half, half)]
        pltpu.make_async_copy(a0_ref, low, w_sem.at[0, 1 - x]).start()
        pltpu.make_async_copy(a1_ref, high, w_sem.at[0, 1 - x]).start()

    def load_there():
        for which, (one, two) in (
            (inner, (in_ref, in2_ref)),
            (jnp.logical_not(inner), (out1_ref, out2_ref)),
        ):

            @pl.when(which)
            def _():
                pltpu.make_async_copy(one, w_ref.at[1, x], w_sem.at[1, x]).start()
                pltpu.make_async_copy(two, w_ref.at[1, 1 - x], w_sem.at[1, 1 - x]).start()

    load_here()
    load_there()
    barrier = pltpu.get_barrier_semaphore()
    for peer in (core_peer, y_peer, z_peer):
        pl.semaphore_signal(barrier, inc=1, device_id=peer, device_id_type=MESH)
    pl.semaphore_wait(barrier, 3)

    def remote(src, dst, i, peer):
        return pltpu.make_async_remote_copy(
            src_ref=src,
            dst_ref=dst,
            send_sem=send_sem.at[i],
            recv_sem=recv_sem.at[i],
            device_id=peer,
            device_id_type=MESH,
        )

    def columns(j):
        return pl.ds(j * wide, wide)

    core_copies = [
        [remote(part_ref.at[s, j], core_ref.at[s, j], s * 2 + j, core_peer) for j in range(2)]
        for s in range(2)
    ]
    y_copies = [remote(ysend_ref.at[j], y_ref.at[j], 4 + j, y_peer) for j in range(2)]
    z_copies = [remote(zsend_ref.at[j], out_ref.at[:, columns(j)], 6 + j, z_peer) for j in range(2)]

    for load in row_loads:
        load.wait()

    def product(to_y, to_core, j):
        start = pl.multiple_of(jnp.where(to_core == z % 2, 0, rows), LQ)
        here = jnp.where(to_y == z // 2, 0, 1)
        return jnp.dot(
            context_ref[pl.ds(start, rows), :],
            w_ref[here, j],
            preferred_element_type=jnp.float32,
        ).astype(jnp.bfloat16)

    for s, to_y in enumerate((1 - y, y)):
        here = jnp.where(to_y == z // 2, 0, 1)
        for j in range(2):
            block = w_ref.at[here, j]
            pltpu.make_async_copy(block, block, w_sem.at[here, j]).wait()
            part_ref[s, j] = product(to_y, 1 - core, j)
            core_copies[s][j].start()
            value = product(to_y, core, j).astype(jnp.float32)
            core_copies[s][j].wait_recv()
            value = value + core_ref[s, j].astype(jnp.float32)
            if s == 0:
                ysend_ref[j] = value.astype(jnp.bfloat16)
                y_copies[j].start()
            else:
                y_copies[j].wait_recv()
                total = (value + y_ref[j].astype(jnp.float32)).astype(jnp.bfloat16)

                @pl.when(stays)
                def _():
                    out_ref[:, columns(j)] = total

                @pl.when(jnp.logical_not(stays))
                def _():
                    zsend_ref[j] = total
                    z_copies[j].start()

    @pl.when(jnp.logical_not(stays))
    def _():
        for copy in z_copies:
            copy.wait()

    for copies in core_copies + [y_copies]:
        for copy in copies:
            copy.wait_send()


def project_call(pieces, own, a0, a1, *lines):
    rows, depth = len(pieces) // 2 * LQ, own.shape[0]
    wide = own.shape[1]
    dtype = own.dtype
    anyspace = pl.BlockSpec(memory_space=pl.ANY)
    return pl.pallas_call(
        functools.partial(project_kernel, len(pieces)),
        out_shape=jax.ShapeDtypeStruct((rows, 2 * wide), dtype),
        in_specs=[anyspace] * (len(pieces) + 7),
        out_specs=pl.BlockSpec(memory_space=pltpu.VMEM),
        scratch_shapes=[
            pltpu.VMEM((2 * rows, depth), dtype),
            pltpu.VMEM((2, 2, depth, wide), dtype),
            pltpu.VMEM((2, 2, rows, wide), dtype),
            pltpu.VMEM((2, 2, rows, wide), dtype),
            pltpu.VMEM((2, rows, wide), dtype),
            pltpu.VMEM((2, rows, wide), dtype),
            pltpu.VMEM((2, rows, wide), dtype),
            pltpu.SemaphoreType.DMA((len(pieces),)),
            pltpu.SemaphoreType.DMA((2, 2)),
            pltpu.SemaphoreType.DMA((8,)),
            pltpu.SemaphoreType.DMA((8,)),
        ],
        compiler_params=pltpu.CompilerParams(
            collective_id=0, has_side_effects=True, vmem_limit_bytes=VMEM_BYTES
        ),
        name="project_sum",
        cost_estimate=pl.CostEstimate(
            flops=2 * 4 * 2 * rows * depth * wide,
            bytes_accessed=4 * depth * wide * 2,
            transcendentals=0,
        ),
    )(*pieces, own, a0, a1, *lines)


def suits_line(mesh, queries, lists):
    passes, heads = mesh.shape["pass"], mesh.shape["head"]
    entries = queries.shape[0] // LQ // passes * lists.shape[1]
    return passes == 2 * LINE and heads == LINE and entries % passes == 0


def solution(mesh):
    in_specs = (
        P("pass", "head"),
        P("pass", "head", None),
        P("pass", None, "head", None),
        P("head", "pass"),
        P(),
        P(),
        P(),
    )
    out_specs = P("pass", "head")

    def run(*args):
        if not suits_line(mesh, args[0], args[4]):
            return jax.shard_map(
                body, mesh=mesh, in_specs=in_specs, out_specs=out_specs, check_vma=False
            )(*args)
        step = jax.shard_map(
            line_steps, mesh=mesh, in_specs=in_specs, out_specs=out_specs, check_vma=False
        )
        return step(*args)

    return run
```

```python
import functools
import math

import jax
import jax.numpy as jnp
from jax import lax
from jax.experimental import pallas as pl
from jax.experimental.pallas import tpu as pltpu
from jax.sharding import PartitionSpec as P


H = 64
KVH = 8
HD = 128
LQ = 128
GROUP = H // KVH
COEF = HD ** (-0.5) * math.log2(math.e)
NEG = -1e30
ROWS = 256


def round_of(a, b, n):
    if n & (n - 1) == 0:
        return a ^ b
    return lax.rem(b - a + n, n)


def pairs_of(k, n):
    if n & (n - 1) == 0:
        return [(p, p ^ k) for p in range(n)]
    return [(p, (p + k) % n) for p in range(n)]


def order_of(n):
    rest = range(1, n)
    return sorted(rest, key=lambda k: (bin(k).count("1"), k))


def gather_kernel(n, most, per_device, order, lists_ref, pslot_ref, qslot_ref, cache_ref, *refs):
    recv_ref, own_row_ref = refs[0], refs[1]
    outs = refs[2 : 2 + len(order)]
    send_row, send_cnt, recv_cnt, buf, in_sem, out_sem = refs[2 + len(order) :]
    me = lax.axis_index("pass")
    pass_dev = cache_ref.shape[0]
    topp, nq = lists_ref.shape
    for k in range(n):
        send_cnt[k] = 0
        recv_cnt[k] = 0
    for i in range(n * most):
        recv_ref[i] = -1
        send_row[i] = 0

    def question(q, carry):
        slot = qslot_ref[q]
        dest = slot // per_device
        local = slot - dest * per_device
        k_send = round_of(me, dest, n)
        for t in range(topp):
            row = pslot_ref[lists_ref[t, q]]
            owner = row // pass_dev

            @pl.when(owner == me)
            def _():
                count = send_cnt[k_send]
                send_row[k_send * most + count] = row - owner * pass_dev
                send_cnt[k_send] = count + 1

            @pl.when(dest == me)
            def _():
                k = round_of(owner, me, n)
                count = recv_cnt[k]
                recv_ref[k * most + count] = local
                recv_cnt[k] = count + 1

        return carry

    lax.fori_loop(0, nq, question, 0)
    for r in range(most):
        own_row_ref[r] = send_row[r]
    copies = []
    for j, k in enumerate(order):
        for r in range(most):
            i = j * most + r
            get = pltpu.make_async_copy(
                cache_ref.at[send_row[k * most + r]], buf.at[i], in_sem.at[i]
            )
            get.start()
            copies.append((get, pltpu.make_async_copy(buf.at[i], outs[j].at[r], out_sem.at[i])))
    for get, put in copies:
        get.wait()
        put.start()
    for get, put in copies:
        put.wait()


def gather(lists, passage_slot, question_slot, cache, n, most, per_device, order):
    item = cache.shape[1:]
    slots = (n - 1) * most
    smem = pl.BlockSpec(memory_space=pltpu.SMEM)
    anyspace = pl.BlockSpec(memory_space=pl.ANY)
    return pl.pallas_call(
        functools.partial(gather_kernel, n, most, per_device, order),
        out_shape=[
            jax.ShapeDtypeStruct((n * most,), jnp.int32),
            jax.ShapeDtypeStruct((most,), jnp.int32),
        ]
        + [jax.ShapeDtypeStruct((most,) + item, cache.dtype)] * len(order),
        in_specs=[smem, smem, smem, anyspace],
        out_specs=[smem, smem] + [anyspace] * len(order),
        scratch_shapes=[
            pltpu.SMEM((n * most,), jnp.int32),
            pltpu.SMEM((n,), jnp.int32),
            pltpu.SMEM((n,), jnp.int32),
            pltpu.VMEM((slots,) + item, cache.dtype),
            pltpu.SemaphoreType.DMA((slots,)),
            pltpu.SemaphoreType.DMA((slots,)),
        ],
        name="gather_items",
        cost_estimate=pl.CostEstimate(
            flops=0, bytes_accessed=2 * slots * math.prod(item) * 2, transcendentals=0
        ),
    )(lists.T, passage_slot, question_slot, cache)


def block_step(q_ref, m_ref, l_ref, acc_ref, question, head, keys, values, causal):
    rows = q_ref.shape[2]
    step = min(ROWS, rows)
    width = keys.shape[0]
    ones = jnp.ones(values.shape, values.dtype)
    extended = jnp.concatenate([values, ones], axis=1)
    for start in range(0, rows, step):
        part = pl.ds(start, step)
        q = q_ref[question, head, part, :]
        scores = (
            lax.dot_general(q, keys, (((1,), (1,)), ((), ())), preferred_element_type=jnp.float32)
            * COEF
        )
        if causal:
            token = lax.broadcasted_iota(jnp.int32, scores.shape, 0) % LQ
            column = lax.broadcasted_iota(jnp.int32, scores.shape, 1)
            scores = jnp.where(column <= token, scores, NEG)
        old = m_ref[question, head, part, :]
        new = jnp.maximum(old, jnp.max(scores, axis=1, keepdims=True))
        weights = jnp.exp2(scores - jnp.concatenate([new] * (width // HD), axis=1))
        mixed = jnp.dot(
            weights.astype(jnp.bfloat16), extended, preferred_element_type=jnp.float32
        )
        alpha = jnp.exp2(old - new)
        m_ref[question, head, part, :] = new
        l_ref[question, head, part, :] = l_ref[question, head, part, :] * alpha + mixed[:, HD:]
        acc_ref[question, head, part, :] = (
            acc_ref[question, head, part, :] * alpha + mixed[:, :HD]
        )


def attend_kernel(first, last, rounds, most, *refs):
    refs = list(refs)
    recv_ref, q_ref = refs.pop(0), refs.pop(0)
    if first:
        row_ref, own_ref, cache_ref = refs.pop(0), refs.pop(0), refs.pop(0)
        sources = None
        entries = most
    else:
        state_in = [refs.pop(0) for _ in range(3)]
        sources = [refs.pop(0) for _ in rounds]
        entries = len(rounds) * most
    if last:
        out_ref = refs.pop(0)
        m_ref, l_ref, acc_ref = [refs.pop(0) for _ in range(3)]
    else:
        m_ref, l_ref, acc_ref = [refs.pop(0) for _ in range(3)]
    buf, sem = refs
    per_device, heads = q_ref.shape[0], q_ref.shape[1]

    def fetch(i, slot):
        if first:
            pltpu.make_async_copy(cache_ref.at[row_ref[i]], buf.at[slot], sem.at[slot]).start()
            return
        for j in range(len(rounds)):

            @pl.when(i // most == j)
            def _():
                pltpu.make_async_copy(
                    sources[j].at[i - j * most], buf.at[slot], sem.at[slot]
                ).start()

    def tag_of(i):
        if first:
            return recv_ref[i]
        k = jnp.int32(0)
        for j, value in enumerate(rounds):
            k = jnp.where(i // most == j, value, k)
        return recv_ref[k * most + lax.rem(i, most)]

    fetch(jnp.int32(0), 0)
    if first:
        m_ref[...] = jnp.full(m_ref.shape, NEG, jnp.float32)
        l_ref[...] = jnp.zeros(l_ref.shape, jnp.float32)
        acc_ref[...] = jnp.zeros(acc_ref.shape, jnp.float32)

        def own_block(question, carry):
            for head in range(heads):
                block = own_ref[question, head]
                block_step(
                    q_ref, m_ref, l_ref, acc_ref, question, head, block[:, :HD], block[:, HD:], True
                )
            return carry

        lax.fori_loop(0, per_device, own_block, 0)
    else:
        m_ref[...] = state_in[0][...]
        l_ref[...] = state_in[1][...]
        acc_ref[...] = state_in[2][...]

    def item(i, carry):
        slot = lax.rem(i, 2)
        pltpu.make_async_copy(buf.at[slot], buf.at[slot], sem.at[slot]).wait()

        @pl.when(i + 1 < entries)
        def _():
            fetch(i + 1, lax.rem(i + 1, 2))

        tag = tag_of(i)

        @pl.when(tag >= 0)
        def _():
            for head in range(heads):
                block_step(
                    q_ref,
                    m_ref,
                    l_ref,
                    acc_ref,
                    tag,
                    head,
                    buf[slot, head, :, :HD],
                    buf[slot, head, :, HD:],
                    False,
                )

        return carry

    lax.fori_loop(0, entries, item, 0)
    if last:
        for question in range(per_device):
            for head in range(heads):
                for g in range(GROUP):
                    part = pl.ds(g * LQ, LQ)
                    column = (head * GROUP + g) * HD
                    out_ref[pl.ds(question * LQ, LQ), pl.ds(column, HD)] = (
                        acc_ref[question, head, part, :] / l_ref[question, head, part, :]
                    ).astype(out_ref.dtype)


def attend_call(first, last, rounds, most, recv, q, rest, item):
    per_device, heads, rows, _ = q.shape
    state = jax.ShapeDtypeStruct(q.shape, jnp.float32)
    smem = pl.BlockSpec(memory_space=pltpu.SMEM)
    vmem = pl.BlockSpec(memory_space=pltpu.VMEM)
    anyspace = pl.BlockSpec(memory_space=pl.ANY)
    if first:
        in_specs = [smem, vmem, smem, vmem, anyspace]
        entries = most
    else:
        in_specs = [smem, vmem] + [vmem] * 3 + [anyspace] * len(rounds)
        entries = most * len(rounds)
    scratch = [pltpu.VMEM((2,) + item, q.dtype), pltpu.SemaphoreType.DMA((2,))]
    if last:
        out_shape = jax.ShapeDtypeStruct((per_device * LQ, heads * GROUP * HD), q.dtype)
        out_specs = vmem
        scratch = [pltpu.VMEM(q.shape, jnp.float32)] * 3 + scratch
    else:
        out_shape = [state] * 3
        out_specs = [vmem] * 3
    weights = entries * heads * rows * item[1]
    return pl.pallas_call(
        functools.partial(attend_kernel, first, last, rounds, most),
        out_shape=out_shape,
        in_specs=in_specs,
        out_specs=out_specs,
        scratch_shapes=scratch,
        name="attend_first" if first else ("attend_last" if last else "attend_more"),
        cost_estimate=pl.CostEstimate(
            flops=weights * HD * 4,
            bytes_accessed=entries * math.prod(item) * 2,
            transcendentals=weights,
        ),
    )(recv, q, *rest)


def weight_blocks(own, n):
    if n & (n - 1):
        return [lax.all_gather(own, "pass", axis=1, tiled=True)]
    have = {0: own}
    bit = n // 2
    while bit:
        for k in list(have):
            have[k ^ bit] = lax.ppermute(have[k], "pass", pairs_of(bit, n))
        bit //= 2
    return [have[k] for k in range(n)]


def project(context, weights):
    parts = [
        jnp.dot(context, weight, preferred_element_type=jnp.float32).astype(jnp.bfloat16)
        for weight in weights
    ]
    me = lax.axis_index("pass")
    bit = len(parts) // 2
    while bit:
        swap = (me & bit) != 0
        parts = [jnp.where(swap, parts[k ^ bit], parts[k]) for k in range(len(parts))]
        bit //= 2
    return jnp.concatenate(parts, axis=1)


def body(queries, own_kv, passage_cache, out_weight, lists, passage_slot, question_slot):
    n = lax.axis_size("pass")
    per_device = queries.shape[0] // LQ
    heads = own_kv.shape[1]
    entries = per_device * lists.shape[1]
    most = (entries + n - 1) // n
    order = order_of(n)
    cache = jnp.transpose(passage_cache, (0, 2, 1, 3))
    recv, own_row, *items = gather(
        lists, passage_slot, question_slot, cache, n, most, per_device, order
    )
    arrived = [
        lax.ppermute(item, "pass", pairs_of(k, n)) for k, item in zip(order, items)
    ]
    weights = weight_blocks(out_weight, n)
    q = (
        queries.reshape(per_device, LQ, heads, GROUP, HD)
        .transpose(0, 2, 3, 1, 4)
        .reshape(per_device, heads, GROUP * LQ, HD)
    )
    own = own_kv.reshape(per_device, LQ, heads, 2 * HD).transpose(0, 2, 1, 3)
    item = cache.shape[1:]
    state = attend_call(True, False, (0,), most, recv, q, (own_row, own, cache), item)
    calls = 3
    bounds = [len(order) * i // calls for i in range(calls + 1)]
    for i in range(calls):
        rounds = tuple(order[bounds[i] : bounds[i + 1]])
        rest = tuple(state) + tuple(arrived[bounds[i] : bounds[i + 1]])
        state = attend_call(False, i == calls - 1, rounds, most, recv, q, rest, item)
    context = state
    return lax.psum_scatter(project(context, weights), "head", scatter_dimension=1, tiled=True)


LINE = 4
EXTRA = 8
VMEM_BYTES = 67043328


def mirror(k, ends=None):
    pairs = [(p, p ^ int(2 * k)) for p in range(2 * LINE)]
    if ends is None:
        return pairs
    return [(p, d) for p, d in pairs if (p // 2 in (0, LINE - 1)) == (ends == "outer")]


def is_inner():
    z = lax.axis_index("pass") // 2
    return jnp.logical_and(z > 0, z < LINE - 1)


def sort_kernel(most, per_device, lists_ref, pslot_ref, qslot_ref, cache_ref, *refs):
    row_ref, tag_ref, far_tag_ref = refs[:3]
    outs = refs[3 : 3 + LINE]
    send_row, near_cnt, send_cnt, far_cnt, buf, in_sem, out_sem = refs[3 + LINE :]
    me = lax.axis_index("pass")
    z, x = me // 2, me % 2
    pass_dev = cache_ref.shape[0]
    topp, nq = lists_ref.shape
    for k in range(LINE):
        near_cnt[k] = 0
        send_cnt[k] = 0
        far_cnt[k] = 0

    def question(q, carry):
        slot = qslot_ref[q]
        dest = slot // per_device
        local = slot - dest * per_device
        k = (dest // 2) ^ z
        same = dest % 2 == x
        for t in range(topp):
            row = pslot_ref[lists_ref[t, q]]
            owner = row // pass_dev
            mine = owner == me

            @pl.when(jnp.logical_and(mine, same))
            def _():
                at = k * most + near_cnt[k]
                row_ref[at] = row - owner * pass_dev
                tag_ref[at] = local
                near_cnt[k] = near_cnt[k] + 1

            @pl.when(jnp.logical_and(mine, jnp.logical_not(same)))
            def _():
                send_row[k * most + send_cnt[k]] = row - owner * pass_dev
                send_cnt[k] = send_cnt[k] + 1

            @pl.when(jnp.logical_and(owner == (me ^ 1), same))
            def _():
                far_tag_ref[k * most + far_cnt[k]] = local
                far_cnt[k] = far_cnt[k] + 1

        return carry

    lax.fori_loop(0, nq, question, 0)
    copies = []
    for k in (1, 2, 3, 0):
        for r in range(most):
            i = k * most + r
            get = pltpu.make_async_copy(cache_ref.at[send_row[i]], buf.at[i], in_sem.at[i])
            get.start()
            copies.append((get, pltpu.make_async_copy(buf.at[i], outs[k].at[r], out_sem.at[i])))
    for get, put in copies:
        get.wait()
        put.start()
    for get, put in copies:
        put.wait()


def sort_items(lists, passage_slot, question_slot, cache, most, per_device):
    item = cache.shape[1:]
    slots = LINE * most
    smem = pl.BlockSpec(memory_space=pltpu.SMEM)
    anyspace = pl.BlockSpec(memory_space=pl.ANY)
    return pl.pallas_call(
        functools.partial(sort_kernel, most, per_device),
        out_shape=[jax.ShapeDtypeStruct((slots,), jnp.int32)] * 3
        + [jax.ShapeDtypeStruct((most,) + item, cache.dtype)] * LINE,
        in_specs=[smem, smem, smem, anyspace],
        out_specs=[smem] * 3 + [anyspace] * LINE,
        scratch_shapes=[
            pltpu.SMEM((slots,), jnp.int32),
            pltpu.SMEM((LINE,), jnp.int32),
            pltpu.SMEM((LINE,), jnp.int32),
            pltpu.SMEM((LINE,), jnp.int32),
            pltpu.VMEM((slots,) + item, cache.dtype),
            pltpu.SemaphoreType.DMA((slots,)),
            pltpu.SemaphoreType.DMA((slots,)),
        ],
        compiler_params=pltpu.CompilerParams(vmem_limit_bytes=VMEM_BYTES),
        name="sort_items",
        cost_estimate=pl.CostEstimate(
            flops=0, bytes_accessed=2 * slots * math.prod(item) * 2, transcendentals=0
        ),
    )(lists.T, passage_slot, question_slot, cache)


def unit():
    r = lax.broadcasted_iota(jnp.int32, (LQ, LQ), 0)
    c = lax.broadcasted_iota(jnp.int32, (LQ, LQ), 1)
    return r == c


def part_step(q_ref, m_ref, l_ref, acc_ref, question, head, keys, values, causal):
    rows = GROUP * LQ
    width = keys.shape[0]
    ones = jnp.ones(values.shape, values.dtype)
    extended = jnp.concatenate([values, ones], axis=1)
    tokens = pl.ds(pl.multiple_of(question * LQ, LQ), LQ)
    for start in range(0, rows, ROWS):
        part = pl.ds(start, ROWS)
        q = jnp.concatenate(
            [
                q_ref[tokens, pl.ds(pl.multiple_of((head * GROUP + g) * HD, HD), HD)]
                for g in range(start // LQ, (start + ROWS) // LQ)
            ],
            axis=0,
        )
        scores = (
            lax.dot_general(q, keys, (((1,), (1,)), ((), ())), preferred_element_type=jnp.float32)
            * COEF
        )
        if causal:
            token = lax.broadcasted_iota(jnp.int32, scores.shape, 0) % LQ
            column = lax.broadcasted_iota(jnp.int32, scores.shape, 1)
            scores = jnp.where(column <= token, scores, NEG)
        old = m_ref[question, head, part, :]
        new = jnp.maximum(old, jnp.max(scores, axis=1, keepdims=True))
        weights = jnp.exp2(scores - jnp.concatenate([new] * (width // HD), axis=1))
        mixed = jnp.dot(
            weights.astype(jnp.bfloat16), extended, preferred_element_type=jnp.float32
        )
        alpha = jnp.exp2(old - new)
        m_ref[question, head, part, :] = new
        l_ref[question, head, part, :] = l_ref[question, head, part, :] * alpha + mixed[:, HD:]
        acc_ref[question, head, part, :] = (
            acc_ref[question, head, part, :] * alpha + mixed[:, :HD]
        )


def part_kernel(k, most, heads, *refs):
    refs = list(refs)
    row_ref, tag_ref, far_tag_ref = refs.pop(0), refs.pop(0), refs.pop(0)
    own_ref = refs.pop(0) if k == 0 else None
    questions = [refs.pop(0) for _ in range(2 if k > 1 else 1)]
    cache_ref, items_ref, out_ref, q_ref, m_ref, l_ref, acc_ref, buf, sem, q_sem = refs
    per_device = q_ref.shape[0] // LQ
    entries = 2 * most

    def fetch(i, slot):
        @pl.when(i < most)
        def _():
            row = row_ref[k * most + jnp.minimum(i, most - 1)]
            pltpu.make_async_copy(cache_ref.at[row], buf.at[slot], sem.at[slot]).start()

        @pl.when(i >= most)
        def _():
            pltpu.make_async_copy(
                items_ref.at[jnp.maximum(i - most, 0)], buf.at[slot], sem.at[slot]
            ).start()

    if len(questions) == 1:
        pltpu.make_async_copy(questions[0], q_ref, q_sem).start()
    else:
        inner = is_inner()

        @pl.when(inner)
        def _():
            pltpu.make_async_copy(questions[0], q_ref, q_sem).start()

        @pl.when(jnp.logical_not(inner))
        def _():
            pltpu.make_async_copy(questions[1], q_ref, q_sem).start()

    fetch(jnp.int32(0), 0)
    m_ref[...] = jnp.full(m_ref.shape, NEG, jnp.float32)
    l_ref[...] = jnp.zeros(l_ref.shape, jnp.float32)
    acc_ref[...] = jnp.zeros(acc_ref.shape, jnp.float32)
    pltpu.make_async_copy(q_ref, q_ref, q_sem).wait()
    if k == 0:

        def own_block(i, carry):
            question, head = i // heads, lax.rem(i, heads)
            part_step(
                q_ref,
                m_ref,
                l_ref,
                acc_ref,
                question,
                head,
                own_ref[question, head, :, :HD],
                own_ref[question, head, :, HD:],
                True,
            )
            return carry

        lax.fori_loop(0, per_device * heads, own_block, 0)

    def item(i, carry):
        slot = lax.rem(i, 2)
        pltpu.make_async_copy(buf.at[slot], buf.at[slot], sem.at[slot]).wait()

        @pl.when(i + 1 < entries)
        def _():
            fetch(i + 1, lax.rem(i + 1, 2))

        at = k * most + lax.rem(i, most)
        tag = jnp.where(i < most, tag_ref[at], far_tag_ref[at])

        for head in range(heads):
            part_step(
                q_ref,
                m_ref,
                l_ref,
                acc_ref,
                tag,
                head,
                buf[slot, head, :, :HD],
                buf[slot, head, :, HD:],
                False,
            )
        return carry

    lax.fori_loop(0, entries, item, 0)
    eye = unit()

    def close(c, carry):
        head, g = c // GROUP, lax.rem(c, GROUP)
        columns = pl.ds(pl.multiple_of(c * HD, HD), HD)
        part = pl.ds(pl.multiple_of(g * LQ, LQ), LQ)
        for question in range(per_device):
            total = l_ref[question, head, part, :]
            some = total > 0.0
            safe = jnp.where(some, total, 1.0)
            out_ref[question, :LQ, columns] = (
                acc_ref[question, head, part, :] / safe
            ).astype(out_ref.dtype)
            level = jnp.where(some, m_ref[question, head, part, :] + jnp.log2(safe), NEG)
            line = jnp.sum(jnp.where(eye, level, 0.0), axis=0, keepdims=True)
            store_level(out_ref, question, columns, line)
        return carry

    lax.fori_loop(0, heads * GROUP, close, 0)


def store_level(out_ref, question, columns, line):
    row_of = lax.broadcasted_iota(jnp.int32, (EXTRA, line.shape[1]), 0)
    high = line.astype(jnp.bfloat16).astype(jnp.float32)
    both = jnp.where(row_of == 0, high, jnp.where(row_of == 1, line - high, 0.0))
    out_ref[question, LQ:, columns] = both.astype(out_ref.dtype)


def part_call(k, most, tables, own, questions, cache, items):
    tokens, columns = questions[0].shape
    heads, item = cache.shape[1], cache.shape[1:]
    state = (tokens // LQ, heads, GROUP * LQ, HD)
    smem = pl.BlockSpec(memory_space=pltpu.SMEM)
    vmem = pl.BlockSpec(memory_space=pltpu.VMEM)
    anyspace = pl.BlockSpec(memory_space=pl.ANY)
    owned = [own] if k == 0 else []
    weights = 2 * most * heads * GROUP * LQ * item[1]
    return pl.pallas_call(
        functools.partial(part_kernel, k, most, heads),
        out_shape=jax.ShapeDtypeStruct((tokens // LQ, LQ + EXTRA, columns), cache.dtype),
        in_specs=[smem] * 3 + [vmem] * len(owned) + [anyspace] * (len(questions) + 2),
        out_specs=vmem,
        scratch_shapes=[
            pltpu.VMEM((tokens, columns), cache.dtype),
            pltpu.VMEM(state, jnp.float32),
            pltpu.VMEM(state, jnp.float32),
            pltpu.VMEM(state, jnp.float32),
            pltpu.VMEM((2,) + item, cache.dtype),
            pltpu.SemaphoreType.DMA((2,)),
            pltpu.SemaphoreType.DMA,
        ],
        compiler_params=pltpu.CompilerParams(vmem_limit_bytes=VMEM_BYTES),
        cost_estimate=pl.CostEstimate(
            flops=weights * HD * 4,
            bytes_accessed=2 * most * math.prod(item) * 2,
            transcendentals=weights,
        ),
    )(*tables, *owned, *questions, cache, items)


def blend(a_ref, b_ref, out_ref, leveled):
    eye = unit()
    ones = jnp.ones((2 * LQ, LQ), jnp.bfloat16)

    def level_of(ref):
        both = ref[0, LQ:, :].astype(jnp.float32)
        return both[:1] + both[1:2]

    one, two = level_of(a_ref), level_of(b_ref)
    top = jnp.maximum(one, two)
    first, second = jnp.exp2(one - top), jnp.exp2(two - top)
    total = first + second
    share = first / total
    high = share.astype(jnp.bfloat16).astype(jnp.float32)
    low = share - high
    for c in range(share.shape[1] // HD):
        columns = slice(c * HD, (c + 1) * HD)
        spread = jnp.concatenate(
            [
                jnp.where(eye, jnp.broadcast_to(v[:, columns], (LQ, LQ)), 0.0).astype(jnp.bfloat16)
                for v in (high, low)
            ],
            axis=1,
        )
        column = jnp.dot(spread, ones, preferred_element_type=jnp.float32)
        a = a_ref[0, :LQ, columns].astype(jnp.float32)
        b = b_ref[0, :LQ, columns].astype(jnp.float32)
        value = (b + (a - b) * column).astype(out_ref.dtype)
        if leveled:
            out_ref[0, :LQ, columns] = value
        else:
            out_ref[:, columns] = value
    if leveled:
        store_level(out_ref, 0, slice(None), top + jnp.log2(total))


def merge_kernel(a_ref, b_ref, out_ref):
    inner = is_inner()

    @pl.when(inner)
    def _():
        blend(a_ref, b_ref, out_ref, True)

    @pl.when(jnp.logical_not(inner))
    def _():
        out_ref[...] = a_ref[...]


def finish_kernel(a_ref, b_ref, out_ref):
    blend(a_ref, b_ref, out_ref, False)


def question_spec(value, at):
    shape = (1,) + value.shape[1:]
    if value.shape[0] == 1:
        return pl.BlockSpec(shape, lambda q: (0, 0, 0))
    if at is None:
        return pl.BlockSpec(shape, lambda q: (q, 0, 0))
    return pl.BlockSpec(shape, lambda q: (at, 0, 0))


def join_call(a, b, at, leveled):
    questions = a.shape[0] if at is None else 1
    columns = a.shape[2]
    if leveled:
        shape, block = (questions,) + a.shape[1:], (1,) + a.shape[1:]
        out_spec = pl.BlockSpec(block, lambda q: (q, 0, 0))
    else:
        shape = (questions * LQ, columns)
        out_spec = pl.BlockSpec((LQ, columns), lambda q: (q, 0))
    size = questions * LQ * columns
    return pl.pallas_call(
        merge_kernel if leveled else finish_kernel,
        out_shape=jax.ShapeDtypeStruct(shape, a.dtype),
        grid=(questions,),
        in_specs=[question_spec(a, at), question_spec(b, at)],
        out_specs=out_spec,
        compiler_params=pltpu.CompilerParams(vmem_limit_bytes=VMEM_BYTES),
        cost_estimate=pl.CostEstimate(flops=size * 8, bytes_accessed=size * 6, transcendentals=0),
    )(a, b)


def line_steps(queries, own_kv, passage_cache, out_weight, lists, passage_slot, question_slot):
    per_device = queries.shape[0] // LQ
    heads = own_kv.shape[1]
    most = per_device * lists.shape[1] // (2 * LINE)
    half = out_weight.shape[0] // 2

    def send(value, pairs):
        return lax.ppermute(value, "pass", pairs)

    def part(k, *args):
        return part_call(k, most, tables, own if k == 0 else None, *args)

    def join(a, b, at=None, leveled=True):
        return join_call(a, b, at, leveled)

    across = [(p, p ^ 1) for p in range(2 * LINE)]
    inner_across = [(p, d) for p, d in across if p // 2 in (1, 2)]
    outer_across = [(p, d) for p, d in across if p // 2 not in (1, 2)]
    near, middle = mirror(1), mirror(3, "inner")
    inward, outward = mirror(1, "outer"), mirror(1, "inner")
    q_near = send(queries, near)
    q_mid = send(queries, middle)
    w_across0 = send(out_weight[:half], across)
    w_across1 = send(out_weight[half:], across)
    cache = jnp.transpose(passage_cache, (0, 2, 1, 3))
    row, tag, far_tag, *items = sort_items(
        lists, passage_slot, question_slot, cache, most, per_device
    )
    tables = (row, tag, far_tag)
    q_out = send(q_mid, outward)
    q_cross = send(q_near, middle)
    q_end = send(q_cross, outward)
    far = [send(items[k], across) for k in range(LINE)]
    own = own_kv.reshape(per_device, LQ, heads, 2 * HD).transpose(0, 2, 1, 3)
    part2 = part(2, [q_cross, q_out], cache, far[2])
    part3 = part(3, [q_mid, q_end], cache, far[3])
    part0 = part(0, [queries], cache, far[0])
    part1 = part(1, [q_near], cache, far[1])
    back2 = send(part2, inward)
    w_in = send(out_weight, mirror(2, "outer"))
    w_out = send(out_weight, mirror(2, "inner"))
    back3 = send(part3, inward)
    w_in_both = send(w_in, inner_across)
    w_out_both = send(w_out, outer_across)
    own_rows, near_rows = [], []
    for q in range(per_device):
        cross3 = send(join(part3, back2, q), middle)
        near0 = join(part0, cross3, q)
        beside = send(near0, near)
        cross2 = send(join(part2, back3, q), middle)
        near1 = join(part1, cross2, q)
        back1 = send(near1, near)
        near_rows.append(join(near1, beside, q, False))
        own_rows.append(join(near0, back1, q, False))
    weights = (out_weight, w_across0, w_across1, w_in, w_in_both, w_out, w_out_both)
    far_out = project_call(near_rows, weights, True)
    home_out = project_call(own_rows, weights, False)
    return jnp.where(at_home(), home_out, far_out)


MESH = pl.DeviceIdType.MESH


def at_home():
    return lax.axis_index("head") % 2 == lax.axis_index("pass") // 2 % 2


def project_kernel(pieces, hops, *refs):
    rows_refs = refs[:pieces]
    own_ref, a0_ref, a1_ref, in_ref, in2_ref, out1_ref, out2_ref = refs[pieces : pieces + 7]
    refs = refs[pieces + 7 :]
    out_ref, context_ref, w_ref, part_ref, core_ref, y_ref, ysend_ref, zsend_ref = refs[:8]
    row_sem, w_sem, send_sem, recv_sem = refs[8:]
    me, head = lax.axis_index("pass"), lax.axis_index("head")
    z, x, y = me // 2, me % 2, head // 2
    wide = w_ref.shape[3]
    half = a0_ref.shape[0]
    inner = is_inner()
    core_peer = (me, head ^ 1)
    y_peer = (me, head ^ 2)
    z_peer = (me ^ 2, head ^ 1)
    sums = jnp.logical_not(at_home()) if hops else at_home()

    row_loads = [
        pltpu.make_async_copy(ref, context_ref.at[pl.ds(i * LQ, LQ)], row_sem.at[i])
        for i, ref in enumerate(rows_refs)
    ]
    for load in row_loads:
        load.start()

    def load_here():
        pltpu.make_async_copy(own_ref, w_ref.at[0, x], w_sem.at[0, x]).start()
        low, high = w_ref.at[0, 1 - x, pl.ds(0, half)], w_ref.at[0, 1 - x, pl.ds(half, half)]
        pltpu.make_async_copy(a0_ref, low, w_sem.at[0, 1 - x]).start()
        pltpu.make_async_copy(a1_ref, high, w_sem.at[0, 1 - x]).start()

    def load_there():
        for which, (one, two) in (
            (inner, (in_ref, in2_ref)),
            (jnp.logical_not(inner), (out1_ref, out2_ref)),
        ):

            @pl.when(which)
            def _():
                pltpu.make_async_copy(one, w_ref.at[1, x], w_sem.at[1, x]).start()
                pltpu.make_async_copy(two, w_ref.at[1, 1 - x], w_sem.at[1, 1 - x]).start()

    here_first = y != z // 2

    @pl.when(here_first)
    def _():
        load_here()
        load_there()

    @pl.when(jnp.logical_not(here_first))
    def _():
        load_there()
        load_here()

    barrier = pltpu.get_barrier_semaphore()
    for peer in (core_peer, y_peer, z_peer):
        pl.semaphore_signal(barrier, inc=1, device_id=peer, device_id_type=MESH)
    pl.semaphore_wait(barrier, 3)

    def remote(src, dst, i, peer):
        return pltpu.make_async_remote_copy(
            src_ref=src,
            dst_ref=dst,
            send_sem=send_sem.at[i],
            recv_sem=recv_sem.at[i],
            device_id=peer,
            device_id_type=MESH,
        )

    def columns(j):
        return pl.ds(j * wide, wide)

    core_copies = [
        [remote(part_ref.at[s, j], core_ref.at[s, j], s * 2 + j, core_peer) for j in range(2)]
        for s in range(2)
    ]
    y_copies = [remote(ysend_ref.at[j], y_ref.at[j], 4 + j, y_peer) for j in range(2)]
    z_copies = [remote(zsend_ref.at[j], out_ref.at[:, columns(j)], 6 + j, z_peer) for j in range(2)]

    for load in row_loads:
        load.wait()

    for s, to_y in enumerate((1 - y, y)):
        here = jnp.where(to_y == z // 2, 0, 1)
        for j in range(2):
            block = w_ref.at[here, j]
            pltpu.make_async_copy(block, block, w_sem.at[here, j]).wait()
            part_ref[s, j] = jnp.dot(
                context_ref[...], w_ref[here, j], preferred_element_type=jnp.float32
            ).astype(part_ref.dtype)

            @pl.when(jnp.logical_not(sums))
            def _():
                core_copies[s][j].start()

            @pl.when(sums)
            def _():
                core_copies[s][j].wait_recv()
                value = part_ref[s, j].astype(jnp.float32) + core_ref[s, j].astype(jnp.float32)
                if s == 0:
                    ysend_ref[j] = value.astype(ysend_ref.dtype)
                    y_copies[j].start()
                else:
                    y_copies[j].wait_recv()
                    total = (value + y_ref[j].astype(jnp.float32)).astype(out_ref.dtype)
                    if hops:
                        zsend_ref[j] = total
                        z_copies[j].start()
                    else:
                        out_ref[:, columns(j)] = total

    @pl.when(sums)
    def _():
        for copy in y_copies:
            copy.wait_send()
        if hops:
            for copy in z_copies:
                copy.wait()

    @pl.when(jnp.logical_not(sums))
    def _():
        for copies in core_copies:
            for copy in copies:
                copy.wait_send()


def project_call(pieces, weights, hops):
    own = weights[0]
    rows, (depth, wide) = len(pieces) * LQ, own.shape
    dtype = own.dtype
    return pl.pallas_call(
        functools.partial(project_kernel, len(pieces), hops),
        out_shape=jax.ShapeDtypeStruct((rows, 2 * wide), dtype),
        in_specs=[pl.BlockSpec(memory_space=pl.ANY)] * (len(pieces) + len(weights)),
        out_specs=pl.BlockSpec(memory_space=pltpu.VMEM),
        scratch_shapes=[
            pltpu.VMEM((rows, depth), dtype),
            pltpu.VMEM((2, 2, depth, wide), dtype),
            pltpu.VMEM((2, 2, rows, wide), dtype),
            pltpu.VMEM((2, 2, rows, wide), dtype),
            pltpu.VMEM((2, rows, wide), dtype),
            pltpu.VMEM((2, rows, wide), dtype),
            pltpu.VMEM((2, rows, wide), dtype),
            pltpu.SemaphoreType.DMA((len(pieces),)),
            pltpu.SemaphoreType.DMA((2, 2)),
            pltpu.SemaphoreType.DMA((8,)),
            pltpu.SemaphoreType.DMA((8,)),
        ],
        compiler_params=pltpu.CompilerParams(
            collective_id=int(hops), has_side_effects=True, vmem_limit_bytes=VMEM_BYTES
        ),
        name="project_far" if hops else "project_home",
        cost_estimate=pl.CostEstimate(
            flops=2 * 4 * rows * depth * wide,
            bytes_accessed=4 * depth * wide * 2,
            transcendentals=0,
        ),
    )(*pieces, *weights)


def suits_line(mesh, queries, lists):
    passes, heads = mesh.shape["pass"], mesh.shape["head"]
    entries = queries.shape[0] // LQ // passes * lists.shape[1]
    return passes == 2 * LINE and heads == LINE and entries % passes == 0


def solution(mesh):
    in_specs = (
        P("pass", "head"),
        P("pass", "head", None),
        P("pass", None, "head", None),
        P("head", "pass"),
        P(),
        P(),
        P(),
    )
    out_specs = P("pass", "head")

    def run(*args):
        if not suits_line(mesh, args[0], args[4]):
            return jax.shard_map(
                body, mesh=mesh, in_specs=in_specs, out_specs=out_specs, check_vma=False
            )(*args)
        step = jax.shard_map(
            line_steps, mesh=mesh, in_specs=in_specs, out_specs=out_specs, check_vma=False
        )
        return step(*args)

    return run
```

```python
import functools
import math

import jax
import jax.numpy as jnp
from jax import lax
from jax.experimental import pallas as pl
from jax.experimental.pallas import tpu as pltpu
from jax.sharding import PartitionSpec as P


H = 64
KVH = 8
HD = 128
LQ = 128
GROUP = H // KVH
COEF = HD ** (-0.5) * math.log2(math.e)
NEG = -1e30
ROWS = 256


def round_of(a, b, n):
    if n & (n - 1) == 0:
        return a ^ b
    return lax.rem(b - a + n, n)


def pairs_of(k, n):
    if n & (n - 1) == 0:
        return [(p, p ^ k) for p in range(n)]
    return [(p, (p + k) % n) for p in range(n)]


def order_of(n):
    rest = range(1, n)
    return sorted(rest, key=lambda k: (bin(k).count("1"), k))


def gather_kernel(n, most, per_device, order, lists_ref, pslot_ref, qslot_ref, cache_ref, *refs):
    recv_ref, own_row_ref = refs[0], refs[1]
    outs = refs[2 : 2 + len(order)]
    send_row, send_cnt, recv_cnt, buf, in_sem, out_sem = refs[2 + len(order) :]
    me = lax.axis_index("pass")
    pass_dev = cache_ref.shape[0]
    topp, nq = lists_ref.shape
    for k in range(n):
        send_cnt[k] = 0
        recv_cnt[k] = 0
    for i in range(n * most):
        recv_ref[i] = -1
        send_row[i] = 0

    def question(q, carry):
        slot = qslot_ref[q]
        dest = slot // per_device
        local = slot - dest * per_device
        k_send = round_of(me, dest, n)
        for t in range(topp):
            row = pslot_ref[lists_ref[t, q]]
            owner = row // pass_dev

            @pl.when(owner == me)
            def _():
                count = send_cnt[k_send]
                send_row[k_send * most + count] = row - owner * pass_dev
                send_cnt[k_send] = count + 1

            @pl.when(dest == me)
            def _():
                k = round_of(owner, me, n)
                count = recv_cnt[k]
                recv_ref[k * most + count] = local
                recv_cnt[k] = count + 1

        return carry

    lax.fori_loop(0, nq, question, 0)
    for r in range(most):
        own_row_ref[r] = send_row[r]
    copies = []
    for j, k in enumerate(order):
        for r in range(most):
            i = j * most + r
            get = pltpu.make_async_copy(
                cache_ref.at[send_row[k * most + r]], buf.at[i], in_sem.at[i]
            )
            get.start()
            copies.append((get, pltpu.make_async_copy(buf.at[i], outs[j].at[r], out_sem.at[i])))
    for get, put in copies:
        get.wait()
        put.start()
    for get, put in copies:
        put.wait()


def gather(lists, passage_slot, question_slot, cache, n, most, per_device, order):
    item = cache.shape[1:]
    slots = (n - 1) * most
    smem = pl.BlockSpec(memory_space=pltpu.SMEM)
    anyspace = pl.BlockSpec(memory_space=pl.ANY)
    return pl.pallas_call(
        functools.partial(gather_kernel, n, most, per_device, order),
        out_shape=[
            jax.ShapeDtypeStruct((n * most,), jnp.int32),
            jax.ShapeDtypeStruct((most,), jnp.int32),
        ]
        + [jax.ShapeDtypeStruct((most,) + item, cache.dtype)] * len(order),
        in_specs=[smem, smem, smem, anyspace],
        out_specs=[smem, smem] + [anyspace] * len(order),
        scratch_shapes=[
            pltpu.SMEM((n * most,), jnp.int32),
            pltpu.SMEM((n,), jnp.int32),
            pltpu.SMEM((n,), jnp.int32),
            pltpu.VMEM((slots,) + item, cache.dtype),
            pltpu.SemaphoreType.DMA((slots,)),
            pltpu.SemaphoreType.DMA((slots,)),
        ],
        name="gather_items",
        cost_estimate=pl.CostEstimate(
            flops=0, bytes_accessed=2 * slots * math.prod(item) * 2, transcendentals=0
        ),
    )(lists.T, passage_slot, question_slot, cache)


def block_step(q_ref, m_ref, l_ref, acc_ref, question, head, keys, values, causal):
    rows = q_ref.shape[2]
    step = min(ROWS, rows)
    width = keys.shape[0]
    ones = jnp.ones(values.shape, values.dtype)
    extended = jnp.concatenate([values, ones], axis=1)
    for start in range(0, rows, step):
        part = pl.ds(start, step)
        q = q_ref[question, head, part, :]
        scores = (
            lax.dot_general(q, keys, (((1,), (1,)), ((), ())), preferred_element_type=jnp.float32)
            * COEF
        )
        if causal:
            token = lax.broadcasted_iota(jnp.int32, scores.shape, 0) % LQ
            column = lax.broadcasted_iota(jnp.int32, scores.shape, 1)
            scores = jnp.where(column <= token, scores, NEG)
        old = m_ref[question, head, part, :]
        new = jnp.maximum(old, jnp.max(scores, axis=1, keepdims=True))
        weights = jnp.exp2(scores - jnp.concatenate([new] * (width // HD), axis=1))
        mixed = jnp.dot(
            weights.astype(jnp.bfloat16), extended, preferred_element_type=jnp.float32
        )
        alpha = jnp.exp2(old - new)
        m_ref[question, head, part, :] = new
        l_ref[question, head, part, :] = l_ref[question, head, part, :] * alpha + mixed[:, HD:]
        acc_ref[question, head, part, :] = (
            acc_ref[question, head, part, :] * alpha + mixed[:, :HD]
        )


def attend_kernel(first, last, rounds, most, *refs):
    refs = list(refs)
    recv_ref, q_ref = refs.pop(0), refs.pop(0)
    if first:
        row_ref, own_ref, cache_ref = refs.pop(0), refs.pop(0), refs.pop(0)
        sources = None
        entries = most
    else:
        state_in = [refs.pop(0) for _ in range(3)]
        sources = [refs.pop(0) for _ in rounds]
        entries = len(rounds) * most
    if last:
        out_ref = refs.pop(0)
        m_ref, l_ref, acc_ref = [refs.pop(0) for _ in range(3)]
    else:
        m_ref, l_ref, acc_ref = [refs.pop(0) for _ in range(3)]
    buf, sem = refs
    per_device, heads = q_ref.shape[0], q_ref.shape[1]

    def fetch(i, slot):
        if first:
            pltpu.make_async_copy(cache_ref.at[row_ref[i]], buf.at[slot], sem.at[slot]).start()
            return
        for j in range(len(rounds)):

            @pl.when(i // most == j)
            def _():
                pltpu.make_async_copy(
                    sources[j].at[i - j * most], buf.at[slot], sem.at[slot]
                ).start()

    def tag_of(i):
        if first:
            return recv_ref[i]
        k = jnp.int32(0)
        for j, value in enumerate(rounds):
            k = jnp.where(i // most == j, value, k)
        return recv_ref[k * most + lax.rem(i, most)]

    fetch(jnp.int32(0), 0)
    if first:
        m_ref[...] = jnp.full(m_ref.shape, NEG, jnp.float32)
        l_ref[...] = jnp.zeros(l_ref.shape, jnp.float32)
        acc_ref[...] = jnp.zeros(acc_ref.shape, jnp.float32)

        def own_block(question, carry):
            for head in range(heads):
                block = own_ref[question, head]
                block_step(
                    q_ref, m_ref, l_ref, acc_ref, question, head, block[:, :HD], block[:, HD:], True
                )
            return carry

        lax.fori_loop(0, per_device, own_block, 0)
    else:
        m_ref[...] = state_in[0][...]
        l_ref[...] = state_in[1][...]
        acc_ref[...] = state_in[2][...]

    def item(i, carry):
        slot = lax.rem(i, 2)
        pltpu.make_async_copy(buf.at[slot], buf.at[slot], sem.at[slot]).wait()

        @pl.when(i + 1 < entries)
        def _():
            fetch(i + 1, lax.rem(i + 1, 2))

        tag = tag_of(i)

        @pl.when(tag >= 0)
        def _():
            for head in range(heads):
                block_step(
                    q_ref,
                    m_ref,
                    l_ref,
                    acc_ref,
                    tag,
                    head,
                    buf[slot, head, :, :HD],
                    buf[slot, head, :, HD:],
                    False,
                )

        return carry

    lax.fori_loop(0, entries, item, 0)
    if last:
        for question in range(per_device):
            for head in range(heads):
                for g in range(GROUP):
                    part = pl.ds(g * LQ, LQ)
                    column = (head * GROUP + g) * HD
                    out_ref[pl.ds(question * LQ, LQ), pl.ds(column, HD)] = (
                        acc_ref[question, head, part, :] / l_ref[question, head, part, :]
                    ).astype(out_ref.dtype)


def attend_call(first, last, rounds, most, recv, q, rest, item):
    per_device, heads, rows, _ = q.shape
    state = jax.ShapeDtypeStruct(q.shape, jnp.float32)
    smem = pl.BlockSpec(memory_space=pltpu.SMEM)
    vmem = pl.BlockSpec(memory_space=pltpu.VMEM)
    anyspace = pl.BlockSpec(memory_space=pl.ANY)
    if first:
        in_specs = [smem, vmem, smem, vmem, anyspace]
        entries = most
    else:
        in_specs = [smem, vmem] + [vmem] * 3 + [anyspace] * len(rounds)
        entries = most * len(rounds)
    scratch = [pltpu.VMEM((2,) + item, q.dtype), pltpu.SemaphoreType.DMA((2,))]
    if last:
        out_shape = jax.ShapeDtypeStruct((per_device * LQ, heads * GROUP * HD), q.dtype)
        out_specs = vmem
        scratch = [pltpu.VMEM(q.shape, jnp.float32)] * 3 + scratch
    else:
        out_shape = [state] * 3
        out_specs = [vmem] * 3
    weights = entries * heads * rows * item[1]
    return pl.pallas_call(
        functools.partial(attend_kernel, first, last, rounds, most),
        out_shape=out_shape,
        in_specs=in_specs,
        out_specs=out_specs,
        scratch_shapes=scratch,
        name="attend_first" if first else ("attend_last" if last else "attend_more"),
        cost_estimate=pl.CostEstimate(
            flops=weights * HD * 4,
            bytes_accessed=entries * math.prod(item) * 2,
            transcendentals=weights,
        ),
    )(recv, q, *rest)


def weight_blocks(own, n):
    if n & (n - 1):
        return [lax.all_gather(own, "pass", axis=1, tiled=True)]
    have = {0: own}
    bit = n // 2
    while bit:
        for k in list(have):
            have[k ^ bit] = lax.ppermute(have[k], "pass", pairs_of(bit, n))
        bit //= 2
    return [have[k] for k in range(n)]


def project(context, weights):
    parts = [
        jnp.dot(context, weight, preferred_element_type=jnp.float32).astype(jnp.bfloat16)
        for weight in weights
    ]
    me = lax.axis_index("pass")
    bit = len(parts) // 2
    while bit:
        swap = (me & bit) != 0
        parts = [jnp.where(swap, parts[k ^ bit], parts[k]) for k in range(len(parts))]
        bit //= 2
    return jnp.concatenate(parts, axis=1)


def body(queries, own_kv, passage_cache, out_weight, lists, passage_slot, question_slot):
    n = lax.axis_size("pass")
    per_device = queries.shape[0] // LQ
    heads = own_kv.shape[1]
    entries = per_device * lists.shape[1]
    most = (entries + n - 1) // n
    order = order_of(n)
    cache = jnp.transpose(passage_cache, (0, 2, 1, 3))
    recv, own_row, *items = gather(
        lists, passage_slot, question_slot, cache, n, most, per_device, order
    )
    arrived = [
        lax.ppermute(item, "pass", pairs_of(k, n)) for k, item in zip(order, items)
    ]
    weights = weight_blocks(out_weight, n)
    q = (
        queries.reshape(per_device, LQ, heads, GROUP, HD)
        .transpose(0, 2, 3, 1, 4)
        .reshape(per_device, heads, GROUP * LQ, HD)
    )
    own = own_kv.reshape(per_device, LQ, heads, 2 * HD).transpose(0, 2, 1, 3)
    item = cache.shape[1:]
    state = attend_call(True, False, (0,), most, recv, q, (own_row, own, cache), item)
    calls = 3
    bounds = [len(order) * i // calls for i in range(calls + 1)]
    for i in range(calls):
        rounds = tuple(order[bounds[i] : bounds[i + 1]])
        rest = tuple(state) + tuple(arrived[bounds[i] : bounds[i + 1]])
        state = attend_call(False, i == calls - 1, rounds, most, recv, q, rest, item)
    context = state
    return lax.psum_scatter(project(context, weights), "head", scatter_dimension=1, tiled=True)


LINE = 4
EXTRA = 8
ITEM_ORDER = (2, 0, 3, 1)
VMEM_BYTES = 67043328


def mirror(k, ends=None):
    pairs = [(p, p ^ int(2 * k)) for p in range(2 * LINE)]
    if ends is None:
        return pairs
    return [(p, d) for p, d in pairs if (p // 2 in (0, LINE - 1)) == (ends == "outer")]


def is_inner():
    z = lax.axis_index("pass") // 2
    return jnp.logical_and(z > 0, z < LINE - 1)


def sort_kernel(most, per_device, lists_ref, pslot_ref, qslot_ref, cache_ref, *refs):
    row_ref, tag_ref, far_tag_ref = refs[:3]
    outs = refs[3 : 3 + LINE]
    send_row, near_cnt, send_cnt, far_cnt, buf, in_sem, out_sem = refs[3 + LINE :]
    me = lax.axis_index("pass")
    z, x = me // 2, me % 2
    pass_dev = cache_ref.shape[0]
    topp, nq = lists_ref.shape
    for k in range(LINE):
        near_cnt[k] = 0
        send_cnt[k] = 0
        far_cnt[k] = 0

    def take(i):
        return pltpu.make_async_copy(cache_ref.at[send_row[i]], buf.at[i], in_sem.at[i])

    def question(q, carry):
        slot = qslot_ref[q]
        dest = slot // per_device
        local = slot - dest * per_device
        k = (dest // 2) ^ z

        @pl.when(dest % 2 == x)
        def _():
            for t in range(topp):
                row = pslot_ref[lists_ref[t, q]]
                owner = row // pass_dev

                @pl.when(owner == me)
                def _():
                    at = k * most + near_cnt[k]
                    row_ref[at] = row - owner * pass_dev
                    tag_ref[at] = local
                    near_cnt[k] = near_cnt[k] + 1

                @pl.when(owner == (me ^ 1))
                def _():
                    far_tag_ref[k * most + far_cnt[k]] = local
                    far_cnt[k] = far_cnt[k] + 1

        @pl.when(dest % 2 != x)
        def _():
            for t in range(topp):
                row = pslot_ref[lists_ref[t, q]]
                owner = row // pass_dev

                @pl.when(owner == me)
                def _():
                    at = k * most + send_cnt[k]
                    send_row[at] = row - owner * pass_dev
                    send_cnt[k] = send_cnt[k] + 1
                    take(at).start()

        return carry

    lax.fori_loop(0, nq, question, 0)
    slots = [k * most + r for k in ITEM_ORDER for r in range(most)]
    puts = [pltpu.make_async_copy(buf.at[i], outs[i // most].at[i % most], out_sem.at[i]) for i in slots]
    for i, put in zip(slots, puts):
        take(i).wait()
        put.start()
    for put in puts:
        put.wait()


def sort_items(lists, passage_slot, question_slot, cache, most, per_device):
    item = cache.shape[1:]
    slots = LINE * most
    smem = pl.BlockSpec(memory_space=pltpu.SMEM)
    anyspace = pl.BlockSpec(memory_space=pl.ANY)
    return pl.pallas_call(
        functools.partial(sort_kernel, most, per_device),
        out_shape=[jax.ShapeDtypeStruct((slots,), jnp.int32)] * 3
        + [jax.ShapeDtypeStruct((most,) + item, cache.dtype)] * LINE,
        in_specs=[smem, smem, smem, anyspace],
        out_specs=[smem] * 3 + [anyspace] * LINE,
        scratch_shapes=[
            pltpu.SMEM((slots,), jnp.int32),
            pltpu.SMEM((LINE,), jnp.int32),
            pltpu.SMEM((LINE,), jnp.int32),
            pltpu.SMEM((LINE,), jnp.int32),
            pltpu.VMEM((slots,) + item, cache.dtype),
            pltpu.SemaphoreType.DMA((slots,)),
            pltpu.SemaphoreType.DMA((slots,)),
        ],
        compiler_params=pltpu.CompilerParams(vmem_limit_bytes=VMEM_BYTES),
        name="sort_items",
        cost_estimate=pl.CostEstimate(
            flops=0, bytes_accessed=2 * slots * math.prod(item) * 2, transcendentals=0
        ),
    )(lists.T, passage_slot, question_slot, cache)


def unit():
    r = lax.broadcasted_iota(jnp.int32, (LQ, LQ), 0)
    c = lax.broadcasted_iota(jnp.int32, (LQ, LQ), 1)
    return r == c


def part_step(q_ref, m_ref, l_ref, acc_ref, question, head, keys, values, causal):
    rows = GROUP * LQ
    width = keys.shape[0]
    ones = jnp.ones(values.shape, values.dtype)
    extended = jnp.concatenate([values, ones], axis=1)
    tokens = pl.ds(pl.multiple_of(question * LQ, LQ), LQ)
    for start in range(0, rows, ROWS):
        part = pl.ds(start, ROWS)
        q = jnp.concatenate(
            [
                q_ref[tokens, pl.ds(pl.multiple_of((head * GROUP + g) * HD, HD), HD)]
                for g in range(start // LQ, (start + ROWS) // LQ)
            ],
            axis=0,
        )
        scores = (
            lax.dot_general(q, keys, (((1,), (1,)), ((), ())), preferred_element_type=jnp.float32)
            * COEF
        )
        if causal:
            token = lax.broadcasted_iota(jnp.int32, scores.shape, 0) % LQ
            column = lax.broadcasted_iota(jnp.int32, scores.shape, 1)
            scores = jnp.where(column <= token, scores, NEG)
        old = m_ref[question, head, part, :]
        new = jnp.maximum(old, jnp.max(scores, axis=1, keepdims=True))
        weights = jnp.exp2(scores - jnp.concatenate([new] * (width // HD), axis=1))
        mixed = jnp.dot(
            weights.astype(jnp.bfloat16), extended, preferred_element_type=jnp.float32
        )
        alpha = jnp.exp2(old - new)
        m_ref[question, head, part, :] = new
        l_ref[question, head, part, :] = l_ref[question, head, part, :] * alpha + mixed[:, HD:]
        acc_ref[question, head, part, :] = (
            acc_ref[question, head, part, :] * alpha + mixed[:, :HD]
        )


def part_kernel(k, most, heads, *refs):
    refs = list(refs)
    row_ref, tag_ref, far_tag_ref = refs.pop(0), refs.pop(0), refs.pop(0)
    own_ref = refs.pop(0) if k == 0 else None
    questions = [refs.pop(0) for _ in range(2 if k > 1 else 1)]
    cache_ref, items_ref, out_ref, q_ref, m_ref, l_ref, acc_ref, buf, sem, q_sem = refs
    per_device = q_ref.shape[0] // LQ
    entries = 2 * most

    def fetch(i, slot):
        @pl.when(i < most)
        def _():
            row = row_ref[k * most + jnp.minimum(i, most - 1)]
            pltpu.make_async_copy(cache_ref.at[row], buf.at[slot], sem.at[slot]).start()

        @pl.when(i >= most)
        def _():
            pltpu.make_async_copy(
                items_ref.at[jnp.maximum(i - most, 0)], buf.at[slot], sem.at[slot]
            ).start()

    if len(questions) == 1:
        pltpu.make_async_copy(questions[0], q_ref, q_sem).start()
    else:
        inner = is_inner()

        @pl.when(inner)
        def _():
            pltpu.make_async_copy(questions[0], q_ref, q_sem).start()

        @pl.when(jnp.logical_not(inner))
        def _():
            pltpu.make_async_copy(questions[1], q_ref, q_sem).start()

    fetch(jnp.int32(0), 0)
    m_ref[...] = jnp.full(m_ref.shape, NEG, jnp.float32)
    l_ref[...] = jnp.zeros(l_ref.shape, jnp.float32)
    acc_ref[...] = jnp.zeros(acc_ref.shape, jnp.float32)
    pltpu.make_async_copy(q_ref, q_ref, q_sem).wait()
    if k == 0:

        def own_block(i, carry):
            question, head = i // heads, lax.rem(i, heads)
            part_step(
                q_ref,
                m_ref,
                l_ref,
                acc_ref,
                question,
                head,
                own_ref[question, head, :, :HD],
                own_ref[question, head, :, HD:],
                True,
            )
            return carry

        lax.fori_loop(0, per_device * heads, own_block, 0)

    def item(i, carry):
        slot = lax.rem(i, 2)
        pltpu.make_async_copy(buf.at[slot], buf.at[slot], sem.at[slot]).wait()

        @pl.when(i + 1 < entries)
        def _():
            fetch(i + 1, lax.rem(i + 1, 2))

        at = k * most + lax.rem(i, most)
        tag = jnp.where(i < most, tag_ref[at], far_tag_ref[at])

        for head in range(heads):
            part_step(
                q_ref,
                m_ref,
                l_ref,
                acc_ref,
                tag,
                head,
                buf[slot, head, :, :HD],
                buf[slot, head, :, HD:],
                False,
            )
        return carry

    lax.fori_loop(0, entries, item, 0)
    eye = unit()

    def close(c, carry):
        head, g = c // GROUP, lax.rem(c, GROUP)
        columns = pl.ds(pl.multiple_of(c * HD, HD), HD)
        part = pl.ds(pl.multiple_of(g * LQ, LQ), LQ)
        for question in range(per_device):
            total = l_ref[question, head, part, :]
            some = total > 0.0
            safe = jnp.where(some, total, 1.0)
            out_ref[question, :LQ, columns] = (
                acc_ref[question, head, part, :] / safe
            ).astype(out_ref.dtype)
            level = jnp.where(some, m_ref[question, head, part, :] + jnp.log2(safe), NEG)
            line = jnp.sum(jnp.where(eye, level, 0.0), axis=0, keepdims=True)
            store_level(out_ref, question, columns, line)
        return carry

    lax.fori_loop(0, heads * GROUP, close, 0)


def store_level(out_ref, question, columns, line):
    row_of = lax.broadcasted_iota(jnp.int32, (EXTRA, line.shape[1]), 0)
    high = line.astype(jnp.bfloat16).astype(jnp.float32)
    both = jnp.where(row_of == 0, high, jnp.where(row_of == 1, line - high, 0.0))
    out_ref[question, LQ:, columns] = both.astype(out_ref.dtype)


def part_call(k, most, tables, own, questions, cache, items):
    tokens, columns = questions[0].shape
    heads, item = cache.shape[1], cache.shape[1:]
    state = (tokens // LQ, heads, GROUP * LQ, HD)
    smem = pl.BlockSpec(memory_space=pltpu.SMEM)
    vmem = pl.BlockSpec(memory_space=pltpu.VMEM)
    anyspace = pl.BlockSpec(memory_space=pl.ANY)
    owned = [own] if k == 0 else []
    weights = 2 * most * heads * GROUP * LQ * item[1]
    return pl.pallas_call(
        functools.partial(part_kernel, k, most, heads),
        out_shape=jax.ShapeDtypeStruct((tokens // LQ, LQ + EXTRA, columns), cache.dtype),
        in_specs=[smem] * 3 + [vmem] * len(owned) + [anyspace] * (len(questions) + 2),
        out_specs=vmem,
        scratch_shapes=[
            pltpu.VMEM((tokens, columns), cache.dtype),
            pltpu.VMEM(state, jnp.float32),
            pltpu.VMEM(state, jnp.float32),
            pltpu.VMEM(state, jnp.float32),
            pltpu.VMEM((2,) + item, cache.dtype),
            pltpu.SemaphoreType.DMA((2,)),
            pltpu.SemaphoreType.DMA,
        ],
        compiler_params=pltpu.CompilerParams(vmem_limit_bytes=VMEM_BYTES),
        cost_estimate=pl.CostEstimate(
            flops=weights * HD * 4,
            bytes_accessed=2 * most * math.prod(item) * 2,
            transcendentals=weights,
        ),
    )(*tables, *owned, *questions, cache, items)


def blend(a_ref, b_ref, out_ref, leveled):
    eye = unit()
    ones = jnp.ones((2 * LQ, LQ), jnp.bfloat16)

    def level_of(ref):
        both = ref[0, LQ:, :].astype(jnp.float32)
        return both[:1] + both[1:2]

    one, two = level_of(a_ref), level_of(b_ref)
    top = jnp.maximum(one, two)
    first, second = jnp.exp2(one - top), jnp.exp2(two - top)
    total = first + second
    share = first / total
    high = share.astype(jnp.bfloat16).astype(jnp.float32)
    low = share - high
    for c in range(share.shape[1] // HD):
        columns = slice(c * HD, (c + 1) * HD)
        spread = jnp.concatenate(
            [
                jnp.where(eye, jnp.broadcast_to(v[:, columns], (LQ, LQ)), 0.0).astype(jnp.bfloat16)
                for v in (high, low)
            ],
            axis=1,
        )
        column = jnp.dot(spread, ones, preferred_element_type=jnp.float32)
        a = a_ref[0, :LQ, columns].astype(jnp.float32)
        b = b_ref[0, :LQ, columns].astype(jnp.float32)
        value = (b + (a - b) * column).astype(out_ref.dtype)
        if leveled:
            out_ref[0, :LQ, columns] = value
        else:
            out_ref[:, columns] = value
    if leveled:
        store_level(out_ref, 0, slice(None), top + jnp.log2(total))


def merge_kernel(a_ref, b_ref, out_ref):
    inner = is_inner()

    @pl.when(inner)
    def _():
        blend(a_ref, b_ref, out_ref, True)

    @pl.when(jnp.logical_not(inner))
    def _():
        out_ref[...] = a_ref[...]


def finish_kernel(a_ref, b_ref, out_ref):
    blend(a_ref, b_ref, out_ref, False)


def question_spec(value, at):
    shape = (1,) + value.shape[1:]
    if value.shape[0] == 1:
        return pl.BlockSpec(shape, lambda q: (0, 0, 0))
    if at is None:
        return pl.BlockSpec(shape, lambda q: (q, 0, 0))
    return pl.BlockSpec(shape, lambda q: (at, 0, 0))


def join_call(a, b, at, leveled):
    questions = a.shape[0] if at is None else 1
    columns = a.shape[2]
    if leveled:
        shape, block = (questions,) + a.shape[1:], (1,) + a.shape[1:]
        out_spec = pl.BlockSpec(block, lambda q: (q, 0, 0))
    else:
        shape = (questions * LQ, columns)
        out_spec = pl.BlockSpec((LQ, columns), lambda q: (q, 0))
    size = questions * LQ * columns
    return pl.pallas_call(
        merge_kernel if leveled else finish_kernel,
        out_shape=jax.ShapeDtypeStruct(shape, a.dtype),
        grid=(questions,),
        in_specs=[question_spec(a, at), question_spec(b, at)],
        out_specs=out_spec,
        compiler_params=pltpu.CompilerParams(vmem_limit_bytes=VMEM_BYTES),
        cost_estimate=pl.CostEstimate(flops=size * 8, bytes_accessed=size * 6, transcendentals=0),
    )(a, b)


def line_steps(queries, own_kv, passage_cache, out_weight, lists, passage_slot, question_slot):
    per_device = queries.shape[0] // LQ
    heads = own_kv.shape[1]
    most = per_device * lists.shape[1] // (2 * LINE)

    def send(value, pairs):
        return lax.ppermute(value, "pass", pairs)

    def part(k, *args):
        return part_call(k, most, tables, own if k == 0 else None, *args)

    def join(a, b, at=None, leveled=True):
        return join_call(a, b, at, leveled)

    across = [(p, p ^ 1) for p in range(2 * LINE)]
    inner_across = [(p, d) for p, d in across if p // 2 in (1, 2)]
    outer_across = [(p, d) for p, d in across if p // 2 not in (1, 2)]
    near, middle = mirror(1), mirror(3, "inner")
    inward, outward = mirror(1, "outer"), mirror(1, "inner")
    q_near = send(queries, near)
    q_mid = send(queries, middle)
    w_across = send(out_weight, across)
    cache = jnp.transpose(passage_cache, (0, 2, 1, 3))
    row, tag, far_tag, *items = sort_items(
        lists, passage_slot, question_slot, cache, most, per_device
    )
    tables = (row, tag, far_tag)
    q_out = send(q_mid, outward)
    q_cross = send(q_near, middle)
    q_end = send(q_cross, outward)
    far = [send(items[k], across) for k in range(LINE)]
    own = own_kv.reshape(per_device, LQ, heads, 2 * HD).transpose(0, 2, 1, 3)
    part2 = part(2, [q_cross, q_out], cache, far[2])
    part3 = part(3, [q_mid, q_end], cache, far[3])
    part0 = part(0, [queries], cache, far[0])
    part1 = part(1, [q_near], cache, far[1])
    back2 = send(part2, inward)
    w_in = send(out_weight, mirror(2, "outer"))
    w_out = send(out_weight, mirror(2, "inner"))
    back3 = send(part3, inward)
    w_in_both = send(w_in, inner_across)
    w_out_both = send(w_out, outer_across)
    own_rows, near_rows = [], []
    for q in range(per_device):
        cross3 = send(join(part3, back2, q), middle)
        near0 = join(part0, cross3, q)
        beside = send(near0, near)
        cross2 = send(join(part2, back3, q), middle)
        near1 = join(part1, cross2, q)
        back1 = send(near1, near)
        near_rows.append(join(near1, beside, q, False))
        own_rows.append(join(near0, back1, q, False))
    weights = (out_weight, w_across, w_in, w_in_both, w_out, w_out_both)
    sums = project_call(near_rows, weights, True)
    far_out = send_far(sums)
    home_out = project_call(own_rows, weights, False)
    return jnp.where(at_home(), home_out, far_out)


def send_far(sums):
    pairs = []
    for p in range(2 * LINE):
        for h in range(LINE):
            if h % 2 != (p // 2) % 2:
                pairs.append((p * LINE + h, (p ^ 2) * LINE + (h ^ 1)))
    return lax.ppermute(sums, ("pass", "head"), pairs)


MESH = pl.DeviceIdType.MESH


def at_home():
    return lax.axis_index("head") % 2 == lax.axis_index("pass") // 2 % 2


def project_kernel(pieces, far, *refs):
    rows_refs = refs[:pieces]
    own_ref, across_ref, in_ref, in2_ref, out1_ref, out2_ref = refs[pieces : pieces + 6]
    refs = refs[pieces + 6 :]
    out_ref, context_ref, w_ref, part_ref, core_ref, y_ref, ysend_ref = refs[:7]
    row_sem, w_sem, send_sem, recv_sem = refs[7:]
    me, head = lax.axis_index("pass"), lax.axis_index("head")
    z, x, y = me // 2, me % 2, head // 2
    wide = w_ref.shape[3]
    inner = is_inner()
    core_peer = (me, head ^ 1)
    y_peer = (me, head ^ 2)
    sums = jnp.logical_not(at_home()) if far else at_home()

    row_loads = [
        pltpu.make_async_copy(ref, context_ref.at[pl.ds(i * LQ, LQ)], row_sem.at[i])
        for i, ref in enumerate(rows_refs)
    ]
    for load in row_loads:
        load.start()

    def load_here():
        pltpu.make_async_copy(own_ref, w_ref.at[0, x], w_sem.at[0, x]).start()
        pltpu.make_async_copy(across_ref, w_ref.at[0, 1 - x], w_sem.at[0, 1 - x]).start()

    def load_there():
        for which, (one, two) in (
            (inner, (in_ref, in2_ref)),
            (jnp.logical_not(inner), (out1_ref, out2_ref)),
        ):

            @pl.when(which)
            def _():
                pltpu.make_async_copy(one, w_ref.at[1, x], w_sem.at[1, x]).start()
                pltpu.make_async_copy(two, w_ref.at[1, 1 - x], w_sem.at[1, 1 - x]).start()

    here_first = y != z // 2

    @pl.when(here_first)
    def _():
        load_here()
        load_there()

    @pl.when(jnp.logical_not(here_first))
    def _():
        load_there()
        load_here()

    barrier = pltpu.get_barrier_semaphore()
    for peer in (core_peer, y_peer):
        pl.semaphore_signal(barrier, inc=1, device_id=peer, device_id_type=MESH)
    pl.semaphore_wait(barrier, 2)

    def remote(src, dst, i, peer):
        return pltpu.make_async_remote_copy(
            src_ref=src,
            dst_ref=dst,
            send_sem=send_sem.at[i],
            recv_sem=recv_sem.at[i],
            device_id=peer,
            device_id_type=MESH,
        )

    def columns(j):
        return pl.ds(j * wide, wide)

    core_copies = [
        [remote(part_ref.at[s, j], core_ref.at[s, j], s * 2 + j, core_peer) for j in range(2)]
        for s in range(2)
    ]
    y_copies = [remote(ysend_ref.at[j], y_ref.at[j], 4 + j, y_peer) for j in range(2)]

    for load in row_loads:
        load.wait()

    for s, to_y in enumerate((1 - y, y)):
        here = jnp.where(to_y == z // 2, 0, 1)
        for j in range(2):
            block = w_ref.at[here, j]
            pltpu.make_async_copy(block, block, w_sem.at[here, j]).wait()
            part_ref[s, j] = jnp.dot(
                context_ref[...], w_ref[here, j], preferred_element_type=jnp.float32
            ).astype(part_ref.dtype)

            @pl.when(jnp.logical_not(sums))
            def _():
                core_copies[s][j].start()

            @pl.when(sums)
            def _():
                core_copies[s][j].wait_recv()
                value = part_ref[s, j].astype(jnp.float32) + core_ref[s, j].astype(jnp.float32)
                if s == 0:
                    ysend_ref[j] = value.astype(ysend_ref.dtype)
                    y_copies[j].start()
                else:
                    y_copies[j].wait_recv()
                    total = (value + y_ref[j].astype(jnp.float32)).astype(out_ref.dtype)
                    out_ref[:, columns(j)] = total

    @pl.when(sums)
    def _():
        for copy in y_copies:
            copy.wait_send()

    @pl.when(jnp.logical_not(sums))
    def _():
        for copies in core_copies:
            for copy in copies:
                copy.wait_send()


def project_call(pieces, weights, far):
    own = weights[0]
    rows, (depth, wide) = len(pieces) * LQ, own.shape
    dtype = own.dtype
    return pl.pallas_call(
        functools.partial(project_kernel, len(pieces), far),
        out_shape=jax.ShapeDtypeStruct((rows, 2 * wide), dtype),
        in_specs=[pl.BlockSpec(memory_space=pl.ANY)] * (len(pieces) + len(weights)),
        out_specs=pl.BlockSpec(memory_space=pltpu.VMEM),
        scratch_shapes=[
            pltpu.VMEM((rows, depth), dtype),
            pltpu.VMEM((2, 2, depth, wide), dtype),
            pltpu.VMEM((2, 2, rows, wide), dtype),
            pltpu.VMEM((2, 2, rows, wide), dtype),
            pltpu.VMEM((2, rows, wide), dtype),
            pltpu.VMEM((2, rows, wide), dtype),
            pltpu.SemaphoreType.DMA((len(pieces),)),
            pltpu.SemaphoreType.DMA((2, 2)),
            pltpu.SemaphoreType.DMA((6,)),
            pltpu.SemaphoreType.DMA((6,)),
        ],
        compiler_params=pltpu.CompilerParams(
            collective_id=int(far), has_side_effects=True, vmem_limit_bytes=VMEM_BYTES
        ),
        name="project_far" if far else "project_home",
        cost_estimate=pl.CostEstimate(
            flops=2 * 4 * rows * depth * wide,
            bytes_accessed=4 * depth * wide * 2,
            transcendentals=0,
        ),
    )(*pieces, *weights)


def suits_line(mesh, queries, lists):
    passes, heads = mesh.shape["pass"], mesh.shape["head"]
    entries = queries.shape[0] // LQ // passes * lists.shape[1]
    return passes == 2 * LINE and heads == LINE and entries % passes == 0


def solution(mesh):
    in_specs = (
        P("pass", "head"),
        P("pass", "head", None),
        P("pass", None, "head", None),
        P("head", "pass"),
        P(),
        P(),
        P(),
    )
    out_specs = P("pass", "head")

    def run(*args):
        if not suits_line(mesh, args[0], args[4]):
            return jax.shard_map(
                body, mesh=mesh, in_specs=in_specs, out_specs=out_specs, check_vma=False
            )(*args)
        step = jax.shard_map(
            line_steps, mesh=mesh, in_specs=in_specs, out_specs=out_specs, check_vma=False
        )
        return step(*args)

    return run
```

```python
import functools
import math

import jax
import jax.numpy as jnp
from jax import lax
from jax.experimental import pallas as pl
from jax.experimental.pallas import tpu as pltpu
from jax.sharding import PartitionSpec as P


H = 64
KVH = 8
HD = 128
LQ = 128
GROUP = H // KVH
COEF = HD ** (-0.5) * math.log2(math.e)
NEG = -1e30
ROWS = 256


def round_of(a, b, n):
    if n & (n - 1) == 0:
        return a ^ b
    return lax.rem(b - a + n, n)


def pairs_of(k, n):
    if n & (n - 1) == 0:
        return [(p, p ^ k) for p in range(n)]
    return [(p, (p + k) % n) for p in range(n)]


def order_of(n):
    rest = range(1, n)
    return sorted(rest, key=lambda k: (bin(k).count("1"), k))


def gather_kernel(n, most, per_device, order, lists_ref, pslot_ref, qslot_ref, cache_ref, *refs):
    recv_ref, own_row_ref = refs[0], refs[1]
    outs = refs[2 : 2 + len(order)]
    send_row, send_cnt, recv_cnt, buf, in_sem, out_sem = refs[2 + len(order) :]
    me = lax.axis_index("pass")
    pass_dev = cache_ref.shape[0]
    topp, nq = lists_ref.shape
    for k in range(n):
        send_cnt[k] = 0
        recv_cnt[k] = 0
    for i in range(n * most):
        recv_ref[i] = -1
        send_row[i] = 0

    def question(q, carry):
        slot = qslot_ref[q]
        dest = slot // per_device
        local = slot - dest * per_device
        k_send = round_of(me, dest, n)
        for t in range(topp):
            row = pslot_ref[lists_ref[t, q]]
            owner = row // pass_dev

            @pl.when(owner == me)
            def _():
                count = send_cnt[k_send]
                send_row[k_send * most + count] = row - owner * pass_dev
                send_cnt[k_send] = count + 1

            @pl.when(dest == me)
            def _():
                k = round_of(owner, me, n)
                count = recv_cnt[k]
                recv_ref[k * most + count] = local
                recv_cnt[k] = count + 1

        return carry

    lax.fori_loop(0, nq, question, 0)
    for r in range(most):
        own_row_ref[r] = send_row[r]
    copies = []
    for j, k in enumerate(order):
        for r in range(most):
            i = j * most + r
            get = pltpu.make_async_copy(
                cache_ref.at[send_row[k * most + r]], buf.at[i], in_sem.at[i]
            )
            get.start()
            copies.append((get, pltpu.make_async_copy(buf.at[i], outs[j].at[r], out_sem.at[i])))
    for get, put in copies:
        get.wait()
        put.start()
    for get, put in copies:
        put.wait()


def gather(lists, passage_slot, question_slot, cache, n, most, per_device, order):
    item = cache.shape[1:]
    slots = (n - 1) * most
    smem = pl.BlockSpec(memory_space=pltpu.SMEM)
    anyspace = pl.BlockSpec(memory_space=pl.ANY)
    return pl.pallas_call(
        functools.partial(gather_kernel, n, most, per_device, order),
        out_shape=[
            jax.ShapeDtypeStruct((n * most,), jnp.int32),
            jax.ShapeDtypeStruct((most,), jnp.int32),
        ]
        + [jax.ShapeDtypeStruct((most,) + item, cache.dtype)] * len(order),
        in_specs=[smem, smem, smem, anyspace],
        out_specs=[smem, smem] + [anyspace] * len(order),
        scratch_shapes=[
            pltpu.SMEM((n * most,), jnp.int32),
            pltpu.SMEM((n,), jnp.int32),
            pltpu.SMEM((n,), jnp.int32),
            pltpu.VMEM((slots,) + item, cache.dtype),
            pltpu.SemaphoreType.DMA((slots,)),
            pltpu.SemaphoreType.DMA((slots,)),
        ],
        name="gather_items",
        cost_estimate=pl.CostEstimate(
            flops=0, bytes_accessed=2 * slots * math.prod(item) * 2, transcendentals=0
        ),
    )(lists.T, passage_slot, question_slot, cache)


def block_step(q_ref, m_ref, l_ref, acc_ref, question, head, keys, values, causal):
    rows = q_ref.shape[2]
    step = min(ROWS, rows)
    width = keys.shape[0]
    ones = jnp.ones(values.shape, values.dtype)
    extended = jnp.concatenate([values, ones], axis=1)
    for start in range(0, rows, step):
        part = pl.ds(start, step)
        q = q_ref[question, head, part, :]
        scores = (
            lax.dot_general(q, keys, (((1,), (1,)), ((), ())), preferred_element_type=jnp.float32)
            * COEF
        )
        if causal:
            token = lax.broadcasted_iota(jnp.int32, scores.shape, 0) % LQ
            column = lax.broadcasted_iota(jnp.int32, scores.shape, 1)
            scores = jnp.where(column <= token, scores, NEG)
        old = m_ref[question, head, part, :]
        new = jnp.maximum(old, jnp.max(scores, axis=1, keepdims=True))
        weights = jnp.exp2(scores - jnp.concatenate([new] * (width // HD), axis=1))
        mixed = jnp.dot(
            weights.astype(jnp.bfloat16), extended, preferred_element_type=jnp.float32
        )
        alpha = jnp.exp2(old - new)
        m_ref[question, head, part, :] = new
        l_ref[question, head, part, :] = l_ref[question, head, part, :] * alpha + mixed[:, HD:]
        acc_ref[question, head, part, :] = (
            acc_ref[question, head, part, :] * alpha + mixed[:, :HD]
        )


def attend_kernel(first, last, rounds, most, *refs):
    refs = list(refs)
    recv_ref, q_ref = refs.pop(0), refs.pop(0)
    if first:
        row_ref, own_ref, cache_ref = refs.pop(0), refs.pop(0), refs.pop(0)
        sources = None
        entries = most
    else:
        state_in = [refs.pop(0) for _ in range(3)]
        sources = [refs.pop(0) for _ in rounds]
        entries = len(rounds) * most
    if last:
        out_ref = refs.pop(0)
        m_ref, l_ref, acc_ref = [refs.pop(0) for _ in range(3)]
    else:
        m_ref, l_ref, acc_ref = [refs.pop(0) for _ in range(3)]
    buf, sem = refs
    per_device, heads = q_ref.shape[0], q_ref.shape[1]

    def fetch(i, slot):
        if first:
            pltpu.make_async_copy(cache_ref.at[row_ref[i]], buf.at[slot], sem.at[slot]).start()
            return
        for j in range(len(rounds)):

            @pl.when(i // most == j)
            def _():
                pltpu.make_async_copy(
                    sources[j].at[i - j * most], buf.at[slot], sem.at[slot]
                ).start()

    def tag_of(i):
        if first:
            return recv_ref[i]
        k = jnp.int32(0)
        for j, value in enumerate(rounds):
            k = jnp.where(i // most == j, value, k)
        return recv_ref[k * most + lax.rem(i, most)]

    fetch(jnp.int32(0), 0)
    if first:
        m_ref[...] = jnp.full(m_ref.shape, NEG, jnp.float32)
        l_ref[...] = jnp.zeros(l_ref.shape, jnp.float32)
        acc_ref[...] = jnp.zeros(acc_ref.shape, jnp.float32)

        def own_block(question, carry):
            for head in range(heads):
                block = own_ref[question, head]
                block_step(
                    q_ref, m_ref, l_ref, acc_ref, question, head, block[:, :HD], block[:, HD:], True
                )
            return carry

        lax.fori_loop(0, per_device, own_block, 0)
    else:
        m_ref[...] = state_in[0][...]
        l_ref[...] = state_in[1][...]
        acc_ref[...] = state_in[2][...]

    def item(i, carry):
        slot = lax.rem(i, 2)
        pltpu.make_async_copy(buf.at[slot], buf.at[slot], sem.at[slot]).wait()

        @pl.when(i + 1 < entries)
        def _():
            fetch(i + 1, lax.rem(i + 1, 2))

        tag = tag_of(i)

        @pl.when(tag >= 0)
        def _():
            for head in range(heads):
                block_step(
                    q_ref,
                    m_ref,
                    l_ref,
                    acc_ref,
                    tag,
                    head,
                    buf[slot, head, :, :HD],
                    buf[slot, head, :, HD:],
                    False,
                )

        return carry

    lax.fori_loop(0, entries, item, 0)
    if last:
        for question in range(per_device):
            for head in range(heads):
                for g in range(GROUP):
                    part = pl.ds(g * LQ, LQ)
                    column = (head * GROUP + g) * HD
                    out_ref[pl.ds(question * LQ, LQ), pl.ds(column, HD)] = (
                        acc_ref[question, head, part, :] / l_ref[question, head, part, :]
                    ).astype(out_ref.dtype)


def attend_call(first, last, rounds, most, recv, q, rest, item):
    per_device, heads, rows, _ = q.shape
    state = jax.ShapeDtypeStruct(q.shape, jnp.float32)
    smem = pl.BlockSpec(memory_space=pltpu.SMEM)
    vmem = pl.BlockSpec(memory_space=pltpu.VMEM)
    anyspace = pl.BlockSpec(memory_space=pl.ANY)
    if first:
        in_specs = [smem, vmem, smem, vmem, anyspace]
        entries = most
    else:
        in_specs = [smem, vmem] + [vmem] * 3 + [anyspace] * len(rounds)
        entries = most * len(rounds)
    scratch = [pltpu.VMEM((2,) + item, q.dtype), pltpu.SemaphoreType.DMA((2,))]
    if last:
        out_shape = jax.ShapeDtypeStruct((per_device * LQ, heads * GROUP * HD), q.dtype)
        out_specs = vmem
        scratch = [pltpu.VMEM(q.shape, jnp.float32)] * 3 + scratch
    else:
        out_shape = [state] * 3
        out_specs = [vmem] * 3
    weights = entries * heads * rows * item[1]
    return pl.pallas_call(
        functools.partial(attend_kernel, first, last, rounds, most),
        out_shape=out_shape,
        in_specs=in_specs,
        out_specs=out_specs,
        scratch_shapes=scratch,
        name="attend_first" if first else ("attend_last" if last else "attend_more"),
        cost_estimate=pl.CostEstimate(
            flops=weights * HD * 4,
            bytes_accessed=entries * math.prod(item) * 2,
            transcendentals=weights,
        ),
    )(recv, q, *rest)


def weight_blocks(own, n):
    if n & (n - 1):
        return [lax.all_gather(own, "pass", axis=1, tiled=True)]
    have = {0: own}
    bit = n // 2
    while bit:
        for k in list(have):
            have[k ^ bit] = lax.ppermute(have[k], "pass", pairs_of(bit, n))
        bit //= 2
    return [have[k] for k in range(n)]


def project(context, weights):
    parts = [
        jnp.dot(context, weight, preferred_element_type=jnp.float32).astype(jnp.bfloat16)
        for weight in weights
    ]
    me = lax.axis_index("pass")
    bit = len(parts) // 2
    while bit:
        swap = (me & bit) != 0
        parts = [jnp.where(swap, parts[k ^ bit], parts[k]) for k in range(len(parts))]
        bit //= 2
    return jnp.concatenate(parts, axis=1)


def body(queries, own_kv, passage_cache, out_weight, lists, passage_slot, question_slot):
    n = lax.axis_size("pass")
    per_device = queries.shape[0] // LQ
    heads = own_kv.shape[1]
    entries = per_device * lists.shape[1]
    most = (entries + n - 1) // n
    order = order_of(n)
    cache = jnp.transpose(passage_cache, (0, 2, 1, 3))
    recv, own_row, *items = gather(
        lists, passage_slot, question_slot, cache, n, most, per_device, order
    )
    arrived = [
        lax.ppermute(item, "pass", pairs_of(k, n)) for k, item in zip(order, items)
    ]
    weights = weight_blocks(out_weight, n)
    q = (
        queries.reshape(per_device, LQ, heads, GROUP, HD)
        .transpose(0, 2, 3, 1, 4)
        .reshape(per_device, heads, GROUP * LQ, HD)
    )
    own = own_kv.reshape(per_device, LQ, heads, 2 * HD).transpose(0, 2, 1, 3)
    item = cache.shape[1:]
    state = attend_call(True, False, (0,), most, recv, q, (own_row, own, cache), item)
    calls = 3
    bounds = [len(order) * i // calls for i in range(calls + 1)]
    for i in range(calls):
        rounds = tuple(order[bounds[i] : bounds[i + 1]])
        rest = tuple(state) + tuple(arrived[bounds[i] : bounds[i + 1]])
        state = attend_call(False, i == calls - 1, rounds, most, recv, q, rest, item)
    context = state
    return lax.psum_scatter(project(context, weights), "head", scatter_dimension=1, tiled=True)


LINE = 4
EXTRA = 8
ITEM_ORDER = (2, 0, 3, 1)
VMEM_BYTES = 67043328


def mirror(k, ends=None):
    pairs = [(p, p ^ int(2 * k)) for p in range(2 * LINE)]
    if ends is None:
        return pairs
    return [(p, d) for p, d in pairs if (p // 2 in (0, LINE - 1)) == (ends == "outer")]


def is_inner():
    z = lax.axis_index("pass") // 2
    return jnp.logical_and(z > 0, z < LINE - 1)


def sort_kernel(most, per_device, lists_ref, pslot_ref, qslot_ref, cache_ref, *refs):
    row_ref, tag_ref, far_tag_ref = refs[:3]
    outs = refs[3 : 3 + LINE]
    send_row, near_cnt, send_cnt, far_cnt, buf, in_sem, out_sem = refs[3 + LINE :]
    me = lax.axis_index("pass")
    z, x = me // 2, me % 2
    pass_dev = cache_ref.shape[0]
    topp, nq = lists_ref.shape
    for k in range(LINE):
        near_cnt[k] = 0
        send_cnt[k] = 0
        far_cnt[k] = 0

    def take(i):
        return pltpu.make_async_copy(cache_ref.at[send_row[i]], buf.at[i], in_sem.at[i])

    def question(q, carry):
        slot = qslot_ref[q]
        dest = slot // per_device
        local = slot - dest * per_device
        k = (dest // 2) ^ z

        @pl.when(dest % 2 == x)
        def _():
            for t in range(topp):
                row = pslot_ref[lists_ref[t, q]]
                owner = row // pass_dev

                @pl.when(owner == me)
                def _():
                    at = k * most + near_cnt[k]
                    row_ref[at] = row - owner * pass_dev
                    tag_ref[at] = local
                    near_cnt[k] = near_cnt[k] + 1

                @pl.when(owner == (me ^ 1))
                def _():
                    far_tag_ref[k * most + far_cnt[k]] = local
                    far_cnt[k] = far_cnt[k] + 1

        @pl.when(dest % 2 != x)
        def _():
            for t in range(topp):
                row = pslot_ref[lists_ref[t, q]]
                owner = row // pass_dev

                @pl.when(owner == me)
                def _():
                    at = k * most + send_cnt[k]
                    send_row[at] = row - owner * pass_dev
                    send_cnt[k] = send_cnt[k] + 1
                    take(at).start()

        return carry

    lax.fori_loop(0, nq, question, 0)
    slots = [k * most + r for k in ITEM_ORDER for r in range(most)]
    puts = [pltpu.make_async_copy(buf.at[i], outs[i // most].at[i % most], out_sem.at[i]) for i in slots]
    for i, put in zip(slots, puts):
        take(i).wait()
        put.start()
    for put in puts:
        put.wait()


def sort_items(lists, passage_slot, question_slot, cache, most, per_device):
    item = cache.shape[1:]
    slots = LINE * most
    smem = pl.BlockSpec(memory_space=pltpu.SMEM)
    anyspace = pl.BlockSpec(memory_space=pl.ANY)
    return pl.pallas_call(
        functools.partial(sort_kernel, most, per_device),
        out_shape=[jax.ShapeDtypeStruct((slots,), jnp.int32)] * 3
        + [jax.ShapeDtypeStruct((most,) + item, cache.dtype)] * LINE,
        in_specs=[smem, smem, smem, anyspace],
        out_specs=[smem] * 3 + [anyspace] * LINE,
        scratch_shapes=[
            pltpu.SMEM((slots,), jnp.int32),
            pltpu.SMEM((LINE,), jnp.int32),
            pltpu.SMEM((LINE,), jnp.int32),
            pltpu.SMEM((LINE,), jnp.int32),
            pltpu.VMEM((slots,) + item, cache.dtype),
            pltpu.SemaphoreType.DMA((slots,)),
            pltpu.SemaphoreType.DMA((slots,)),
        ],
        compiler_params=pltpu.CompilerParams(vmem_limit_bytes=VMEM_BYTES),
        name="sort_items",
        cost_estimate=pl.CostEstimate(
            flops=0, bytes_accessed=2 * slots * math.prod(item) * 2, transcendentals=0
        ),
    )(lists.T, passage_slot, question_slot, cache)


def unit():
    r = lax.broadcasted_iota(jnp.int32, (LQ, LQ), 0)
    c = lax.broadcasted_iota(jnp.int32, (LQ, LQ), 1)
    return r == c


def part_step(q_ref, m_ref, l_ref, acc_ref, question, head, keys, values, causal):
    rows = GROUP * LQ
    width = keys.shape[0]
    ones = jnp.ones(values.shape, values.dtype)
    extended = jnp.concatenate([values, ones], axis=1)
    tokens = pl.ds(pl.multiple_of(question * LQ, LQ), LQ)
    for start in range(0, rows, ROWS):
        part = pl.ds(start, ROWS)
        q = jnp.concatenate(
            [
                q_ref[tokens, pl.ds(pl.multiple_of((head * GROUP + g) * HD, HD), HD)]
                for g in range(start // LQ, (start + ROWS) // LQ)
            ],
            axis=0,
        )
        scores = (
            lax.dot_general(q, keys, (((1,), (1,)), ((), ())), preferred_element_type=jnp.float32)
            * COEF
        )
        if causal:
            token = lax.broadcasted_iota(jnp.int32, scores.shape, 0) % LQ
            column = lax.broadcasted_iota(jnp.int32, scores.shape, 1)
            scores = jnp.where(column <= token, scores, NEG)
        old = m_ref[question, head, part, :]
        new = jnp.maximum(old, jnp.max(scores, axis=1, keepdims=True))
        weights = jnp.exp2(scores - jnp.concatenate([new] * (width // HD), axis=1))
        mixed = jnp.dot(
            weights.astype(jnp.bfloat16), extended, preferred_element_type=jnp.float32
        )
        alpha = jnp.exp2(old - new)
        m_ref[question, head, part, :] = new
        l_ref[question, head, part, :] = l_ref[question, head, part, :] * alpha + mixed[:, HD:]
        acc_ref[question, head, part, :] = (
            acc_ref[question, head, part, :] * alpha + mixed[:, :HD]
        )


def part_kernel(k, most, heads, *refs):
    refs = list(refs)
    row_ref, tag_ref, far_tag_ref = refs.pop(0), refs.pop(0), refs.pop(0)
    own_ref = refs.pop(0) if k == 0 else None
    questions = [refs.pop(0) for _ in range(2 if k > 1 else 1)]
    cache_ref, items_ref, out_ref, q_ref, m_ref, l_ref, acc_ref, buf, sem, q_sem = refs
    per_device = q_ref.shape[0] // LQ
    entries = 2 * most

    def fetch(i, slot):
        @pl.when(i < most)
        def _():
            row = row_ref[k * most + jnp.minimum(i, most - 1)]
            pltpu.make_async_copy(cache_ref.at[row], buf.at[slot], sem.at[slot]).start()

        @pl.when(i >= most)
        def _():
            pltpu.make_async_copy(
                items_ref.at[jnp.maximum(i - most, 0)], buf.at[slot], sem.at[slot]
            ).start()

    if len(questions) == 1:
        pltpu.make_async_copy(questions[0], q_ref, q_sem).start()
    else:
        inner = is_inner()

        @pl.when(inner)
        def _():
            pltpu.make_async_copy(questions[0], q_ref, q_sem).start()

        @pl.when(jnp.logical_not(inner))
        def _():
            pltpu.make_async_copy(questions[1], q_ref, q_sem).start()

    fetch(jnp.int32(0), 0)
    m_ref[...] = jnp.full(m_ref.shape, NEG, jnp.float32)
    l_ref[...] = jnp.zeros(l_ref.shape, jnp.float32)
    acc_ref[...] = jnp.zeros(acc_ref.shape, jnp.float32)
    pltpu.make_async_copy(q_ref, q_ref, q_sem).wait()
    if k == 0:

        def own_block(i, carry):
            question, head = i // heads, lax.rem(i, heads)
            part_step(
                q_ref,
                m_ref,
                l_ref,
                acc_ref,
                question,
                head,
                own_ref[question, head, :, :HD],
                own_ref[question, head, :, HD:],
                True,
            )
            return carry

        lax.fori_loop(0, per_device * heads, own_block, 0)

    def item(i, carry):
        slot = lax.rem(i, 2)
        pltpu.make_async_copy(buf.at[slot], buf.at[slot], sem.at[slot]).wait()

        @pl.when(i + 1 < entries)
        def _():
            fetch(i + 1, lax.rem(i + 1, 2))

        at = k * most + lax.rem(i, most)
        tag = jnp.where(i < most, tag_ref[at], far_tag_ref[at])

        for head in range(heads):
            part_step(
                q_ref,
                m_ref,
                l_ref,
                acc_ref,
                tag,
                head,
                buf[slot, head, :, :HD],
                buf[slot, head, :, HD:],
                False,
            )
        return carry

    lax.fori_loop(0, entries, item, 0)
    eye = unit()

    def close(c, carry):
        head, g = c // GROUP, lax.rem(c, GROUP)
        columns = pl.ds(pl.multiple_of(c * HD, HD), HD)
        part = pl.ds(pl.multiple_of(g * LQ, LQ), LQ)
        for question in range(per_device):
            total = l_ref[question, head, part, :]
            some = total > 0.0
            safe = jnp.where(some, total, 1.0)
            out_ref[question, :LQ, columns] = (
                acc_ref[question, head, part, :] / safe
            ).astype(out_ref.dtype)
            level = jnp.where(some, m_ref[question, head, part, :] + jnp.log2(safe), NEG)
            line = jnp.sum(jnp.where(eye, level, 0.0), axis=0, keepdims=True)
            store_level(out_ref, question, columns, line)
        return carry

    lax.fori_loop(0, heads * GROUP, close, 0)


def store_level(out_ref, question, columns, line):
    row_of = lax.broadcasted_iota(jnp.int32, (EXTRA, line.shape[1]), 0)
    high = line.astype(jnp.bfloat16).astype(jnp.float32)
    both = jnp.where(row_of == 0, high, jnp.where(row_of == 1, line - high, 0.0))
    out_ref[question, LQ:, columns] = both.astype(out_ref.dtype)


def part_call(k, most, tables, own, questions, cache, items):
    tokens, columns = questions[0].shape
    heads, item = cache.shape[1], cache.shape[1:]
    state = (tokens // LQ, heads, GROUP * LQ, HD)
    smem = pl.BlockSpec(memory_space=pltpu.SMEM)
    vmem = pl.BlockSpec(memory_space=pltpu.VMEM)
    anyspace = pl.BlockSpec(memory_space=pl.ANY)
    owned = [own] if k == 0 else []
    weights = 2 * most * heads * GROUP * LQ * item[1]
    return pl.pallas_call(
        functools.partial(part_kernel, k, most, heads),
        out_shape=jax.ShapeDtypeStruct((tokens // LQ, LQ + EXTRA, columns), cache.dtype),
        in_specs=[smem] * 3 + [vmem] * len(owned) + [anyspace] * (len(questions) + 2),
        out_specs=vmem,
        scratch_shapes=[
            pltpu.VMEM((tokens, columns), cache.dtype),
            pltpu.VMEM(state, jnp.float32),
            pltpu.VMEM(state, jnp.float32),
            pltpu.VMEM(state, jnp.float32),
            pltpu.VMEM((2,) + item, cache.dtype),
            pltpu.SemaphoreType.DMA((2,)),
            pltpu.SemaphoreType.DMA,
        ],
        compiler_params=pltpu.CompilerParams(vmem_limit_bytes=VMEM_BYTES),
        cost_estimate=pl.CostEstimate(
            flops=weights * HD * 4,
            bytes_accessed=2 * most * math.prod(item) * 2,
            transcendentals=weights,
        ),
    )(*tables, *owned, *questions, cache, items)


def blend(a_ref, b_ref, out_ref, leveled):
    eye = unit()
    ones = jnp.ones((2 * LQ, LQ), jnp.bfloat16)

    def level_of(ref):
        both = ref[0, LQ:, :].astype(jnp.float32)
        return both[:1] + both[1:2]

    one, two = level_of(a_ref), level_of(b_ref)
    top = jnp.maximum(one, two)
    first, second = jnp.exp2(one - top), jnp.exp2(two - top)
    total = first + second
    share = first / total
    high = share.astype(jnp.bfloat16).astype(jnp.float32)
    low = share - high
    for c in range(share.shape[1] // HD):
        columns = slice(c * HD, (c + 1) * HD)
        spread = jnp.concatenate(
            [
                jnp.where(eye, jnp.broadcast_to(v[:, columns], (LQ, LQ)), 0.0).astype(jnp.bfloat16)
                for v in (high, low)
            ],
            axis=1,
        )
        column = jnp.dot(spread, ones, preferred_element_type=jnp.float32)
        a = a_ref[0, :LQ, columns].astype(jnp.float32)
        b = b_ref[0, :LQ, columns].astype(jnp.float32)
        value = (b + (a - b) * column).astype(out_ref.dtype)
        if leveled:
            out_ref[0, :LQ, columns] = value
        else:
            out_ref[:, columns] = value
    if leveled:
        store_level(out_ref, 0, slice(None), top + jnp.log2(total))


def merge_kernel(a_ref, b_ref, out_ref):
    inner = is_inner()

    @pl.when(inner)
    def _():
        blend(a_ref, b_ref, out_ref, True)

    @pl.when(jnp.logical_not(inner))
    def _():
        out_ref[...] = a_ref[...]


def finish_kernel(a_ref, b_ref, out_ref):
    blend(a_ref, b_ref, out_ref, False)


def question_spec(value, at):
    shape = (1,) + value.shape[1:]
    if value.shape[0] == 1:
        return pl.BlockSpec(shape, lambda q: (0, 0, 0))
    if at is None:
        return pl.BlockSpec(shape, lambda q: (q, 0, 0))
    return pl.BlockSpec(shape, lambda q: (at, 0, 0))


def join_call(a, b, at, leveled):
    questions = a.shape[0] if at is None else 1
    columns = a.shape[2]
    if leveled:
        shape, block = (questions,) + a.shape[1:], (1,) + a.shape[1:]
        out_spec = pl.BlockSpec(block, lambda q: (q, 0, 0))
    else:
        shape = (questions * LQ, columns)
        out_spec = pl.BlockSpec((LQ, columns), lambda q: (q, 0))
    size = questions * LQ * columns
    return pl.pallas_call(
        merge_kernel if leveled else finish_kernel,
        out_shape=jax.ShapeDtypeStruct(shape, a.dtype),
        grid=(questions,),
        in_specs=[question_spec(a, at), question_spec(b, at)],
        out_specs=out_spec,
        compiler_params=pltpu.CompilerParams(vmem_limit_bytes=VMEM_BYTES),
        cost_estimate=pl.CostEstimate(flops=size * 8, bytes_accessed=size * 6, transcendentals=0),
    )(a, b)


def line_steps(queries, own_kv, passage_cache, out_weight, lists, passage_slot, question_slot):
    per_device = queries.shape[0] // LQ
    heads = own_kv.shape[1]
    most = per_device * lists.shape[1] // (2 * LINE)

    def send(value, pairs):
        return lax.ppermute(value, "pass", pairs)

    def part(k, *args):
        return part_call(k, most, tables, own if k == 0 else None, *args)

    def join(a, b, at=None, leveled=True):
        return join_call(a, b, at, leveled)

    across = [(p, p ^ 1) for p in range(2 * LINE)]
    inner_across = [(p, d) for p, d in across if p // 2 in (1, 2)]
    outer_across = [(p, d) for p, d in across if p // 2 not in (1, 2)]
    near, middle = mirror(1), mirror(3, "inner")
    inward, outward = mirror(1, "outer"), mirror(1, "inner")
    q_near = send(queries, near)
    q_mid = send(queries, middle)
    w_across = send(out_weight, across)
    cache = jnp.transpose(passage_cache, (0, 2, 1, 3))
    row, tag, far_tag, *items = sort_items(
        lists, passage_slot, question_slot, cache, most, per_device
    )
    tables = (row, tag, far_tag)
    q_out = send(q_mid, outward)
    q_cross = send(q_near, middle)
    q_end = send(q_cross, outward)
    far = [send(items[k], across) for k in range(LINE)]
    own = own_kv.reshape(per_device, LQ, heads, 2 * HD).transpose(0, 2, 1, 3)
    part2 = part(2, [q_cross, q_out], cache, far[2])
    part3 = part(3, [q_mid, q_end], cache, far[3])
    part0 = part(0, [queries], cache, far[0])
    part1 = part(1, [q_near], cache, far[1])
    back2 = send(part2, inward)
    w_in = send(out_weight, mirror(2, "outer"))
    w_out = send(out_weight, mirror(2, "inner"))
    back3 = send(part3, inward)
    w_in_both = send(w_in, inner_across)
    w_out_both = send(w_out, outer_across)
    own_rows, near_rows = [], []
    for q in range(per_device):
        cross3 = send(join(part3, back2, q), middle)
        near0 = join(part0, cross3, q)
        beside = send(near0, near)
        cross2 = send(join(part2, back3, q), middle)
        near1 = join(part1, cross2, q)
        back1 = send(near1, near)
        near_rows.append(join(near1, beside, q, False))
        own_rows.append(join(near0, back1, q, False))
    weights = (out_weight, w_across, w_in, w_in_both, w_out, w_out_both)
    far_send, far_keep = project_call(near_rows, weights, None)
    far_sent = send_far(far_send)
    return project_call(own_rows, weights, (far_keep, far_sent))


def send_far(sums):
    pairs = []
    for p in range(2 * LINE):
        for h in range(LINE):
            if h % 2 != (p // 2) % 2:
                pairs.append((p * LINE + h, p * LINE + (h ^ 2)))
    return lax.ppermute(sums, ("pass", "head"), pairs)


MESH = pl.DeviceIdType.MESH


def at_home():
    return lax.axis_index("head") % 2 == lax.axis_index("pass") // 2 % 2


def project_kernel(pieces, far, *refs):
    rows_refs = refs[:pieces]
    own_ref, across_ref, in_ref, in2_ref, out1_ref, out2_ref = refs[pieces : pieces + 6]
    refs = refs[pieces + 6 :]
    if far:
        send_ref, keep_ref = refs[:2]
    else:
        far_keep_ref, far_sent_ref, out_ref = refs[:3]
        refs = refs[1:]
    context_ref, w_ref, part_ref, core_ref, row_sem, w_sem, send_sem, recv_sem = refs[2:10]
    me, head = lax.axis_index("pass"), lax.axis_index("head")
    z, x, y = me // 2, me % 2, head // 2
    wide = w_ref.shape[3]
    inner = is_inner()
    core_peer, y_peer, z_peer = (me, head ^ 1), (me, head ^ 2), (me ^ 2, head ^ 1)
    home = at_home()
    sums = jnp.logical_not(home) if far else home

    row_loads = [
        pltpu.make_async_copy(ref, context_ref.at[pl.ds(i * LQ, LQ)], row_sem.at[i])
        for i, ref in enumerate(rows_refs)
    ]
    for load in row_loads:
        load.start()

    def load_here():
        pltpu.make_async_copy(own_ref, w_ref.at[0, x], w_sem.at[0, x]).start()
        pltpu.make_async_copy(across_ref, w_ref.at[0, 1 - x], w_sem.at[0, 1 - x]).start()

    def load_there():
        for which, (one, two) in (
            (inner, (in_ref, in2_ref)),
            (jnp.logical_not(inner), (out1_ref, out2_ref)),
        ):

            @pl.when(which)
            def _():
                pltpu.make_async_copy(one, w_ref.at[1, x], w_sem.at[1, x]).start()
                pltpu.make_async_copy(two, w_ref.at[1, 1 - x], w_sem.at[1, 1 - x]).start()

    here_first = y != z // 2

    @pl.when(here_first)
    def _():
        load_here()
        load_there()

    @pl.when(jnp.logical_not(here_first))
    def _():
        load_there()
        load_here()

    barrier = pltpu.get_barrier_semaphore()
    peers = (core_peer,) if far else (core_peer, y_peer, z_peer)
    for peer in peers:
        pl.semaphore_signal(barrier, inc=1, device_id=peer, device_id_type=MESH)
    pl.semaphore_wait(barrier, len(peers))

    def remote(src, dst, i, peer):
        return pltpu.make_async_remote_copy(
            src_ref=src,
            dst_ref=dst,
            send_sem=send_sem.at[i],
            recv_sem=recv_sem.at[i],
            device_id=peer,
            device_id_type=MESH,
        )

    def columns(j):
        return pl.ds(j * wide, wide)

    core_copies = [
        [remote(part_ref.at[s, j], core_ref.at[s, j], s * 2 + j, core_peer) for j in range(2)]
        for s in range(2)
    ]
    if not far:
        y_ref, ysend_ref, zsend_ref = refs[10:]
        y_copies = [remote(ysend_ref.at[j], y_ref.at[j], 4 + j, y_peer) for j in range(2)]
        z_copies = [
            remote(zsend_ref.at[j], out_ref.at[:, columns(j)], 6 + j, z_peer) for j in range(2)
        ]

        @pl.when(jnp.logical_not(home))
        def _():
            for j in range(2):
                zsend_ref[j] = (
                    far_keep_ref[j].astype(jnp.float32) + far_sent_ref[j].astype(jnp.float32)
                ).astype(zsend_ref.dtype)
                z_copies[j].start()

    for load in row_loads:
        load.wait()

    def multiply(s, to_y, j):
        here = jnp.where(to_y == z // 2, 0, 1)
        block = w_ref.at[here, j]
        pltpu.make_async_copy(block, block, w_sem.at[here, j]).wait()
        part_ref[s, j] = jnp.dot(
            context_ref[...], w_ref[here, j], preferred_element_type=jnp.float32
        ).astype(part_ref.dtype)

        @pl.when(jnp.logical_not(sums))
        def _():
            core_copies[s][j].start()

    def add_up(s, j):
        @pl.when(sums)
        def _():
            core_copies[s][j].wait_recv()
            value = part_ref[s, j].astype(jnp.float32) + core_ref[s, j].astype(jnp.float32)
            if far:
                target = keep_ref if s else send_ref
                target[j] = value.astype(target.dtype)
            elif s == 0:
                ysend_ref[j] = value.astype(ysend_ref.dtype)
                y_copies[j].start()
            else:
                y_copies[j].wait_recv()
                out_ref[:, columns(j)] = (value + y_ref[j].astype(jnp.float32)).astype(
                    out_ref.dtype
                )

    late = None
    for s, to_y in enumerate((1 - y, y)):
        for j in range(2):
            multiply(s, to_y, j)
            if late is not None:
                add_up(*late)
            late = (s, j)
    add_up(*late)

    @pl.when(jnp.logical_not(sums))
    def _():
        for copies in core_copies:
            for copy in copies:
                copy.wait_send()

    if not far:

        @pl.when(home)
        def _():
            for copy in y_copies:
                copy.wait_send()

        @pl.when(jnp.logical_not(home))
        def _():
            for copy in z_copies:
                copy.wait()


def project_call(pieces, weights, far_sums):
    own = weights[0]
    rows, (depth, wide) = len(pieces) * LQ, own.shape
    dtype = own.dtype
    far = far_sums is None
    vmem = pl.BlockSpec(memory_space=pltpu.VMEM)
    blocks = (2, rows, wide)
    scratch = [
        pltpu.VMEM((rows, depth), dtype),
        pltpu.VMEM((2, 2, depth, wide), dtype),
        pltpu.VMEM((2,) + blocks, dtype),
        pltpu.VMEM((2,) + blocks, dtype),
        pltpu.SemaphoreType.DMA((len(pieces),)),
        pltpu.SemaphoreType.DMA((2, 2)),
        pltpu.SemaphoreType.DMA((8,)),
        pltpu.SemaphoreType.DMA((8,)),
    ]
    if far:
        out_shape = [jax.ShapeDtypeStruct(blocks, dtype)] * 2
        out_specs = [vmem] * 2
    else:
        out_shape = jax.ShapeDtypeStruct((rows, 2 * wide), dtype)
        out_specs = vmem
        scratch += [pltpu.VMEM(blocks, dtype)] * 3
    return pl.pallas_call(
        functools.partial(project_kernel, len(pieces), far),
        out_shape=out_shape,
        in_specs=[pl.BlockSpec(memory_space=pl.ANY)] * (len(pieces) + len(weights))
        + [vmem] * (0 if far else 2),
        out_specs=out_specs,
        scratch_shapes=scratch,
        compiler_params=pltpu.CompilerParams(
            collective_id=int(far), has_side_effects=True, vmem_limit_bytes=VMEM_BYTES
        ),
        name="project_far" if far else "project_home",
        cost_estimate=pl.CostEstimate(
            flops=2 * 4 * rows * depth * wide,
            bytes_accessed=4 * depth * wide * 2,
            transcendentals=0,
        ),
    )(*pieces, *weights, *(far_sums or ()))


def suits_line(mesh, queries, lists):
    passes, heads = mesh.shape["pass"], mesh.shape["head"]
    entries = queries.shape[0] // LQ // passes * lists.shape[1]
    return passes == 2 * LINE and heads == LINE and entries % passes == 0


def solution(mesh):
    in_specs = (
        P("pass", "head"),
        P("pass", "head", None),
        P("pass", None, "head", None),
        P("head", "pass"),
        P(),
        P(),
        P(),
    )
    out_specs = P("pass", "head")

    def run(*args):
        if not suits_line(mesh, args[0], args[4]):
            return jax.shard_map(
                body, mesh=mesh, in_specs=in_specs, out_specs=out_specs, check_vma=False
            )(*args)
        step = jax.shard_map(
            line_steps, mesh=mesh, in_specs=in_specs, out_specs=out_specs, check_vma=False
        )
        return step(*args)

    return run
```

```python
import functools
import math

import jax
import jax.numpy as jnp
from jax import lax
from jax.experimental import pallas as pl
from jax.experimental.pallas import tpu as pltpu
from jax.sharding import PartitionSpec as P


H = 64
KVH = 8
HD = 128
LQ = 128
GROUP = H // KVH
COEF = HD ** (-0.5) * math.log2(math.e)
NEG = -1e30
ROWS = 256


def round_of(a, b, n):
    if n & (n - 1) == 0:
        return a ^ b
    return lax.rem(b - a + n, n)


def pairs_of(k, n):
    if n & (n - 1) == 0:
        return [(p, p ^ k) for p in range(n)]
    return [(p, (p + k) % n) for p in range(n)]


def order_of(n):
    rest = range(1, n)
    return sorted(rest, key=lambda k: (bin(k).count("1"), k))


def gather_kernel(n, most, per_device, order, lists_ref, pslot_ref, qslot_ref, cache_ref, *refs):
    recv_ref, own_row_ref = refs[0], refs[1]
    outs = refs[2 : 2 + len(order)]
    send_row, send_cnt, recv_cnt, buf, in_sem, out_sem = refs[2 + len(order) :]
    me = lax.axis_index("pass")
    pass_dev = cache_ref.shape[0]
    topp, nq = lists_ref.shape
    for k in range(n):
        send_cnt[k] = 0
        recv_cnt[k] = 0
    for i in range(n * most):
        recv_ref[i] = -1
        send_row[i] = 0

    def question(q, carry):
        slot = qslot_ref[q]
        dest = slot // per_device
        local = slot - dest * per_device
        k_send = round_of(me, dest, n)
        for t in range(topp):
            row = pslot_ref[lists_ref[t, q]]
            owner = row // pass_dev

            @pl.when(owner == me)
            def _():
                count = send_cnt[k_send]
                send_row[k_send * most + count] = row - owner * pass_dev
                send_cnt[k_send] = count + 1

            @pl.when(dest == me)
            def _():
                k = round_of(owner, me, n)
                count = recv_cnt[k]
                recv_ref[k * most + count] = local
                recv_cnt[k] = count + 1

        return carry

    lax.fori_loop(0, nq, question, 0)
    for r in range(most):
        own_row_ref[r] = send_row[r]
    copies = []
    for j, k in enumerate(order):
        for r in range(most):
            i = j * most + r
            get = pltpu.make_async_copy(
                cache_ref.at[send_row[k * most + r]], buf.at[i], in_sem.at[i]
            )
            get.start()
            copies.append((get, pltpu.make_async_copy(buf.at[i], outs[j].at[r], out_sem.at[i])))
    for get, put in copies:
        get.wait()
        put.start()
    for get, put in copies:
        put.wait()


def gather(lists, passage_slot, question_slot, cache, n, most, per_device, order):
    item = cache.shape[1:]
    slots = (n - 1) * most
    smem = pl.BlockSpec(memory_space=pltpu.SMEM)
    anyspace = pl.BlockSpec(memory_space=pl.ANY)
    return pl.pallas_call(
        functools.partial(gather_kernel, n, most, per_device, order),
        out_shape=[
            jax.ShapeDtypeStruct((n * most,), jnp.int32),
            jax.ShapeDtypeStruct((most,), jnp.int32),
        ]
        + [jax.ShapeDtypeStruct((most,) + item, cache.dtype)] * len(order),
        in_specs=[smem, smem, smem, anyspace],
        out_specs=[smem, smem] + [anyspace] * len(order),
        scratch_shapes=[
            pltpu.SMEM((n * most,), jnp.int32),
            pltpu.SMEM((n,), jnp.int32),
            pltpu.SMEM((n,), jnp.int32),
            pltpu.VMEM((slots,) + item, cache.dtype),
            pltpu.SemaphoreType.DMA((slots,)),
            pltpu.SemaphoreType.DMA((slots,)),
        ],
        name="gather_items",
        cost_estimate=pl.CostEstimate(
            flops=0, bytes_accessed=2 * slots * math.prod(item) * 2, transcendentals=0
        ),
    )(lists.T, passage_slot, question_slot, cache)


def block_step(q_ref, m_ref, l_ref, acc_ref, question, head, keys, values, causal):
    rows = q_ref.shape[2]
    step = min(ROWS, rows)
    width = keys.shape[0]
    ones = jnp.ones(values.shape, values.dtype)
    extended = jnp.concatenate([values, ones], axis=1)
    for start in range(0, rows, step):
        part = pl.ds(start, step)
        q = q_ref[question, head, part, :]
        scores = (
            lax.dot_general(q, keys, (((1,), (1,)), ((), ())), preferred_element_type=jnp.float32)
            * COEF
        )
        if causal:
            token = lax.broadcasted_iota(jnp.int32, scores.shape, 0) % LQ
            column = lax.broadcasted_iota(jnp.int32, scores.shape, 1)
            scores = jnp.where(column <= token, scores, NEG)
        old = m_ref[question, head, part, :]
        new = jnp.maximum(old, jnp.max(scores, axis=1, keepdims=True))
        weights = jnp.exp2(scores - jnp.concatenate([new] * (width // HD), axis=1))
        mixed = jnp.dot(
            weights.astype(jnp.bfloat16), extended, preferred_element_type=jnp.float32
        )
        alpha = jnp.exp2(old - new)
        m_ref[question, head, part, :] = new
        l_ref[question, head, part, :] = l_ref[question, head, part, :] * alpha + mixed[:, HD:]
        acc_ref[question, head, part, :] = (
            acc_ref[question, head, part, :] * alpha + mixed[:, :HD]
        )


def attend_kernel(first, last, rounds, most, *refs):
    refs = list(refs)
    recv_ref, q_ref = refs.pop(0), refs.pop(0)
    if first:
        row_ref, own_ref, cache_ref = refs.pop(0), refs.pop(0), refs.pop(0)
        sources = None
        entries = most
    else:
        state_in = [refs.pop(0) for _ in range(3)]
        sources = [refs.pop(0) for _ in rounds]
        entries = len(rounds) * most
    if last:
        out_ref = refs.pop(0)
        m_ref, l_ref, acc_ref = [refs.pop(0) for _ in range(3)]
    else:
        m_ref, l_ref, acc_ref = [refs.pop(0) for _ in range(3)]
    buf, sem = refs
    per_device, heads = q_ref.shape[0], q_ref.shape[1]

    def fetch(i, slot):
        if first:
            pltpu.make_async_copy(cache_ref.at[row_ref[i]], buf.at[slot], sem.at[slot]).start()
            return
        for j in range(len(rounds)):

            @pl.when(i // most == j)
            def _():
                pltpu.make_async_copy(
                    sources[j].at[i - j * most], buf.at[slot], sem.at[slot]
                ).start()

    def tag_of(i):
        if first:
            return recv_ref[i]
        k = jnp.int32(0)
        for j, value in enumerate(rounds):
            k = jnp.where(i // most == j, value, k)
        return recv_ref[k * most + lax.rem(i, most)]

    fetch(jnp.int32(0), 0)
    if first:
        m_ref[...] = jnp.full(m_ref.shape, NEG, jnp.float32)
        l_ref[...] = jnp.zeros(l_ref.shape, jnp.float32)
        acc_ref[...] = jnp.zeros(acc_ref.shape, jnp.float32)

        def own_block(question, carry):
            for head in range(heads):
                block = own_ref[question, head]
                block_step(
                    q_ref, m_ref, l_ref, acc_ref, question, head, block[:, :HD], block[:, HD:], True
                )
            return carry

        lax.fori_loop(0, per_device, own_block, 0)
    else:
        m_ref[...] = state_in[0][...]
        l_ref[...] = state_in[1][...]
        acc_ref[...] = state_in[2][...]

    def item(i, carry):
        slot = lax.rem(i, 2)
        pltpu.make_async_copy(buf.at[slot], buf.at[slot], sem.at[slot]).wait()

        @pl.when(i + 1 < entries)
        def _():
            fetch(i + 1, lax.rem(i + 1, 2))

        tag = tag_of(i)

        @pl.when(tag >= 0)
        def _():
            for head in range(heads):
                block_step(
                    q_ref,
                    m_ref,
                    l_ref,
                    acc_ref,
                    tag,
                    head,
                    buf[slot, head, :, :HD],
                    buf[slot, head, :, HD:],
                    False,
                )

        return carry

    lax.fori_loop(0, entries, item, 0)
    if last:
        for question in range(per_device):
            for head in range(heads):
                for g in range(GROUP):
                    part = pl.ds(g * LQ, LQ)
                    column = (head * GROUP + g) * HD
                    out_ref[pl.ds(question * LQ, LQ), pl.ds(column, HD)] = (
                        acc_ref[question, head, part, :] / l_ref[question, head, part, :]
                    ).astype(out_ref.dtype)


def attend_call(first, last, rounds, most, recv, q, rest, item):
    per_device, heads, rows, _ = q.shape
    state = jax.ShapeDtypeStruct(q.shape, jnp.float32)
    smem = pl.BlockSpec(memory_space=pltpu.SMEM)
    vmem = pl.BlockSpec(memory_space=pltpu.VMEM)
    anyspace = pl.BlockSpec(memory_space=pl.ANY)
    if first:
        in_specs = [smem, vmem, smem, vmem, anyspace]
        entries = most
    else:
        in_specs = [smem, vmem] + [vmem] * 3 + [anyspace] * len(rounds)
        entries = most * len(rounds)
    scratch = [pltpu.VMEM((2,) + item, q.dtype), pltpu.SemaphoreType.DMA((2,))]
    if last:
        out_shape = jax.ShapeDtypeStruct((per_device * LQ, heads * GROUP * HD), q.dtype)
        out_specs = vmem
        scratch = [pltpu.VMEM(q.shape, jnp.float32)] * 3 + scratch
    else:
        out_shape = [state] * 3
        out_specs = [vmem] * 3
    weights = entries * heads * rows * item[1]
    return pl.pallas_call(
        functools.partial(attend_kernel, first, last, rounds, most),
        out_shape=out_shape,
        in_specs=in_specs,
        out_specs=out_specs,
        scratch_shapes=scratch,
        name="attend_first" if first else ("attend_last" if last else "attend_more"),
        cost_estimate=pl.CostEstimate(
            flops=weights * HD * 4,
            bytes_accessed=entries * math.prod(item) * 2,
            transcendentals=weights,
        ),
    )(recv, q, *rest)


def weight_blocks(own, n):
    if n & (n - 1):
        return [lax.all_gather(own, "pass", axis=1, tiled=True)]
    have = {0: own}
    bit = n // 2
    while bit:
        for k in list(have):
            have[k ^ bit] = lax.ppermute(have[k], "pass", pairs_of(bit, n))
        bit //= 2
    return [have[k] for k in range(n)]


def project(context, weights):
    parts = [
        jnp.dot(context, weight, preferred_element_type=jnp.float32).astype(jnp.bfloat16)
        for weight in weights
    ]
    me = lax.axis_index("pass")
    bit = len(parts) // 2
    while bit:
        swap = (me & bit) != 0
        parts = [jnp.where(swap, parts[k ^ bit], parts[k]) for k in range(len(parts))]
        bit //= 2
    return jnp.concatenate(parts, axis=1)


def body(queries, own_kv, passage_cache, out_weight, lists, passage_slot, question_slot):
    n = lax.axis_size("pass")
    per_device = queries.shape[0] // LQ
    heads = own_kv.shape[1]
    entries = per_device * lists.shape[1]
    most = (entries + n - 1) // n
    order = order_of(n)
    cache = jnp.transpose(passage_cache, (0, 2, 1, 3))
    recv, own_row, *items = gather(
        lists, passage_slot, question_slot, cache, n, most, per_device, order
    )
    arrived = [
        lax.ppermute(item, "pass", pairs_of(k, n)) for k, item in zip(order, items)
    ]
    weights = weight_blocks(out_weight, n)
    q = (
        queries.reshape(per_device, LQ, heads, GROUP, HD)
        .transpose(0, 2, 3, 1, 4)
        .reshape(per_device, heads, GROUP * LQ, HD)
    )
    own = own_kv.reshape(per_device, LQ, heads, 2 * HD).transpose(0, 2, 1, 3)
    item = cache.shape[1:]
    state = attend_call(True, False, (0,), most, recv, q, (own_row, own, cache), item)
    calls = 3
    bounds = [len(order) * i // calls for i in range(calls + 1)]
    for i in range(calls):
        rounds = tuple(order[bounds[i] : bounds[i + 1]])
        rest = tuple(state) + tuple(arrived[bounds[i] : bounds[i + 1]])
        state = attend_call(False, i == calls - 1, rounds, most, recv, q, rest, item)
    context = state
    return lax.psum_scatter(project(context, weights), "head", scatter_dimension=1, tiled=True)


LINE = 4
EXTRA = 8
ITEM_ORDER = (2, 0, 3, 1)
VMEM_BYTES = 67043328
WIDE = 2


def mirror(k, ends=None):
    pairs = [(p, p ^ int(2 * k)) for p in range(2 * LINE)]
    if ends is None:
        return pairs
    return [(p, d) for p, d in pairs if (p // 2 in (0, LINE - 1)) == (ends == "outer")]


def is_inner():
    z = lax.axis_index("pass") // 2
    return jnp.logical_and(z > 0, z < LINE - 1)


def sort_kernel(most, per_device, lists_ref, pslot_ref, qslot_ref, cache_ref, *refs):
    row_ref, tag_ref, far_tag_ref = refs[:3]
    outs = refs[3 : 3 + LINE]
    send_row, near_cnt, send_cnt, far_cnt, buf, in_sem, out_sem = refs[3 + LINE :]
    me = lax.axis_index("pass")
    z, x = me // 2, me % 2
    pass_dev = cache_ref.shape[0]
    topp, nq = lists_ref.shape
    for k in range(LINE):
        near_cnt[k] = 0
        send_cnt[k] = 0
        far_cnt[k] = 0

    def take(i):
        return pltpu.make_async_copy(cache_ref.at[send_row[i]], buf.at[i], in_sem.at[i])

    def question(q, carry):
        slot = qslot_ref[q]
        dest = slot // per_device
        local = slot - dest * per_device
        k = (dest // 2) ^ z

        @pl.when(dest % 2 == x)
        def _():
            for t in range(topp):
                row = pslot_ref[lists_ref[t, q]]
                owner = row // pass_dev

                @pl.when(owner == me)
                def _():
                    at = k * most + near_cnt[k]
                    row_ref[at] = row - owner * pass_dev
                    tag_ref[at] = local
                    near_cnt[k] = near_cnt[k] + 1

                @pl.when(owner == (me ^ 1))
                def _():
                    far_tag_ref[k * most + far_cnt[k]] = local
                    far_cnt[k] = far_cnt[k] + 1

        @pl.when(dest % 2 != x)
        def _():
            for t in range(topp):
                row = pslot_ref[lists_ref[t, q]]
                owner = row // pass_dev

                @pl.when(owner == me)
                def _():
                    at = k * most + send_cnt[k]
                    send_row[at] = row - owner * pass_dev
                    send_cnt[k] = send_cnt[k] + 1
                    take(at).start()

        return carry

    lax.fori_loop(0, nq, question, 0)
    slots = [k * most + r for k in ITEM_ORDER for r in range(most)]
    puts = [pltpu.make_async_copy(buf.at[i], outs[i // most].at[i % most], out_sem.at[i]) for i in slots]
    for i, put in zip(slots, puts):
        take(i).wait()
        put.start()
    for put in puts:
        put.wait()


def sort_items(lists, passage_slot, question_slot, cache, most, per_device):
    item = cache.shape[1:]
    slots = LINE * most
    smem = pl.BlockSpec(memory_space=pltpu.SMEM)
    anyspace = pl.BlockSpec(memory_space=pl.ANY)
    return pl.pallas_call(
        functools.partial(sort_kernel, most, per_device),
        out_shape=[jax.ShapeDtypeStruct((slots,), jnp.int32)] * 3
        + [jax.ShapeDtypeStruct((most,) + item, cache.dtype)] * LINE,
        in_specs=[smem, smem, smem, anyspace],
        out_specs=[smem] * 3 + [anyspace] * LINE,
        scratch_shapes=[
            pltpu.SMEM((slots,), jnp.int32),
            pltpu.SMEM((LINE,), jnp.int32),
            pltpu.SMEM((LINE,), jnp.int32),
            pltpu.SMEM((LINE,), jnp.int32),
            pltpu.VMEM((slots,) + item, cache.dtype),
            pltpu.SemaphoreType.DMA((slots,)),
            pltpu.SemaphoreType.DMA((slots,)),
        ],
        compiler_params=pltpu.CompilerParams(vmem_limit_bytes=VMEM_BYTES),
        name="sort_items",
        cost_estimate=pl.CostEstimate(
            flops=0, bytes_accessed=2 * slots * math.prod(item) * 2, transcendentals=0
        ),
    )(lists.T, passage_slot, question_slot, cache)


def part_step(q_ref, m_ref, l_ref, acc_ref, question, head, keys, values, causal):
    turned = values.T
    tokens = pl.ds(pl.multiple_of(question * LQ, LQ), LQ)
    for start in range(0, GROUP, WIDE):
        q = jnp.concatenate(
            [
                q_ref[tokens, pl.ds(pl.multiple_of((head * GROUP + g) * HD, HD), HD)]
                for g in range(start, start + WIDE)
            ],
            axis=0,
        )
        columns = pl.ds(start * LQ, WIDE * LQ)
        scores = lax.dot_general(
            keys, q, (((1,), (1,)), ((), ())), preferred_element_type=jnp.float32
        )
        if causal:
            key = lax.broadcasted_iota(jnp.int32, scores.shape, 0)
            token = lax.broadcasted_iota(jnp.int32, scores.shape, 1) % LQ
            scores = jnp.where(key <= token, scores, NEG)
        old = m_ref[question, head, :, columns]
        new = jnp.maximum(old, jnp.max(scores, axis=0, keepdims=True))
        weights = jnp.exp2((scores - new) * COEF)
        alpha = jnp.exp2((old - new) * COEF)
        m_ref[question, head, :, columns] = new
        l_ref[question, head, :, columns] = l_ref[question, head, :, columns] * alpha + jnp.sum(
            weights, axis=0, keepdims=True
        )
        acc_ref[question, head, :, columns] = acc_ref[
            question, head, :, columns
        ] * alpha + jnp.dot(turned, weights.astype(turned.dtype), preferred_element_type=jnp.float32)


def part_kernel(k, most, heads, *refs):
    refs = list(refs)
    row_ref, tag_ref, far_tag_ref = refs.pop(0), refs.pop(0), refs.pop(0)
    own_ref = refs.pop(0) if k == 0 else None
    questions = [refs.pop(0) for _ in range(2 if k > 1 else 1)]
    cache_ref, items_ref, out_ref, q_ref, m_ref, l_ref, acc_ref, buf, sem, q_sem = refs
    per_device = q_ref.shape[0] // LQ
    entries = 2 * most

    def fetch(i, slot):
        @pl.when(i < most)
        def _():
            row = row_ref[k * most + jnp.minimum(i, most - 1)]
            pltpu.make_async_copy(cache_ref.at[row], buf.at[slot], sem.at[slot]).start()

        @pl.when(i >= most)
        def _():
            pltpu.make_async_copy(
                items_ref.at[jnp.maximum(i - most, 0)], buf.at[slot], sem.at[slot]
            ).start()

    if len(questions) == 1:
        pltpu.make_async_copy(questions[0], q_ref, q_sem).start()
    else:
        inner = is_inner()

        @pl.when(inner)
        def _():
            pltpu.make_async_copy(questions[0], q_ref, q_sem).start()

        @pl.when(jnp.logical_not(inner))
        def _():
            pltpu.make_async_copy(questions[1], q_ref, q_sem).start()

    fetch(jnp.int32(0), 0)
    m_ref[...] = jnp.full(m_ref.shape, NEG, jnp.float32)
    l_ref[...] = jnp.zeros(l_ref.shape, jnp.float32)
    acc_ref[...] = jnp.zeros(acc_ref.shape, jnp.float32)
    pltpu.make_async_copy(q_ref, q_ref, q_sem).wait()
    if k == 0:

        def own_block(i, carry):
            question, head = i // heads, lax.rem(i, heads)
            part_step(
                q_ref,
                m_ref,
                l_ref,
                acc_ref,
                question,
                head,
                own_ref[question, head, :, :HD],
                own_ref[question, head, :, HD:],
                True,
            )
            return carry

        lax.fori_loop(0, per_device * heads, own_block, 0)

    def item(i, carry):
        slot = lax.rem(i, 2)
        pltpu.make_async_copy(buf.at[slot], buf.at[slot], sem.at[slot]).wait()

        @pl.when(i + 1 < entries)
        def _():
            fetch(i + 1, lax.rem(i + 1, 2))

        at = k * most + lax.rem(i, most)
        tag = jnp.where(i < most, tag_ref[at], far_tag_ref[at])

        for head in range(heads):
            part_step(
                q_ref,
                m_ref,
                l_ref,
                acc_ref,
                tag,
                head,
                buf[slot, head, :, :HD],
                buf[slot, head, :, HD:],
                False,
            )
        return carry

    lax.fori_loop(0, entries, item, 0)

    def close(i, carry):
        question, head = i // heads, lax.rem(i, heads)
        columns = pl.ds(pl.multiple_of(head * GROUP * LQ, GROUP * LQ), GROUP * LQ)
        total = l_ref[question, head]
        some = total > 0.0
        safe = jnp.where(some, total, 1.0)
        out_ref[question, :HD, columns] = (acc_ref[question, head] / safe).astype(out_ref.dtype)
        level = jnp.where(some, m_ref[question, head] * COEF + jnp.log2(safe), NEG)
        store_level(out_ref, question, columns, level)
        return carry

    lax.fori_loop(0, per_device * heads, close, 0)


def store_level(out_ref, question, columns, line):
    row_of = lax.broadcasted_iota(jnp.int32, (EXTRA, line.shape[1]), 0)
    high = line.astype(jnp.bfloat16).astype(jnp.float32)
    both = jnp.where(row_of == 0, high, jnp.where(row_of == 1, line - high, 0.0))
    out_ref[question, HD:, columns] = both.astype(out_ref.dtype)


def part_call(k, most, tables, own, questions, cache, items):
    tokens, columns = questions[0].shape
    heads, item = cache.shape[1], cache.shape[1:]
    state = (tokens // LQ, heads, HD, GROUP * LQ)
    row_state = (tokens // LQ, heads, 1, GROUP * LQ)
    smem = pl.BlockSpec(memory_space=pltpu.SMEM)
    vmem = pl.BlockSpec(memory_space=pltpu.VMEM)
    anyspace = pl.BlockSpec(memory_space=pl.ANY)
    owned = [own] if k == 0 else []
    weights = 2 * most * heads * GROUP * LQ * item[1]
    return pl.pallas_call(
        functools.partial(part_kernel, k, most, heads),
        out_shape=jax.ShapeDtypeStruct((tokens // LQ, HD + EXTRA, columns), cache.dtype),
        in_specs=[smem] * 3 + [vmem] * len(owned) + [anyspace] * (len(questions) + 2),
        out_specs=vmem,
        scratch_shapes=[
            pltpu.VMEM((tokens, columns), cache.dtype),
            pltpu.VMEM(row_state, jnp.float32),
            pltpu.VMEM(row_state, jnp.float32),
            pltpu.VMEM(state, jnp.float32),
            pltpu.VMEM((2,) + item, cache.dtype),
            pltpu.SemaphoreType.DMA((2,)),
            pltpu.SemaphoreType.DMA,
        ],
        compiler_params=pltpu.CompilerParams(vmem_limit_bytes=VMEM_BYTES),
        cost_estimate=pl.CostEstimate(
            flops=weights * HD * 4,
            bytes_accessed=2 * most * math.prod(item) * 2,
            transcendentals=weights,
        ),
    )(*tables, *owned, *questions, cache, items)


def blend(a_ref, b_ref, out_ref, leveled):
    def level_of(ref):
        both = ref[0, HD:, :].astype(jnp.float32)
        return both[:1] + both[1:2]

    one, two = level_of(a_ref), level_of(b_ref)
    top = jnp.maximum(one, two)
    first, second = jnp.exp2(one - top), jnp.exp2(two - top)
    total = first + second
    share = first / total
    for c in range(share.shape[1] // LQ):
        columns = slice(c * LQ, (c + 1) * LQ)
        a = a_ref[0, :HD, columns].astype(jnp.float32)
        b = b_ref[0, :HD, columns].astype(jnp.float32)
        value = b + (a - b) * share[:, columns]
        if leveled:
            out_ref[0, :HD, columns] = value.astype(out_ref.dtype)
        else:
            out_ref[:, columns] = value.T.astype(out_ref.dtype)
    if leveled:
        store_level(out_ref, 0, slice(None), top + jnp.log2(total))


def merge_kernel(a_ref, b_ref, out_ref):
    inner = is_inner()

    @pl.when(inner)
    def _():
        blend(a_ref, b_ref, out_ref, True)

    @pl.when(jnp.logical_not(inner))
    def _():
        out_ref[...] = a_ref[...]


def finish_kernel(a_ref, b_ref, out_ref):
    blend(a_ref, b_ref, out_ref, False)


def question_spec(value, at):
    shape = (1,) + value.shape[1:]
    if value.shape[0] == 1:
        return pl.BlockSpec(shape, lambda q: (0, 0, 0))
    if at is None:
        return pl.BlockSpec(shape, lambda q: (q, 0, 0))
    return pl.BlockSpec(shape, lambda q: (at, 0, 0))


def join_call(a, b, at, leveled):
    questions = a.shape[0] if at is None else 1
    columns = a.shape[2]
    if leveled:
        shape, block = (questions,) + a.shape[1:], (1,) + a.shape[1:]
        out_spec = pl.BlockSpec(block, lambda q: (q, 0, 0))
    else:
        shape = (questions * LQ, columns)
        out_spec = pl.BlockSpec((LQ, columns), lambda q: (q, 0))
    size = questions * LQ * columns
    return pl.pallas_call(
        merge_kernel if leveled else finish_kernel,
        out_shape=jax.ShapeDtypeStruct(shape, a.dtype),
        grid=(questions,),
        in_specs=[question_spec(a, at), question_spec(b, at)],
        out_specs=out_spec,
        compiler_params=pltpu.CompilerParams(vmem_limit_bytes=VMEM_BYTES),
        cost_estimate=pl.CostEstimate(flops=size * 8, bytes_accessed=size * 6, transcendentals=0),
    )(a, b)


def line_steps(queries, own_kv, passage_cache, out_weight, lists, passage_slot, question_slot):
    per_device = queries.shape[0] // LQ
    heads = own_kv.shape[1]
    most = per_device * lists.shape[1] // (2 * LINE)

    def send(value, pairs):
        return lax.ppermute(value, "pass", pairs)

    def part(k, *args):
        return part_call(k, most, tables, own if k == 0 else None, *args)

    def join(a, b, at=None, leveled=True):
        return join_call(a, b, at, leveled)

    across = [(p, p ^ 1) for p in range(2 * LINE)]
    inner_across = [(p, d) for p, d in across if p // 2 in (1, 2)]
    outer_across = [(p, d) for p, d in across if p // 2 not in (1, 2)]
    near, middle = mirror(1), mirror(3, "inner")
    inward, outward = mirror(1, "outer"), mirror(1, "inner")
    q_near = send(queries, near)
    q_mid = send(queries, middle)
    w_across = send(out_weight, across)
    cache = jnp.transpose(passage_cache, (0, 2, 1, 3))
    row, tag, far_tag, *items = sort_items(
        lists, passage_slot, question_slot, cache, most, per_device
    )
    tables = (row, tag, far_tag)
    q_out = send(q_mid, outward)
    q_cross = send(q_near, middle)
    q_end = send(q_cross, outward)
    far = [send(items[k], across) for k in range(LINE)]
    own = own_kv.reshape(per_device, LQ, heads, 2 * HD).transpose(0, 2, 1, 3)
    part2 = part(2, [q_cross, q_out], cache, far[2])
    part3 = part(3, [q_mid, q_end], cache, far[3])
    part0 = part(0, [queries], cache, far[0])
    part1 = part(1, [q_near], cache, far[1])
    back2 = send(part2, inward)
    w_in = send(out_weight, mirror(2, "outer"))
    w_out = send(out_weight, mirror(2, "inner"))
    back3 = send(part3, inward)
    w_in_both = send(w_in, inner_across)
    w_out_both = send(w_out, outer_across)
    own_rows, near_rows = [], []
    for q in range(per_device):
        cross3 = send(join(part3, back2, q), middle)
        near0 = join(part0, cross3, q)
        beside = send(near0, near)
        cross2 = send(join(part2, back3, q), middle)
        near1 = join(part1, cross2, q)
        back1 = send(near1, near)
        near_rows.append(join(near1, beside, q, False))
        own_rows.append(join(near0, back1, q, False))
    weights = (out_weight, w_across, w_in, w_in_both, w_out, w_out_both)
    far_send, far_keep = project_call(near_rows, weights, None)
    far_sent = send_far(far_send)
    return project_call(own_rows, weights, (far_keep, far_sent))


def send_far(sums):
    pairs = []
    for p in range(2 * LINE):
        for h in range(LINE):
            if h % 2 != (p // 2) % 2:
                pairs.append((p * LINE + h, p * LINE + (h ^ 2)))
    return lax.ppermute(sums, ("pass", "head"), pairs)


MESH = pl.DeviceIdType.MESH


def at_home():
    return lax.axis_index("head") % 2 == lax.axis_index("pass") // 2 % 2


def project_kernel(pieces, far, *refs):
    rows_refs = refs[:pieces]
    own_ref, across_ref, in_ref, in2_ref, out1_ref, out2_ref = refs[pieces : pieces + 6]
    refs = refs[pieces + 6 :]
    if far:
        send_ref, keep_ref = refs[:2]
    else:
        far_keep_ref, far_sent_ref, out_ref = refs[:3]
        refs = refs[1:]
    context_ref, w_ref, part_ref, core_ref, row_sem, w_sem, send_sem, recv_sem = refs[2:10]
    me, head = lax.axis_index("pass"), lax.axis_index("head")
    z, x, y = me // 2, me % 2, head // 2
    wide = w_ref.shape[3]
    inner = is_inner()
    core_peer, y_peer, z_peer = (me, head ^ 1), (me, head ^ 2), (me ^ 2, head ^ 1)
    home = at_home()
    sums = jnp.logical_not(home) if far else home

    row_loads = [
        pltpu.make_async_copy(ref, context_ref.at[pl.ds(i * LQ, LQ)], row_sem.at[i])
        for i, ref in enumerate(rows_refs)
    ]
    for load in row_loads:
        load.start()

    def load_here():
        pltpu.make_async_copy(own_ref, w_ref.at[0, x], w_sem.at[0, x]).start()
        pltpu.make_async_copy(across_ref, w_ref.at[0, 1 - x], w_sem.at[0, 1 - x]).start()

    def load_there():
        for which, (one, two) in (
            (inner, (in_ref, in2_ref)),
            (jnp.logical_not(inner), (out1_ref, out2_ref)),
        ):

            @pl.when(which)
            def _():
                pltpu.make_async_copy(one, w_ref.at[1, x], w_sem.at[1, x]).start()
                pltpu.make_async_copy(two, w_ref.at[1, 1 - x], w_sem.at[1, 1 - x]).start()

    here_first = y != z // 2

    @pl.when(here_first)
    def _():
        load_here()
        load_there()

    @pl.when(jnp.logical_not(here_first))
    def _():
        load_there()
        load_here()

    barrier = pltpu.get_barrier_semaphore()
    peers = (core_peer,) if far else (core_peer, y_peer, z_peer)
    for peer in peers:
        pl.semaphore_signal(barrier, inc=1, device_id=peer, device_id_type=MESH)
    pl.semaphore_wait(barrier, len(peers))

    def remote(src, dst, i, peer):
        return pltpu.make_async_remote_copy(
            src_ref=src,
            dst_ref=dst,
            send_sem=send_sem.at[i],
            recv_sem=recv_sem.at[i],
            device_id=peer,
            device_id_type=MESH,
        )

    def columns(j):
        return pl.ds(j * wide, wide)

    core_copies = [
        [remote(part_ref.at[s, j], core_ref.at[s, j], s * 2 + j, core_peer) for j in range(2)]
        for s in range(2)
    ]
    if not far:
        y_ref, ysend_ref, zsend_ref = refs[10:]
        y_copies = [remote(ysend_ref.at[j], y_ref.at[j], 4 + j, y_peer) for j in range(2)]
        z_copies = [
            remote(zsend_ref.at[j], out_ref.at[:, columns(j)], 6 + j, z_peer) for j in range(2)
        ]

        @pl.when(jnp.logical_not(home))
        def _():
            for j in range(2):
                zsend_ref[j] = (
                    far_keep_ref[j].astype(jnp.float32) + far_sent_ref[j].astype(jnp.float32)
                ).astype(zsend_ref.dtype)
                z_copies[j].start()

    for load in row_loads:
        load.wait()

    def multiply(s, to_y, j):
        here = jnp.where(to_y == z // 2, 0, 1)
        block = w_ref.at[here, j]
        pltpu.make_async_copy(block, block, w_sem.at[here, j]).wait()
        part_ref[s, j] = jnp.dot(
            context_ref[...], w_ref[here, j], preferred_element_type=jnp.float32
        ).astype(part_ref.dtype)

        @pl.when(jnp.logical_not(sums))
        def _():
            core_copies[s][j].start()

    def add_up(s, j):
        @pl.when(sums)
        def _():
            core_copies[s][j].wait_recv()
            value = part_ref[s, j].astype(jnp.float32) + core_ref[s, j].astype(jnp.float32)
            if far:
                target = keep_ref if s else send_ref
                target[j] = value.astype(target.dtype)
            elif s == 0:
                ysend_ref[j] = value.astype(ysend_ref.dtype)
                y_copies[j].start()
            else:
                y_copies[j].wait_recv()
                out_ref[:, columns(j)] = (value + y_ref[j].astype(jnp.float32)).astype(
                    out_ref.dtype
                )

    late = None
    for s, to_y in enumerate((1 - y, y)):
        for j in range(2):
            multiply(s, to_y, j)
            if late is not None:
                add_up(*late)
            late = (s, j)
    add_up(*late)

    @pl.when(jnp.logical_not(sums))
    def _():
        for copies in core_copies:
            for copy in copies:
                copy.wait_send()

    if not far:

        @pl.when(home)
        def _():
            for copy in y_copies:
                copy.wait_send()

        @pl.when(jnp.logical_not(home))
        def _():
            for copy in z_copies:
                copy.wait()


def project_call(pieces, weights, far_sums):
    own = weights[0]
    rows, (depth, wide) = len(pieces) * LQ, own.shape
    dtype = own.dtype
    far = far_sums is None
    vmem = pl.BlockSpec(memory_space=pltpu.VMEM)
    blocks = (2, rows, wide)
    scratch = [
        pltpu.VMEM((rows, depth), dtype),
        pltpu.VMEM((2, 2, depth, wide), dtype),
        pltpu.VMEM((2,) + blocks, dtype),
        pltpu.VMEM((2,) + blocks, dtype),
        pltpu.SemaphoreType.DMA((len(pieces),)),
        pltpu.SemaphoreType.DMA((2, 2)),
        pltpu.SemaphoreType.DMA((8,)),
        pltpu.SemaphoreType.DMA((8,)),
    ]
    if far:
        out_shape = [jax.ShapeDtypeStruct(blocks, dtype)] * 2
        out_specs = [vmem] * 2
    else:
        out_shape = jax.ShapeDtypeStruct((rows, 2 * wide), dtype)
        out_specs = vmem
        scratch += [pltpu.VMEM(blocks, dtype)] * 3
    return pl.pallas_call(
        functools.partial(project_kernel, len(pieces), far),
        out_shape=out_shape,
        in_specs=[pl.BlockSpec(memory_space=pl.ANY)] * (len(pieces) + len(weights))
        + [vmem] * (0 if far else 2),
        out_specs=out_specs,
        scratch_shapes=scratch,
        compiler_params=pltpu.CompilerParams(
            collective_id=int(far), has_side_effects=True, vmem_limit_bytes=VMEM_BYTES
        ),
        name="project_far" if far else "project_home",
        cost_estimate=pl.CostEstimate(
            flops=2 * 4 * rows * depth * wide,
            bytes_accessed=4 * depth * wide * 2,
            transcendentals=0,
        ),
    )(*pieces, *weights, *(far_sums or ()))


def suits_line(mesh, queries, lists):
    passes, heads = mesh.shape["pass"], mesh.shape["head"]
    entries = queries.shape[0] // LQ // passes * lists.shape[1]
    return passes == 2 * LINE and heads == LINE and entries % passes == 0


def solution(mesh):
    in_specs = (
        P("pass", "head"),
        P("pass", "head", None),
        P("pass", None, "head", None),
        P("head", "pass"),
        P(),
        P(),
        P(),
    )
    out_specs = P("pass", "head")

    def run(*args):
        if not suits_line(mesh, args[0], args[4]):
            return jax.shard_map(
                body, mesh=mesh, in_specs=in_specs, out_specs=out_specs, check_vma=False
            )(*args)
        step = jax.shard_map(
            line_steps, mesh=mesh, in_specs=in_specs, out_specs=out_specs, check_vma=False
        )
        return step(*args)

    return run
```

```python
import functools
import math

import jax
import jax.numpy as jnp
from jax import lax
from jax.experimental import pallas as pl
from jax.experimental.pallas import tpu as pltpu
from jax.sharding import PartitionSpec as P


H = 64
KVH = 8
HD = 128
LQ = 128
GROUP = H // KVH
COEF = HD ** (-0.5) * math.log2(math.e)
NEG = -1e30
ROWS = 256


def round_of(a, b, n):
    if n & (n - 1) == 0:
        return a ^ b
    return lax.rem(b - a + n, n)


def pairs_of(k, n):
    if n & (n - 1) == 0:
        return [(p, p ^ k) for p in range(n)]
    return [(p, (p + k) % n) for p in range(n)]


def order_of(n):
    rest = range(1, n)
    return sorted(rest, key=lambda k: (bin(k).count("1"), k))


def gather_kernel(n, most, per_device, order, lists_ref, pslot_ref, qslot_ref, cache_ref, *refs):
    recv_ref, own_row_ref = refs[0], refs[1]
    outs = refs[2 : 2 + len(order)]
    send_row, send_cnt, recv_cnt, buf, in_sem, out_sem = refs[2 + len(order) :]
    me = lax.axis_index("pass")
    pass_dev = cache_ref.shape[0]
    topp, nq = lists_ref.shape
    for k in range(n):
        send_cnt[k] = 0
        recv_cnt[k] = 0
    for i in range(n * most):
        recv_ref[i] = -1
        send_row[i] = 0

    def question(q, carry):
        slot = qslot_ref[q]
        dest = slot // per_device
        local = slot - dest * per_device
        k_send = round_of(me, dest, n)
        for t in range(topp):
            row = pslot_ref[lists_ref[t, q]]
            owner = row // pass_dev

            @pl.when(owner == me)
            def _():
                count = send_cnt[k_send]
                send_row[k_send * most + count] = row - owner * pass_dev
                send_cnt[k_send] = count + 1

            @pl.when(dest == me)
            def _():
                k = round_of(owner, me, n)
                count = recv_cnt[k]
                recv_ref[k * most + count] = local
                recv_cnt[k] = count + 1

        return carry

    lax.fori_loop(0, nq, question, 0)
    for r in range(most):
        own_row_ref[r] = send_row[r]
    copies = []
    for j, k in enumerate(order):
        for r in range(most):
            i = j * most + r
            get = pltpu.make_async_copy(
                cache_ref.at[send_row[k * most + r]], buf.at[i], in_sem.at[i]
            )
            get.start()
            copies.append((get, pltpu.make_async_copy(buf.at[i], outs[j].at[r], out_sem.at[i])))
    for get, put in copies:
        get.wait()
        put.start()
    for get, put in copies:
        put.wait()


def gather(lists, passage_slot, question_slot, cache, n, most, per_device, order):
    item = cache.shape[1:]
    slots = (n - 1) * most
    smem = pl.BlockSpec(memory_space=pltpu.SMEM)
    anyspace = pl.BlockSpec(memory_space=pl.ANY)
    return pl.pallas_call(
        functools.partial(gather_kernel, n, most, per_device, order),
        out_shape=[
            jax.ShapeDtypeStruct((n * most,), jnp.int32),
            jax.ShapeDtypeStruct((most,), jnp.int32),
        ]
        + [jax.ShapeDtypeStruct((most,) + item, cache.dtype)] * len(order),
        in_specs=[smem, smem, smem, anyspace],
        out_specs=[smem, smem] + [anyspace] * len(order),
        scratch_shapes=[
            pltpu.SMEM((n * most,), jnp.int32),
            pltpu.SMEM((n,), jnp.int32),
            pltpu.SMEM((n,), jnp.int32),
            pltpu.VMEM((slots,) + item, cache.dtype),
            pltpu.SemaphoreType.DMA((slots,)),
            pltpu.SemaphoreType.DMA((slots,)),
        ],
        name="gather_items",
        cost_estimate=pl.CostEstimate(
            flops=0, bytes_accessed=2 * slots * math.prod(item) * 2, transcendentals=0
        ),
    )(lists.T, passage_slot, question_slot, cache)


def block_step(q_ref, m_ref, l_ref, acc_ref, question, head, keys, values, causal):
    rows = q_ref.shape[2]
    step = min(ROWS, rows)
    width = keys.shape[0]
    ones = jnp.ones(values.shape, values.dtype)
    extended = jnp.concatenate([values, ones], axis=1)
    for start in range(0, rows, step):
        part = pl.ds(start, step)
        q = q_ref[question, head, part, :]
        scores = (
            lax.dot_general(q, keys, (((1,), (1,)), ((), ())), preferred_element_type=jnp.float32)
            * COEF
        )
        if causal:
            token = lax.broadcasted_iota(jnp.int32, scores.shape, 0) % LQ
            column = lax.broadcasted_iota(jnp.int32, scores.shape, 1)
            scores = jnp.where(column <= token, scores, NEG)
        old = m_ref[question, head, part, :]
        new = jnp.maximum(old, jnp.max(scores, axis=1, keepdims=True))
        weights = jnp.exp2(scores - jnp.concatenate([new] * (width // HD), axis=1))
        mixed = jnp.dot(
            weights.astype(jnp.bfloat16), extended, preferred_element_type=jnp.float32
        )
        alpha = jnp.exp2(old - new)
        m_ref[question, head, part, :] = new
        l_ref[question, head, part, :] = l_ref[question, head, part, :] * alpha + mixed[:, HD:]
        acc_ref[question, head, part, :] = (
            acc_ref[question, head, part, :] * alpha + mixed[:, :HD]
        )


def attend_kernel(first, last, rounds, most, *refs):
    refs = list(refs)
    recv_ref, q_ref = refs.pop(0), refs.pop(0)
    if first:
        row_ref, own_ref, cache_ref = refs.pop(0), refs.pop(0), refs.pop(0)
        sources = None
        entries = most
    else:
        state_in = [refs.pop(0) for _ in range(3)]
        sources = [refs.pop(0) for _ in rounds]
        entries = len(rounds) * most
    if last:
        out_ref = refs.pop(0)
        m_ref, l_ref, acc_ref = [refs.pop(0) for _ in range(3)]
    else:
        m_ref, l_ref, acc_ref = [refs.pop(0) for _ in range(3)]
    buf, sem = refs
    per_device, heads = q_ref.shape[0], q_ref.shape[1]

    def fetch(i, slot):
        if first:
            pltpu.make_async_copy(cache_ref.at[row_ref[i]], buf.at[slot], sem.at[slot]).start()
            return
        for j in range(len(rounds)):

            @pl.when(i // most == j)
            def _():
                pltpu.make_async_copy(
                    sources[j].at[i - j * most], buf.at[slot], sem.at[slot]
                ).start()

    def tag_of(i):
        if first:
            return recv_ref[i]
        k = jnp.int32(0)
        for j, value in enumerate(rounds):
            k = jnp.where(i // most == j, value, k)
        return recv_ref[k * most + lax.rem(i, most)]

    fetch(jnp.int32(0), 0)
    if first:
        m_ref[...] = jnp.full(m_ref.shape, NEG, jnp.float32)
        l_ref[...] = jnp.zeros(l_ref.shape, jnp.float32)
        acc_ref[...] = jnp.zeros(acc_ref.shape, jnp.float32)

        def own_block(question, carry):
            for head in range(heads):
                block = own_ref[question, head]
                block_step(
                    q_ref, m_ref, l_ref, acc_ref, question, head, block[:, :HD], block[:, HD:], True
                )
            return carry

        lax.fori_loop(0, per_device, own_block, 0)
    else:
        m_ref[...] = state_in[0][...]
        l_ref[...] = state_in[1][...]
        acc_ref[...] = state_in[2][...]

    def item(i, carry):
        slot = lax.rem(i, 2)
        pltpu.make_async_copy(buf.at[slot], buf.at[slot], sem.at[slot]).wait()

        @pl.when(i + 1 < entries)
        def _():
            fetch(i + 1, lax.rem(i + 1, 2))

        tag = tag_of(i)

        @pl.when(tag >= 0)
        def _():
            for head in range(heads):
                block_step(
                    q_ref,
                    m_ref,
                    l_ref,
                    acc_ref,
                    tag,
                    head,
                    buf[slot, head, :, :HD],
                    buf[slot, head, :, HD:],
                    False,
                )

        return carry

    lax.fori_loop(0, entries, item, 0)
    if last:
        for question in range(per_device):
            for head in range(heads):
                for g in range(GROUP):
                    part = pl.ds(g * LQ, LQ)
                    column = (head * GROUP + g) * HD
                    out_ref[pl.ds(question * LQ, LQ), pl.ds(column, HD)] = (
                        acc_ref[question, head, part, :] / l_ref[question, head, part, :]
                    ).astype(out_ref.dtype)


def attend_call(first, last, rounds, most, recv, q, rest, item):
    per_device, heads, rows, _ = q.shape
    state = jax.ShapeDtypeStruct(q.shape, jnp.float32)
    smem = pl.BlockSpec(memory_space=pltpu.SMEM)
    vmem = pl.BlockSpec(memory_space=pltpu.VMEM)
    anyspace = pl.BlockSpec(memory_space=pl.ANY)
    if first:
        in_specs = [smem, vmem, smem, vmem, anyspace]
        entries = most
    else:
        in_specs = [smem, vmem] + [vmem] * 3 + [anyspace] * len(rounds)
        entries = most * len(rounds)
    scratch = [pltpu.VMEM((2,) + item, q.dtype), pltpu.SemaphoreType.DMA((2,))]
    if last:
        out_shape = jax.ShapeDtypeStruct((per_device * LQ, heads * GROUP * HD), q.dtype)
        out_specs = vmem
        scratch = [pltpu.VMEM(q.shape, jnp.float32)] * 3 + scratch
    else:
        out_shape = [state] * 3
        out_specs = [vmem] * 3
    weights = entries * heads * rows * item[1]
    return pl.pallas_call(
        functools.partial(attend_kernel, first, last, rounds, most),
        out_shape=out_shape,
        in_specs=in_specs,
        out_specs=out_specs,
        scratch_shapes=scratch,
        name="attend_first" if first else ("attend_last" if last else "attend_more"),
        cost_estimate=pl.CostEstimate(
            flops=weights * HD * 4,
            bytes_accessed=entries * math.prod(item) * 2,
            transcendentals=weights,
        ),
    )(recv, q, *rest)


def weight_blocks(own, n):
    if n & (n - 1):
        return [lax.all_gather(own, "pass", axis=1, tiled=True)]
    have = {0: own}
    bit = n // 2
    while bit:
        for k in list(have):
            have[k ^ bit] = lax.ppermute(have[k], "pass", pairs_of(bit, n))
        bit //= 2
    return [have[k] for k in range(n)]


def project(context, weights):
    parts = [
        jnp.dot(context, weight, preferred_element_type=jnp.float32).astype(jnp.bfloat16)
        for weight in weights
    ]
    me = lax.axis_index("pass")
    bit = len(parts) // 2
    while bit:
        swap = (me & bit) != 0
        parts = [jnp.where(swap, parts[k ^ bit], parts[k]) for k in range(len(parts))]
        bit //= 2
    return jnp.concatenate(parts, axis=1)


def body(queries, own_kv, passage_cache, out_weight, lists, passage_slot, question_slot):
    n = lax.axis_size("pass")
    per_device = queries.shape[0] // LQ
    heads = own_kv.shape[1]
    entries = per_device * lists.shape[1]
    most = (entries + n - 1) // n
    order = order_of(n)
    cache = jnp.transpose(passage_cache, (0, 2, 1, 3))
    recv, own_row, *items = gather(
        lists, passage_slot, question_slot, cache, n, most, per_device, order
    )
    arrived = [
        lax.ppermute(item, "pass", pairs_of(k, n)) for k, item in zip(order, items)
    ]
    weights = weight_blocks(out_weight, n)
    q = (
        queries.reshape(per_device, LQ, heads, GROUP, HD)
        .transpose(0, 2, 3, 1, 4)
        .reshape(per_device, heads, GROUP * LQ, HD)
    )
    own = own_kv.reshape(per_device, LQ, heads, 2 * HD).transpose(0, 2, 1, 3)
    item = cache.shape[1:]
    state = attend_call(True, False, (0,), most, recv, q, (own_row, own, cache), item)
    calls = 3
    bounds = [len(order) * i // calls for i in range(calls + 1)]
    for i in range(calls):
        rounds = tuple(order[bounds[i] : bounds[i + 1]])
        rest = tuple(state) + tuple(arrived[bounds[i] : bounds[i + 1]])
        state = attend_call(False, i == calls - 1, rounds, most, recv, q, rest, item)
    context = state
    return lax.psum_scatter(project(context, weights), "head", scatter_dimension=1, tiled=True)


LINE = 4
EXTRA = 8
ITEM_ORDER = (2, 0, 3, 1)
VMEM_BYTES = 67043328


def mirror(k, ends=None):
    pairs = [(p, p ^ int(2 * k)) for p in range(2 * LINE)]
    if ends is None:
        return pairs
    return [(p, d) for p, d in pairs if (p // 2 in (0, LINE - 1)) == (ends == "outer")]


def is_inner():
    z = lax.axis_index("pass") // 2
    return jnp.logical_and(z > 0, z < LINE - 1)


def sort_kernel(most, per_device, lists_ref, pslot_ref, qslot_ref, cache_ref, *refs):
    row_ref, tag_ref, far_tag_ref = refs[:3]
    outs = refs[3 : 3 + LINE]
    send_row, near_cnt, send_cnt, far_cnt, buf, in_sem, out_sem = refs[3 + LINE :]
    me = lax.axis_index("pass")
    z, x = me // 2, me % 2
    pass_dev = cache_ref.shape[0]
    topp, nq = lists_ref.shape
    for k in range(LINE):
        near_cnt[k] = 0
        send_cnt[k] = 0
        far_cnt[k] = 0

    def take(i):
        return pltpu.make_async_copy(cache_ref.at[send_row[i]], buf.at[i], in_sem.at[i])

    def question(q, carry):
        slot = qslot_ref[q]
        dest = slot // per_device
        local = slot - dest * per_device
        k = (dest // 2) ^ z

        @pl.when(dest % 2 == x)
        def _():
            for t in range(topp):
                row = pslot_ref[lists_ref[t, q]]
                owner = row // pass_dev

                @pl.when(owner == me)
                def _():
                    at = k * most + near_cnt[k]
                    row_ref[at] = row - owner * pass_dev
                    tag_ref[at] = local
                    near_cnt[k] = near_cnt[k] + 1

                @pl.when(owner == (me ^ 1))
                def _():
                    far_tag_ref[k * most + far_cnt[k]] = local
                    far_cnt[k] = far_cnt[k] + 1

        @pl.when(dest % 2 != x)
        def _():
            for t in range(topp):
                row = pslot_ref[lists_ref[t, q]]
                owner = row // pass_dev

                @pl.when(owner == me)
                def _():
                    at = k * most + send_cnt[k]
                    send_row[at] = row - owner * pass_dev
                    send_cnt[k] = send_cnt[k] + 1
                    take(at).start()

        return carry

    lax.fori_loop(0, nq, question, 0)
    slots = [k * most + r for k in ITEM_ORDER for r in range(most)]
    puts = [pltpu.make_async_copy(buf.at[i], outs[i // most].at[i % most], out_sem.at[i]) for i in slots]
    for i, put in zip(slots, puts):
        take(i).wait()
        put.start()
    for put in puts:
        put.wait()


def sort_items(lists, passage_slot, question_slot, cache, most, per_device):
    item = cache.shape[1:]
    slots = LINE * most
    smem = pl.BlockSpec(memory_space=pltpu.SMEM)
    anyspace = pl.BlockSpec(memory_space=pl.ANY)
    return pl.pallas_call(
        functools.partial(sort_kernel, most, per_device),
        out_shape=[jax.ShapeDtypeStruct((slots,), jnp.int32)] * 3
        + [jax.ShapeDtypeStruct((most,) + item, cache.dtype)] * LINE,
        in_specs=[smem, smem, smem, anyspace],
        out_specs=[smem] * 3 + [anyspace] * LINE,
        scratch_shapes=[
            pltpu.SMEM((slots,), jnp.int32),
            pltpu.SMEM((LINE,), jnp.int32),
            pltpu.SMEM((LINE,), jnp.int32),
            pltpu.SMEM((LINE,), jnp.int32),
            pltpu.VMEM((slots,) + item, cache.dtype),
            pltpu.SemaphoreType.DMA((slots,)),
            pltpu.SemaphoreType.DMA((slots,)),
        ],
        compiler_params=pltpu.CompilerParams(vmem_limit_bytes=VMEM_BYTES),
        name="sort_items",
        cost_estimate=pl.CostEstimate(
            flops=0, bytes_accessed=2 * slots * math.prod(item) * 2, transcendentals=0
        ),
    )(lists.T, passage_slot, question_slot, cache)


def unit():
    r = lax.broadcasted_iota(jnp.int32, (LQ, LQ), 0)
    c = lax.broadcasted_iota(jnp.int32, (LQ, LQ), 1)
    return r == c


def part_step(q_ref, m_ref, l_ref, acc_ref, question, head, keys, values, causal):
    rows = GROUP * LQ
    width = keys.shape[0]
    ones = jnp.ones(values.shape, values.dtype)
    extended = jnp.concatenate([values, ones], axis=1)
    tokens = pl.ds(pl.multiple_of(question * LQ, LQ), LQ)
    for start in range(0, rows, ROWS):
        part = pl.ds(start, ROWS)
        q = jnp.concatenate(
            [
                q_ref[tokens, pl.ds(pl.multiple_of((head * GROUP + g) * HD, HD), HD)]
                for g in range(start // LQ, (start + ROWS) // LQ)
            ],
            axis=0,
        )
        scores = (
            lax.dot_general(q, keys, (((1,), (1,)), ((), ())), preferred_element_type=jnp.float32)
            * COEF
        )
        if causal:
            token = lax.broadcasted_iota(jnp.int32, scores.shape, 0) % LQ
            column = lax.broadcasted_iota(jnp.int32, scores.shape, 1)
            scores = jnp.where(column <= token, scores, NEG)
        old = m_ref[question, head, part, :]
        new = jnp.maximum(old, jnp.max(scores, axis=1, keepdims=True))
        weights = jnp.exp2(scores - jnp.concatenate([new] * (width // HD), axis=1))
        mixed = jnp.dot(
            weights.astype(jnp.bfloat16), extended, preferred_element_type=jnp.float32
        )
        alpha = jnp.exp2(old - new)
        m_ref[question, head, part, :] = new
        l_ref[question, head, part, :] = l_ref[question, head, part, :] * alpha + mixed[:, HD:]
        acc_ref[question, head, part, :] = (
            acc_ref[question, head, part, :] * alpha + mixed[:, :HD]
        )


def part_kernel(k, most, first, last, heads, *refs):
    refs = list(refs)
    row_ref, tag_ref, far_tag_ref = refs.pop(0), refs.pop(0), refs.pop(0)
    own_ref = refs.pop(0) if k == 0 else None
    questions = [refs.pop(0) for _ in range(2 if k > 1 else 1)]
    cache_ref = refs.pop(0)
    items_ref = refs.pop(0) if last > most else None
    out_ref, q_ref, m_ref, l_ref, acc_ref, buf, sem, q_sem = refs
    per_device = q_ref.shape[0] // LQ

    def fetch(i, slot):
        if first < most:

            @pl.when(i < most)
            def _():
                row = row_ref[k * most + jnp.minimum(i, most - 1)]
                pltpu.make_async_copy(cache_ref.at[row], buf.at[slot], sem.at[slot]).start()

        if last > most:

            @pl.when(i >= most)
            def _():
                pltpu.make_async_copy(
                    items_ref.at[jnp.maximum(i - most, 0)], buf.at[slot], sem.at[slot]
                ).start()

    if len(questions) == 1:
        pltpu.make_async_copy(questions[0], q_ref, q_sem).start()
    else:
        inner = is_inner()

        @pl.when(inner)
        def _():
            pltpu.make_async_copy(questions[0], q_ref, q_sem).start()

        @pl.when(jnp.logical_not(inner))
        def _():
            pltpu.make_async_copy(questions[1], q_ref, q_sem).start()

    fetch(jnp.int32(first), first % 2)
    m_ref[...] = jnp.full(m_ref.shape, NEG, jnp.float32)
    l_ref[...] = jnp.zeros(l_ref.shape, jnp.float32)
    acc_ref[...] = jnp.zeros(acc_ref.shape, jnp.float32)
    pltpu.make_async_copy(q_ref, q_ref, q_sem).wait()
    if k == 0:

        def own_block(i, carry):
            question, head = i // heads, lax.rem(i, heads)
            part_step(
                q_ref,
                m_ref,
                l_ref,
                acc_ref,
                question,
                head,
                own_ref[question, head, :, :HD],
                own_ref[question, head, :, HD:],
                True,
            )
            return carry

        lax.fori_loop(0, per_device * heads, own_block, 0)

    def item(i, carry):
        slot = lax.rem(i, 2)
        pltpu.make_async_copy(buf.at[slot], buf.at[slot], sem.at[slot]).wait()

        @pl.when(i + 1 < last)
        def _():
            fetch(i + 1, lax.rem(i + 1, 2))

        at = k * most + lax.rem(i, most)
        tag = jnp.where(i < most, tag_ref[at], far_tag_ref[at])

        for head in range(heads):
            part_step(
                q_ref,
                m_ref,
                l_ref,
                acc_ref,
                tag,
                head,
                buf[slot, head, :, :HD],
                buf[slot, head, :, HD:],
                False,
            )
        return carry

    lax.fori_loop(first, last, item, 0)
    eye = unit()

    def close(c, carry):
        head, g = c // GROUP, lax.rem(c, GROUP)
        columns = pl.ds(pl.multiple_of(c * HD, HD), HD)
        part = pl.ds(pl.multiple_of(g * LQ, LQ), LQ)
        for question in range(per_device):
            total = l_ref[question, head, part, :]
            some = total > 0.0
            safe = jnp.where(some, total, 1.0)
            out_ref[question, :LQ, columns] = (
                acc_ref[question, head, part, :] / safe
            ).astype(out_ref.dtype)
            level = jnp.where(some, m_ref[question, head, part, :] + jnp.log2(safe), NEG)
            line = jnp.sum(jnp.where(eye, level, 0.0), axis=0, keepdims=True)
            store_level(out_ref, question, columns, line)
        return carry

    lax.fori_loop(0, heads * GROUP, close, 0)


def store_level(out_ref, question, columns, line):
    row_of = lax.broadcasted_iota(jnp.int32, (EXTRA, line.shape[1]), 0)
    high = line.astype(jnp.bfloat16).astype(jnp.float32)
    both = jnp.where(row_of == 0, high, jnp.where(row_of == 1, line - high, 0.0))
    out_ref[question, LQ:, columns] = both.astype(out_ref.dtype)


def part_call(k, most, tables, own, questions, cache, items, local=True):
    tokens, columns = questions[0].shape
    heads, item = cache.shape[1], cache.shape[1:]
    state = (tokens // LQ, heads, GROUP * LQ, HD)
    smem = pl.BlockSpec(memory_space=pltpu.SMEM)
    vmem = pl.BlockSpec(memory_space=pltpu.VMEM)
    anyspace = pl.BlockSpec(memory_space=pl.ANY)
    owned = [own] if k == 0 else []
    received = [items] if items is not None else []
    first, last = 0 if local else most, 2 * most if received else most
    weights = (last - first) * heads * GROUP * LQ * item[1]
    return pl.pallas_call(
        functools.partial(part_kernel, k, most, first, last, heads),
        out_shape=jax.ShapeDtypeStruct((tokens // LQ, LQ + EXTRA, columns), cache.dtype),
        in_specs=[smem] * 3
        + [vmem] * len(owned)
        + [anyspace] * (len(questions) + 1 + len(received)),
        out_specs=vmem,
        scratch_shapes=[
            pltpu.VMEM((tokens, columns), cache.dtype),
            pltpu.VMEM(state, jnp.float32),
            pltpu.VMEM(state, jnp.float32),
            pltpu.VMEM(state, jnp.float32),
            pltpu.VMEM((2,) + item, cache.dtype),
            pltpu.SemaphoreType.DMA((2,)),
            pltpu.SemaphoreType.DMA,
        ],
        compiler_params=pltpu.CompilerParams(vmem_limit_bytes=VMEM_BYTES),
        cost_estimate=pl.CostEstimate(
            flops=weights * HD * 4,
            bytes_accessed=(last - first) * math.prod(item) * 2,
            transcendentals=weights,
        ),
    )(*tables, *owned, *questions, cache, *received)


def blend(refs, out_ref, leveled):
    eye = unit()
    ones = jnp.ones((2 * LQ, LQ), jnp.bfloat16)

    def level_of(ref):
        both = ref[0, LQ:, :].astype(jnp.float32)
        return both[:1] + both[1:2]

    levels = [level_of(ref) for ref in refs]
    top = functools.reduce(jnp.maximum, levels)
    weights = [jnp.exp2(level - top) for level in levels]
    total = functools.reduce(jnp.add, weights)
    shares = []
    for weight in weights[1:]:
        share = weight / total
        high = share.astype(jnp.bfloat16).astype(jnp.float32)
        shares.append((high, share - high))
    for c in range(total.shape[1] // HD):
        columns = slice(c * HD, (c + 1) * HD)
        base = refs[0][0, :LQ, columns].astype(jnp.float32)
        value = base
        for ref, pair in zip(refs[1:], shares):
            spread = jnp.concatenate(
                [
                    jnp.where(eye, jnp.broadcast_to(v[:, columns], (LQ, LQ)), 0.0).astype(
                        jnp.bfloat16
                    )
                    for v in pair
                ],
                axis=1,
            )
            column = jnp.dot(spread, ones, preferred_element_type=jnp.float32)
            value = value + (ref[0, :LQ, columns].astype(jnp.float32) - base) * column
        value = value.astype(out_ref.dtype)
        if leveled:
            out_ref[0, :LQ, columns] = value
        else:
            out_ref[:, columns] = value
    if leveled:
        store_level(out_ref, 0, slice(None), top + jnp.log2(total))


def merge_kernel(*refs):
    *parts, out_ref = refs
    inner = is_inner()

    @pl.when(inner)
    def _():
        blend(parts, out_ref, True)

    @pl.when(jnp.logical_not(inner))
    def _():
        if len(parts) > 2:
            blend(parts[:-1], out_ref, True)
        else:
            out_ref[...] = parts[0][...]


def finish_kernel(a_ref, b_ref, out_ref):
    blend((a_ref, b_ref), out_ref, False)


def question_spec(value, at):
    shape = (1,) + value.shape[1:]
    if value.shape[0] == 1:
        return pl.BlockSpec(shape, lambda q: (0, 0, 0))
    return pl.BlockSpec(shape, lambda q: (at, 0, 0))


def join_call(parts, at, leveled):
    columns = parts[0].shape[2]
    if leveled:
        shape = (1,) + parts[0].shape[1:]
        out_spec = pl.BlockSpec(shape, lambda q: (0, 0, 0))
    else:
        shape = (LQ, columns)
        out_spec = pl.BlockSpec(shape, lambda q: (0, 0))
    size = LQ * columns
    return pl.pallas_call(
        merge_kernel if leveled else finish_kernel,
        out_shape=jax.ShapeDtypeStruct(shape, parts[0].dtype),
        grid=(1,),
        in_specs=[question_spec(part, at) for part in parts],
        out_specs=out_spec,
        compiler_params=pltpu.CompilerParams(vmem_limit_bytes=VMEM_BYTES),
        cost_estimate=pl.CostEstimate(flops=size * 8, bytes_accessed=size * 6, transcendentals=0),
    )(*parts)


def line_steps(queries, own_kv, passage_cache, out_weight, lists, passage_slot, question_slot):
    per_device = queries.shape[0] // LQ
    heads = own_kv.shape[1]
    most = per_device * lists.shape[1] // (2 * LINE)

    def send(value, pairs):
        return lax.ppermute(value, "pass", pairs)

    def part(k, *args, local=True):
        return part_call(k, most, tables, own if k == 0 else None, *args, local=local)

    def join(at, *parts, leveled=True):
        return join_call(parts, at, leveled)

    across = [(p, p ^ 1) for p in range(2 * LINE)]
    inner_across = [(p, d) for p, d in across if p // 2 in (1, 2)]
    outer_across = [(p, d) for p, d in across if p // 2 not in (1, 2)]
    near, middle = mirror(1), mirror(3, "inner")
    inward, outward = mirror(1, "outer"), mirror(1, "inner")
    q_near = send(queries, near)
    q_mid = send(queries, middle)
    half = out_weight.shape[0] // 2
    w_across0 = send(out_weight[:half], across)
    w_across1 = send(out_weight[half:], across)
    cache = jnp.transpose(passage_cache, (0, 2, 1, 3))
    row, tag, far_tag, *items = sort_items(
        lists, passage_slot, question_slot, cache, most, per_device
    )
    tables = (row, tag, far_tag)
    q_out = send(q_mid, outward)
    q_cross = send(q_near, middle)
    q_end = send(q_cross, outward)
    far = [send(items[k], across) for k in range(LINE)]
    own = own_kv.reshape(per_device, LQ, heads, 2 * HD).transpose(0, 2, 1, 3)
    part2 = part(2, [q_cross, q_out], cache, far[2])
    part3 = part(3, [q_mid, q_end], cache, far[3])
    part0 = part(0, [queries], cache, far[0])
    part1 = part(1, [q_near], cache, None)
    part1_far = part(1, [q_near], cache, far[1], local=False)
    back2 = send(part2, inward)
    w_in = send(out_weight, mirror(2, "outer"))
    w_out = send(out_weight, mirror(2, "inner"))
    back3 = send(part3, inward)
    w_in_both = send(w_in, inner_across)
    w_out_both = send(w_out, outer_across)
    own_rows, near_rows = [], []
    for q in range(per_device):
        cross3 = send(join(q, part3, back2), middle)
        near0 = join(q, part0, cross3)
        beside = send(near0, near)
        cross2 = send(join(q, part2, back3), middle)
        near1 = join(q, part1, part1_far, cross2)
        back1 = send(near1, near)
        near_rows.append(join(q, near1, beside, leveled=False))
        own_rows.append(join(q, near0, back1, leveled=False))
    weights = (out_weight, w_across0, w_across1, w_in, w_in_both, w_out, w_out_both)
    far_send, far_keep = project_call(near_rows, weights, None)
    far_sent = send_far(far_send)
    return project_call(own_rows, weights, (far_keep, far_sent))


def send_far(sums):
    pairs = []
    for p in range(2 * LINE):
        for h in range(LINE):
            if h % 2 != (p // 2) % 2:
                pairs.append((p * LINE + h, p * LINE + (h ^ 2)))
    return lax.ppermute(sums, ("pass", "head"), pairs)


MESH = pl.DeviceIdType.MESH


def at_home():
    return lax.axis_index("head") % 2 == lax.axis_index("pass") // 2 % 2


def project_kernel(pieces, far, *refs):
    rows_refs = refs[:pieces]
    own_ref, a0_ref, a1_ref, in_ref, in2_ref, out1_ref, out2_ref = refs[pieces : pieces + 7]
    refs = refs[pieces + 7 :]
    if far:
        send_ref, keep_ref = refs[:2]
    else:
        far_keep_ref, far_sent_ref, out_ref = refs[:3]
        refs = refs[1:]
    context_ref, w_ref, part_ref, core_ref, row_sem, w_sem, send_sem, recv_sem = refs[2:10]
    me, head = lax.axis_index("pass"), lax.axis_index("head")
    z, x, y = me // 2, me % 2, head // 2
    wide = w_ref.shape[3]
    inner = is_inner()
    core_peer, y_peer, z_peer = (me, head ^ 1), (me, head ^ 2), (me ^ 2, head ^ 1)
    home = at_home()
    sums = jnp.logical_not(home) if far else home

    row_loads = [
        pltpu.make_async_copy(ref, context_ref.at[pl.ds(i * LQ, LQ)], row_sem.at[i])
        for i, ref in enumerate(rows_refs)
    ]
    for load in row_loads:
        load.start()

    def load_here():
        pltpu.make_async_copy(own_ref, w_ref.at[0, x], w_sem.at[0, x]).start()
        half = a0_ref.shape[0]
        low, high = w_ref.at[0, 1 - x, pl.ds(0, half)], w_ref.at[0, 1 - x, pl.ds(half, half)]
        pltpu.make_async_copy(a0_ref, low, w_sem.at[0, 1 - x]).start()
        pltpu.make_async_copy(a1_ref, high, w_sem.at[0, 1 - x]).start()

    def load_there():
        for which, (one, two) in (
            (inner, (in_ref, in2_ref)),
            (jnp.logical_not(inner), (out1_ref, out2_ref)),
        ):

            @pl.when(which)
            def _():
                pltpu.make_async_copy(one, w_ref.at[1, x], w_sem.at[1, x]).start()
                pltpu.make_async_copy(two, w_ref.at[1, 1 - x], w_sem.at[1, 1 - x]).start()

    here_first = y != z // 2

    @pl.when(here_first)
    def _():
        load_here()
        load_there()

    @pl.when(jnp.logical_not(here_first))
    def _():
        load_there()
        load_here()

    barrier = pltpu.get_barrier_semaphore()
    peers = (core_peer,) if far else (core_peer, y_peer, z_peer)
    for peer in peers:
        pl.semaphore_signal(barrier, inc=1, device_id=peer, device_id_type=MESH)
    pl.semaphore_wait(barrier, len(peers))

    def remote(src, dst, i, peer):
        return pltpu.make_async_remote_copy(
            src_ref=src,
            dst_ref=dst,
            send_sem=send_sem.at[i],
            recv_sem=recv_sem.at[i],
            device_id=peer,
            device_id_type=MESH,
        )

    def columns(j):
        return pl.ds(j * wide, wide)

    core_copies = [
        [remote(part_ref.at[s, j], core_ref.at[s, j], s * 2 + j, core_peer) for j in range(2)]
        for s in range(2)
    ]
    if not far:
        y_ref, ysend_ref, zsend_ref = refs[10:]
        y_copies = [remote(ysend_ref.at[j], y_ref.at[j], 4 + j, y_peer) for j in range(2)]
        z_copies = [
            remote(zsend_ref.at[j], out_ref.at[:, columns(j)], 6 + j, z_peer) for j in range(2)
        ]

        @pl.when(jnp.logical_not(home))
        def _():
            for j in range(2):
                zsend_ref[j] = (
                    far_keep_ref[j].astype(jnp.float32) + far_sent_ref[j].astype(jnp.float32)
                ).astype(zsend_ref.dtype)
                z_copies[j].start()

    for load in row_loads:
        load.wait()

    def multiply(s, to_y, j):
        here = jnp.where(to_y == z // 2, 0, 1)
        block = w_ref.at[here, j]
        pltpu.make_async_copy(block, block, w_sem.at[here, j]).wait()
        part_ref[s, j] = jnp.dot(
            context_ref[...], w_ref[here, j], preferred_element_type=jnp.float32
        ).astype(part_ref.dtype)

        @pl.when(jnp.logical_not(sums))
        def _():
            core_copies[s][j].start()

    def add_up(s, j):
        @pl.when(sums)
        def _():
            core_copies[s][j].wait_recv()
            value = part_ref[s, j].astype(jnp.float32) + core_ref[s, j].astype(jnp.float32)
            if far:
                target = keep_ref if s else send_ref
                target[j] = value.astype(target.dtype)
            elif s == 0:
                ysend_ref[j] = value.astype(ysend_ref.dtype)
                y_copies[j].start()
            else:
                y_copies[j].wait_recv()
                out_ref[:, columns(j)] = (value + y_ref[j].astype(jnp.float32)).astype(
                    out_ref.dtype
                )

    late = None
    for s, to_y in enumerate((1 - y, y)):
        for j in range(2):
            multiply(s, to_y, j)
            if late is not None:
                add_up(*late)
            late = (s, j)
    add_up(*late)

    @pl.when(jnp.logical_not(sums))
    def _():
        for copies in core_copies:
            for copy in copies:
                copy.wait_send()

    if not far:

        @pl.when(home)
        def _():
            for copy in y_copies:
                copy.wait_send()

        @pl.when(jnp.logical_not(home))
        def _():
            for copy in z_copies:
                copy.wait()


def project_call(pieces, weights, far_sums):
    own = weights[0]
    rows, (depth, wide) = len(pieces) * LQ, own.shape
    dtype = own.dtype
    far = far_sums is None
    vmem = pl.BlockSpec(memory_space=pltpu.VMEM)
    blocks = (2, rows, wide)
    scratch = [
        pltpu.VMEM((rows, depth), dtype),
        pltpu.VMEM((2, 2, depth, wide), dtype),
        pltpu.VMEM((2,) + blocks, dtype),
        pltpu.VMEM((2,) + blocks, dtype),
        pltpu.SemaphoreType.DMA((len(pieces),)),
        pltpu.SemaphoreType.DMA((2, 2)),
        pltpu.SemaphoreType.DMA((8,)),
        pltpu.SemaphoreType.DMA((8,)),
    ]
    if far:
        out_shape = [jax.ShapeDtypeStruct(blocks, dtype)] * 2
        out_specs = [vmem] * 2
    else:
        out_shape = jax.ShapeDtypeStruct((rows, 2 * wide), dtype)
        out_specs = vmem
        scratch += [pltpu.VMEM(blocks, dtype)] * 3
    return pl.pallas_call(
        functools.partial(project_kernel, len(pieces), far),
        out_shape=out_shape,
        in_specs=[pl.BlockSpec(memory_space=pl.ANY)] * (len(pieces) + len(weights))
        + [vmem] * (0 if far else 2),
        out_specs=out_specs,
        scratch_shapes=scratch,
        compiler_params=pltpu.CompilerParams(
            collective_id=int(far), has_side_effects=True, vmem_limit_bytes=VMEM_BYTES
        ),
        name="project_far" if far else "project_home",
        cost_estimate=pl.CostEstimate(
            flops=2 * 4 * rows * depth * wide,
            bytes_accessed=4 * depth * wide * 2,
            transcendentals=0,
        ),
    )(*pieces, *weights, *(far_sums or ()))


def suits_line(mesh, queries, lists):
    passes, heads = mesh.shape["pass"], mesh.shape["head"]
    entries = queries.shape[0] // LQ // passes * lists.shape[1]
    return passes == 2 * LINE and heads == LINE and entries % passes == 0


def solution(mesh):
    in_specs = (
        P("pass", "head"),
        P("pass", "head", None),
        P("pass", None, "head", None),
        P("head", "pass"),
        P(),
        P(),
        P(),
    )
    out_specs = P("pass", "head")

    def run(*args):
        if not suits_line(mesh, args[0], args[4]):
            return jax.shard_map(
                body, mesh=mesh, in_specs=in_specs, out_specs=out_specs, check_vma=False
            )(*args)
        step = jax.shard_map(
            line_steps, mesh=mesh, in_specs=in_specs, out_specs=out_specs, check_vma=False
        )
        return step(*args)

    return run
```

```python
import functools
import math

import jax
import jax.numpy as jnp
from jax import lax
from jax.experimental import pallas as pl
from jax.experimental.pallas import tpu as pltpu
from jax.sharding import PartitionSpec as P


H = 64
KVH = 8
HD = 128
LQ = 128
GROUP = H // KVH
COEF = HD ** (-0.5) * math.log2(math.e)
NEG = -1e30
ROWS = 256


def round_of(a, b, n):
    if n & (n - 1) == 0:
        return a ^ b
    return lax.rem(b - a + n, n)


def pairs_of(k, n):
    if n & (n - 1) == 0:
        return [(p, p ^ k) for p in range(n)]
    return [(p, (p + k) % n) for p in range(n)]


def order_of(n):
    rest = range(1, n)
    return sorted(rest, key=lambda k: (bin(k).count("1"), k))


def gather_kernel(n, most, per_device, order, lists_ref, pslot_ref, qslot_ref, cache_ref, *refs):
    recv_ref, own_row_ref = refs[0], refs[1]
    outs = refs[2 : 2 + len(order)]
    send_row, send_cnt, recv_cnt, buf, in_sem, out_sem = refs[2 + len(order) :]
    me = lax.axis_index("pass")
    pass_dev = cache_ref.shape[0]
    topp, nq = lists_ref.shape
    for k in range(n):
        send_cnt[k] = 0
        recv_cnt[k] = 0
    for i in range(n * most):
        recv_ref[i] = -1
        send_row[i] = 0

    def question(q, carry):
        slot = qslot_ref[q]
        dest = slot // per_device
        local = slot - dest * per_device
        k_send = round_of(me, dest, n)
        for t in range(topp):
            row = pslot_ref[lists_ref[t, q]]
            owner = row // pass_dev

            @pl.when(owner == me)
            def _():
                count = send_cnt[k_send]
                send_row[k_send * most + count] = row - owner * pass_dev
                send_cnt[k_send] = count + 1

            @pl.when(dest == me)
            def _():
                k = round_of(owner, me, n)
                count = recv_cnt[k]
                recv_ref[k * most + count] = local
                recv_cnt[k] = count + 1

        return carry

    lax.fori_loop(0, nq, question, 0)
    for r in range(most):
        own_row_ref[r] = send_row[r]
    copies = []
    for j, k in enumerate(order):
        for r in range(most):
            i = j * most + r
            get = pltpu.make_async_copy(
                cache_ref.at[send_row[k * most + r]], buf.at[i], in_sem.at[i]
            )
            get.start()
            copies.append((get, pltpu.make_async_copy(buf.at[i], outs[j].at[r], out_sem.at[i])))
    for get, put in copies:
        get.wait()
        put.start()
    for get, put in copies:
        put.wait()


def gather(lists, passage_slot, question_slot, cache, n, most, per_device, order):
    item = cache.shape[1:]
    slots = (n - 1) * most
    smem = pl.BlockSpec(memory_space=pltpu.SMEM)
    anyspace = pl.BlockSpec(memory_space=pl.ANY)
    return pl.pallas_call(
        functools.partial(gather_kernel, n, most, per_device, order),
        out_shape=[
            jax.ShapeDtypeStruct((n * most,), jnp.int32),
            jax.ShapeDtypeStruct((most,), jnp.int32),
        ]
        + [jax.ShapeDtypeStruct((most,) + item, cache.dtype)] * len(order),
        in_specs=[smem, smem, smem, anyspace],
        out_specs=[smem, smem] + [anyspace] * len(order),
        scratch_shapes=[
            pltpu.SMEM((n * most,), jnp.int32),
            pltpu.SMEM((n,), jnp.int32),
            pltpu.SMEM((n,), jnp.int32),
            pltpu.VMEM((slots,) + item, cache.dtype),
            pltpu.SemaphoreType.DMA((slots,)),
            pltpu.SemaphoreType.DMA((slots,)),
        ],
        name="gather_items",
        cost_estimate=pl.CostEstimate(
            flops=0, bytes_accessed=2 * slots * math.prod(item) * 2, transcendentals=0
        ),
    )(lists.T, passage_slot, question_slot, cache)


def block_step(q_ref, m_ref, l_ref, acc_ref, question, head, keys, values, causal):
    rows = q_ref.shape[2]
    step = min(ROWS, rows)
    width = keys.shape[0]
    ones = jnp.ones(values.shape, values.dtype)
    extended = jnp.concatenate([values, ones], axis=1)
    for start in range(0, rows, step):
        part = pl.ds(start, step)
        q = q_ref[question, head, part, :]
        scores = (
            lax.dot_general(q, keys, (((1,), (1,)), ((), ())), preferred_element_type=jnp.float32)
            * COEF
        )
        if causal:
            token = lax.broadcasted_iota(jnp.int32, scores.shape, 0) % LQ
            column = lax.broadcasted_iota(jnp.int32, scores.shape, 1)
            scores = jnp.where(column <= token, scores, NEG)
        old = m_ref[question, head, part, :]
        new = jnp.maximum(old, jnp.max(scores, axis=1, keepdims=True))
        weights = jnp.exp2(scores - jnp.concatenate([new] * (width // HD), axis=1))
        mixed = jnp.dot(
            weights.astype(jnp.bfloat16), extended, preferred_element_type=jnp.float32
        )
        alpha = jnp.exp2(old - new)
        m_ref[question, head, part, :] = new
        l_ref[question, head, part, :] = l_ref[question, head, part, :] * alpha + mixed[:, HD:]
        acc_ref[question, head, part, :] = (
            acc_ref[question, head, part, :] * alpha + mixed[:, :HD]
        )


def attend_kernel(first, last, rounds, most, *refs):
    refs = list(refs)
    recv_ref, q_ref = refs.pop(0), refs.pop(0)
    if first:
        row_ref, own_ref, cache_ref = refs.pop(0), refs.pop(0), refs.pop(0)
        sources = None
        entries = most
    else:
        state_in = [refs.pop(0) for _ in range(3)]
        sources = [refs.pop(0) for _ in rounds]
        entries = len(rounds) * most
    if last:
        out_ref = refs.pop(0)
        m_ref, l_ref, acc_ref = [refs.pop(0) for _ in range(3)]
    else:
        m_ref, l_ref, acc_ref = [refs.pop(0) for _ in range(3)]
    buf, sem = refs
    per_device, heads = q_ref.shape[0], q_ref.shape[1]

    def fetch(i, slot):
        if first:
            pltpu.make_async_copy(cache_ref.at[row_ref[i]], buf.at[slot], sem.at[slot]).start()
            return
        for j in range(len(rounds)):

            @pl.when(i // most == j)
            def _():
                pltpu.make_async_copy(
                    sources[j].at[i - j * most], buf.at[slot], sem.at[slot]
                ).start()

    def tag_of(i):
        if first:
            return recv_ref[i]
        k = jnp.int32(0)
        for j, value in enumerate(rounds):
            k = jnp.where(i // most == j, value, k)
        return recv_ref[k * most + lax.rem(i, most)]

    fetch(jnp.int32(0), 0)
    if first:
        m_ref[...] = jnp.full(m_ref.shape, NEG, jnp.float32)
        l_ref[...] = jnp.zeros(l_ref.shape, jnp.float32)
        acc_ref[...] = jnp.zeros(acc_ref.shape, jnp.float32)

        def own_block(question, carry):
            for head in range(heads):
                block = own_ref[question, head]
                block_step(
                    q_ref, m_ref, l_ref, acc_ref, question, head, block[:, :HD], block[:, HD:], True
                )
            return carry

        lax.fori_loop(0, per_device, own_block, 0)
    else:
        m_ref[...] = state_in[0][...]
        l_ref[...] = state_in[1][...]
        acc_ref[...] = state_in[2][...]

    def item(i, carry):
        slot = lax.rem(i, 2)
        pltpu.make_async_copy(buf.at[slot], buf.at[slot], sem.at[slot]).wait()

        @pl.when(i + 1 < entries)
        def _():
            fetch(i + 1, lax.rem(i + 1, 2))

        tag = tag_of(i)

        @pl.when(tag >= 0)
        def _():
            for head in range(heads):
                block_step(
                    q_ref,
                    m_ref,
                    l_ref,
                    acc_ref,
                    tag,
                    head,
                    buf[slot, head, :, :HD],
                    buf[slot, head, :, HD:],
                    False,
                )

        return carry

    lax.fori_loop(0, entries, item, 0)
    if last:
        for question in range(per_device):
            for head in range(heads):
                for g in range(GROUP):
                    part = pl.ds(g * LQ, LQ)
                    column = (head * GROUP + g) * HD
                    out_ref[pl.ds(question * LQ, LQ), pl.ds(column, HD)] = (
                        acc_ref[question, head, part, :] / l_ref[question, head, part, :]
                    ).astype(out_ref.dtype)


def attend_call(first, last, rounds, most, recv, q, rest, item):
    per_device, heads, rows, _ = q.shape
    state = jax.ShapeDtypeStruct(q.shape, jnp.float32)
    smem = pl.BlockSpec(memory_space=pltpu.SMEM)
    vmem = pl.BlockSpec(memory_space=pltpu.VMEM)
    anyspace = pl.BlockSpec(memory_space=pl.ANY)
    if first:
        in_specs = [smem, vmem, smem, vmem, anyspace]
        entries = most
    else:
        in_specs = [smem, vmem] + [vmem] * 3 + [anyspace] * len(rounds)
        entries = most * len(rounds)
    scratch = [pltpu.VMEM((2,) + item, q.dtype), pltpu.SemaphoreType.DMA((2,))]
    if last:
        out_shape = jax.ShapeDtypeStruct((per_device * LQ, heads * GROUP * HD), q.dtype)
        out_specs = vmem
        scratch = [pltpu.VMEM(q.shape, jnp.float32)] * 3 + scratch
    else:
        out_shape = [state] * 3
        out_specs = [vmem] * 3
    weights = entries * heads * rows * item[1]
    return pl.pallas_call(
        functools.partial(attend_kernel, first, last, rounds, most),
        out_shape=out_shape,
        in_specs=in_specs,
        out_specs=out_specs,
        scratch_shapes=scratch,
        name="attend_first" if first else ("attend_last" if last else "attend_more"),
        cost_estimate=pl.CostEstimate(
            flops=weights * HD * 4,
            bytes_accessed=entries * math.prod(item) * 2,
            transcendentals=weights,
        ),
    )(recv, q, *rest)


def weight_blocks(own, n):
    if n & (n - 1):
        return [lax.all_gather(own, "pass", axis=1, tiled=True)]
    have = {0: own}
    bit = n // 2
    while bit:
        for k in list(have):
            have[k ^ bit] = lax.ppermute(have[k], "pass", pairs_of(bit, n))
        bit //= 2
    return [have[k] for k in range(n)]


def project(context, weights):
    parts = [
        jnp.dot(context, weight, preferred_element_type=jnp.float32).astype(jnp.bfloat16)
        for weight in weights
    ]
    me = lax.axis_index("pass")
    bit = len(parts) // 2
    while bit:
        swap = (me & bit) != 0
        parts = [jnp.where(swap, parts[k ^ bit], parts[k]) for k in range(len(parts))]
        bit //= 2
    return jnp.concatenate(parts, axis=1)


def body(queries, own_kv, passage_cache, out_weight, lists, passage_slot, question_slot):
    n = lax.axis_size("pass")
    per_device = queries.shape[0] // LQ
    heads = own_kv.shape[1]
    entries = per_device * lists.shape[1]
    most = (entries + n - 1) // n
    order = order_of(n)
    cache = jnp.transpose(passage_cache, (0, 2, 1, 3))
    recv, own_row, *items = gather(
        lists, passage_slot, question_slot, cache, n, most, per_device, order
    )
    arrived = [
        lax.ppermute(item, "pass", pairs_of(k, n)) for k, item in zip(order, items)
    ]
    weights = weight_blocks(out_weight, n)
    q = (
        queries.reshape(per_device, LQ, heads, GROUP, HD)
        .transpose(0, 2, 3, 1, 4)
        .reshape(per_device, heads, GROUP * LQ, HD)
    )
    own = own_kv.reshape(per_device, LQ, heads, 2 * HD).transpose(0, 2, 1, 3)
    item = cache.shape[1:]
    state = attend_call(True, False, (0,), most, recv, q, (own_row, own, cache), item)
    calls = 3
    bounds = [len(order) * i // calls for i in range(calls + 1)]
    for i in range(calls):
        rounds = tuple(order[bounds[i] : bounds[i + 1]])
        rest = tuple(state) + tuple(arrived[bounds[i] : bounds[i + 1]])
        state = attend_call(False, i == calls - 1, rounds, most, recv, q, rest, item)
    context = state
    return lax.psum_scatter(project(context, weights), "head", scatter_dimension=1, tiled=True)


LINE = 4
EXTRA = 8
ITEM_ORDER = (2, 0, 3, 1)
VMEM_BYTES = 67043328


def mirror(k, ends=None):
    pairs = [(p, p ^ int(2 * k)) for p in range(2 * LINE)]
    if ends is None:
        return pairs
    return [(p, d) for p, d in pairs if (p // 2 in (0, LINE - 1)) == (ends == "outer")]


def is_inner():
    z = lax.axis_index("pass") // 2
    return jnp.logical_and(z > 0, z < LINE - 1)


def sort_kernel(most, per_device, lists_ref, pslot_ref, qslot_ref, cache_ref, *refs):
    row_ref, tag_ref, far_tag_ref = refs[:3]
    outs = refs[3 : 3 + LINE]
    send_row, near_cnt, send_cnt, far_cnt, buf, in_sem, out_sem = refs[3 + LINE :]
    me = lax.axis_index("pass")
    z, x = me // 2, me % 2
    pass_dev = cache_ref.shape[0]
    topp, nq = lists_ref.shape
    for k in range(LINE):
        near_cnt[k] = 0
        send_cnt[k] = 0
        far_cnt[k] = 0

    def take(i):
        return pltpu.make_async_copy(cache_ref.at[send_row[i]], buf.at[i], in_sem.at[i])

    def question(q, carry):
        slot = qslot_ref[q]
        dest = slot // per_device
        local = slot - dest * per_device
        k = (dest // 2) ^ z

        @pl.when(dest % 2 == x)
        def _():
            for t in range(topp):
                row = pslot_ref[lists_ref[t, q]]
                owner = row // pass_dev

                @pl.when(owner == me)
                def _():
                    at = k * most + near_cnt[k]
                    row_ref[at] = row - owner * pass_dev
                    tag_ref[at] = local
                    near_cnt[k] = near_cnt[k] + 1

                @pl.when(owner == (me ^ 1))
                def _():
                    far_tag_ref[k * most + far_cnt[k]] = local
                    far_cnt[k] = far_cnt[k] + 1

        @pl.when(dest % 2 != x)
        def _():
            for t in range(topp):
                row = pslot_ref[lists_ref[t, q]]
                owner = row // pass_dev

                @pl.when(owner == me)
                def _():
                    at = k * most + send_cnt[k]
                    send_row[at] = row - owner * pass_dev
                    send_cnt[k] = send_cnt[k] + 1
                    take(at).start()

        return carry

    lax.fori_loop(0, nq, question, 0)
    slots = [k * most + r for k in ITEM_ORDER for r in range(most)]
    puts = [pltpu.make_async_copy(buf.at[i], outs[i // most].at[i % most], out_sem.at[i]) for i in slots]
    for i, put in zip(slots, puts):
        take(i).wait()
        put.start()
    for put in puts:
        put.wait()


def sort_items(lists, passage_slot, question_slot, cache, most, per_device):
    item = cache.shape[1:]
    slots = LINE * most
    smem = pl.BlockSpec(memory_space=pltpu.SMEM)
    anyspace = pl.BlockSpec(memory_space=pl.ANY)
    return pl.pallas_call(
        functools.partial(sort_kernel, most, per_device),
        out_shape=[jax.ShapeDtypeStruct((slots,), jnp.int32)] * 3
        + [jax.ShapeDtypeStruct((most,) + item, cache.dtype)] * LINE,
        in_specs=[smem, smem, smem, anyspace],
        out_specs=[smem] * 3 + [anyspace] * LINE,
        scratch_shapes=[
            pltpu.SMEM((slots,), jnp.int32),
            pltpu.SMEM((LINE,), jnp.int32),
            pltpu.SMEM((LINE,), jnp.int32),
            pltpu.SMEM((LINE,), jnp.int32),
            pltpu.VMEM((slots,) + item, cache.dtype),
            pltpu.SemaphoreType.DMA((slots,)),
            pltpu.SemaphoreType.DMA((slots,)),
        ],
        compiler_params=pltpu.CompilerParams(vmem_limit_bytes=VMEM_BYTES),
        name="sort_items",
        cost_estimate=pl.CostEstimate(
            flops=0, bytes_accessed=2 * slots * math.prod(item) * 2, transcendentals=0
        ),
    )(lists.T, passage_slot, question_slot, cache)


def unit():
    r = lax.broadcasted_iota(jnp.int32, (LQ, LQ), 0)
    c = lax.broadcasted_iota(jnp.int32, (LQ, LQ), 1)
    return r == c


def part_step(q_ref, m_ref, l_ref, acc_ref, question, head, keys, values, causal):
    rows = GROUP * LQ
    width = keys.shape[0]
    ones = jnp.ones(values.shape, values.dtype)
    extended = jnp.concatenate([values, ones], axis=1)
    tokens = pl.ds(pl.multiple_of(question * LQ, LQ), LQ)
    for start in range(0, rows, ROWS):
        part = pl.ds(start, ROWS)
        q = jnp.concatenate(
            [
                q_ref[tokens, pl.ds(pl.multiple_of((head * GROUP + g) * HD, HD), HD)]
                for g in range(start // LQ, (start + ROWS) // LQ)
            ],
            axis=0,
        )
        scores = (
            lax.dot_general(q, keys, (((1,), (1,)), ((), ())), preferred_element_type=jnp.float32)
            * COEF
        )
        if causal:
            token = lax.broadcasted_iota(jnp.int32, scores.shape, 0) % LQ
            column = lax.broadcasted_iota(jnp.int32, scores.shape, 1)
            scores = jnp.where(column <= token, scores, NEG)
        old = m_ref[question, head, part, :]
        new = jnp.maximum(old, jnp.max(scores, axis=1, keepdims=True))
        weights = jnp.exp2(scores - jnp.concatenate([new] * (width // HD), axis=1))
        mixed = jnp.dot(
            weights.astype(jnp.bfloat16), extended, preferred_element_type=jnp.float32
        )
        alpha = jnp.exp2(old - new)
        m_ref[question, head, part, :] = new
        l_ref[question, head, part, :] = l_ref[question, head, part, :] * alpha + mixed[:, HD:]
        acc_ref[question, head, part, :] = (
            acc_ref[question, head, part, :] * alpha + mixed[:, :HD]
        )


def part_kernel(k, most, first, last, heads, *refs):
    refs = list(refs)
    row_ref, tag_ref, far_tag_ref = refs.pop(0), refs.pop(0), refs.pop(0)
    own_ref = refs.pop(0) if k == 0 else None
    questions = [refs.pop(0) for _ in range(2 if k > 1 else 1)]
    cache_ref = refs.pop(0)
    items_ref = refs.pop(0) if last > most else None
    out_ref, q_ref, m_ref, l_ref, acc_ref, buf, sem, q_sem = refs
    per_device = q_ref.shape[0] // LQ

    def fetch(i, slot):
        if first < most:

            @pl.when(i < most)
            def _():
                row = row_ref[k * most + jnp.minimum(i, most - 1)]
                pltpu.make_async_copy(cache_ref.at[row], buf.at[slot], sem.at[slot]).start()

        if last > most:

            @pl.when(i >= most)
            def _():
                pltpu.make_async_copy(
                    items_ref.at[jnp.maximum(i - most, 0)], buf.at[slot], sem.at[slot]
                ).start()

    if len(questions) == 1:
        pltpu.make_async_copy(questions[0], q_ref, q_sem).start()
    else:
        inner = is_inner()

        @pl.when(inner)
        def _():
            pltpu.make_async_copy(questions[0], q_ref, q_sem).start()

        @pl.when(jnp.logical_not(inner))
        def _():
            pltpu.make_async_copy(questions[1], q_ref, q_sem).start()

    fetch(jnp.int32(first), first % 2)
    m_ref[...] = jnp.full(m_ref.shape, NEG, jnp.float32)
    l_ref[...] = jnp.zeros(l_ref.shape, jnp.float32)
    acc_ref[...] = jnp.zeros(acc_ref.shape, jnp.float32)
    pltpu.make_async_copy(q_ref, q_ref, q_sem).wait()
    if k == 0:

        def own_block(i, carry):
            question, head = i // heads, lax.rem(i, heads)
            part_step(
                q_ref,
                m_ref,
                l_ref,
                acc_ref,
                question,
                head,
                own_ref[question, head, :, :HD],
                own_ref[question, head, :, HD:],
                True,
            )
            return carry

        lax.fori_loop(0, per_device * heads, own_block, 0)

    def item(i, carry):
        slot = lax.rem(i, 2)
        pltpu.make_async_copy(buf.at[slot], buf.at[slot], sem.at[slot]).wait()

        @pl.when(i + 1 < last)
        def _():
            fetch(i + 1, lax.rem(i + 1, 2))

        at = k * most + lax.rem(i, most)
        tag = jnp.where(i < most, tag_ref[at], far_tag_ref[at])

        for head in range(heads):
            part_step(
                q_ref,
                m_ref,
                l_ref,
                acc_ref,
                tag,
                head,
                buf[slot, head, :, :HD],
                buf[slot, head, :, HD:],
                False,
            )
        return carry

    lax.fori_loop(first, last, item, 0)
    eye = unit()

    def close(c, carry):
        head, g = c // GROUP, lax.rem(c, GROUP)
        columns = pl.ds(pl.multiple_of(c * HD, HD), HD)
        part = pl.ds(pl.multiple_of(g * LQ, LQ), LQ)
        for question in range(per_device):
            total = l_ref[question, head, part, :]
            some = total > 0.0
            safe = jnp.where(some, total, 1.0)
            out_ref[question, :LQ, columns] = (
                acc_ref[question, head, part, :] / safe
            ).astype(out_ref.dtype)
            level = jnp.where(some, m_ref[question, head, part, :] + jnp.log2(safe), NEG)
            line = jnp.sum(jnp.where(eye, level, 0.0), axis=0, keepdims=True)
            store_level(out_ref, question, columns, line)
        return carry

    lax.fori_loop(0, heads * GROUP, close, 0)


def store_level(out_ref, question, columns, line):
    row_of = lax.broadcasted_iota(jnp.int32, (EXTRA, line.shape[1]), 0)
    high = line.astype(jnp.bfloat16).astype(jnp.float32)
    both = jnp.where(row_of == 0, high, jnp.where(row_of == 1, line - high, 0.0))
    out_ref[question, LQ:, columns] = both.astype(out_ref.dtype)


def part_call(k, most, tables, own, questions, cache, items, local=True):
    tokens, columns = questions[0].shape
    heads, item = cache.shape[1], cache.shape[1:]
    state = (tokens // LQ, heads, GROUP * LQ, HD)
    smem = pl.BlockSpec(memory_space=pltpu.SMEM)
    vmem = pl.BlockSpec(memory_space=pltpu.VMEM)
    anyspace = pl.BlockSpec(memory_space=pl.ANY)
    owned = [own] if k == 0 else []
    received = [items] if items is not None else []
    first, last = 0 if local else most, 2 * most if received else most
    weights = (last - first) * heads * GROUP * LQ * item[1]
    return pl.pallas_call(
        functools.partial(part_kernel, k, most, first, last, heads),
        out_shape=jax.ShapeDtypeStruct((tokens // LQ, LQ + EXTRA, columns), cache.dtype),
        in_specs=[smem] * 3
        + [vmem] * len(owned)
        + [anyspace] * (len(questions) + 1 + len(received)),
        out_specs=vmem,
        scratch_shapes=[
            pltpu.VMEM((tokens, columns), cache.dtype),
            pltpu.VMEM(state, jnp.float32),
            pltpu.VMEM(state, jnp.float32),
            pltpu.VMEM(state, jnp.float32),
            pltpu.VMEM((2,) + item, cache.dtype),
            pltpu.SemaphoreType.DMA((2,)),
            pltpu.SemaphoreType.DMA,
        ],
        compiler_params=pltpu.CompilerParams(vmem_limit_bytes=VMEM_BYTES),
        cost_estimate=pl.CostEstimate(
            flops=weights * HD * 4,
            bytes_accessed=(last - first) * math.prod(item) * 2,
            transcendentals=weights,
        ),
    )(*tables, *owned, *questions, cache, *received)


def blend(refs, share_ref, out_ref, leveled):
    eye = unit()
    ones = jnp.ones((2 * LQ, LQ), jnp.bfloat16)

    def level_of(ref):
        both = ref[0, LQ:, :].astype(jnp.float32)
        return both[:1] + both[1:2]

    levels = [level_of(ref) for ref in refs]
    top = functools.reduce(jnp.maximum, levels)
    weights = [jnp.exp2(level - top) for level in levels]
    total = functools.reduce(jnp.add, weights)
    for n, weight in enumerate(weights[1:]):
        share = weight / total
        high = share.astype(jnp.bfloat16).astype(jnp.float32)
        share_ref[2 * n : 2 * n + 1, :] = high
        share_ref[2 * n + 1 : 2 * n + 2, :] = share - high

    def tile(c, carry):
        columns = pl.ds(pl.multiple_of(c * HD, HD), HD)
        base = refs[0][0, :LQ, columns].astype(jnp.float32)
        value = base
        for n, ref in enumerate(refs[1:]):
            spread = jnp.concatenate(
                [
                    jnp.where(
                        eye, jnp.broadcast_to(share_ref[r : r + 1, columns], (LQ, LQ)), 0.0
                    ).astype(jnp.bfloat16)
                    for r in (2 * n, 2 * n + 1)
                ],
                axis=1,
            )
            column = jnp.dot(spread, ones, preferred_element_type=jnp.float32)
            value = value + (ref[0, :LQ, columns].astype(jnp.float32) - base) * column
        value = value.astype(out_ref.dtype)
        if leveled:
            out_ref[0, :LQ, columns] = value
        else:
            out_ref[:, columns] = value
        return carry

    lax.fori_loop(0, total.shape[1] // HD, tile, 0, unroll=4)
    if leveled:
        store_level(out_ref, 0, slice(None), top + jnp.log2(total))


def merge_kernel(*refs):
    *parts, out_ref, share_ref = refs
    inner = is_inner()

    @pl.when(inner)
    def _():
        blend(parts, share_ref, out_ref, True)

    @pl.when(jnp.logical_not(inner))
    def _():
        if len(parts) > 2:
            blend(parts[:-1], share_ref, out_ref, True)
        else:
            out_ref[...] = parts[0][...]


def finish_kernel(a_ref, b_ref, out_ref, share_ref):
    blend((a_ref, b_ref), share_ref, out_ref, False)


def question_spec(value, at):
    shape = (1,) + value.shape[1:]
    if value.shape[0] == 1:
        return pl.BlockSpec(shape, lambda q: (0, 0, 0))
    return pl.BlockSpec(shape, lambda q: (at, 0, 0))


def join_call(parts, at, leveled):
    columns = parts[0].shape[2]
    if leveled:
        shape = (1,) + parts[0].shape[1:]
        out_spec = pl.BlockSpec(shape, lambda q: (0, 0, 0))
    else:
        shape = (LQ, columns)
        out_spec = pl.BlockSpec(shape, lambda q: (0, 0))
    size = LQ * columns
    return pl.pallas_call(
        merge_kernel if leveled else finish_kernel,
        out_shape=jax.ShapeDtypeStruct(shape, parts[0].dtype),
        grid=(1,),
        in_specs=[question_spec(part, at) for part in parts],
        out_specs=out_spec,
        scratch_shapes=[pltpu.VMEM((8, columns), jnp.float32)],
        compiler_params=pltpu.CompilerParams(vmem_limit_bytes=VMEM_BYTES),
        cost_estimate=pl.CostEstimate(flops=size * 8, bytes_accessed=size * 6, transcendentals=0),
    )(*parts)


def line_steps(queries, own_kv, passage_cache, out_weight, lists, passage_slot, question_slot):
    per_device = queries.shape[0] // LQ
    heads = own_kv.shape[1]
    most = per_device * lists.shape[1] // (2 * LINE)

    def send(value, pairs):
        return lax.ppermute(value, "pass", pairs)

    def part(k, *args, local=True):
        return part_call(k, most, tables, own if k == 0 else None, *args, local=local)

    def join(at, *parts, leveled=True):
        return join_call(parts, at, leveled)

    across = [(p, p ^ 1) for p in range(2 * LINE)]
    inner_across = [(p, d) for p, d in across if p // 2 in (1, 2)]
    outer_across = [(p, d) for p, d in across if p // 2 not in (1, 2)]
    near, middle = mirror(1), mirror(3, "inner")
    inward, outward = mirror(1, "outer"), mirror(1, "inner")
    q_near = send(queries, near)
    q_mid = send(queries, middle)
    half = out_weight.shape[0] // 2
    w_across = send(out_weight, across)
    cache = jnp.transpose(passage_cache, (0, 2, 1, 3))
    row, tag, far_tag, *items = sort_items(
        lists, passage_slot, question_slot, cache, most, per_device
    )
    tables = (row, tag, far_tag)
    q_out = send(q_mid, outward)
    q_cross = send(q_near, middle)
    q_end = send(q_cross, outward)
    far = [send(items[k], across) for k in range(LINE)]
    own = own_kv.reshape(per_device, LQ, heads, 2 * HD).transpose(0, 2, 1, 3)
    part2 = part(2, [q_cross, q_out], cache, far[2])
    part3 = part(3, [q_mid, q_end], cache, far[3])
    part0 = part(0, [queries], cache, far[0])
    part1 = part(1, [q_near], cache, None)
    part1_far = part(1, [q_near], cache, far[1], local=False)
    back2 = send(part2, inward)
    w_in0 = send(out_weight[:half], mirror(2, "outer"))
    w_in1 = send(out_weight[half:], mirror(2, "outer"))
    w_out = send(out_weight, mirror(2, "inner"))
    back3 = send(part3, inward)
    w_in0_both = send(w_in0, inner_across)
    w_in1_both = send(w_in1, inner_across)
    w_out_both = send(w_out, outer_across)
    own_rows, near_rows = [], []
    for q in range(per_device):
        cross3 = send(join(q, part3, back2), middle)
        near0 = join(q, part0, cross3)
        beside = send(near0, near)
        cross2 = send(join(q, part2, back3), middle)
        near1 = join(q, part1, part1_far, cross2)
        back1 = send(near1, near)
        near_rows.append(join(q, near1, beside, leveled=False))
        own_rows.append(join(q, near0, back1, leveled=False))
    weights = (out_weight, w_across, w_in0, w_in1, w_in0_both, w_in1_both, w_out, w_out_both)
    far_send, far_keep = project_call(near_rows, weights, None)
    far_sent = send_far(far_send)
    return project_call(own_rows, weights, (far_keep, far_sent))


def send_far(sums):
    pairs = []
    for p in range(2 * LINE):
        for h in range(LINE):
            if h % 2 != (p // 2) % 2:
                pairs.append((p * LINE + h, p * LINE + (h ^ 2)))
    return lax.ppermute(sums, ("pass", "head"), pairs)


MESH = pl.DeviceIdType.MESH


def at_home():
    return lax.axis_index("head") % 2 == lax.axis_index("pass") // 2 % 2


def project_kernel(pieces, far, *refs):
    rows_refs = refs[:pieces]
    own_ref, across_ref, *line_refs = refs[pieces : pieces + 8]
    refs = refs[pieces + 8 :]
    if far:
        send_ref, keep_ref = refs[:2]
    else:
        far_keep_ref, far_sent_ref, out_ref = refs[:3]
        refs = refs[1:]
    context_ref, w_ref, part_ref, core_ref, row_sem, w_sem, send_sem, recv_sem = refs[2:10]
    me, head = lax.axis_index("pass"), lax.axis_index("head")
    z, x, y = me // 2, me % 2, head // 2
    wide = w_ref.shape[3]
    inner = is_inner()
    core_peer, y_peer, z_peer = (me, head ^ 1), (me, head ^ 2), (me ^ 2, head ^ 1)
    home = at_home()
    sums = jnp.logical_not(home) if far else home

    row_loads = [
        pltpu.make_async_copy(ref, context_ref.at[pl.ds(i * LQ, LQ)], row_sem.at[i])
        for i, ref in enumerate(rows_refs)
    ]
    for load in row_loads:
        load.start()

    def load_here():
        pltpu.make_async_copy(own_ref, w_ref.at[0, x], w_sem.at[0, x]).start()
        pltpu.make_async_copy(across_ref, w_ref.at[0, 1 - x], w_sem.at[0, 1 - x]).start()

    def load_there():
        @pl.when(inner)
        def _():
            for side, low, high in ((x, 0, 1), (1 - x, 2, 3)):
                half = line_refs[low].shape[0]
                for at, ref in ((0, line_refs[low]), (half, line_refs[high])):
                    block = w_ref.at[1, side, pl.ds(at, half)]
                    pltpu.make_async_copy(ref, block, w_sem.at[1, side]).start()

        @pl.when(jnp.logical_not(inner))
        def _():
            for side, ref in ((x, line_refs[4]), (1 - x, line_refs[5])):
                pltpu.make_async_copy(ref, w_ref.at[1, side], w_sem.at[1, side]).start()

    here_first = y != z // 2

    @pl.when(here_first)
    def _():
        load_here()
        load_there()

    @pl.when(jnp.logical_not(here_first))
    def _():
        load_there()
        load_here()

    barrier = pltpu.get_barrier_semaphore()
    peers = (core_peer,) if far else (core_peer, y_peer, z_peer)
    for peer in peers:
        pl.semaphore_signal(barrier, inc=1, device_id=peer, device_id_type=MESH)
    pl.semaphore_wait(barrier, len(peers))

    def remote(src, dst, i, peer):
        return pltpu.make_async_remote_copy(
            src_ref=src,
            dst_ref=dst,
            send_sem=send_sem.at[i],
            recv_sem=recv_sem.at[i],
            device_id=peer,
            device_id_type=MESH,
        )

    chunks = part_ref.shape[1]
    step = part_ref.shape[3]

    def columns(j):
        return pl.ds(j * step, step)

    core_copies = [
        [remote(part_ref.at[s, j], core_ref.at[s, j], s * chunks + j, core_peer) for j in range(chunks)]
        for s in range(2)
    ]
    if not far:
        y_ref, ysend_ref, zsend_ref = refs[10:]
        y_copies = [
            remote(ysend_ref.at[j], y_ref.at[j], 2 * chunks + j, y_peer) for j in range(chunks)
        ]
        z_copies = [
            remote(zsend_ref.at[j], out_ref.at[:, columns(j)], 3 * chunks + j, z_peer)
            for j in range(chunks)
        ]

        @pl.when(jnp.logical_not(home))
        def _():
            for j in range(chunks):
                zsend_ref[j] = (
                    far_keep_ref[j].astype(jnp.float32) + far_sent_ref[j].astype(jnp.float32)
                ).astype(zsend_ref.dtype)
                z_copies[j].start()

    for load in row_loads:
        load.wait()

    def multiply(s, to_y, j):
        here = jnp.where(to_y == z // 2, 0, 1)
        side, at = j * step // wide, j * step % wide
        if at == 0:
            block = w_ref.at[here, side]
            pltpu.make_async_copy(block, block, w_sem.at[here, side]).wait()
        part_ref[s, j] = jnp.dot(
            context_ref[...],
            w_ref[here, side, :, pl.ds(at, step)],
            preferred_element_type=jnp.float32,
        ).astype(part_ref.dtype)

        @pl.when(jnp.logical_not(sums))
        def _():
            core_copies[s][j].start()

    def add_up(s, j):
        @pl.when(sums)
        def _():
            core_copies[s][j].wait_recv()
            value = part_ref[s, j].astype(jnp.float32) + core_ref[s, j].astype(jnp.float32)
            if far:
                target = keep_ref if s else send_ref
                target[j] = value.astype(target.dtype)
            elif s == 0:
                ysend_ref[j] = value.astype(ysend_ref.dtype)
                y_copies[j].start()
            else:
                y_copies[j].wait_recv()
                out_ref[:, columns(j)] = (value + y_ref[j].astype(jnp.float32)).astype(
                    out_ref.dtype
                )

    late = None
    for s, to_y in enumerate((1 - y, y)):
        for j in range(chunks):
            multiply(s, to_y, j)
            if late is not None:
                add_up(*late)
            late = (s, j)
    add_up(*late)

    @pl.when(jnp.logical_not(sums))
    def _():
        for copies in core_copies:
            for copy in copies:
                copy.wait_send()

    if not far:

        @pl.when(home)
        def _():
            for copy in y_copies:
                copy.wait_send()

        @pl.when(jnp.logical_not(home))
        def _():
            for copy in z_copies:
                copy.wait()


def project_call(pieces, weights, far_sums):
    own = weights[0]
    rows, (depth, wide) = len(pieces) * LQ, own.shape
    dtype = own.dtype
    far = far_sums is None
    vmem = pl.BlockSpec(memory_space=pltpu.VMEM)
    step = math.gcd(wide, 256)
    chunks = 2 * wide // step
    blocks = (chunks, rows, step)
    scratch = [
        pltpu.VMEM((rows, depth), dtype),
        pltpu.VMEM((2, 2, depth, wide), dtype),
        pltpu.VMEM((2,) + blocks, dtype),
        pltpu.VMEM((2,) + blocks, dtype),
        pltpu.SemaphoreType.DMA((len(pieces),)),
        pltpu.SemaphoreType.DMA((2, 2)),
        pltpu.SemaphoreType.DMA((4 * chunks,)),
        pltpu.SemaphoreType.DMA((4 * chunks,)),
    ]
    if far:
        out_shape = [jax.ShapeDtypeStruct(blocks, dtype)] * 2
        out_specs = [vmem] * 2
    else:
        out_shape = jax.ShapeDtypeStruct((rows, 2 * wide), dtype)
        out_specs = vmem
        scratch += [pltpu.VMEM(blocks, dtype)] * 3
    return pl.pallas_call(
        functools.partial(project_kernel, len(pieces), far),
        out_shape=out_shape,
        in_specs=[pl.BlockSpec(memory_space=pl.ANY)] * (len(pieces) + len(weights))
        + [vmem] * (0 if far else 2),
        out_specs=out_specs,
        scratch_shapes=scratch,
        compiler_params=pltpu.CompilerParams(
            collective_id=int(far), has_side_effects=True, vmem_limit_bytes=VMEM_BYTES
        ),
        name="project_far" if far else "project_home",
        cost_estimate=pl.CostEstimate(
            flops=2 * 4 * rows * depth * wide,
            bytes_accessed=4 * depth * wide * 2,
            transcendentals=0,
        ),
    )(*pieces, *weights, *(far_sums or ()))


def suits_line(mesh, queries, lists):
    passes, heads = mesh.shape["pass"], mesh.shape["head"]
    entries = queries.shape[0] // LQ // passes * lists.shape[1]
    return passes == 2 * LINE and heads == LINE and entries % passes == 0


def solution(mesh):
    in_specs = (
        P("pass", "head"),
        P("pass", "head", None),
        P("pass", None, "head", None),
        P("head", "pass"),
        P(),
        P(),
        P(),
    )
    out_specs = P("pass", "head")

    def run(*args):
        if not suits_line(mesh, args[0], args[4]):
            return jax.shard_map(
                body, mesh=mesh, in_specs=in_specs, out_specs=out_specs, check_vma=False
            )(*args)
        step = jax.shard_map(
            line_steps, mesh=mesh, in_specs=in_specs, out_specs=out_specs, check_vma=False
        )
        return step(*args)

    return run
```

```python
import functools
import math

import jax
import jax.numpy as jnp
from jax import lax
from jax.experimental import pallas as pl
from jax.experimental.pallas import tpu as pltpu
from jax.sharding import PartitionSpec as P


H = 64
KVH = 8
HD = 128
LQ = 128
GROUP = H // KVH
COEF = HD ** (-0.5) * math.log2(math.e)
NEG = -1e30
ROWS = 256


def round_of(a, b, n):
    if n & (n - 1) == 0:
        return a ^ b
    return lax.rem(b - a + n, n)


def pairs_of(k, n):
    if n & (n - 1) == 0:
        return [(p, p ^ k) for p in range(n)]
    return [(p, (p + k) % n) for p in range(n)]


def order_of(n):
    rest = range(1, n)
    return sorted(rest, key=lambda k: (bin(k).count("1"), k))


def gather_kernel(n, most, per_device, order, lists_ref, pslot_ref, qslot_ref, cache_ref, *refs):
    recv_ref, own_row_ref = refs[0], refs[1]
    outs = refs[2 : 2 + len(order)]
    send_row, send_cnt, recv_cnt, buf, in_sem, out_sem = refs[2 + len(order) :]
    me = lax.axis_index("pass")
    pass_dev = cache_ref.shape[0]
    topp, nq = lists_ref.shape
    for k in range(n):
        send_cnt[k] = 0
        recv_cnt[k] = 0
    for i in range(n * most):
        recv_ref[i] = -1
        send_row[i] = 0

    def question(q, carry):
        slot = qslot_ref[q]
        dest = slot // per_device
        local = slot - dest * per_device
        k_send = round_of(me, dest, n)
        for t in range(topp):
            row = pslot_ref[lists_ref[t, q]]
            owner = row // pass_dev

            @pl.when(owner == me)
            def _():
                count = send_cnt[k_send]
                send_row[k_send * most + count] = row - owner * pass_dev
                send_cnt[k_send] = count + 1

            @pl.when(dest == me)
            def _():
                k = round_of(owner, me, n)
                count = recv_cnt[k]
                recv_ref[k * most + count] = local
                recv_cnt[k] = count + 1

        return carry

    lax.fori_loop(0, nq, question, 0)
    for r in range(most):
        own_row_ref[r] = send_row[r]
    copies = []
    for j, k in enumerate(order):
        for r in range(most):
            i = j * most + r
            get = pltpu.make_async_copy(
                cache_ref.at[send_row[k * most + r]], buf.at[i], in_sem.at[i]
            )
            get.start()
            copies.append((get, pltpu.make_async_copy(buf.at[i], outs[j].at[r], out_sem.at[i])))
    for get, put in copies:
        get.wait()
        put.start()
    for get, put in copies:
        put.wait()


def gather(lists, passage_slot, question_slot, cache, n, most, per_device, order):
    item = cache.shape[1:]
    slots = (n - 1) * most
    smem = pl.BlockSpec(memory_space=pltpu.SMEM)
    anyspace = pl.BlockSpec(memory_space=pl.ANY)
    return pl.pallas_call(
        functools.partial(gather_kernel, n, most, per_device, order),
        out_shape=[
            jax.ShapeDtypeStruct((n * most,), jnp.int32),
            jax.ShapeDtypeStruct((most,), jnp.int32),
        ]
        + [jax.ShapeDtypeStruct((most,) + item, cache.dtype)] * len(order),
        in_specs=[smem, smem, smem, anyspace],
        out_specs=[smem, smem] + [anyspace] * len(order),
        scratch_shapes=[
            pltpu.SMEM((n * most,), jnp.int32),
            pltpu.SMEM((n,), jnp.int32),
            pltpu.SMEM((n,), jnp.int32),
            pltpu.VMEM((slots,) + item, cache.dtype),
            pltpu.SemaphoreType.DMA((slots,)),
            pltpu.SemaphoreType.DMA((slots,)),
        ],
        name="gather_items",
        cost_estimate=pl.CostEstimate(
            flops=0, bytes_accessed=2 * slots * math.prod(item) * 2, transcendentals=0
        ),
    )(lists.T, passage_slot, question_slot, cache)


def block_step(q_ref, m_ref, l_ref, acc_ref, question, head, keys, values, causal):
    rows = q_ref.shape[2]
    step = min(ROWS, rows)
    width = keys.shape[0]
    ones = jnp.ones(values.shape, values.dtype)
    extended = jnp.concatenate([values, ones], axis=1)
    for start in range(0, rows, step):
        part = pl.ds(start, step)
        q = q_ref[question, head, part, :]
        scores = (
            lax.dot_general(q, keys, (((1,), (1,)), ((), ())), preferred_element_type=jnp.float32)
            * COEF
        )
        if causal:
            token = lax.broadcasted_iota(jnp.int32, scores.shape, 0) % LQ
            column = lax.broadcasted_iota(jnp.int32, scores.shape, 1)
            scores = jnp.where(column <= token, scores, NEG)
        old = m_ref[question, head, part, :]
        new = jnp.maximum(old, jnp.max(scores, axis=1, keepdims=True))
        weights = jnp.exp2(scores - jnp.concatenate([new] * (width // HD), axis=1))
        mixed = jnp.dot(
            weights.astype(jnp.bfloat16), extended, preferred_element_type=jnp.float32
        )
        alpha = jnp.exp2(old - new)
        m_ref[question, head, part, :] = new
        l_ref[question, head, part, :] = l_ref[question, head, part, :] * alpha + mixed[:, HD:]
        acc_ref[question, head, part, :] = (
            acc_ref[question, head, part, :] * alpha + mixed[:, :HD]
        )


def attend_kernel(first, last, rounds, most, *refs):
    refs = list(refs)
    recv_ref, q_ref = refs.pop(0), refs.pop(0)
    if first:
        row_ref, own_ref, cache_ref = refs.pop(0), refs.pop(0), refs.pop(0)
        sources = None
        entries = most
    else:
        state_in = [refs.pop(0) for _ in range(3)]
        sources = [refs.pop(0) for _ in rounds]
        entries = len(rounds) * most
    if last:
        out_ref = refs.pop(0)
        m_ref, l_ref, acc_ref = [refs.pop(0) for _ in range(3)]
    else:
        m_ref, l_ref, acc_ref = [refs.pop(0) for _ in range(3)]
    buf, sem = refs
    per_device, heads = q_ref.shape[0], q_ref.shape[1]

    def fetch(i, slot):
        if first:
            pltpu.make_async_copy(cache_ref.at[row_ref[i]], buf.at[slot], sem.at[slot]).start()
            return
        for j in range(len(rounds)):

            @pl.when(i // most == j)
            def _():
                pltpu.make_async_copy(
                    sources[j].at[i - j * most], buf.at[slot], sem.at[slot]
                ).start()

    def tag_of(i):
        if first:
            return recv_ref[i]
        k = jnp.int32(0)
        for j, value in enumerate(rounds):
            k = jnp.where(i // most == j, value, k)
        return recv_ref[k * most + lax.rem(i, most)]

    fetch(jnp.int32(0), 0)
    if first:
        m_ref[...] = jnp.full(m_ref.shape, NEG, jnp.float32)
        l_ref[...] = jnp.zeros(l_ref.shape, jnp.float32)
        acc_ref[...] = jnp.zeros(acc_ref.shape, jnp.float32)

        def own_block(question, carry):
            for head in range(heads):
                block = own_ref[question, head]
                block_step(
                    q_ref, m_ref, l_ref, acc_ref, question, head, block[:, :HD], block[:, HD:], True
                )
            return carry

        lax.fori_loop(0, per_device, own_block, 0)
    else:
        m_ref[...] = state_in[0][...]
        l_ref[...] = state_in[1][...]
        acc_ref[...] = state_in[2][...]

    def item(i, carry):
        slot = lax.rem(i, 2)
        pltpu.make_async_copy(buf.at[slot], buf.at[slot], sem.at[slot]).wait()

        @pl.when(i + 1 < entries)
        def _():
            fetch(i + 1, lax.rem(i + 1, 2))

        tag = tag_of(i)

        @pl.when(tag >= 0)
        def _():
            for head in range(heads):
                block_step(
                    q_ref,
                    m_ref,
                    l_ref,
                    acc_ref,
                    tag,
                    head,
                    buf[slot, head, :, :HD],
                    buf[slot, head, :, HD:],
                    False,
                )

        return carry

    lax.fori_loop(0, entries, item, 0)
    if last:
        for question in range(per_device):
            for head in range(heads):
                for g in range(GROUP):
                    part = pl.ds(g * LQ, LQ)
                    column = (head * GROUP + g) * HD
                    out_ref[pl.ds(question * LQ, LQ), pl.ds(column, HD)] = (
                        acc_ref[question, head, part, :] / l_ref[question, head, part, :]
                    ).astype(out_ref.dtype)


def attend_call(first, last, rounds, most, recv, q, rest, item):
    per_device, heads, rows, _ = q.shape
    state = jax.ShapeDtypeStruct(q.shape, jnp.float32)
    smem = pl.BlockSpec(memory_space=pltpu.SMEM)
    vmem = pl.BlockSpec(memory_space=pltpu.VMEM)
    anyspace = pl.BlockSpec(memory_space=pl.ANY)
    if first:
        in_specs = [smem, vmem, smem, vmem, anyspace]
        entries = most
    else:
        in_specs = [smem, vmem] + [vmem] * 3 + [anyspace] * len(rounds)
        entries = most * len(rounds)
    scratch = [pltpu.VMEM((2,) + item, q.dtype), pltpu.SemaphoreType.DMA((2,))]
    if last:
        out_shape = jax.ShapeDtypeStruct((per_device * LQ, heads * GROUP * HD), q.dtype)
        out_specs = vmem
        scratch = [pltpu.VMEM(q.shape, jnp.float32)] * 3 + scratch
    else:
        out_shape = [state] * 3
        out_specs = [vmem] * 3
    weights = entries * heads * rows * item[1]
    return pl.pallas_call(
        functools.partial(attend_kernel, first, last, rounds, most),
        out_shape=out_shape,
        in_specs=in_specs,
        out_specs=out_specs,
        scratch_shapes=scratch,
        name="attend_first" if first else ("attend_last" if last else "attend_more"),
        cost_estimate=pl.CostEstimate(
            flops=weights * HD * 4,
            bytes_accessed=entries * math.prod(item) * 2,
            transcendentals=weights,
        ),
    )(recv, q, *rest)


def weight_blocks(own, n):
    if n & (n - 1):
        return [lax.all_gather(own, "pass", axis=1, tiled=True)]
    have = {0: own}
    bit = n // 2
    while bit:
        for k in list(have):
            have[k ^ bit] = lax.ppermute(have[k], "pass", pairs_of(bit, n))
        bit //= 2
    return [have[k] for k in range(n)]


def project(context, weights):
    parts = [
        jnp.dot(context, weight, preferred_element_type=jnp.float32).astype(jnp.bfloat16)
        for weight in weights
    ]
    me = lax.axis_index("pass")
    bit = len(parts) // 2
    while bit:
        swap = (me & bit) != 0
        parts = [jnp.where(swap, parts[k ^ bit], parts[k]) for k in range(len(parts))]
        bit //= 2
    return jnp.concatenate(parts, axis=1)


def body(queries, own_kv, passage_cache, out_weight, lists, passage_slot, question_slot):
    n = lax.axis_size("pass")
    per_device = queries.shape[0] // LQ
    heads = own_kv.shape[1]
    entries = per_device * lists.shape[1]
    most = (entries + n - 1) // n
    order = order_of(n)
    cache = jnp.transpose(passage_cache, (0, 2, 1, 3))
    recv, own_row, *items = gather(
        lists, passage_slot, question_slot, cache, n, most, per_device, order
    )
    arrived = [
        lax.ppermute(item, "pass", pairs_of(k, n)) for k, item in zip(order, items)
    ]
    weights = weight_blocks(out_weight, n)
    q = (
        queries.reshape(per_device, LQ, heads, GROUP, HD)
        .transpose(0, 2, 3, 1, 4)
        .reshape(per_device, heads, GROUP * LQ, HD)
    )
    own = own_kv.reshape(per_device, LQ, heads, 2 * HD).transpose(0, 2, 1, 3)
    item = cache.shape[1:]
    state = attend_call(True, False, (0,), most, recv, q, (own_row, own, cache), item)
    calls = 3
    bounds = [len(order) * i // calls for i in range(calls + 1)]
    for i in range(calls):
        rounds = tuple(order[bounds[i] : bounds[i + 1]])
        rest = tuple(state) + tuple(arrived[bounds[i] : bounds[i + 1]])
        state = attend_call(False, i == calls - 1, rounds, most, recv, q, rest, item)
    context = state
    return lax.psum_scatter(project(context, weights), "head", scatter_dimension=1, tiled=True)


LINE = 4
EXTRA = 8
ITEM_ORDER = (2, 0, 3, 1)
VMEM_BYTES = 67043328


def mirror(k, ends=None):
    pairs = [(p, p ^ int(2 * k)) for p in range(2 * LINE)]
    if ends is None:
        return pairs
    return [(p, d) for p, d in pairs if (p // 2 in (0, LINE - 1)) == (ends == "outer")]


def is_inner():
    z = lax.axis_index("pass") // 2
    return jnp.logical_and(z > 0, z < LINE - 1)


def sort_kernel(most, per_device, lists_ref, pslot_ref, qslot_ref, cache_ref, *refs):
    row_ref, tag_ref, far_tag_ref = refs[:3]
    outs = refs[3 : 3 + LINE]
    send_row, near_cnt, send_cnt, far_cnt, buf, in_sem, out_sem = refs[3 + LINE :]
    me = lax.axis_index("pass")
    z, x = me // 2, me % 2
    pass_dev = cache_ref.shape[0]
    topp, nq = lists_ref.shape
    for k in range(LINE):
        near_cnt[k] = 0
        send_cnt[k] = 0
        far_cnt[k] = 0

    def take(i):
        return pltpu.make_async_copy(cache_ref.at[send_row[i]], buf.at[i], in_sem.at[i])

    def question(q, carry):
        slot = qslot_ref[q]
        dest = slot // per_device
        local = slot - dest * per_device
        k = (dest // 2) ^ z

        @pl.when(dest % 2 == x)
        def _():
            for t in range(topp):
                row = pslot_ref[lists_ref[t, q]]
                owner = row // pass_dev

                @pl.when(owner == me)
                def _():
                    at = k * most + near_cnt[k]
                    row_ref[at] = row - owner * pass_dev
                    tag_ref[at] = local
                    near_cnt[k] = near_cnt[k] + 1

                @pl.when(owner == (me ^ 1))
                def _():
                    far_tag_ref[k * most + far_cnt[k]] = local
                    far_cnt[k] = far_cnt[k] + 1

        @pl.when(dest % 2 != x)
        def _():
            for t in range(topp):
                row = pslot_ref[lists_ref[t, q]]
                owner = row // pass_dev

                @pl.when(owner == me)
                def _():
                    at = k * most + send_cnt[k]
                    send_row[at] = row - owner * pass_dev
                    send_cnt[k] = send_cnt[k] + 1
                    take(at).start()

        return carry

    lax.fori_loop(0, nq, question, 0)
    slots = [k * most + r for k in ITEM_ORDER for r in range(most)]
    puts = [pltpu.make_async_copy(buf.at[i], outs[i // most].at[i % most], out_sem.at[i]) for i in slots]
    for i, put in zip(slots, puts):
        take(i).wait()
        put.start()
    for put in puts:
        put.wait()


def sort_items(lists, passage_slot, question_slot, cache, most, per_device):
    item = cache.shape[1:]
    slots = LINE * most
    smem = pl.BlockSpec(memory_space=pltpu.SMEM)
    anyspace = pl.BlockSpec(memory_space=pl.ANY)
    return pl.pallas_call(
        functools.partial(sort_kernel, most, per_device),
        out_shape=[jax.ShapeDtypeStruct((slots,), jnp.int32)] * 3
        + [jax.ShapeDtypeStruct((most,) + item, cache.dtype)] * LINE,
        in_specs=[smem, smem, smem, anyspace],
        out_specs=[smem] * 3 + [anyspace] * LINE,
        scratch_shapes=[
            pltpu.SMEM((slots,), jnp.int32),
            pltpu.SMEM((LINE,), jnp.int32),
            pltpu.SMEM((LINE,), jnp.int32),
            pltpu.SMEM((LINE,), jnp.int32),
            pltpu.VMEM((slots,) + item, cache.dtype),
            pltpu.SemaphoreType.DMA((slots,)),
            pltpu.SemaphoreType.DMA((slots,)),
        ],
        compiler_params=pltpu.CompilerParams(vmem_limit_bytes=VMEM_BYTES),
        name="sort_items",
        cost_estimate=pl.CostEstimate(
            flops=0, bytes_accessed=2 * slots * math.prod(item) * 2, transcendentals=0
        ),
    )(lists.T, passage_slot, question_slot, cache)


def unit():
    r = lax.broadcasted_iota(jnp.int32, (LQ, LQ), 0)
    c = lax.broadcasted_iota(jnp.int32, (LQ, LQ), 1)
    return r == c


def part_step(q_ref, m_ref, l_ref, acc_ref, question, head, keys, values, causal):
    rows = GROUP * LQ
    width = keys.shape[0]
    ones = jnp.ones(values.shape, values.dtype)
    extended = jnp.concatenate([values, ones], axis=1)
    tokens = pl.ds(pl.multiple_of(question * LQ, LQ), LQ)
    for start in range(0, rows, ROWS):
        part = pl.ds(start, ROWS)
        q = jnp.concatenate(
            [
                q_ref[tokens, pl.ds(pl.multiple_of((head * GROUP + g) * HD, HD), HD)]
                for g in range(start // LQ, (start + ROWS) // LQ)
            ],
            axis=0,
        )
        scores = (
            lax.dot_general(q, keys, (((1,), (1,)), ((), ())), preferred_element_type=jnp.float32)
            * COEF
        )
        if causal:
            token = lax.broadcasted_iota(jnp.int32, scores.shape, 0) % LQ
            column = lax.broadcasted_iota(jnp.int32, scores.shape, 1)
            scores = jnp.where(column <= token, scores, NEG)
        old = m_ref[question, head, part, :]
        new = jnp.maximum(old, jnp.max(scores, axis=1, keepdims=True))
        weights = jnp.exp2(scores - jnp.concatenate([new] * (width // HD), axis=1))
        mixed = jnp.dot(
            weights.astype(jnp.bfloat16), extended, preferred_element_type=jnp.float32
        )
        alpha = jnp.exp2(old - new)
        m_ref[question, head, part, :] = new
        l_ref[question, head, part, :] = l_ref[question, head, part, :] * alpha + mixed[:, HD:]
        acc_ref[question, head, part, :] = (
            acc_ref[question, head, part, :] * alpha + mixed[:, :HD]
        )


def part_kernel(k, most, first, last, heads, *refs):
    refs = list(refs)
    row_ref, tag_ref, far_tag_ref = refs.pop(0), refs.pop(0), refs.pop(0)
    own_ref = refs.pop(0) if k == 0 else None
    questions = [refs.pop(0) for _ in range(2 if k > 1 else 1)]
    cache_ref = refs.pop(0)
    items_ref = refs.pop(0) if last > most else None
    out_ref, q_ref, m_ref, l_ref, acc_ref, buf, sem, q_sem = refs
    per_device = q_ref.shape[0] // LQ

    def fetch(i, slot):
        if first < most:

            @pl.when(i < most)
            def _():
                row = row_ref[k * most + jnp.minimum(i, most - 1)]
                pltpu.make_async_copy(cache_ref.at[row], buf.at[slot], sem.at[slot]).start()

        if last > most:

            @pl.when(i >= most)
            def _():
                pltpu.make_async_copy(
                    items_ref.at[jnp.maximum(i - most, 0)], buf.at[slot], sem.at[slot]
                ).start()

    if len(questions) == 1:
        pltpu.make_async_copy(questions[0], q_ref, q_sem).start()
    else:
        inner = is_inner()

        @pl.when(inner)
        def _():
            pltpu.make_async_copy(questions[0], q_ref, q_sem).start()

        @pl.when(jnp.logical_not(inner))
        def _():
            pltpu.make_async_copy(questions[1], q_ref, q_sem).start()

    fetch(jnp.int32(first), first % 2)
    m_ref[...] = jnp.full(m_ref.shape, NEG, jnp.float32)
    l_ref[...] = jnp.zeros(l_ref.shape, jnp.float32)
    acc_ref[...] = jnp.zeros(acc_ref.shape, jnp.float32)
    pltpu.make_async_copy(q_ref, q_ref, q_sem).wait()
    if k == 0:

        def own_block(i, carry):
            question, head = i // heads, lax.rem(i, heads)
            part_step(
                q_ref,
                m_ref,
                l_ref,
                acc_ref,
                question,
                head,
                own_ref[question, head, :, :HD],
                own_ref[question, head, :, HD:],
                True,
            )
            return carry

        lax.fori_loop(0, per_device * heads, own_block, 0)

    def item(i, carry):
        slot = lax.rem(i, 2)
        pltpu.make_async_copy(buf.at[slot], buf.at[slot], sem.at[slot]).wait()

        @pl.when(i + 1 < last)
        def _():
            fetch(i + 1, lax.rem(i + 1, 2))

        at = k * most + lax.rem(i, most)
        tag = jnp.where(i < most, tag_ref[at], far_tag_ref[at])

        for head in range(heads):
            part_step(
                q_ref,
                m_ref,
                l_ref,
                acc_ref,
                tag,
                head,
                buf[slot, head, :, :HD],
                buf[slot, head, :, HD:],
                False,
            )
        return carry

    lax.fori_loop(first, last, item, 0)
    eye = unit()

    def close(c, carry):
        head, g = c // GROUP, lax.rem(c, GROUP)
        columns = pl.ds(pl.multiple_of(c * HD, HD), HD)
        part = pl.ds(pl.multiple_of(g * LQ, LQ), LQ)
        for question in range(per_device):
            total = l_ref[question, head, part, :]
            some = total > 0.0
            safe = jnp.where(some, total, 1.0)
            out_ref[question, :LQ, columns] = (
                acc_ref[question, head, part, :] / safe
            ).astype(out_ref.dtype)
            level = jnp.where(some, m_ref[question, head, part, :] + jnp.log2(safe), NEG)
            line = jnp.sum(jnp.where(eye, level, 0.0), axis=0, keepdims=True)
            store_level(out_ref, question, columns, line)
        return carry

    lax.fori_loop(0, heads * GROUP, close, 0)


def store_level(out_ref, question, columns, line):
    row_of = lax.broadcasted_iota(jnp.int32, (EXTRA, line.shape[1]), 0)
    high = line.astype(jnp.bfloat16).astype(jnp.float32)
    both = jnp.where(row_of == 0, high, jnp.where(row_of == 1, line - high, 0.0))
    out_ref[question, LQ:, columns] = both.astype(out_ref.dtype)


def part_call(k, most, tables, own, questions, cache, items, local=True):
    tokens, columns = questions[0].shape
    heads, item = cache.shape[1], cache.shape[1:]
    state = (tokens // LQ, heads, GROUP * LQ, HD)
    smem = pl.BlockSpec(memory_space=pltpu.SMEM)
    vmem = pl.BlockSpec(memory_space=pltpu.VMEM)
    anyspace = pl.BlockSpec(memory_space=pl.ANY)
    owned = [own] if k == 0 else []
    received = [items] if items is not None else []
    first, last = 0 if local else most, 2 * most if received else most
    weights = (last - first) * heads * GROUP * LQ * item[1]
    return pl.pallas_call(
        functools.partial(part_kernel, k, most, first, last, heads),
        out_shape=jax.ShapeDtypeStruct((tokens // LQ, LQ + EXTRA, columns), cache.dtype),
        in_specs=[smem] * 3
        + [vmem] * len(owned)
        + [anyspace] * (len(questions) + 1 + len(received)),
        out_specs=vmem,
        scratch_shapes=[
            pltpu.VMEM((tokens, columns), cache.dtype),
            pltpu.VMEM(state, jnp.float32),
            pltpu.VMEM(state, jnp.float32),
            pltpu.VMEM(state, jnp.float32),
            pltpu.VMEM((2,) + item, cache.dtype),
            pltpu.SemaphoreType.DMA((2,)),
            pltpu.SemaphoreType.DMA,
        ],
        compiler_params=pltpu.CompilerParams(vmem_limit_bytes=VMEM_BYTES),
        cost_estimate=pl.CostEstimate(
            flops=weights * HD * 4,
            bytes_accessed=(last - first) * math.prod(item) * 2,
            transcendentals=weights,
        ),
    )(*tables, *owned, *questions, cache, *received)


def blend(refs, out_ref, leveled):
    eye = unit()
    ones = jnp.ones((2 * LQ, LQ), jnp.bfloat16)

    def level_of(ref):
        both = ref[0, LQ:, :].astype(jnp.float32)
        return both[:1] + both[1:2]

    levels = [level_of(ref) for ref in refs]
    top = functools.reduce(jnp.maximum, levels)
    weights = [jnp.exp2(level - top) for level in levels]
    total = functools.reduce(jnp.add, weights)
    shares = []
    for weight in weights[1:]:
        share = weight / total
        high = share.astype(jnp.bfloat16).astype(jnp.float32)
        shares.append((high, share - high))
    for c in range(total.shape[1] // HD):
        columns = slice(c * HD, (c + 1) * HD)
        base = refs[0][0, :LQ, columns].astype(jnp.float32)
        value = base
        for ref, pair in zip(refs[1:], shares):
            spread = jnp.concatenate(
                [
                    jnp.where(eye, jnp.broadcast_to(v[:, columns], (LQ, LQ)), 0.0).astype(
                        jnp.bfloat16
                    )
                    for v in pair
                ],
                axis=1,
            )
            column = jnp.dot(spread, ones, preferred_element_type=jnp.float32)
            value = value + (ref[0, :LQ, columns].astype(jnp.float32) - base) * column
        value = value.astype(out_ref.dtype)
        if leveled:
            out_ref[0, :LQ, columns] = value
        else:
            out_ref[:, columns] = value
    if leveled:
        store_level(out_ref, 0, slice(None), top + jnp.log2(total))


def merge_kernel(*refs):
    *parts, out_ref = refs
    inner = is_inner()

    @pl.when(inner)
    def _():
        blend(parts, out_ref, True)

    @pl.when(jnp.logical_not(inner))
    def _():
        if len(parts) > 2:
            blend(parts[:-1], out_ref, True)
        else:
            out_ref[...] = parts[0][...]


def finish_kernel(a_ref, b_ref, out_ref):
    blend((a_ref, b_ref), out_ref, False)


def question_spec(value, at):
    shape = (1,) + value.shape[1:]
    if value.shape[0] == 1:
        return pl.BlockSpec(shape, lambda q: (0, 0, 0))
    return pl.BlockSpec(shape, lambda q: (at, 0, 0))


def join_call(parts, at, leveled):
    columns = parts[0].shape[2]
    if leveled:
        shape = (1,) + parts[0].shape[1:]
        out_spec = pl.BlockSpec(shape, lambda q: (0, 0, 0))
    else:
        shape = (LQ, columns)
        out_spec = pl.BlockSpec(shape, lambda q: (0, 0))
    size = LQ * columns
    return pl.pallas_call(
        merge_kernel if leveled else finish_kernel,
        out_shape=jax.ShapeDtypeStruct(shape, parts[0].dtype),
        grid=(1,),
        in_specs=[question_spec(part, at) for part in parts],
        out_specs=out_spec,
        compiler_params=pltpu.CompilerParams(vmem_limit_bytes=VMEM_BYTES),
        cost_estimate=pl.CostEstimate(flops=size * 8, bytes_accessed=size * 6, transcendentals=0),
    )(*parts)


def line_steps(queries, own_kv, passage_cache, out_weight, lists, passage_slot, question_slot):
    per_device = queries.shape[0] // LQ
    heads = own_kv.shape[1]
    most = per_device * lists.shape[1] // (2 * LINE)

    def send(value, pairs):
        return lax.ppermute(value, "pass", pairs)

    def part(k, *args, local=True):
        return part_call(k, most, tables, own if k == 0 else None, *args, local=local)

    def join(at, *parts, leveled=True):
        return join_call(parts, at, leveled)

    across = [(p, p ^ 1) for p in range(2 * LINE)]
    inner_across = [(p, d) for p, d in across if p // 2 in (1, 2)]
    outer_across = [(p, d) for p, d in across if p // 2 not in (1, 2)]
    near, middle = mirror(1), mirror(3, "inner")
    inward, outward = mirror(1, "outer"), mirror(1, "inner")
    q_near = send(queries, near)
    q_mid = send(queries, middle)
    half = out_weight.shape[0] // 2
    w_across0 = send(out_weight[:half], across)
    cache = jnp.transpose(passage_cache, (0, 2, 1, 3))
    row, tag, far_tag, *items = sort_items(
        lists, passage_slot, question_slot, cache, most, per_device
    )
    tables = (row, tag, far_tag)
    later, _ = lax.optimization_barrier((out_weight, row))
    w_across1 = send(later[half:], across)
    q_out = send(q_mid, outward)
    q_cross = send(q_near, middle)
    q_end = send(q_cross, outward)
    far = [send(items[k], across) for k in range(LINE)]
    own = own_kv.reshape(per_device, LQ, heads, 2 * HD).transpose(0, 2, 1, 3)
    part2 = part(2, [q_cross, q_out], cache, far[2])
    part3 = part(3, [q_mid, q_end], cache, far[3])
    part0 = part(0, [queries], cache, far[0])
    part1 = part(1, [q_near], cache, None)
    part1_far = part(1, [q_near], cache, far[1], local=False)
    back2 = send(part2, inward)
    w_in = send(out_weight, mirror(2, "outer"))
    w_out = send(out_weight, mirror(2, "inner"))
    back3 = send(part3, inward)
    w_in_both = send(w_in, inner_across)
    w_out_both = send(w_out, outer_across)
    own_rows, near_rows = [], []
    for q in range(per_device):
        cross3 = send(join(q, part3, back2), middle)
        near0 = join(q, part0, cross3)
        beside = send(near0, near)
        cross2 = send(join(q, part2, back3), middle)
        near1 = join(q, part1, part1_far, cross2)
        back1 = send(near1, near)
        if q + 1 < per_device:
            near_rows.append(join(q, near1, beside, leveled=False))
            own_rows.append(join(q, near0, back1, leveled=False))
        else:
            near_rows += [near1, beside]
            own_rows += [near0, back1]
    weights = (out_weight, w_across0, w_across1, w_in, w_in_both, w_out, w_out_both)
    far_send, far_keep = project_call(near_rows, weights, None)
    far_sent = send_far(far_send)
    return project_call(own_rows, weights, (far_keep, far_sent))


def send_far(sums):
    pairs = []
    for p in range(2 * LINE):
        for h in range(LINE):
            if h % 2 != (p // 2) % 2:
                pairs.append((p * LINE + h, p * LINE + (h ^ 2)))
    return lax.ppermute(sums, ("pass", "head"), pairs)


MESH = pl.DeviceIdType.MESH


def at_home():
    return lax.axis_index("head") % 2 == lax.axis_index("pass") // 2 % 2


def project_kernel(pieces, far, *refs):
    rows_refs = refs[:pieces]
    own_ref, a0_ref, a1_ref, in_ref, in2_ref, out1_ref, out2_ref = refs[pieces : pieces + 7]
    refs = refs[pieces + 7 :]
    if far:
        send_ref, keep_ref = refs[:2]
    else:
        far_keep_ref, far_sent_ref, out_ref = refs[:3]
        refs = refs[1:]
    context_ref, w_ref, part_ref, core_ref, pair_ref, row_sem, w_sem, send_sem, recv_sem = refs[2:11]
    me, head = lax.axis_index("pass"), lax.axis_index("head")
    z, x, y = me // 2, me % 2, head // 2
    wide = w_ref.shape[3]
    inner = is_inner()
    core_peer, y_peer, z_peer = (me, head ^ 1), (me, head ^ 2), (me ^ 2, head ^ 1)
    home = at_home()
    sums = jnp.logical_not(home) if far else home

    done = pieces - 2
    row_loads = [
        pltpu.make_async_copy(ref, pair_ref.at[i], row_sem.at[done + i])
        for i, ref in enumerate(rows_refs[done:])
    ]
    row_loads += [
        pltpu.make_async_copy(ref, context_ref.at[pl.ds(i * LQ, LQ)], row_sem.at[i])
        for i, ref in enumerate(rows_refs[:done])
    ]
    for load in row_loads:
        load.start()

    def load_here():
        pltpu.make_async_copy(own_ref, w_ref.at[0, x], w_sem.at[0, x]).start()
        half = a0_ref.shape[0]
        low, high = w_ref.at[0, 1 - x, pl.ds(0, half)], w_ref.at[0, 1 - x, pl.ds(half, half)]
        pltpu.make_async_copy(a0_ref, low, w_sem.at[0, 1 - x]).start()
        pltpu.make_async_copy(a1_ref, high, w_sem.at[0, 1 - x]).start()

    def load_there():
        for which, (one, two) in (
            (inner, (in_ref, in2_ref)),
            (jnp.logical_not(inner), (out1_ref, out2_ref)),
        ):

            @pl.when(which)
            def _():
                pltpu.make_async_copy(one, w_ref.at[1, x], w_sem.at[1, x]).start()
                pltpu.make_async_copy(two, w_ref.at[1, 1 - x], w_sem.at[1, 1 - x]).start()

    here_first = y != z // 2

    @pl.when(here_first)
    def _():
        load_here()
        load_there()

    @pl.when(jnp.logical_not(here_first))
    def _():
        load_there()
        load_here()

    barrier = pltpu.get_barrier_semaphore()
    peers = (core_peer,) if far else (core_peer, y_peer, z_peer)
    for peer in peers:
        pl.semaphore_signal(barrier, inc=1, device_id=peer, device_id_type=MESH)
    pl.semaphore_wait(barrier, len(peers))

    def remote(src, dst, i, peer):
        return pltpu.make_async_remote_copy(
            src_ref=src,
            dst_ref=dst,
            send_sem=send_sem.at[i],
            recv_sem=recv_sem.at[i],
            device_id=peer,
            device_id_type=MESH,
        )

    def columns(j):
        return pl.ds(j * wide, wide)

    core_copies = [
        [remote(part_ref.at[s, j], core_ref.at[s, j], s * 2 + j, core_peer) for j in range(2)]
        for s in range(2)
    ]
    if not far:
        y_ref, ysend_ref, zsend_ref = refs[11:]
        y_copies = [remote(ysend_ref.at[j], y_ref.at[j], 4 + j, y_peer) for j in range(2)]
        z_copies = [
            remote(zsend_ref.at[j], out_ref.at[:, columns(j)], 6 + j, z_peer) for j in range(2)
        ]

        @pl.when(jnp.logical_not(home))
        def _():
            for j in range(2):
                zsend_ref[j] = (
                    far_keep_ref[j].astype(jnp.float32) + far_sent_ref[j].astype(jnp.float32)
                ).astype(zsend_ref.dtype)
                z_copies[j].start()

    for load in row_loads:
        load.wait()
    blend((pair_ref.at[0], pair_ref.at[1]), context_ref.at[pl.ds(done * LQ, LQ)], False)

    def multiply(s, to_y, j):
        here = jnp.where(to_y == z // 2, 0, 1)
        block = w_ref.at[here, j]
        pltpu.make_async_copy(block, block, w_sem.at[here, j]).wait()
        part_ref[s, j] = jnp.dot(
            context_ref[...], w_ref[here, j], preferred_element_type=jnp.float32
        ).astype(part_ref.dtype)

        @pl.when(jnp.logical_not(sums))
        def _():
            core_copies[s][j].start()

    def add_up(s, j):
        @pl.when(sums)
        def _():
            core_copies[s][j].wait_recv()
            value = part_ref[s, j].astype(jnp.float32) + core_ref[s, j].astype(jnp.float32)
            if far:
                target = keep_ref if s else send_ref
                target[j] = value.astype(target.dtype)
            elif s == 0:
                ysend_ref[j] = value.astype(ysend_ref.dtype)
                y_copies[j].start()
            else:
                y_copies[j].wait_recv()
                out_ref[:, columns(j)] = (value + y_ref[j].astype(jnp.float32)).astype(
                    out_ref.dtype
                )

    late = None
    for s, to_y in enumerate((1 - y, y)):
        for j in range(2):
            multiply(s, to_y, j)
            if late is not None:
                add_up(*late)
            late = (s, j)
    add_up(*late)

    @pl.when(jnp.logical_not(sums))
    def _():
        for copies in core_copies:
            for copy in copies:
                copy.wait_send()

    if not far:

        @pl.when(home)
        def _():
            for copy in y_copies:
                copy.wait_send()

        @pl.when(jnp.logical_not(home))
        def _():
            for copy in z_copies:
                copy.wait()


def project_call(pieces, weights, far_sums):
    own = weights[0]
    rows, (depth, wide) = (len(pieces) - 1) * LQ, own.shape
    dtype = own.dtype
    far = far_sums is None
    vmem = pl.BlockSpec(memory_space=pltpu.VMEM)
    blocks = (2, rows, wide)
    scratch = [
        pltpu.VMEM((rows, depth), dtype),
        pltpu.VMEM((2, 2, depth, wide), dtype),
        pltpu.VMEM((2,) + blocks, dtype),
        pltpu.VMEM((2,) + blocks, dtype),
        pltpu.VMEM((2,) + pieces[-1].shape, dtype),
        pltpu.SemaphoreType.DMA((len(pieces),)),
        pltpu.SemaphoreType.DMA((2, 2)),
        pltpu.SemaphoreType.DMA((8,)),
        pltpu.SemaphoreType.DMA((8,)),
    ]
    if far:
        out_shape = [jax.ShapeDtypeStruct(blocks, dtype)] * 2
        out_specs = [vmem] * 2
    else:
        out_shape = jax.ShapeDtypeStruct((rows, 2 * wide), dtype)
        out_specs = vmem
        scratch += [pltpu.VMEM(blocks, dtype)] * 3
    return pl.pallas_call(
        functools.partial(project_kernel, len(pieces), far),
        out_shape=out_shape,
        in_specs=[pl.BlockSpec(memory_space=pl.ANY)] * (len(pieces) + len(weights))
        + [vmem] * (0 if far else 2),
        out_specs=out_specs,
        scratch_shapes=scratch,
        compiler_params=pltpu.CompilerParams(
            collective_id=int(far), has_side_effects=True, vmem_limit_bytes=VMEM_BYTES
        ),
        name="project_far" if far else "project_home",
        cost_estimate=pl.CostEstimate(
            flops=2 * 4 * rows * depth * wide,
            bytes_accessed=4 * depth * wide * 2,
            transcendentals=0,
        ),
    )(*pieces, *weights, *(far_sums or ()))


def suits_line(mesh, queries, lists):
    passes, heads = mesh.shape["pass"], mesh.shape["head"]
    entries = queries.shape[0] // LQ // passes * lists.shape[1]
    several = queries.shape[0] // LQ >= 2 * passes
    return passes == 2 * LINE and heads == LINE and several and entries % passes == 0


def solution(mesh):
    in_specs = (
        P("pass", "head"),
        P("pass", "head", None),
        P("pass", None, "head", None),
        P("head", "pass"),
        P(),
        P(),
        P(),
    )
    out_specs = P("pass", "head")

    def run(*args):
        if not suits_line(mesh, args[0], args[4]):
            return jax.shard_map(
                body, mesh=mesh, in_specs=in_specs, out_specs=out_specs, check_vma=False
            )(*args)
        step = jax.shard_map(
            line_steps, mesh=mesh, in_specs=in_specs, out_specs=out_specs, check_vma=False
        )
        return step(*args)

    return run
```

```python
import functools
import math

import jax
import jax.numpy as jnp
from jax import lax
from jax.experimental import pallas as pl
from jax.experimental.pallas import tpu as pltpu
from jax.sharding import PartitionSpec as P


H = 64
KVH = 8
HD = 128
LQ = 128
GROUP = H // KVH
COEF = HD ** (-0.5) * math.log2(math.e)
NEG = -1e30
ROWS = 256


def round_of(a, b, n):
    if n & (n - 1) == 0:
        return a ^ b
    return lax.rem(b - a + n, n)


def pairs_of(k, n):
    if n & (n - 1) == 0:
        return [(p, p ^ k) for p in range(n)]
    return [(p, (p + k) % n) for p in range(n)]


def order_of(n):
    rest = range(1, n)
    return sorted(rest, key=lambda k: (bin(k).count("1"), k))


def gather_kernel(n, most, per_device, order, lists_ref, pslot_ref, qslot_ref, cache_ref, *refs):
    recv_ref, own_row_ref = refs[0], refs[1]
    outs = refs[2 : 2 + len(order)]
    send_row, send_cnt, recv_cnt, buf, in_sem, out_sem = refs[2 + len(order) :]
    me = lax.axis_index("pass")
    pass_dev = cache_ref.shape[0]
    topp, nq = lists_ref.shape
    for k in range(n):
        send_cnt[k] = 0
        recv_cnt[k] = 0
    for i in range(n * most):
        recv_ref[i] = -1
        send_row[i] = 0

    def question(q, carry):
        slot = qslot_ref[q]
        dest = slot // per_device
        local = slot - dest * per_device
        k_send = round_of(me, dest, n)
        for t in range(topp):
            row = pslot_ref[lists_ref[t, q]]
            owner = row // pass_dev

            @pl.when(owner == me)
            def _():
                count = send_cnt[k_send]
                send_row[k_send * most + count] = row - owner * pass_dev
                send_cnt[k_send] = count + 1

            @pl.when(dest == me)
            def _():
                k = round_of(owner, me, n)
                count = recv_cnt[k]
                recv_ref[k * most + count] = local
                recv_cnt[k] = count + 1

        return carry

    lax.fori_loop(0, nq, question, 0)
    for r in range(most):
        own_row_ref[r] = send_row[r]
    copies = []
    for j, k in enumerate(order):
        for r in range(most):
            i = j * most + r
            get = pltpu.make_async_copy(
                cache_ref.at[send_row[k * most + r]], buf.at[i], in_sem.at[i]
            )
            get.start()
            copies.append((get, pltpu.make_async_copy(buf.at[i], outs[j].at[r], out_sem.at[i])))
    for get, put in copies:
        get.wait()
        put.start()
    for get, put in copies:
        put.wait()


def gather(lists, passage_slot, question_slot, cache, n, most, per_device, order):
    item = cache.shape[1:]
    slots = (n - 1) * most
    smem = pl.BlockSpec(memory_space=pltpu.SMEM)
    anyspace = pl.BlockSpec(memory_space=pl.ANY)
    return pl.pallas_call(
        functools.partial(gather_kernel, n, most, per_device, order),
        out_shape=[
            jax.ShapeDtypeStruct((n * most,), jnp.int32),
            jax.ShapeDtypeStruct((most,), jnp.int32),
        ]
        + [jax.ShapeDtypeStruct((most,) + item, cache.dtype)] * len(order),
        in_specs=[smem, smem, smem, anyspace],
        out_specs=[smem, smem] + [anyspace] * len(order),
        scratch_shapes=[
            pltpu.SMEM((n * most,), jnp.int32),
            pltpu.SMEM((n,), jnp.int32),
            pltpu.SMEM((n,), jnp.int32),
            pltpu.VMEM((slots,) + item, cache.dtype),
            pltpu.SemaphoreType.DMA((slots,)),
            pltpu.SemaphoreType.DMA((slots,)),
        ],
        name="gather_items",
        cost_estimate=pl.CostEstimate(
            flops=0, bytes_accessed=2 * slots * math.prod(item) * 2, transcendentals=0
        ),
    )(lists.T, passage_slot, question_slot, cache)


def block_step(q_ref, m_ref, l_ref, acc_ref, question, head, keys, values, causal):
    rows = q_ref.shape[2]
    step = min(ROWS, rows)
    width = keys.shape[0]
    ones = jnp.ones(values.shape, values.dtype)
    extended = jnp.concatenate([values, ones], axis=1)
    for start in range(0, rows, step):
        part = pl.ds(start, step)
        q = q_ref[question, head, part, :]
        scores = (
            lax.dot_general(q, keys, (((1,), (1,)), ((), ())), preferred_element_type=jnp.float32)
            * COEF
        )
        if causal:
            token = lax.broadcasted_iota(jnp.int32, scores.shape, 0) % LQ
            column = lax.broadcasted_iota(jnp.int32, scores.shape, 1)
            scores = jnp.where(column <= token, scores, NEG)
        old = m_ref[question, head, part, :]
        new = jnp.maximum(old, jnp.max(scores, axis=1, keepdims=True))
        weights = jnp.exp2(scores - jnp.concatenate([new] * (width // HD), axis=1))
        mixed = jnp.dot(
            weights.astype(jnp.bfloat16), extended, preferred_element_type=jnp.float32
        )
        alpha = jnp.exp2(old - new)
        m_ref[question, head, part, :] = new
        l_ref[question, head, part, :] = l_ref[question, head, part, :] * alpha + mixed[:, HD:]
        acc_ref[question, head, part, :] = (
            acc_ref[question, head, part, :] * alpha + mixed[:, :HD]
        )


def attend_kernel(first, last, rounds, most, *refs):
    refs = list(refs)
    recv_ref, q_ref = refs.pop(0), refs.pop(0)
    if first:
        row_ref, own_ref, cache_ref = refs.pop(0), refs.pop(0), refs.pop(0)
        sources = None
        entries = most
    else:
        state_in = [refs.pop(0) for _ in range(3)]
        sources = [refs.pop(0) for _ in rounds]
        entries = len(rounds) * most
    if last:
        out_ref = refs.pop(0)
        m_ref, l_ref, acc_ref = [refs.pop(0) for _ in range(3)]
    else:
        m_ref, l_ref, acc_ref = [refs.pop(0) for _ in range(3)]
    buf, sem = refs
    per_device, heads = q_ref.shape[0], q_ref.shape[1]

    def fetch(i, slot):
        if first:
            pltpu.make_async_copy(cache_ref.at[row_ref[i]], buf.at[slot], sem.at[slot]).start()
            return
        for j in range(len(rounds)):

            @pl.when(i // most == j)
            def _():
                pltpu.make_async_copy(
                    sources[j].at[i - j * most], buf.at[slot], sem.at[slot]
                ).start()

    def tag_of(i):
        if first:
            return recv_ref[i]
        k = jnp.int32(0)
        for j, value in enumerate(rounds):
            k = jnp.where(i // most == j, value, k)
        return recv_ref[k * most + lax.rem(i, most)]

    fetch(jnp.int32(0), 0)
    if first:
        m_ref[...] = jnp.full(m_ref.shape, NEG, jnp.float32)
        l_ref[...] = jnp.zeros(l_ref.shape, jnp.float32)
        acc_ref[...] = jnp.zeros(acc_ref.shape, jnp.float32)

        def own_block(question, carry):
            for head in range(heads):
                block = own_ref[question, head]
                block_step(
                    q_ref, m_ref, l_ref, acc_ref, question, head, block[:, :HD], block[:, HD:], True
                )
            return carry

        lax.fori_loop(0, per_device, own_block, 0)
    else:
        m_ref[...] = state_in[0][...]
        l_ref[...] = state_in[1][...]
        acc_ref[...] = state_in[2][...]

    def item(i, carry):
        slot = lax.rem(i, 2)
        pltpu.make_async_copy(buf.at[slot], buf.at[slot], sem.at[slot]).wait()

        @pl.when(i + 1 < entries)
        def _():
            fetch(i + 1, lax.rem(i + 1, 2))

        tag = tag_of(i)

        @pl.when(tag >= 0)
        def _():
            for head in range(heads):
                block_step(
                    q_ref,
                    m_ref,
                    l_ref,
                    acc_ref,
                    tag,
                    head,
                    buf[slot, head, :, :HD],
                    buf[slot, head, :, HD:],
                    False,
                )

        return carry

    lax.fori_loop(0, entries, item, 0)
    if last:
        for question in range(per_device):
            for head in range(heads):
                for g in range(GROUP):
                    part = pl.ds(g * LQ, LQ)
                    column = (head * GROUP + g) * HD
                    out_ref[pl.ds(question * LQ, LQ), pl.ds(column, HD)] = (
                        acc_ref[question, head, part, :] / l_ref[question, head, part, :]
                    ).astype(out_ref.dtype)


def attend_call(first, last, rounds, most, recv, q, rest, item):
    per_device, heads, rows, _ = q.shape
    state = jax.ShapeDtypeStruct(q.shape, jnp.float32)
    smem = pl.BlockSpec(memory_space=pltpu.SMEM)
    vmem = pl.BlockSpec(memory_space=pltpu.VMEM)
    anyspace = pl.BlockSpec(memory_space=pl.ANY)
    if first:
        in_specs = [smem, vmem, smem, vmem, anyspace]
        entries = most
    else:
        in_specs = [smem, vmem] + [vmem] * 3 + [anyspace] * len(rounds)
        entries = most * len(rounds)
    scratch = [pltpu.VMEM((2,) + item, q.dtype), pltpu.SemaphoreType.DMA((2,))]
    if last:
        out_shape = jax.ShapeDtypeStruct((per_device * LQ, heads * GROUP * HD), q.dtype)
        out_specs = vmem
        scratch = [pltpu.VMEM(q.shape, jnp.float32)] * 3 + scratch
    else:
        out_shape = [state] * 3
        out_specs = [vmem] * 3
    weights = entries * heads * rows * item[1]
    return pl.pallas_call(
        functools.partial(attend_kernel, first, last, rounds, most),
        out_shape=out_shape,
        in_specs=in_specs,
        out_specs=out_specs,
        scratch_shapes=scratch,
        name="attend_first" if first else ("attend_last" if last else "attend_more"),
        cost_estimate=pl.CostEstimate(
            flops=weights * HD * 4,
            bytes_accessed=entries * math.prod(item) * 2,
            transcendentals=weights,
        ),
    )(recv, q, *rest)


def weight_blocks(own, n):
    if n & (n - 1):
        return [lax.all_gather(own, "pass", axis=1, tiled=True)]
    have = {0: own}
    bit = n // 2
    while bit:
        for k in list(have):
            have[k ^ bit] = lax.ppermute(have[k], "pass", pairs_of(bit, n))
        bit //= 2
    return [have[k] for k in range(n)]


def project(context, weights):
    parts = [
        jnp.dot(context, weight, preferred_element_type=jnp.float32).astype(jnp.bfloat16)
        for weight in weights
    ]
    me = lax.axis_index("pass")
    bit = len(parts) // 2
    while bit:
        swap = (me & bit) != 0
        parts = [jnp.where(swap, parts[k ^ bit], parts[k]) for k in range(len(parts))]
        bit //= 2
    return jnp.concatenate(parts, axis=1)


def body(queries, own_kv, passage_cache, out_weight, lists, passage_slot, question_slot):
    n = lax.axis_size("pass")
    per_device = queries.shape[0] // LQ
    heads = own_kv.shape[1]
    entries = per_device * lists.shape[1]
    most = (entries + n - 1) // n
    order = order_of(n)
    cache = jnp.transpose(passage_cache, (0, 2, 1, 3))
    recv, own_row, *items = gather(
        lists, passage_slot, question_slot, cache, n, most, per_device, order
    )
    arrived = [
        lax.ppermute(item, "pass", pairs_of(k, n)) for k, item in zip(order, items)
    ]
    weights = weight_blocks(out_weight, n)
    q = (
        queries.reshape(per_device, LQ, heads, GROUP, HD)
        .transpose(0, 2, 3, 1, 4)
        .reshape(per_device, heads, GROUP * LQ, HD)
    )
    own = own_kv.reshape(per_device, LQ, heads, 2 * HD).transpose(0, 2, 1, 3)
    item = cache.shape[1:]
    state = attend_call(True, False, (0,), most, recv, q, (own_row, own, cache), item)
    calls = 3
    bounds = [len(order) * i // calls for i in range(calls + 1)]
    for i in range(calls):
        rounds = tuple(order[bounds[i] : bounds[i + 1]])
        rest = tuple(state) + tuple(arrived[bounds[i] : bounds[i + 1]])
        state = attend_call(False, i == calls - 1, rounds, most, recv, q, rest, item)
    context = state
    return lax.psum_scatter(project(context, weights), "head", scatter_dimension=1, tiled=True)


LINE = 4
EXTRA = 8
ITEM_ORDER = (2, 0, 3, 1)
VMEM_BYTES = 67043328


def mirror(k, ends=None):
    pairs = [(p, p ^ int(2 * k)) for p in range(2 * LINE)]
    if ends is None:
        return pairs
    return [(p, d) for p, d in pairs if (p // 2 in (0, LINE - 1)) == (ends == "outer")]


def is_inner():
    z = lax.axis_index("pass") // 2
    return jnp.logical_and(z > 0, z < LINE - 1)


def sort_kernel(most, per_device, lists_ref, pslot_ref, qslot_ref, cache_ref, *refs):
    row_ref, tag_ref, far_tag_ref = refs[:3]
    outs = refs[3 : 3 + LINE]
    send_row, near_cnt, send_cnt, far_cnt, buf, in_sem, out_sem = refs[3 + LINE :]
    me = lax.axis_index("pass")
    z, x = me // 2, me % 2
    pass_dev = cache_ref.shape[0]
    topp, nq = lists_ref.shape
    for k in range(LINE):
        near_cnt[k] = 0
        send_cnt[k] = 0
        far_cnt[k] = 0

    def take(i):
        return pltpu.make_async_copy(cache_ref.at[send_row[i]], buf.at[i], in_sem.at[i])

    def question(q, carry):
        slot = qslot_ref[q]
        dest = slot // per_device
        local = slot - dest * per_device
        k = (dest // 2) ^ z

        @pl.when(dest % 2 == x)
        def _():
            for t in range(topp):
                row = pslot_ref[lists_ref[t, q]]
                owner = row // pass_dev

                @pl.when(owner == me)
                def _():
                    at = k * most + near_cnt[k]
                    row_ref[at] = row - owner * pass_dev
                    tag_ref[at] = local
                    near_cnt[k] = near_cnt[k] + 1

                @pl.when(owner == (me ^ 1))
                def _():
                    far_tag_ref[k * most + far_cnt[k]] = local
                    far_cnt[k] = far_cnt[k] + 1

        @pl.when(dest % 2 != x)
        def _():
            for t in range(topp):
                row = pslot_ref[lists_ref[t, q]]
                owner = row // pass_dev

                @pl.when(owner == me)
                def _():
                    at = k * most + send_cnt[k]
                    send_row[at] = row - owner * pass_dev
                    send_cnt[k] = send_cnt[k] + 1
                    take(at).start()

        return carry

    lax.fori_loop(0, nq, question, 0)
    slots = [k * most + r for k in ITEM_ORDER for r in range(most)]
    puts = [pltpu.make_async_copy(buf.at[i], outs[i // most].at[i % most], out_sem.at[i]) for i in slots]
    for i, put in zip(slots, puts):
        take(i).wait()
        put.start()
    for put in puts:
        put.wait()


def sort_items(lists, passage_slot, question_slot, cache, most, per_device):
    item = cache.shape[1:]
    slots = LINE * most
    smem = pl.BlockSpec(memory_space=pltpu.SMEM)
    anyspace = pl.BlockSpec(memory_space=pl.ANY)
    return pl.pallas_call(
        functools.partial(sort_kernel, most, per_device),
        out_shape=[jax.ShapeDtypeStruct((slots,), jnp.int32)] * 3
        + [jax.ShapeDtypeStruct((most,) + item, cache.dtype)] * LINE,
        in_specs=[smem, smem, smem, anyspace],
        out_specs=[smem] * 3 + [anyspace] * LINE,
        scratch_shapes=[
            pltpu.SMEM((slots,), jnp.int32),
            pltpu.SMEM((LINE,), jnp.int32),
            pltpu.SMEM((LINE,), jnp.int32),
            pltpu.SMEM((LINE,), jnp.int32),
            pltpu.VMEM((slots,) + item, cache.dtype),
            pltpu.SemaphoreType.DMA((slots,)),
            pltpu.SemaphoreType.DMA((slots,)),
        ],
        compiler_params=pltpu.CompilerParams(vmem_limit_bytes=VMEM_BYTES),
        name="sort_items",
        cost_estimate=pl.CostEstimate(
            flops=0, bytes_accessed=2 * slots * math.prod(item) * 2, transcendentals=0
        ),
    )(lists.T, passage_slot, question_slot, cache)


def unit():
    r = lax.broadcasted_iota(jnp.int32, (LQ, LQ), 0)
    c = lax.broadcasted_iota(jnp.int32, (LQ, LQ), 1)
    return r == c


def part_step(q_ref, m_ref, l_ref, acc_ref, question, head, keys, values, causal):
    rows = GROUP * LQ
    width = keys.shape[0]
    ones = jnp.ones(values.shape, values.dtype)
    extended = jnp.concatenate([values, ones], axis=1)
    tokens = pl.ds(pl.multiple_of(question * LQ, LQ), LQ)
    for start in range(0, rows, ROWS):
        part = pl.ds(start, ROWS)
        q = jnp.concatenate(
            [
                q_ref[tokens, pl.ds(pl.multiple_of((head * GROUP + g) * HD, HD), HD)]
                for g in range(start // LQ, (start + ROWS) // LQ)
            ],
            axis=0,
        )
        scores = (
            lax.dot_general(q, keys, (((1,), (1,)), ((), ())), preferred_element_type=jnp.float32)
            * COEF
        )
        if causal:
            token = lax.broadcasted_iota(jnp.int32, scores.shape, 0) % LQ
            column = lax.broadcasted_iota(jnp.int32, scores.shape, 1)
            scores = jnp.where(column <= token, scores, NEG)
        old = m_ref[question, head, part, :]
        new = jnp.maximum(old, jnp.max(scores, axis=1, keepdims=True))
        weights = jnp.exp2(scores - jnp.concatenate([new] * (width // HD), axis=1))
        mixed = jnp.dot(
            weights.astype(jnp.bfloat16), extended, preferred_element_type=jnp.float32
        )
        alpha = jnp.exp2(old - new)
        m_ref[question, head, part, :] = new
        l_ref[question, head, part, :] = l_ref[question, head, part, :] * alpha + mixed[:, HD:]
        acc_ref[question, head, part, :] = (
            acc_ref[question, head, part, :] * alpha + mixed[:, :HD]
        )


def part_kernel(k, most, first, last, heads, *refs):
    refs = list(refs)
    row_ref, tag_ref, far_tag_ref = refs.pop(0), refs.pop(0), refs.pop(0)
    own_ref = refs.pop(0) if k == 0 else None
    questions = [refs.pop(0) for _ in range(2 if k > 1 else 1)]
    cache_ref = refs.pop(0)
    items_ref = refs.pop(0) if last > most else None
    out_ref, q_ref, m_ref, l_ref, acc_ref, buf, sem, q_sem = refs
    per_device = q_ref.shape[0] // LQ

    def fetch(i, slot):
        if first < most:

            @pl.when(i < most)
            def _():
                row = row_ref[k * most + jnp.minimum(i, most - 1)]
                pltpu.make_async_copy(cache_ref.at[row], buf.at[slot], sem.at[slot]).start()

        if last > most:

            @pl.when(i >= most)
            def _():
                pltpu.make_async_copy(
                    items_ref.at[jnp.maximum(i - most, 0)], buf.at[slot], sem.at[slot]
                ).start()

    if len(questions) == 1:
        pltpu.make_async_copy(questions[0], q_ref, q_sem).start()
    else:
        inner = is_inner()

        @pl.when(inner)
        def _():
            pltpu.make_async_copy(questions[0], q_ref, q_sem).start()

        @pl.when(jnp.logical_not(inner))
        def _():
            pltpu.make_async_copy(questions[1], q_ref, q_sem).start()

    fetch(jnp.int32(first), first % 2)
    m_ref[...] = jnp.full(m_ref.shape, NEG, jnp.float32)
    l_ref[...] = jnp.zeros(l_ref.shape, jnp.float32)
    acc_ref[...] = jnp.zeros(acc_ref.shape, jnp.float32)
    pltpu.make_async_copy(q_ref, q_ref, q_sem).wait()
    if k == 0:

        def own_block(i, carry):
            question, head = i // heads, lax.rem(i, heads)
            part_step(
                q_ref,
                m_ref,
                l_ref,
                acc_ref,
                question,
                head,
                own_ref[question, head, :, :HD],
                own_ref[question, head, :, HD:],
                True,
            )
            return carry

        lax.fori_loop(0, per_device * heads, own_block, 0)

    def item(i, carry):
        slot = lax.rem(i, 2)
        pltpu.make_async_copy(buf.at[slot], buf.at[slot], sem.at[slot]).wait()

        @pl.when(i + 1 < last)
        def _():
            fetch(i + 1, lax.rem(i + 1, 2))

        at = k * most + lax.rem(i, most)
        tag = jnp.where(i < most, tag_ref[at], far_tag_ref[at])

        for head in range(heads):
            part_step(
                q_ref,
                m_ref,
                l_ref,
                acc_ref,
                tag,
                head,
                buf[slot, head, :, :HD],
                buf[slot, head, :, HD:],
                False,
            )
        return carry

    lax.fori_loop(first, last, item, 0)
    eye = unit()

    def close(c, carry):
        head, g = c // GROUP, lax.rem(c, GROUP)
        columns = pl.ds(pl.multiple_of(c * HD, HD), HD)
        part = pl.ds(pl.multiple_of(g * LQ, LQ), LQ)
        for question in range(per_device):
            total = l_ref[question, head, part, :]
            some = total > 0.0
            safe = jnp.where(some, total, 1.0)
            out_ref[question, :LQ, columns] = (
                acc_ref[question, head, part, :] / safe
            ).astype(out_ref.dtype)
            level = jnp.where(some, m_ref[question, head, part, :] + jnp.log2(safe), NEG)
            line = jnp.sum(jnp.where(eye, level, 0.0), axis=0, keepdims=True)
            store_level(out_ref, question, columns, line)
        return carry

    lax.fori_loop(0, heads * GROUP, close, 0)


def store_level(out_ref, question, columns, line):
    row_of = lax.broadcasted_iota(jnp.int32, (EXTRA, line.shape[1]), 0)
    high = line.astype(jnp.bfloat16).astype(jnp.float32)
    both = jnp.where(row_of == 0, high, jnp.where(row_of == 1, line - high, 0.0))
    out_ref[question, LQ:, columns] = both.astype(out_ref.dtype)


def part_call(k, most, tables, own, questions, cache, items, local=True):
    tokens, columns = questions[0].shape
    heads, item = cache.shape[1], cache.shape[1:]
    state = (tokens // LQ, heads, GROUP * LQ, HD)
    smem = pl.BlockSpec(memory_space=pltpu.SMEM)
    vmem = pl.BlockSpec(memory_space=pltpu.VMEM)
    anyspace = pl.BlockSpec(memory_space=pl.ANY)
    owned = [own] if k == 0 else []
    received = [items] if items is not None else []
    first, last = 0 if local else most, 2 * most if received else most
    weights = (last - first) * heads * GROUP * LQ * item[1]
    return pl.pallas_call(
        functools.partial(part_kernel, k, most, first, last, heads),
        out_shape=jax.ShapeDtypeStruct((tokens // LQ, LQ + EXTRA, columns), cache.dtype),
        in_specs=[smem] * 3
        + [vmem] * len(owned)
        + [anyspace] * (len(questions) + 1 + len(received)),
        out_specs=vmem,
        scratch_shapes=[
            pltpu.VMEM((tokens, columns), cache.dtype),
            pltpu.VMEM(state, jnp.float32),
            pltpu.VMEM(state, jnp.float32),
            pltpu.VMEM(state, jnp.float32),
            pltpu.VMEM((2,) + item, cache.dtype),
            pltpu.SemaphoreType.DMA((2,)),
            pltpu.SemaphoreType.DMA,
        ],
        compiler_params=pltpu.CompilerParams(vmem_limit_bytes=VMEM_BYTES),
        cost_estimate=pl.CostEstimate(
            flops=weights * HD * 4,
            bytes_accessed=(last - first) * math.prod(item) * 2,
            transcendentals=weights,
        ),
    )(*tables, *owned, *questions, cache, *received)


def blend(refs, out_ref, leveled):
    eye = unit()
    ones = jnp.ones((2 * LQ, LQ), jnp.bfloat16)

    def level_of(ref):
        both = ref[0, LQ:, :].astype(jnp.float32)
        return both[:1] + both[1:2]

    levels = [level_of(ref) for ref in refs]
    top = functools.reduce(jnp.maximum, levels)
    weights = [jnp.exp2(level - top) for level in levels]
    total = functools.reduce(jnp.add, weights)
    shares = []
    for weight in weights[1:]:
        share = weight / total
        high = share.astype(jnp.bfloat16).astype(jnp.float32)
        shares.append((high, share - high))
    for c in range(total.shape[1] // HD):
        columns = slice(c * HD, (c + 1) * HD)
        base = refs[0][0, :LQ, columns].astype(jnp.float32)
        value = base
        for ref, pair in zip(refs[1:], shares):
            spread = jnp.concatenate(
                [
                    jnp.where(eye, jnp.broadcast_to(v[:, columns], (LQ, LQ)), 0.0).astype(
                        jnp.bfloat16
                    )
                    for v in pair
                ],
                axis=1,
            )
            column = jnp.dot(spread, ones, preferred_element_type=jnp.float32)
            value = value + (ref[0, :LQ, columns].astype(jnp.float32) - base) * column
        value = value.astype(out_ref.dtype)
        if leveled:
            out_ref[0, :LQ, columns] = value
        else:
            out_ref[:, columns] = value
    if leveled:
        store_level(out_ref, 0, slice(None), top + jnp.log2(total))


def merge_kernel(*refs):
    *parts, out_ref = refs
    inner = is_inner()

    @pl.when(inner)
    def _():
        blend(parts, out_ref, True)

    @pl.when(jnp.logical_not(inner))
    def _():
        if len(parts) > 2:
            blend(parts[:-1], out_ref, True)
        else:
            out_ref[...] = parts[0][...]


def finish_kernel(a_ref, b_ref, out_ref):
    blend((a_ref, b_ref), out_ref, False)


def question_spec(value, at):
    shape = (1,) + value.shape[1:]
    if value.shape[0] == 1:
        return pl.BlockSpec(shape, lambda q: (0, 0, 0))
    return pl.BlockSpec(shape, lambda q: (at, 0, 0))


def join_call(parts, at, leveled):
    columns = parts[0].shape[2]
    if leveled:
        shape = (1,) + parts[0].shape[1:]
        out_spec = pl.BlockSpec(shape, lambda q: (0, 0, 0))
    else:
        shape = (LQ, columns)
        out_spec = pl.BlockSpec(shape, lambda q: (0, 0))
    size = LQ * columns
    return pl.pallas_call(
        merge_kernel if leveled else finish_kernel,
        out_shape=jax.ShapeDtypeStruct(shape, parts[0].dtype),
        grid=(1,),
        in_specs=[question_spec(part, at) for part in parts],
        out_specs=out_spec,
        compiler_params=pltpu.CompilerParams(vmem_limit_bytes=VMEM_BYTES),
        cost_estimate=pl.CostEstimate(flops=size * 8, bytes_accessed=size * 6, transcendentals=0),
    )(*parts)


def line_steps(queries, own_kv, passage_cache, out_weight, lists, passage_slot, question_slot):
    per_device = queries.shape[0] // LQ
    heads = own_kv.shape[1]
    most = per_device * lists.shape[1] // (2 * LINE)

    def send(value, pairs):
        return lax.ppermute(value, "pass", pairs)

    def part(k, *args, local=True):
        return part_call(k, most, tables, own if k == 0 else None, *args, local=local)

    def join(at, *parts, leveled=True):
        return join_call(parts, at, leveled)

    across = [(p, p ^ 1) for p in range(2 * LINE)]
    inner_across = [(p, d) for p, d in across if p // 2 in (1, 2)]
    outer_across = [(p, d) for p, d in across if p // 2 not in (1, 2)]
    near, middle = mirror(1), mirror(3, "inner")
    inward, outward = mirror(1, "outer"), mirror(1, "inner")
    q_near = send(queries, near)
    q_mid = send(queries, middle)
    half = out_weight.shape[0] // 2
    w_across0 = send(out_weight[:half], across)
    cache = jnp.transpose(passage_cache, (0, 2, 1, 3))
    row, tag, far_tag, *items = sort_items(
        lists, passage_slot, question_slot, cache, most, per_device
    )
    tables = (row, tag, far_tag)
    later, _ = lax.optimization_barrier((out_weight, row))
    w_across1 = send(later[half:], across)
    q_out = send(q_mid, outward)
    q_cross = send(q_near, middle)
    q_end = send(q_cross, outward)
    far = [send(items[k], across) for k in range(LINE)]
    own = own_kv.reshape(per_device, LQ, heads, 2 * HD).transpose(0, 2, 1, 3)
    part2 = part(2, [q_cross, q_out], cache, far[2])
    part3 = part(3, [q_mid, q_end], cache, far[3])
    part0 = part(0, [queries], cache, far[0])
    part1 = part(1, [q_near], cache, None)
    part1_far = part(1, [q_near], cache, far[1], local=False)
    back2 = send(part2, inward)
    w_in = send(out_weight, mirror(2, "outer"))
    w_out = send(out_weight, mirror(2, "inner"))
    back3 = send(part3, inward)
    w_in_both = send(w_in, inner_across)
    w_out_both = send(w_out, outer_across)
    own_rows, near_rows = [], []
    for q in range(per_device):
        cross3 = send(join(q, part3, back2), middle)
        near0 = join(q, part0, cross3)
        beside = send(near0, near)
        cross2 = send(join(q, part2, back3), middle)
        near1 = join(q, part1, part1_far, cross2)
        back1 = send(near1, near)
        if q + 1 < per_device:
            near_rows.append(join(q, near1, beside, leveled=False))
            own_rows.append(join(q, near0, back1, leveled=False))
        else:
            near_rows += [near1, beside]
            own_rows += [near0, back1]
    weights = (out_weight, w_across0, w_across1, w_in, w_in_both, w_out, w_out_both)
    far_sums = project_call(near_rows, weights, None)
    return project_call(own_rows, weights, far_sums)


MESH = pl.DeviceIdType.MESH


def at_home():
    return lax.axis_index("head") % 2 == lax.axis_index("pass") // 2 % 2


def project_kernel(pieces, far, *refs):
    rows_refs = refs[:pieces]
    own_ref, a0_ref, a1_ref, in_ref, in2_ref, out1_ref, out2_ref = refs[pieces : pieces + 7]
    refs = refs[pieces + 7 :]
    if not far:
        far_ref, *refs = refs
    out_ref, context_ref, w_ref, part_ref, core_ref, pair_ref, y_ref, ysend_ref = refs[:8]
    row_sem, w_sem, send_sem, recv_sem = refs[8:]
    me, head = lax.axis_index("pass"), lax.axis_index("head")
    z, x, y = me // 2, me % 2, head // 2
    wide = w_ref.shape[3]
    inner = is_inner()
    core_peer, y_peer, z_peer = (me, head ^ 1), (me, head ^ 2), (me ^ 2, head ^ 1)
    home = at_home()
    sums = jnp.logical_not(home) if far else home

    done = pieces - 2
    row_loads = [
        pltpu.make_async_copy(ref, pair_ref.at[i], row_sem.at[done + i])
        for i, ref in enumerate(rows_refs[done:])
    ]
    row_loads += [
        pltpu.make_async_copy(ref, context_ref.at[pl.ds(i * LQ, LQ)], row_sem.at[i])
        for i, ref in enumerate(rows_refs[:done])
    ]
    for load in row_loads:
        load.start()

    def load_here():
        pltpu.make_async_copy(own_ref, w_ref.at[0, x], w_sem.at[0, x]).start()
        half = a0_ref.shape[0]
        low, high = w_ref.at[0, 1 - x, pl.ds(0, half)], w_ref.at[0, 1 - x, pl.ds(half, half)]
        pltpu.make_async_copy(a0_ref, low, w_sem.at[0, 1 - x]).start()
        pltpu.make_async_copy(a1_ref, high, w_sem.at[0, 1 - x]).start()

    def load_there():
        for which, (one, two) in (
            (inner, (in_ref, in2_ref)),
            (jnp.logical_not(inner), (out1_ref, out2_ref)),
        ):

            @pl.when(which)
            def _():
                pltpu.make_async_copy(one, w_ref.at[1, x], w_sem.at[1, x]).start()
                pltpu.make_async_copy(two, w_ref.at[1, 1 - x], w_sem.at[1, 1 - x]).start()

    here_first = y != z // 2

    @pl.when(here_first)
    def _():
        load_here()
        load_there()

    @pl.when(jnp.logical_not(here_first))
    def _():
        load_there()
        load_here()

    barrier = pltpu.get_barrier_semaphore()
    peers = (core_peer, y_peer) if far else (core_peer, y_peer, z_peer)
    for peer in peers:
        pl.semaphore_signal(barrier, inc=1, device_id=peer, device_id_type=MESH)
    pl.semaphore_wait(barrier, len(peers))

    def remote(src, dst, i, peer):
        return pltpu.make_async_remote_copy(
            src_ref=src,
            dst_ref=dst,
            send_sem=send_sem.at[i],
            recv_sem=recv_sem.at[i],
            device_id=peer,
            device_id_type=MESH,
        )

    def columns(j):
        return pl.ds(j * wide, wide)

    core_copies = [
        [remote(part_ref.at[s, j], core_ref.at[s, j], s * 2 + j, core_peer) for j in range(2)]
        for s in range(2)
    ]
    y_copies = [remote(ysend_ref.at[j], y_ref.at[j], 4 + j, y_peer) for j in range(2)]
    if not far:
        z_copies = [
            remote(far_ref.at[j], out_ref.at[:, columns(j)], 6 + j, z_peer) for j in range(2)
        ]

        @pl.when(jnp.logical_not(home))
        def _():
            for copy in z_copies:
                copy.start()

    for load in row_loads:
        load.wait()
    blend((pair_ref.at[0], pair_ref.at[1]), context_ref.at[pl.ds(done * LQ, LQ)], False)

    def multiply(s, to_y, j):
        here = jnp.where(to_y == z // 2, 0, 1)
        block = w_ref.at[here, j]
        pltpu.make_async_copy(block, block, w_sem.at[here, j]).wait()
        part_ref[s, j] = jnp.dot(
            context_ref[...], w_ref[here, j], preferred_element_type=jnp.float32
        ).astype(part_ref.dtype)

        @pl.when(jnp.logical_not(sums))
        def _():
            core_copies[s][j].start()

    def add_up(s, j):
        @pl.when(sums)
        def _():
            core_copies[s][j].wait_recv()
            value = part_ref[s, j].astype(jnp.float32) + core_ref[s, j].astype(jnp.float32)
            if s == 0:
                ysend_ref[j] = value.astype(ysend_ref.dtype)
                y_copies[j].start()
                return
            y_copies[j].wait_recv()
            total = (value + y_ref[j].astype(jnp.float32)).astype(out_ref.dtype)
            if far:
                out_ref[j] = total
            else:
                out_ref[:, columns(j)] = total

    late = None
    for s, to_y in enumerate((1 - y, y)):
        for j in range(2):
            multiply(s, to_y, j)
            if late is not None:
                add_up(*late)
            late = (s, j)
    add_up(*late)

    @pl.when(jnp.logical_not(sums))
    def _():
        for copies in core_copies:
            for copy in copies:
                copy.wait_send()

    @pl.when(sums)
    def _():
        for copy in y_copies:
            copy.wait_send()

    if not far:

        @pl.when(jnp.logical_not(home))
        def _():
            for copy in z_copies:
                copy.wait()


def project_call(pieces, weights, far_sums):
    own = weights[0]
    rows, (depth, wide) = (len(pieces) - 1) * LQ, own.shape
    dtype = own.dtype
    far = far_sums is None
    vmem = pl.BlockSpec(memory_space=pltpu.VMEM)
    blocks = (2, rows, wide)
    scratch = [
        pltpu.VMEM((rows, depth), dtype),
        pltpu.VMEM((2, 2, depth, wide), dtype),
        pltpu.VMEM((2,) + blocks, dtype),
        pltpu.VMEM((2,) + blocks, dtype),
        pltpu.VMEM((2,) + pieces[-1].shape, dtype),
        pltpu.VMEM(blocks, dtype),
        pltpu.VMEM(blocks, dtype),
        pltpu.SemaphoreType.DMA((len(pieces),)),
        pltpu.SemaphoreType.DMA((2, 2)),
        pltpu.SemaphoreType.DMA((8,)),
        pltpu.SemaphoreType.DMA((8,)),
    ]
    shape = blocks if far else (rows, 2 * wide)
    return pl.pallas_call(
        functools.partial(project_kernel, len(pieces), far),
        out_shape=jax.ShapeDtypeStruct(shape, dtype),
        in_specs=[pl.BlockSpec(memory_space=pl.ANY)] * (len(pieces) + len(weights))
        + [vmem] * (0 if far else 1),
        out_specs=vmem,
        scratch_shapes=scratch,
        compiler_params=pltpu.CompilerParams(
            collective_id=int(far), has_side_effects=True, vmem_limit_bytes=VMEM_BYTES
        ),
        name="project_far" if far else "project_home",
        cost_estimate=pl.CostEstimate(
            flops=2 * 4 * rows * depth * wide,
            bytes_accessed=4 * depth * wide * 2,
            transcendentals=0,
        ),
    )(*pieces, *weights, *([] if far else [far_sums]))


def suits_line(mesh, queries, lists):
    passes, heads = mesh.shape["pass"], mesh.shape["head"]
    entries = queries.shape[0] // LQ // passes * lists.shape[1]
    several = queries.shape[0] // LQ >= 2 * passes
    return passes == 2 * LINE and heads == LINE and several and entries % passes == 0


def solution(mesh):
    in_specs = (
        P("pass", "head"),
        P("pass", "head", None),
        P("pass", None, "head", None),
        P("head", "pass"),
        P(),
        P(),
        P(),
    )
    out_specs = P("pass", "head")

    def run(*args):
        if not suits_line(mesh, args[0], args[4]):
            return jax.shard_map(
                body, mesh=mesh, in_specs=in_specs, out_specs=out_specs, check_vma=False
            )(*args)
        step = jax.shard_map(
            line_steps, mesh=mesh, in_specs=in_specs, out_specs=out_specs, check_vma=False
        )
        return step(*args)

    return run
```

```python
import functools
import math

import jax
import jax.numpy as jnp
from jax import lax
from jax.experimental import pallas as pl
from jax.experimental.pallas import tpu as pltpu
from jax.sharding import PartitionSpec as P


H = 64
KVH = 8
HD = 128
LQ = 128
GROUP = H // KVH
COEF = HD ** (-0.5) * math.log2(math.e)
NEG = -1e30
ROWS = 256


def round_of(a, b, n):
    if n & (n - 1) == 0:
        return a ^ b
    return lax.rem(b - a + n, n)


def pairs_of(k, n):
    if n & (n - 1) == 0:
        return [(p, p ^ k) for p in range(n)]
    return [(p, (p + k) % n) for p in range(n)]


def order_of(n):
    rest = range(1, n)
    return sorted(rest, key=lambda k: (bin(k).count("1"), k))


def gather_kernel(n, most, per_device, order, lists_ref, pslot_ref, qslot_ref, cache_ref, *refs):
    recv_ref, own_row_ref = refs[0], refs[1]
    outs = refs[2 : 2 + len(order)]
    send_row, send_cnt, recv_cnt, buf, in_sem, out_sem = refs[2 + len(order) :]
    me = lax.axis_index("pass")
    pass_dev = cache_ref.shape[0]
    topp, nq = lists_ref.shape
    for k in range(n):
        send_cnt[k] = 0
        recv_cnt[k] = 0
    for i in range(n * most):
        recv_ref[i] = -1
        send_row[i] = 0

    def question(q, carry):
        slot = qslot_ref[q]
        dest = slot // per_device
        local = slot - dest * per_device
        k_send = round_of(me, dest, n)
        for t in range(topp):
            row = pslot_ref[lists_ref[t, q]]
            owner = row // pass_dev

            @pl.when(owner == me)
            def _():
                count = send_cnt[k_send]
                send_row[k_send * most + count] = row - owner * pass_dev
                send_cnt[k_send] = count + 1

            @pl.when(dest == me)
            def _():
                k = round_of(owner, me, n)
                count = recv_cnt[k]
                recv_ref[k * most + count] = local
                recv_cnt[k] = count + 1

        return carry

    lax.fori_loop(0, nq, question, 0)
    for r in range(most):
        own_row_ref[r] = send_row[r]
    copies = []
    for j, k in enumerate(order):
        for r in range(most):
            i = j * most + r
            get = pltpu.make_async_copy(
                cache_ref.at[send_row[k * most + r]], buf.at[i], in_sem.at[i]
            )
            get.start()
            copies.append((get, pltpu.make_async_copy(buf.at[i], outs[j].at[r], out_sem.at[i])))
    for get, put in copies:
        get.wait()
        put.start()
    for get, put in copies:
        put.wait()


def gather(lists, passage_slot, question_slot, cache, n, most, per_device, order):
    item = cache.shape[1:]
    slots = (n - 1) * most
    smem = pl.BlockSpec(memory_space=pltpu.SMEM)
    anyspace = pl.BlockSpec(memory_space=pl.ANY)
    return pl.pallas_call(
        functools.partial(gather_kernel, n, most, per_device, order),
        out_shape=[
            jax.ShapeDtypeStruct((n * most,), jnp.int32),
            jax.ShapeDtypeStruct((most,), jnp.int32),
        ]
        + [jax.ShapeDtypeStruct((most,) + item, cache.dtype)] * len(order),
        in_specs=[smem, smem, smem, anyspace],
        out_specs=[smem, smem] + [anyspace] * len(order),
        scratch_shapes=[
            pltpu.SMEM((n * most,), jnp.int32),
            pltpu.SMEM((n,), jnp.int32),
            pltpu.SMEM((n,), jnp.int32),
            pltpu.VMEM((slots,) + item, cache.dtype),
            pltpu.SemaphoreType.DMA((slots,)),
            pltpu.SemaphoreType.DMA((slots,)),
        ],
        name="gather_items",
        cost_estimate=pl.CostEstimate(
            flops=0, bytes_accessed=2 * slots * math.prod(item) * 2, transcendentals=0
        ),
    )(lists.T, passage_slot, question_slot, cache)


def block_step(q_ref, m_ref, l_ref, acc_ref, question, head, keys, values, causal):
    rows = q_ref.shape[2]
    step = min(ROWS, rows)
    width = keys.shape[0]
    ones = jnp.ones(values.shape, values.dtype)
    extended = jnp.concatenate([values, ones], axis=1)
    for start in range(0, rows, step):
        part = pl.ds(start, step)
        q = q_ref[question, head, part, :]
        scores = (
            lax.dot_general(q, keys, (((1,), (1,)), ((), ())), preferred_element_type=jnp.float32)
            * COEF
        )
        if causal:
            token = lax.broadcasted_iota(jnp.int32, scores.shape, 0) % LQ
            column = lax.broadcasted_iota(jnp.int32, scores.shape, 1)
            scores = jnp.where(column <= token, scores, NEG)
        old = m_ref[question, head, part, :]
        new = jnp.maximum(old, jnp.max(scores, axis=1, keepdims=True))
        weights = jnp.exp2(scores - jnp.concatenate([new] * (width // HD), axis=1))
        mixed = jnp.dot(
            weights.astype(jnp.bfloat16), extended, preferred_element_type=jnp.float32
        )
        alpha = jnp.exp2(old - new)
        m_ref[question, head, part, :] = new
        l_ref[question, head, part, :] = l_ref[question, head, part, :] * alpha + mixed[:, HD:]
        acc_ref[question, head, part, :] = (
            acc_ref[question, head, part, :] * alpha + mixed[:, :HD]
        )


def attend_kernel(first, last, rounds, most, *refs):
    refs = list(refs)
    recv_ref, q_ref = refs.pop(0), refs.pop(0)
    if first:
        row_ref, own_ref, cache_ref = refs.pop(0), refs.pop(0), refs.pop(0)
        sources = None
        entries = most
    else:
        state_in = [refs.pop(0) for _ in range(3)]
        sources = [refs.pop(0) for _ in rounds]
        entries = len(rounds) * most
    if last:
        out_ref = refs.pop(0)
        m_ref, l_ref, acc_ref = [refs.pop(0) for _ in range(3)]
    else:
        m_ref, l_ref, acc_ref = [refs.pop(0) for _ in range(3)]
    buf, sem = refs
    per_device, heads = q_ref.shape[0], q_ref.shape[1]

    def fetch(i, slot):
        if first:
            pltpu.make_async_copy(cache_ref.at[row_ref[i]], buf.at[slot], sem.at[slot]).start()
            return
        for j in range(len(rounds)):

            @pl.when(i // most == j)
            def _():
                pltpu.make_async_copy(
                    sources[j].at[i - j * most], buf.at[slot], sem.at[slot]
                ).start()

    def tag_of(i):
        if first:
            return recv_ref[i]
        k = jnp.int32(0)
        for j, value in enumerate(rounds):
            k = jnp.where(i // most == j, value, k)
        return recv_ref[k * most + lax.rem(i, most)]

    fetch(jnp.int32(0), 0)
    if first:
        m_ref[...] = jnp.full(m_ref.shape, NEG, jnp.float32)
        l_ref[...] = jnp.zeros(l_ref.shape, jnp.float32)
        acc_ref[...] = jnp.zeros(acc_ref.shape, jnp.float32)

        def own_block(question, carry):
            for head in range(heads):
                block = own_ref[question, head]
                block_step(
                    q_ref, m_ref, l_ref, acc_ref, question, head, block[:, :HD], block[:, HD:], True
                )
            return carry

        lax.fori_loop(0, per_device, own_block, 0)
    else:
        m_ref[...] = state_in[0][...]
        l_ref[...] = state_in[1][...]
        acc_ref[...] = state_in[2][...]

    def item(i, carry):
        slot = lax.rem(i, 2)
        pltpu.make_async_copy(buf.at[slot], buf.at[slot], sem.at[slot]).wait()

        @pl.when(i + 1 < entries)
        def _():
            fetch(i + 1, lax.rem(i + 1, 2))

        tag = tag_of(i)

        @pl.when(tag >= 0)
        def _():
            for head in range(heads):
                block_step(
                    q_ref,
                    m_ref,
                    l_ref,
                    acc_ref,
                    tag,
                    head,
                    buf[slot, head, :, :HD],
                    buf[slot, head, :, HD:],
                    False,
                )

        return carry

    lax.fori_loop(0, entries, item, 0)
    if last:
        for question in range(per_device):
            for head in range(heads):
                for g in range(GROUP):
                    part = pl.ds(g * LQ, LQ)
                    column = (head * GROUP + g) * HD
                    out_ref[pl.ds(question * LQ, LQ), pl.ds(column, HD)] = (
                        acc_ref[question, head, part, :] / l_ref[question, head, part, :]
                    ).astype(out_ref.dtype)


def attend_call(first, last, rounds, most, recv, q, rest, item):
    per_device, heads, rows, _ = q.shape
    state = jax.ShapeDtypeStruct(q.shape, jnp.float32)
    smem = pl.BlockSpec(memory_space=pltpu.SMEM)
    vmem = pl.BlockSpec(memory_space=pltpu.VMEM)
    anyspace = pl.BlockSpec(memory_space=pl.ANY)
    if first:
        in_specs = [smem, vmem, smem, vmem, anyspace]
        entries = most
    else:
        in_specs = [smem, vmem] + [vmem] * 3 + [anyspace] * len(rounds)
        entries = most * len(rounds)
    scratch = [pltpu.VMEM((2,) + item, q.dtype), pltpu.SemaphoreType.DMA((2,))]
    if last:
        out_shape = jax.ShapeDtypeStruct((per_device * LQ, heads * GROUP * HD), q.dtype)
        out_specs = vmem
        scratch = [pltpu.VMEM(q.shape, jnp.float32)] * 3 + scratch
    else:
        out_shape = [state] * 3
        out_specs = [vmem] * 3
    weights = entries * heads * rows * item[1]
    return pl.pallas_call(
        functools.partial(attend_kernel, first, last, rounds, most),
        out_shape=out_shape,
        in_specs=in_specs,
        out_specs=out_specs,
        scratch_shapes=scratch,
        name="attend_first" if first else ("attend_last" if last else "attend_more"),
        cost_estimate=pl.CostEstimate(
            flops=weights * HD * 4,
            bytes_accessed=entries * math.prod(item) * 2,
            transcendentals=weights,
        ),
    )(recv, q, *rest)


def weight_blocks(own, n):
    if n & (n - 1):
        return [lax.all_gather(own, "pass", axis=1, tiled=True)]
    have = {0: own}
    bit = n // 2
    while bit:
        for k in list(have):
            have[k ^ bit] = lax.ppermute(have[k], "pass", pairs_of(bit, n))
        bit //= 2
    return [have[k] for k in range(n)]


def project(context, weights):
    parts = [
        jnp.dot(context, weight, preferred_element_type=jnp.float32).astype(jnp.bfloat16)
        for weight in weights
    ]
    me = lax.axis_index("pass")
    bit = len(parts) // 2
    while bit:
        swap = (me & bit) != 0
        parts = [jnp.where(swap, parts[k ^ bit], parts[k]) for k in range(len(parts))]
        bit //= 2
    return jnp.concatenate(parts, axis=1)


def body(queries, own_kv, passage_cache, out_weight, lists, passage_slot, question_slot):
    n = lax.axis_size("pass")
    per_device = queries.shape[0] // LQ
    heads = own_kv.shape[1]
    entries = per_device * lists.shape[1]
    most = (entries + n - 1) // n
    order = order_of(n)
    cache = jnp.transpose(passage_cache, (0, 2, 1, 3))
    recv, own_row, *items = gather(
        lists, passage_slot, question_slot, cache, n, most, per_device, order
    )
    arrived = [
        lax.ppermute(item, "pass", pairs_of(k, n)) for k, item in zip(order, items)
    ]
    weights = weight_blocks(out_weight, n)
    q = (
        queries.reshape(per_device, LQ, heads, GROUP, HD)
        .transpose(0, 2, 3, 1, 4)
        .reshape(per_device, heads, GROUP * LQ, HD)
    )
    own = own_kv.reshape(per_device, LQ, heads, 2 * HD).transpose(0, 2, 1, 3)
    item = cache.shape[1:]
    state = attend_call(True, False, (0,), most, recv, q, (own_row, own, cache), item)
    calls = 3
    bounds = [len(order) * i // calls for i in range(calls + 1)]
    for i in range(calls):
        rounds = tuple(order[bounds[i] : bounds[i + 1]])
        rest = tuple(state) + tuple(arrived[bounds[i] : bounds[i + 1]])
        state = attend_call(False, i == calls - 1, rounds, most, recv, q, rest, item)
    context = state
    return lax.psum_scatter(project(context, weights), "head", scatter_dimension=1, tiled=True)


LINE = 4
EXTRA = 8
ITEM_ORDER = (2, 0, 3, 1)
VMEM_BYTES = 67043328


def mirror(k, ends=None):
    pairs = [(p, p ^ int(2 * k)) for p in range(2 * LINE)]
    if ends is None:
        return pairs
    return [(p, d) for p, d in pairs if (p // 2 in (0, LINE - 1)) == (ends == "outer")]


def is_inner():
    z = lax.axis_index("pass") // 2
    return jnp.logical_and(z > 0, z < LINE - 1)


def sort_kernel(most, per_device, lists_ref, pslot_ref, qslot_ref, cache_ref, *refs):
    row_ref, tag_ref, far_tag_ref = refs[:3]
    outs = refs[3 : 3 + LINE]
    send_row, near_cnt, send_cnt, far_cnt, buf, in_sem, out_sem = refs[3 + LINE :]
    me = lax.axis_index("pass")
    z, x = me // 2, me % 2
    pass_dev = cache_ref.shape[0]
    topp, nq = lists_ref.shape
    for k in range(LINE):
        near_cnt[k] = 0
        send_cnt[k] = 0
        far_cnt[k] = 0

    def take(i):
        return pltpu.make_async_copy(cache_ref.at[send_row[i]], buf.at[i], in_sem.at[i])

    def question(q, carry):
        slot = qslot_ref[q]
        dest = slot // per_device
        local = slot - dest * per_device
        k = (dest // 2) ^ z

        @pl.when(dest % 2 == x)
        def _():
            for t in range(topp):
                row = pslot_ref[lists_ref[t, q]]
                owner = row // pass_dev

                @pl.when(owner == me)
                def _():
                    at = k * most + near_cnt[k]
                    row_ref[at] = row - owner * pass_dev
                    tag_ref[at] = local
                    near_cnt[k] = near_cnt[k] + 1

                @pl.when(owner == (me ^ 1))
                def _():
                    far_tag_ref[k * most + far_cnt[k]] = local
                    far_cnt[k] = far_cnt[k] + 1

        @pl.when(dest % 2 != x)
        def _():
            for t in range(topp):
                row = pslot_ref[lists_ref[t, q]]
                owner = row // pass_dev

                @pl.when(owner == me)
                def _():
                    at = k * most + send_cnt[k]
                    send_row[at] = row - owner * pass_dev
                    send_cnt[k] = send_cnt[k] + 1
                    take(at).start()

        return carry

    lax.fori_loop(0, nq, question, 0)
    slots = [k * most + r for k in ITEM_ORDER for r in range(most)]
    puts = [pltpu.make_async_copy(buf.at[i], outs[i // most].at[i % most], out_sem.at[i]) for i in slots]
    for i, put in zip(slots, puts):
        take(i).wait()
        put.start()
    for put in puts:
        put.wait()


def sort_items(lists, passage_slot, question_slot, cache, most, per_device):
    item = cache.shape[1:]
    slots = LINE * most
    smem = pl.BlockSpec(memory_space=pltpu.SMEM)
    anyspace = pl.BlockSpec(memory_space=pl.ANY)
    return pl.pallas_call(
        functools.partial(sort_kernel, most, per_device),
        out_shape=[jax.ShapeDtypeStruct((slots,), jnp.int32)] * 3
        + [jax.ShapeDtypeStruct((most,) + item, cache.dtype)] * LINE,
        in_specs=[smem, smem, smem, anyspace],
        out_specs=[smem] * 3 + [anyspace] * LINE,
        scratch_shapes=[
            pltpu.SMEM((slots,), jnp.int32),
            pltpu.SMEM((LINE,), jnp.int32),
            pltpu.SMEM((LINE,), jnp.int32),
            pltpu.SMEM((LINE,), jnp.int32),
            pltpu.VMEM((slots,) + item, cache.dtype),
            pltpu.SemaphoreType.DMA((slots,)),
            pltpu.SemaphoreType.DMA((slots,)),
        ],
        compiler_params=pltpu.CompilerParams(vmem_limit_bytes=VMEM_BYTES),
        name="sort_items",
        cost_estimate=pl.CostEstimate(
            flops=0, bytes_accessed=2 * slots * math.prod(item) * 2, transcendentals=0
        ),
    )(lists.T, passage_slot, question_slot, cache)


def unit():
    r = lax.broadcasted_iota(jnp.int32, (LQ, LQ), 0)
    c = lax.broadcasted_iota(jnp.int32, (LQ, LQ), 1)
    return r == c


def part_step(q_ref, m_ref, l_ref, acc_ref, question, head, keys, values, causal):
    rows = GROUP * LQ
    width = keys.shape[0]
    ones = jnp.ones(values.shape, values.dtype)
    extended = jnp.concatenate([values, ones], axis=1)
    tokens = pl.ds(pl.multiple_of(question * LQ, LQ), LQ)
    for start in range(0, rows, ROWS):
        part = pl.ds(start, ROWS)
        q = jnp.concatenate(
            [
                q_ref[tokens, pl.ds(pl.multiple_of((head * GROUP + g) * HD, HD), HD)]
                for g in range(start // LQ, (start + ROWS) // LQ)
            ],
            axis=0,
        )
        scores = (
            lax.dot_general(q, keys, (((1,), (1,)), ((), ())), preferred_element_type=jnp.float32)
            * COEF
        )
        if causal:
            token = lax.broadcasted_iota(jnp.int32, scores.shape, 0) % LQ
            column = lax.broadcasted_iota(jnp.int32, scores.shape, 1)
            scores = jnp.where(column <= token, scores, NEG)
        old = m_ref[question, head, part, :]
        new = jnp.maximum(old, jnp.max(scores, axis=1, keepdims=True))
        weights = jnp.exp2(scores - jnp.concatenate([new] * (width // HD), axis=1))
        mixed = jnp.dot(
            weights.astype(jnp.bfloat16), extended, preferred_element_type=jnp.float32
        )
        alpha = jnp.exp2(old - new)
        m_ref[question, head, part, :] = new
        l_ref[question, head, part, :] = l_ref[question, head, part, :] * alpha + mixed[:, HD:]
        acc_ref[question, head, part, :] = (
            acc_ref[question, head, part, :] * alpha + mixed[:, :HD]
        )


def part_kernel(k, most, first, last, heads, *refs):
    refs = list(refs)
    row_ref, tag_ref, far_tag_ref = refs.pop(0), refs.pop(0), refs.pop(0)
    own_ref = refs.pop(0) if k == 0 else None
    questions = [refs.pop(0) for _ in range(2 if k > 1 else 1)]
    cache_ref = refs.pop(0)
    items_ref = refs.pop(0) if last > most else None
    out_ref, q_ref, m_ref, l_ref, acc_ref, buf, sem, q_sem = refs
    per_device = q_ref.shape[0] // LQ

    def fetch(i, slot):
        if first < most:

            @pl.when(i < most)
            def _():
                row = row_ref[k * most + jnp.minimum(i, most - 1)]
                pltpu.make_async_copy(cache_ref.at[row], buf.at[slot], sem.at[slot]).start()

        if last > most:

            @pl.when(i >= most)
            def _():
                pltpu.make_async_copy(
                    items_ref.at[jnp.maximum(i - most, 0)], buf.at[slot], sem.at[slot]
                ).start()

    if len(questions) == 1:
        pltpu.make_async_copy(questions[0], q_ref, q_sem).start()
    else:
        inner = is_inner()

        @pl.when(inner)
        def _():
            pltpu.make_async_copy(questions[0], q_ref, q_sem).start()

        @pl.when(jnp.logical_not(inner))
        def _():
            pltpu.make_async_copy(questions[1], q_ref, q_sem).start()

    fetch(jnp.int32(first), first % 2)
    m_ref[...] = jnp.full(m_ref.shape, NEG, jnp.float32)
    l_ref[...] = jnp.zeros(l_ref.shape, jnp.float32)
    acc_ref[...] = jnp.zeros(acc_ref.shape, jnp.float32)
    pltpu.make_async_copy(q_ref, q_ref, q_sem).wait()
    if k == 0:

        def own_block(i, carry):
            question, head = i // heads, lax.rem(i, heads)
            part_step(
                q_ref,
                m_ref,
                l_ref,
                acc_ref,
                question,
                head,
                own_ref[question, head, :, :HD],
                own_ref[question, head, :, HD:],
                True,
            )
            return carry

        lax.fori_loop(0, per_device * heads, own_block, 0)

    def item(i, carry):
        slot = lax.rem(i, 2)
        pltpu.make_async_copy(buf.at[slot], buf.at[slot], sem.at[slot]).wait()

        @pl.when(i + 1 < last)
        def _():
            fetch(i + 1, lax.rem(i + 1, 2))

        at = k * most + lax.rem(i, most)
        tag = jnp.where(i < most, tag_ref[at], far_tag_ref[at])

        for head in range(heads):
            part_step(
                q_ref,
                m_ref,
                l_ref,
                acc_ref,
                tag,
                head,
                buf[slot, head, :, :HD],
                buf[slot, head, :, HD:],
                False,
            )
        return carry

    lax.fori_loop(first, last, item, 0)
    eye = unit()

    def close(c, carry):
        head, g = c // GROUP, lax.rem(c, GROUP)
        columns = pl.ds(pl.multiple_of(c * HD, HD), HD)
        part = pl.ds(pl.multiple_of(g * LQ, LQ), LQ)
        for question in range(per_device):
            total = l_ref[question, head, part, :]
            some = total > 0.0
            safe = jnp.where(some, total, 1.0)
            out_ref[question, :LQ, columns] = (
                acc_ref[question, head, part, :] / safe
            ).astype(out_ref.dtype)
            level = jnp.where(some, m_ref[question, head, part, :] + jnp.log2(safe), NEG)
            line = jnp.sum(jnp.where(eye, level, 0.0), axis=0, keepdims=True)
            store_level(out_ref, question, columns, line)
        return carry

    lax.fori_loop(0, heads * GROUP, close, 0)


def store_level(out_ref, question, columns, line):
    row_of = lax.broadcasted_iota(jnp.int32, (EXTRA, line.shape[1]), 0)
    high = line.astype(jnp.bfloat16).astype(jnp.float32)
    both = jnp.where(row_of == 0, high, jnp.where(row_of == 1, line - high, 0.0))
    out_ref[question, LQ:, columns] = both.astype(out_ref.dtype)


def part_call(k, most, tables, own, questions, cache, items, local=True):
    tokens, columns = questions[0].shape
    heads, item = cache.shape[1], cache.shape[1:]
    state = (tokens // LQ, heads, GROUP * LQ, HD)
    smem = pl.BlockSpec(memory_space=pltpu.SMEM)
    vmem = pl.BlockSpec(memory_space=pltpu.VMEM)
    anyspace = pl.BlockSpec(memory_space=pl.ANY)
    owned = [own] if k == 0 else []
    received = [items] if items is not None else []
    first, last = 0 if local else most, 2 * most if received else most
    weights = (last - first) * heads * GROUP * LQ * item[1]
    return pl.pallas_call(
        functools.partial(part_kernel, k, most, first, last, heads),
        out_shape=jax.ShapeDtypeStruct((tokens // LQ, LQ + EXTRA, columns), cache.dtype),
        in_specs=[smem] * 3
        + [vmem] * len(owned)
        + [anyspace] * (len(questions) + 1 + len(received)),
        out_specs=vmem,
        scratch_shapes=[
            pltpu.VMEM((tokens, columns), cache.dtype),
            pltpu.VMEM(state, jnp.float32),
            pltpu.VMEM(state, jnp.float32),
            pltpu.VMEM(state, jnp.float32),
            pltpu.VMEM((2,) + item, cache.dtype),
            pltpu.SemaphoreType.DMA((2,)),
            pltpu.SemaphoreType.DMA,
        ],
        compiler_params=pltpu.CompilerParams(vmem_limit_bytes=VMEM_BYTES),
        cost_estimate=pl.CostEstimate(
            flops=weights * HD * 4,
            bytes_accessed=(last - first) * math.prod(item) * 2,
            transcendentals=weights,
        ),
    )(*tables, *owned, *questions, cache, *received)


def blend(refs, out_ref, leveled):
    eye = unit()
    ones = jnp.ones((2 * LQ, LQ), jnp.bfloat16)

    def level_of(ref):
        both = ref[0, LQ:, :].astype(jnp.float32)
        return both[:1] + both[1:2]

    levels = [level_of(ref) for ref in refs]
    top = functools.reduce(jnp.maximum, levels)
    weights = [jnp.exp2(level - top) for level in levels]
    total = functools.reduce(jnp.add, weights)
    shares = []
    for weight in weights[1:]:
        share = weight / total
        high = share.astype(jnp.bfloat16).astype(jnp.float32)
        shares.append((high, share - high))
    for c in range(total.shape[1] // HD):
        columns = slice(c * HD, (c + 1) * HD)
        base = refs[0][0, :LQ, columns].astype(jnp.float32)
        value = base
        for ref, pair in zip(refs[1:], shares):
            spread = jnp.concatenate(
                [
                    jnp.where(eye, jnp.broadcast_to(v[:, columns], (LQ, LQ)), 0.0).astype(
                        jnp.bfloat16
                    )
                    for v in pair
                ],
                axis=1,
            )
            column = jnp.dot(spread, ones, preferred_element_type=jnp.float32)
            value = value + (ref[0, :LQ, columns].astype(jnp.float32) - base) * column
        value = value.astype(out_ref.dtype)
        if leveled:
            out_ref[0, :LQ, columns] = value
        else:
            out_ref[:, columns] = value
    if leveled:
        store_level(out_ref, 0, slice(None), top + jnp.log2(total))


def merge_kernel(*refs):
    *parts, out_ref = refs
    inner = is_inner()

    @pl.when(inner)
    def _():
        blend(parts, out_ref, True)

    @pl.when(jnp.logical_not(inner))
    def _():
        if len(parts) > 2:
            blend(parts[:-1], out_ref, True)
        else:
            out_ref[...] = parts[0][...]


def finish_kernel(a_ref, b_ref, out_ref):
    blend((a_ref, b_ref), out_ref, False)


def question_spec(value, at):
    shape = (1,) + value.shape[1:]
    if value.shape[0] == 1:
        return pl.BlockSpec(shape, lambda q: (0, 0, 0))
    return pl.BlockSpec(shape, lambda q: (at, 0, 0))


def join_call(parts, at, leveled):
    columns = parts[0].shape[2]
    if leveled:
        shape = (1,) + parts[0].shape[1:]
        out_spec = pl.BlockSpec(shape, lambda q: (0, 0, 0))
    else:
        shape = (LQ, columns)
        out_spec = pl.BlockSpec(shape, lambda q: (0, 0))
    size = LQ * columns
    return pl.pallas_call(
        merge_kernel if leveled else finish_kernel,
        out_shape=jax.ShapeDtypeStruct(shape, parts[0].dtype),
        grid=(1,),
        in_specs=[question_spec(part, at) for part in parts],
        out_specs=out_spec,
        compiler_params=pltpu.CompilerParams(vmem_limit_bytes=VMEM_BYTES),
        cost_estimate=pl.CostEstimate(flops=size * 8, bytes_accessed=size * 6, transcendentals=0),
    )(*parts)


def line_steps(queries, own_kv, passage_cache, out_weight, lists, passage_slot, question_slot):
    per_device = queries.shape[0] // LQ
    heads = own_kv.shape[1]
    most = per_device * lists.shape[1] // (2 * LINE)

    def send(value, pairs):
        return lax.ppermute(value, "pass", pairs)

    def part(k, *args, local=True):
        return part_call(k, most, tables, own if k == 0 else None, *args, local=local)

    def join(at, *parts, leveled=True):
        return join_call(parts, at, leveled)

    across = [(p, p ^ 1) for p in range(2 * LINE)]
    inner_across = [(p, d) for p, d in across if p // 2 in (1, 2)]
    outer_across = [(p, d) for p, d in across if p // 2 not in (1, 2)]
    near, middle = mirror(1), mirror(3, "inner")
    inward, outward = mirror(1, "outer"), mirror(1, "inner")
    q_near = send(queries, near)
    q_mid = send(queries, middle)
    half = out_weight.shape[0] // 2
    w_across0 = send(out_weight[:half], across)
    cache = jnp.transpose(passage_cache, (0, 2, 1, 3))
    row, tag, far_tag, *items = sort_items(
        lists, passage_slot, question_slot, cache, most, per_device
    )
    tables = (row, tag, far_tag)
    later, _ = lax.optimization_barrier((out_weight, row))
    w_across1 = send(later[half:], across)
    q_out = send(q_mid, outward)
    q_cross = send(q_near, middle)
    q_end = send(q_cross, outward)
    far = [send(items[k], across) for k in range(LINE)]
    own = own_kv.reshape(per_device, LQ, heads, 2 * HD).transpose(0, 2, 1, 3)
    part2 = part(2, [q_cross, q_out], cache, far[2])
    part3 = part(3, [q_mid, q_end], cache, far[3])
    part0 = part(0, [queries], cache, far[0])
    part1 = part(1, [q_near], cache, None)
    part1_far = part(1, [q_near], cache, far[1], local=False)
    back2 = send(part2, inward)
    w_in = send(out_weight, mirror(2, "outer"))
    w_out = send(out_weight, mirror(2, "inner"))
    back3 = send(part3, inward)
    w_in_both = send(w_in, inner_across)
    w_out_both = send(w_out, outer_across)
    own_pairs, near_rows, near_pairs = [], [], []
    for q in range(per_device):
        cross3 = send(join(q, part3, back2), middle)
        near0 = join(q, part0, cross3)
        beside = send(near0, near)
        cross2 = send(join(q, part2, back3), middle)
        near1 = join(q, part1, part1_far, cross2)
        back1 = send(near1, near)
        own_pairs += [near0, back1]
        if q + 1 < per_device:
            near_rows.append(join(q, near1, beside, leveled=False))
        else:
            near_pairs += [near1, beside]
    weights = (out_weight, w_across0, w_across1, w_in, w_in_both, w_out, w_out_both)
    far_sums = project_call(near_rows, near_pairs, weights, None)
    return project_call([], own_pairs, weights, far_sums)


MESH = pl.DeviceIdType.MESH


def at_home():
    return lax.axis_index("head") % 2 == lax.axis_index("pass") // 2 % 2


def project_kernel(done, pieces, far, *refs):
    rows_refs = refs[:pieces]
    own_ref, a0_ref, a1_ref, in_ref, in2_ref, out1_ref, out2_ref = refs[pieces : pieces + 7]
    refs = refs[pieces + 7 :]
    if not far:
        far_ref, *refs = refs
    out_ref, context_ref, w_ref, part_ref, core_ref, pair_ref, y_ref, ysend_ref = refs[:8]
    row_sem, w_sem, send_sem, recv_sem = refs[8:]
    me, head = lax.axis_index("pass"), lax.axis_index("head")
    z, x, y = me // 2, me % 2, head // 2
    wide = w_ref.shape[3]
    inner = is_inner()
    core_peer, y_peer, z_peer = (me, head ^ 1), (me, head ^ 2), (me ^ 2, head ^ 1)
    home = at_home()
    sums = jnp.logical_not(home) if far else home

    row_loads = [
        pltpu.make_async_copy(ref, pair_ref.at[i // 2, i % 2], row_sem.at[done + i])
        for i, ref in enumerate(rows_refs[done:])
    ]
    row_loads += [
        pltpu.make_async_copy(ref, context_ref.at[pl.ds(i * LQ, LQ)], row_sem.at[i])
        for i, ref in enumerate(rows_refs[:done])
    ]
    for load in row_loads:
        load.start()

    def load_here():
        pltpu.make_async_copy(own_ref, w_ref.at[0, x], w_sem.at[0, x]).start()
        half = a0_ref.shape[0]
        low, high = w_ref.at[0, 1 - x, pl.ds(0, half)], w_ref.at[0, 1 - x, pl.ds(half, half)]
        pltpu.make_async_copy(a0_ref, low, w_sem.at[0, 1 - x]).start()
        pltpu.make_async_copy(a1_ref, high, w_sem.at[0, 1 - x]).start()

    def load_there():
        for which, (one, two) in (
            (inner, (in_ref, in2_ref)),
            (jnp.logical_not(inner), (out1_ref, out2_ref)),
        ):

            @pl.when(which)
            def _():
                pltpu.make_async_copy(one, w_ref.at[1, x], w_sem.at[1, x]).start()
                pltpu.make_async_copy(two, w_ref.at[1, 1 - x], w_sem.at[1, 1 - x]).start()

    here_first = y != z // 2

    @pl.when(here_first)
    def _():
        load_here()
        load_there()

    @pl.when(jnp.logical_not(here_first))
    def _():
        load_there()
        load_here()

    barrier = pltpu.get_barrier_semaphore()
    peers = (core_peer, y_peer) if far else (core_peer, y_peer, z_peer)
    for peer in peers:
        pl.semaphore_signal(barrier, inc=1, device_id=peer, device_id_type=MESH)
    pl.semaphore_wait(barrier, len(peers))

    def remote(src, dst, i, peer):
        return pltpu.make_async_remote_copy(
            src_ref=src,
            dst_ref=dst,
            send_sem=send_sem.at[i],
            recv_sem=recv_sem.at[i],
            device_id=peer,
            device_id_type=MESH,
        )

    def columns(j):
        return pl.ds(j * wide, wide)

    core_copies = [
        [remote(part_ref.at[s, j], core_ref.at[s, j], s * 2 + j, core_peer) for j in range(2)]
        for s in range(2)
    ]
    y_copies = [remote(ysend_ref.at[j], y_ref.at[j], 4 + j, y_peer) for j in range(2)]
    if not far:
        z_copies = [
            remote(far_ref.at[j], out_ref.at[:, columns(j)], 6 + j, z_peer) for j in range(2)
        ]

        @pl.when(jnp.logical_not(home))
        def _():
            for copy in z_copies:
                copy.start()

    for load in row_loads:
        load.wait()
    for i in range((pieces - done) // 2):
        pair = (pair_ref.at[i, 0], pair_ref.at[i, 1])
        blend(pair, context_ref.at[pl.ds((done + i) * LQ, LQ)], False)

    def multiply(s, to_y, j):
        here = jnp.where(to_y == z // 2, 0, 1)
        block = w_ref.at[here, j]
        pltpu.make_async_copy(block, block, w_sem.at[here, j]).wait()
        part_ref[s, j] = jnp.dot(
            context_ref[...], w_ref[here, j], preferred_element_type=jnp.float32
        ).astype(part_ref.dtype)

        @pl.when(jnp.logical_not(sums))
        def _():
            core_copies[s][j].start()

    def add_up(s, j):
        @pl.when(sums)
        def _():
            core_copies[s][j].wait_recv()
            value = part_ref[s, j].astype(jnp.float32) + core_ref[s, j].astype(jnp.float32)
            if s == 0:
                ysend_ref[j] = value.astype(ysend_ref.dtype)
                y_copies[j].start()
                return
            y_copies[j].wait_recv()
            total = (value + y_ref[j].astype(jnp.float32)).astype(out_ref.dtype)
            if far:
                out_ref[j] = total
            else:
                out_ref[:, columns(j)] = total

    late = None
    for s, to_y in enumerate((1 - y, y)):
        for j in range(2):
            multiply(s, to_y, j)
            if late is not None:
                add_up(*late)
            late = (s, j)
    add_up(*late)

    @pl.when(jnp.logical_not(sums))
    def _():
        for copies in core_copies:
            for copy in copies:
                copy.wait_send()

    @pl.when(sums)
    def _():
        for copy in y_copies:
            copy.wait_send()

    if not far:

        @pl.when(jnp.logical_not(home))
        def _():
            for copy in z_copies:
                copy.wait()


def project_call(finished, pairs, weights, far_sums):
    own = weights[0]
    pieces = finished + pairs
    rows, (depth, wide) = (len(finished) + len(pairs) // 2) * LQ, own.shape
    dtype = own.dtype
    far = far_sums is None
    vmem = pl.BlockSpec(memory_space=pltpu.VMEM)
    blocks = (2, rows, wide)
    scratch = [
        pltpu.VMEM((rows, depth), dtype),
        pltpu.VMEM((2, 2, depth, wide), dtype),
        pltpu.VMEM((2,) + blocks, dtype),
        pltpu.VMEM((2,) + blocks, dtype),
        pltpu.VMEM((len(pairs) // 2, 2) + pairs[0].shape, dtype),
        pltpu.VMEM(blocks, dtype),
        pltpu.VMEM(blocks, dtype),
        pltpu.SemaphoreType.DMA((len(pieces),)),
        pltpu.SemaphoreType.DMA((2, 2)),
        pltpu.SemaphoreType.DMA((8,)),
        pltpu.SemaphoreType.DMA((8,)),
    ]
    shape = blocks if far else (rows, 2 * wide)
    return pl.pallas_call(
        functools.partial(project_kernel, len(finished), len(pieces), far),
        out_shape=jax.ShapeDtypeStruct(shape, dtype),
        in_specs=[pl.BlockSpec(memory_space=pl.ANY)] * (len(pieces) + len(weights))
        + [vmem] * (0 if far else 1),
        out_specs=vmem,
        scratch_shapes=scratch,
        compiler_params=pltpu.CompilerParams(
            collective_id=int(far), has_side_effects=True, vmem_limit_bytes=VMEM_BYTES
        ),
        name="project_far" if far else "project_home",
        cost_estimate=pl.CostEstimate(
            flops=2 * 4 * rows * depth * wide,
            bytes_accessed=4 * depth * wide * 2,
            transcendentals=0,
        ),
    )(*pieces, *weights, *([] if far else [far_sums]))


def suits_line(mesh, queries, lists):
    passes, heads = mesh.shape["pass"], mesh.shape["head"]
    entries = queries.shape[0] // LQ // passes * lists.shape[1]
    several = queries.shape[0] // LQ >= 2 * passes
    return passes == 2 * LINE and heads == LINE and several and entries % passes == 0


def solution(mesh):
    in_specs = (
        P("pass", "head"),
        P("pass", "head", None),
        P("pass", None, "head", None),
        P("head", "pass"),
        P(),
        P(),
        P(),
    )
    out_specs = P("pass", "head")

    def run(*args):
        if not suits_line(mesh, args[0], args[4]):
            return jax.shard_map(
                body, mesh=mesh, in_specs=in_specs, out_specs=out_specs, check_vma=False
            )(*args)
        step = jax.shard_map(
            line_steps, mesh=mesh, in_specs=in_specs, out_specs=out_specs, check_vma=False
        )
        return step(*args)

    return run
```

```python
import functools
import math

import jax
import jax.numpy as jnp
from jax import lax
from jax.experimental import pallas as pl
from jax.experimental.pallas import tpu as pltpu
from jax.sharding import PartitionSpec as P


H = 64
KVH = 8
HD = 128
LQ = 128
GROUP = H // KVH
COEF = HD ** (-0.5) * math.log2(math.e)
NEG = -1e30
ROWS = 256


def round_of(a, b, n):
    if n & (n - 1) == 0:
        return a ^ b
    return lax.rem(b - a + n, n)


def pairs_of(k, n):
    if n & (n - 1) == 0:
        return [(p, p ^ k) for p in range(n)]
    return [(p, (p + k) % n) for p in range(n)]


def order_of(n):
    rest = range(1, n)
    return sorted(rest, key=lambda k: (bin(k).count("1"), k))


def gather_kernel(n, most, per_device, order, lists_ref, pslot_ref, qslot_ref, cache_ref, *refs):
    recv_ref, own_row_ref = refs[0], refs[1]
    outs = refs[2 : 2 + len(order)]
    send_row, send_cnt, recv_cnt, buf, in_sem, out_sem = refs[2 + len(order) :]
    me = lax.axis_index("pass")
    pass_dev = cache_ref.shape[0]
    topp, nq = lists_ref.shape
    for k in range(n):
        send_cnt[k] = 0
        recv_cnt[k] = 0
    for i in range(n * most):
        recv_ref[i] = -1
        send_row[i] = 0

    def question(q, carry):
        slot = qslot_ref[q]
        dest = slot // per_device
        local = slot - dest * per_device
        k_send = round_of(me, dest, n)
        for t in range(topp):
            row = pslot_ref[lists_ref[t, q]]
            owner = row // pass_dev

            @pl.when(owner == me)
            def _():
                count = send_cnt[k_send]
                send_row[k_send * most + count] = row - owner * pass_dev
                send_cnt[k_send] = count + 1

            @pl.when(dest == me)
            def _():
                k = round_of(owner, me, n)
                count = recv_cnt[k]
                recv_ref[k * most + count] = local
                recv_cnt[k] = count + 1

        return carry

    lax.fori_loop(0, nq, question, 0)
    for r in range(most):
        own_row_ref[r] = send_row[r]
    copies = []
    for j, k in enumerate(order):
        for r in range(most):
            i = j * most + r
            get = pltpu.make_async_copy(
                cache_ref.at[send_row[k * most + r]], buf.at[i], in_sem.at[i]
            )
            get.start()
            copies.append((get, pltpu.make_async_copy(buf.at[i], outs[j].at[r], out_sem.at[i])))
    for get, put in copies:
        get.wait()
        put.start()
    for get, put in copies:
        put.wait()


def gather(lists, passage_slot, question_slot, cache, n, most, per_device, order):
    item = cache.shape[1:]
    slots = (n - 1) * most
    smem = pl.BlockSpec(memory_space=pltpu.SMEM)
    anyspace = pl.BlockSpec(memory_space=pl.ANY)
    return pl.pallas_call(
        functools.partial(gather_kernel, n, most, per_device, order),
        out_shape=[
            jax.ShapeDtypeStruct((n * most,), jnp.int32),
            jax.ShapeDtypeStruct((most,), jnp.int32),
        ]
        + [jax.ShapeDtypeStruct((most,) + item, cache.dtype)] * len(order),
        in_specs=[smem, smem, smem, anyspace],
        out_specs=[smem, smem] + [anyspace] * len(order),
        scratch_shapes=[
            pltpu.SMEM((n * most,), jnp.int32),
            pltpu.SMEM((n,), jnp.int32),
            pltpu.SMEM((n,), jnp.int32),
            pltpu.VMEM((slots,) + item, cache.dtype),
            pltpu.SemaphoreType.DMA((slots,)),
            pltpu.SemaphoreType.DMA((slots,)),
        ],
        name="gather_items",
        cost_estimate=pl.CostEstimate(
            flops=0, bytes_accessed=2 * slots * math.prod(item) * 2, transcendentals=0
        ),
    )(lists.T, passage_slot, question_slot, cache)


def block_step(q_ref, m_ref, l_ref, acc_ref, question, head, keys, values, causal):
    rows = q_ref.shape[2]
    step = min(ROWS, rows)
    width = keys.shape[0]
    ones = jnp.ones(values.shape, values.dtype)
    extended = jnp.concatenate([values, ones], axis=1)
    for start in range(0, rows, step):
        part = pl.ds(start, step)
        q = q_ref[question, head, part, :]
        scores = (
            lax.dot_general(q, keys, (((1,), (1,)), ((), ())), preferred_element_type=jnp.float32)
            * COEF
        )
        if causal:
            token = lax.broadcasted_iota(jnp.int32, scores.shape, 0) % LQ
            column = lax.broadcasted_iota(jnp.int32, scores.shape, 1)
            scores = jnp.where(column <= token, scores, NEG)
        old = m_ref[question, head, part, :]
        new = jnp.maximum(old, jnp.max(scores, axis=1, keepdims=True))
        weights = jnp.exp2(scores - jnp.concatenate([new] * (width // HD), axis=1))
        mixed = jnp.dot(
            weights.astype(jnp.bfloat16), extended, preferred_element_type=jnp.float32
        )
        alpha = jnp.exp2(old - new)
        m_ref[question, head, part, :] = new
        l_ref[question, head, part, :] = l_ref[question, head, part, :] * alpha + mixed[:, HD:]
        acc_ref[question, head, part, :] = (
            acc_ref[question, head, part, :] * alpha + mixed[:, :HD]
        )


def attend_kernel(first, last, rounds, most, *refs):
    refs = list(refs)
    recv_ref, q_ref = refs.pop(0), refs.pop(0)
    if first:
        row_ref, own_ref, cache_ref = refs.pop(0), refs.pop(0), refs.pop(0)
        sources = None
        entries = most
    else:
        state_in = [refs.pop(0) for _ in range(3)]
        sources = [refs.pop(0) for _ in rounds]
        entries = len(rounds) * most
    if last:
        out_ref = refs.pop(0)
        m_ref, l_ref, acc_ref = [refs.pop(0) for _ in range(3)]
    else:
        m_ref, l_ref, acc_ref = [refs.pop(0) for _ in range(3)]
    buf, sem = refs
    per_device, heads = q_ref.shape[0], q_ref.shape[1]

    def fetch(i, slot):
        if first:
            pltpu.make_async_copy(cache_ref.at[row_ref[i]], buf.at[slot], sem.at[slot]).start()
            return
        for j in range(len(rounds)):

            @pl.when(i // most == j)
            def _():
                pltpu.make_async_copy(
                    sources[j].at[i - j * most], buf.at[slot], sem.at[slot]
                ).start()

    def tag_of(i):
        if first:
            return recv_ref[i]
        k = jnp.int32(0)
        for j, value in enumerate(rounds):
            k = jnp.where(i // most == j, value, k)
        return recv_ref[k * most + lax.rem(i, most)]

    fetch(jnp.int32(0), 0)
    if first:
        m_ref[...] = jnp.full(m_ref.shape, NEG, jnp.float32)
        l_ref[...] = jnp.zeros(l_ref.shape, jnp.float32)
        acc_ref[...] = jnp.zeros(acc_ref.shape, jnp.float32)

        def own_block(question, carry):
            for head in range(heads):
                block = own_ref[question, head]
                block_step(
                    q_ref, m_ref, l_ref, acc_ref, question, head, block[:, :HD], block[:, HD:], True
                )
            return carry

        lax.fori_loop(0, per_device, own_block, 0)
    else:
        m_ref[...] = state_in[0][...]
        l_ref[...] = state_in[1][...]
        acc_ref[...] = state_in[2][...]

    def item(i, carry):
        slot = lax.rem(i, 2)
        pltpu.make_async_copy(buf.at[slot], buf.at[slot], sem.at[slot]).wait()

        @pl.when(i + 1 < entries)
        def _():
            fetch(i + 1, lax.rem(i + 1, 2))

        tag = tag_of(i)

        @pl.when(tag >= 0)
        def _():
            for head in range(heads):
                block_step(
                    q_ref,
                    m_ref,
                    l_ref,
                    acc_ref,
                    tag,
                    head,
                    buf[slot, head, :, :HD],
                    buf[slot, head, :, HD:],
                    False,
                )

        return carry

    lax.fori_loop(0, entries, item, 0)
    if last:
        for question in range(per_device):
            for head in range(heads):
                for g in range(GROUP):
                    part = pl.ds(g * LQ, LQ)
                    column = (head * GROUP + g) * HD
                    out_ref[pl.ds(question * LQ, LQ), pl.ds(column, HD)] = (
                        acc_ref[question, head, part, :] / l_ref[question, head, part, :]
                    ).astype(out_ref.dtype)


def attend_call(first, last, rounds, most, recv, q, rest, item):
    per_device, heads, rows, _ = q.shape
    state = jax.ShapeDtypeStruct(q.shape, jnp.float32)
    smem = pl.BlockSpec(memory_space=pltpu.SMEM)
    vmem = pl.BlockSpec(memory_space=pltpu.VMEM)
    anyspace = pl.BlockSpec(memory_space=pl.ANY)
    if first:
        in_specs = [smem, vmem, smem, vmem, anyspace]
        entries = most
    else:
        in_specs = [smem, vmem] + [vmem] * 3 + [anyspace] * len(rounds)
        entries = most * len(rounds)
    scratch = [pltpu.VMEM((2,) + item, q.dtype), pltpu.SemaphoreType.DMA((2,))]
    if last:
        out_shape = jax.ShapeDtypeStruct((per_device * LQ, heads * GROUP * HD), q.dtype)
        out_specs = vmem
        scratch = [pltpu.VMEM(q.shape, jnp.float32)] * 3 + scratch
    else:
        out_shape = [state] * 3
        out_specs = [vmem] * 3
    weights = entries * heads * rows * item[1]
    return pl.pallas_call(
        functools.partial(attend_kernel, first, last, rounds, most),
        out_shape=out_shape,
        in_specs=in_specs,
        out_specs=out_specs,
        scratch_shapes=scratch,
        name="attend_first" if first else ("attend_last" if last else "attend_more"),
        cost_estimate=pl.CostEstimate(
            flops=weights * HD * 4,
            bytes_accessed=entries * math.prod(item) * 2,
            transcendentals=weights,
        ),
    )(recv, q, *rest)


def weight_blocks(own, n):
    if n & (n - 1):
        return [lax.all_gather(own, "pass", axis=1, tiled=True)]
    have = {0: own}
    bit = n // 2
    while bit:
        for k in list(have):
            have[k ^ bit] = lax.ppermute(have[k], "pass", pairs_of(bit, n))
        bit //= 2
    return [have[k] for k in range(n)]


def project(context, weights):
    parts = [
        jnp.dot(context, weight, preferred_element_type=jnp.float32).astype(jnp.bfloat16)
        for weight in weights
    ]
    me = lax.axis_index("pass")
    bit = len(parts) // 2
    while bit:
        swap = (me & bit) != 0
        parts = [jnp.where(swap, parts[k ^ bit], parts[k]) for k in range(len(parts))]
        bit //= 2
    return jnp.concatenate(parts, axis=1)


def body(queries, own_kv, passage_cache, out_weight, lists, passage_slot, question_slot):
    n = lax.axis_size("pass")
    per_device = queries.shape[0] // LQ
    heads = own_kv.shape[1]
    entries = per_device * lists.shape[1]
    most = (entries + n - 1) // n
    order = order_of(n)
    cache = jnp.transpose(passage_cache, (0, 2, 1, 3))
    recv, own_row, *items = gather(
        lists, passage_slot, question_slot, cache, n, most, per_device, order
    )
    arrived = [
        lax.ppermute(item, "pass", pairs_of(k, n)) for k, item in zip(order, items)
    ]
    weights = weight_blocks(out_weight, n)
    q = (
        queries.reshape(per_device, LQ, heads, GROUP, HD)
        .transpose(0, 2, 3, 1, 4)
        .reshape(per_device, heads, GROUP * LQ, HD)
    )
    own = own_kv.reshape(per_device, LQ, heads, 2 * HD).transpose(0, 2, 1, 3)
    item = cache.shape[1:]
    state = attend_call(True, False, (0,), most, recv, q, (own_row, own, cache), item)
    calls = 3
    bounds = [len(order) * i // calls for i in range(calls + 1)]
    for i in range(calls):
        rounds = tuple(order[bounds[i] : bounds[i + 1]])
        rest = tuple(state) + tuple(arrived[bounds[i] : bounds[i + 1]])
        state = attend_call(False, i == calls - 1, rounds, most, recv, q, rest, item)
    context = state
    return lax.psum_scatter(project(context, weights), "head", scatter_dimension=1, tiled=True)


LINE = 4
EXTRA = 8
ITEM_ORDER = (2, 0, 3, 1)
VMEM_BYTES = 67043328


def mirror(k, ends=None):
    pairs = [(p, p ^ int(2 * k)) for p in range(2 * LINE)]
    if ends is None:
        return pairs
    return [(p, d) for p, d in pairs if (p // 2 in (0, LINE - 1)) == (ends == "outer")]


def is_inner():
    z = lax.axis_index("pass") // 2
    return jnp.logical_and(z > 0, z < LINE - 1)


def sort_kernel(most, per_device, lists_ref, pslot_ref, qslot_ref, cache_ref, *refs):
    row_ref, tag_ref, far_tag_ref = refs[:3]
    outs = refs[3 : 3 + LINE]
    send_row, near_cnt, send_cnt, far_cnt, buf, in_sem, out_sem = refs[3 + LINE :]
    me = lax.axis_index("pass")
    z, x = me // 2, me % 2
    pass_dev = cache_ref.shape[0]
    topp, nq = lists_ref.shape
    for k in range(LINE):
        near_cnt[k] = 0
        send_cnt[k] = 0
        far_cnt[k] = 0

    def take(i):
        return pltpu.make_async_copy(cache_ref.at[send_row[i]], buf.at[i], in_sem.at[i])

    def question(q, carry):
        slot = qslot_ref[q]
        dest = slot // per_device
        local = slot - dest * per_device
        k = (dest // 2) ^ z

        @pl.when(dest % 2 == x)
        def _():
            for t in range(topp):
                row = pslot_ref[lists_ref[t, q]]
                owner = row // pass_dev

                @pl.when(owner == me)
                def _():
                    at = k * most + near_cnt[k]
                    row_ref[at] = row - owner * pass_dev
                    tag_ref[at] = local
                    near_cnt[k] = near_cnt[k] + 1

                @pl.when(owner == (me ^ 1))
                def _():
                    far_tag_ref[k * most + far_cnt[k]] = local
                    far_cnt[k] = far_cnt[k] + 1

        @pl.when(dest % 2 != x)
        def _():
            for t in range(topp):
                row = pslot_ref[lists_ref[t, q]]
                owner = row // pass_dev

                @pl.when(owner == me)
                def _():
                    at = k * most + send_cnt[k]
                    send_row[at] = row - owner * pass_dev
                    send_cnt[k] = send_cnt[k] + 1
                    take(at).start()

        return carry

    lax.fori_loop(0, nq, question, 0)
    slots = [k * most + r for k in ITEM_ORDER for r in range(most)]
    puts = [pltpu.make_async_copy(buf.at[i], outs[i // most].at[i % most], out_sem.at[i]) for i in slots]
    for i, put in zip(slots, puts):
        take(i).wait()
        put.start()
    for put in puts:
        put.wait()


def sort_items(lists, passage_slot, question_slot, cache, most, per_device):
    item = cache.shape[1:]
    slots = LINE * most
    smem = pl.BlockSpec(memory_space=pltpu.SMEM)
    anyspace = pl.BlockSpec(memory_space=pl.ANY)
    return pl.pallas_call(
        functools.partial(sort_kernel, most, per_device),
        out_shape=[jax.ShapeDtypeStruct((slots,), jnp.int32)] * 3
        + [jax.ShapeDtypeStruct((most,) + item, cache.dtype)] * LINE,
        in_specs=[smem, smem, smem, anyspace],
        out_specs=[smem] * 3 + [anyspace] * LINE,
        scratch_shapes=[
            pltpu.SMEM((slots,), jnp.int32),
            pltpu.SMEM((LINE,), jnp.int32),
            pltpu.SMEM((LINE,), jnp.int32),
            pltpu.SMEM((LINE,), jnp.int32),
            pltpu.VMEM((slots,) + item, cache.dtype),
            pltpu.SemaphoreType.DMA((slots,)),
            pltpu.SemaphoreType.DMA((slots,)),
        ],
        compiler_params=pltpu.CompilerParams(vmem_limit_bytes=VMEM_BYTES),
        name="sort_items",
        cost_estimate=pl.CostEstimate(
            flops=0, bytes_accessed=2 * slots * math.prod(item) * 2, transcendentals=0
        ),
    )(lists.T, passage_slot, question_slot, cache)


def unit():
    r = lax.broadcasted_iota(jnp.int32, (LQ, LQ), 0)
    c = lax.broadcasted_iota(jnp.int32, (LQ, LQ), 1)
    return r == c


def part_step(q_ref, m_ref, l_ref, acc_ref, question, head, keys, values, causal):
    rows = GROUP * LQ
    width = keys.shape[0]
    ones = jnp.ones(values.shape, values.dtype)
    extended = jnp.concatenate([values, ones], axis=1)
    tokens = pl.ds(pl.multiple_of(question * LQ, LQ), LQ)
    for start in range(0, rows, ROWS):
        part = pl.ds(start, ROWS)
        q = jnp.concatenate(
            [
                q_ref[tokens, pl.ds(pl.multiple_of((head * GROUP + g) * HD, HD), HD)]
                for g in range(start // LQ, (start + ROWS) // LQ)
            ],
            axis=0,
        )
        scores = (
            lax.dot_general(q, keys, (((1,), (1,)), ((), ())), preferred_element_type=jnp.float32)
            * COEF
        )
        if causal:
            token = lax.broadcasted_iota(jnp.int32, scores.shape, 0) % LQ
            column = lax.broadcasted_iota(jnp.int32, scores.shape, 1)
            scores = jnp.where(column <= token, scores, NEG)
        old = m_ref[question, head, part, :]
        new = jnp.maximum(old, jnp.max(scores, axis=1, keepdims=True))
        weights = jnp.exp2(scores - jnp.concatenate([new] * (width // HD), axis=1))
        mixed = jnp.dot(
            weights.astype(jnp.bfloat16), extended, preferred_element_type=jnp.float32
        )
        alpha = jnp.exp2(old - new)
        m_ref[question, head, part, :] = new
        l_ref[question, head, part, :] = l_ref[question, head, part, :] * alpha + mixed[:, HD:]
        acc_ref[question, head, part, :] = (
            acc_ref[question, head, part, :] * alpha + mixed[:, :HD]
        )


def part_kernel(k, most, first, last, heads, *refs):
    refs = list(refs)
    row_ref, tag_ref, far_tag_ref = refs.pop(0), refs.pop(0), refs.pop(0)
    own_ref = refs.pop(0) if k == 0 else None
    questions = [refs.pop(0) for _ in range(2 if k > 1 else 1)]
    cache_ref = refs.pop(0)
    items_ref = refs.pop(0) if last > most else None
    out_ref, q_ref, m_ref, l_ref, acc_ref, buf, sem, q_sem = refs
    per_device = q_ref.shape[0] // LQ

    def fetch(i, slot):
        if first < most:

            @pl.when(i < most)
            def _():
                row = row_ref[k * most + jnp.minimum(i, most - 1)]
                pltpu.make_async_copy(cache_ref.at[row], buf.at[slot], sem.at[slot]).start()

        if last > most:

            @pl.when(i >= most)
            def _():
                pltpu.make_async_copy(
                    items_ref.at[jnp.maximum(i - most, 0)], buf.at[slot], sem.at[slot]
                ).start()

    if len(questions) == 1:
        pltpu.make_async_copy(questions[0], q_ref, q_sem).start()
    else:
        inner = is_inner()

        @pl.when(inner)
        def _():
            pltpu.make_async_copy(questions[0], q_ref, q_sem).start()

        @pl.when(jnp.logical_not(inner))
        def _():
            pltpu.make_async_copy(questions[1], q_ref, q_sem).start()

    fetch(jnp.int32(first), first % 2)
    m_ref[...] = jnp.full(m_ref.shape, NEG, jnp.float32)
    l_ref[...] = jnp.zeros(l_ref.shape, jnp.float32)
    acc_ref[...] = jnp.zeros(acc_ref.shape, jnp.float32)
    pltpu.make_async_copy(q_ref, q_ref, q_sem).wait()
    if k == 0:

        def own_block(i, carry):
            question, head = i // heads, lax.rem(i, heads)
            part_step(
                q_ref,
                m_ref,
                l_ref,
                acc_ref,
                question,
                head,
                own_ref[question, head, :, :HD],
                own_ref[question, head, :, HD:],
                True,
            )
            return carry

        lax.fori_loop(0, per_device * heads, own_block, 0)

    def item(i, carry):
        slot = lax.rem(i, 2)
        pltpu.make_async_copy(buf.at[slot], buf.at[slot], sem.at[slot]).wait()

        @pl.when(i + 1 < last)
        def _():
            fetch(i + 1, lax.rem(i + 1, 2))

        at = k * most + lax.rem(i, most)
        tag = jnp.where(i < most, tag_ref[at], far_tag_ref[at])

        for head in range(heads):
            part_step(
                q_ref,
                m_ref,
                l_ref,
                acc_ref,
                tag,
                head,
                buf[slot, head, :, :HD],
                buf[slot, head, :, HD:],
                False,
            )
        return carry

    lax.fori_loop(first, last, item, 0)
    eye = unit()

    def close(c, carry):
        head, g = c // GROUP, lax.rem(c, GROUP)
        columns = pl.ds(pl.multiple_of(c * HD, HD), HD)
        part = pl.ds(pl.multiple_of(g * LQ, LQ), LQ)
        for question in range(per_device):
            total = l_ref[question, head, part, :]
            some = total > 0.0
            safe = jnp.where(some, total, 1.0)
            out_ref[question, :LQ, columns] = (
                acc_ref[question, head, part, :] / safe
            ).astype(out_ref.dtype)
            level = jnp.where(some, m_ref[question, head, part, :] + jnp.log2(safe), NEG)
            line = jnp.sum(jnp.where(eye, level, 0.0), axis=0, keepdims=True)
            store_level(out_ref, question, columns, line)
        return carry

    lax.fori_loop(0, heads * GROUP, close, 0)


def store_level(out_ref, question, columns, line):
    row_of = lax.broadcasted_iota(jnp.int32, (EXTRA, line.shape[1]), 0)
    high = line.astype(jnp.bfloat16).astype(jnp.float32)
    both = jnp.where(row_of == 0, high, jnp.where(row_of == 1, line - high, 0.0))
    out_ref[question, LQ:, columns] = both.astype(out_ref.dtype)


def part_call(k, most, tables, own, questions, cache, items, local=True):
    tokens, columns = questions[0].shape
    heads, item = cache.shape[1], cache.shape[1:]
    state = (tokens // LQ, heads, GROUP * LQ, HD)
    smem = pl.BlockSpec(memory_space=pltpu.SMEM)
    vmem = pl.BlockSpec(memory_space=pltpu.VMEM)
    anyspace = pl.BlockSpec(memory_space=pl.ANY)
    owned = [own] if k == 0 else []
    received = [items] if items is not None else []
    first, last = 0 if local else most, 2 * most if received else most
    weights = (last - first) * heads * GROUP * LQ * item[1]
    return pl.pallas_call(
        functools.partial(part_kernel, k, most, first, last, heads),
        out_shape=jax.ShapeDtypeStruct((tokens // LQ, LQ + EXTRA, columns), cache.dtype),
        in_specs=[smem] * 3
        + [vmem] * len(owned)
        + [anyspace] * (len(questions) + 1 + len(received)),
        out_specs=vmem,
        scratch_shapes=[
            pltpu.VMEM((tokens, columns), cache.dtype),
            pltpu.VMEM(state, jnp.float32),
            pltpu.VMEM(state, jnp.float32),
            pltpu.VMEM(state, jnp.float32),
            pltpu.VMEM((2,) + item, cache.dtype),
            pltpu.SemaphoreType.DMA((2,)),
            pltpu.SemaphoreType.DMA,
        ],
        compiler_params=pltpu.CompilerParams(vmem_limit_bytes=VMEM_BYTES),
        cost_estimate=pl.CostEstimate(
            flops=weights * HD * 4,
            bytes_accessed=(last - first) * math.prod(item) * 2,
            transcendentals=weights,
        ),
    )(*tables, *owned, *questions, cache, *received)


def blend(refs, out_ref, leveled):
    eye = unit()
    ones = jnp.ones((2 * LQ, LQ), jnp.bfloat16)

    def level_of(ref):
        both = ref[0, LQ:, :].astype(jnp.float32)
        return both[:1] + both[1:2]

    levels = [level_of(ref) for ref in refs]
    top = functools.reduce(jnp.maximum, levels)
    weights = [jnp.exp2(level - top) for level in levels]
    total = functools.reduce(jnp.add, weights)
    shares = []
    for weight in weights[1:]:
        share = weight / total
        high = share.astype(jnp.bfloat16).astype(jnp.float32)
        shares.append((high, share - high))
    for c in range(total.shape[1] // HD):
        columns = slice(c * HD, (c + 1) * HD)
        base = refs[0][0, :LQ, columns].astype(jnp.float32)
        value = base
        for ref, pair in zip(refs[1:], shares):
            spread = jnp.concatenate(
                [
                    jnp.where(eye, jnp.broadcast_to(v[:, columns], (LQ, LQ)), 0.0).astype(
                        jnp.bfloat16
                    )
                    for v in pair
                ],
                axis=1,
            )
            column = jnp.dot(spread, ones, preferred_element_type=jnp.float32)
            value = value + (ref[0, :LQ, columns].astype(jnp.float32) - base) * column
        value = value.astype(out_ref.dtype)
        if leveled:
            out_ref[0, :LQ, columns] = value
        else:
            out_ref[:, columns] = value
    if leveled:
        store_level(out_ref, 0, slice(None), top + jnp.log2(total))


def merge_kernel(*refs):
    *parts, out_ref = refs
    inner = is_inner()

    @pl.when(inner)
    def _():
        blend(parts, out_ref, True)

    @pl.when(jnp.logical_not(inner))
    def _():
        if len(parts) > 2:
            blend(parts[:-1], out_ref, True)
        else:
            out_ref[...] = parts[0][...]


def finish_kernel(a_ref, b_ref, out_ref):
    blend((a_ref, b_ref), out_ref, False)


def question_spec(value, at):
    shape = (1,) + value.shape[1:]
    if value.shape[0] == 1:
        return pl.BlockSpec(shape, lambda q: (0, 0, 0))
    return pl.BlockSpec(shape, lambda q: (at, 0, 0))


def join_call(parts, at, leveled):
    columns = parts[0].shape[2]
    if leveled:
        shape = (1,) + parts[0].shape[1:]
        out_spec = pl.BlockSpec(shape, lambda q: (0, 0, 0))
    else:
        shape = (LQ, columns)
        out_spec = pl.BlockSpec(shape, lambda q: (0, 0))
    size = LQ * columns
    return pl.pallas_call(
        merge_kernel if leveled else finish_kernel,
        out_shape=jax.ShapeDtypeStruct(shape, parts[0].dtype),
        grid=(1,),
        in_specs=[question_spec(part, at) for part in parts],
        out_specs=out_spec,
        compiler_params=pltpu.CompilerParams(vmem_limit_bytes=VMEM_BYTES),
        cost_estimate=pl.CostEstimate(flops=size * 8, bytes_accessed=size * 6, transcendentals=0),
    )(*parts)


def line_steps(queries, own_kv, passage_cache, out_weight, lists, passage_slot, question_slot):
    per_device = queries.shape[0] // LQ
    heads = own_kv.shape[1]
    most = per_device * lists.shape[1] // (2 * LINE)

    def send(value, pairs):
        return lax.ppermute(value, "pass", pairs)

    def part(k, *args, local=True):
        return part_call(k, most, tables, own if k == 0 else None, *args, local=local)

    def join(at, *parts, leveled=True):
        return join_call(parts, at, leveled)

    across = [(p, p ^ 1) for p in range(2 * LINE)]
    inner_across = [(p, d) for p, d in across if p // 2 in (1, 2)]
    outer_across = [(p, d) for p, d in across if p // 2 not in (1, 2)]
    near, middle = mirror(1), mirror(3, "inner")
    inward, outward = mirror(1, "outer"), mirror(1, "inner")
    q_near = send(queries, near)
    q_mid = send(queries, middle)
    quarter = out_weight.shape[0] // 4
    w_across0 = send(out_weight[:quarter], across)
    cache = jnp.transpose(passage_cache, (0, 2, 1, 3))
    row, tag, far_tag, *items = sort_items(
        lists, passage_slot, question_slot, cache, most, per_device
    )
    tables = (row, tag, far_tag)
    later, _ = lax.optimization_barrier((out_weight, row))
    w_across1 = send(later[quarter:], across)
    q_out = send(q_mid, outward)
    q_cross = send(q_near, middle)
    q_end = send(q_cross, outward)
    far = [send(items[k], across) for k in range(LINE)]
    own = own_kv.reshape(per_device, LQ, heads, 2 * HD).transpose(0, 2, 1, 3)
    part2 = part(2, [q_cross, q_out], cache, far[2])
    part3 = part(3, [q_mid, q_end], cache, far[3])
    part0 = part(0, [queries], cache, far[0])
    part1 = part(1, [q_near], cache, None)
    part1_far = part(1, [q_near], cache, far[1], local=False)
    back2 = send(part2, inward)
    w_in = send(out_weight, mirror(2, "outer"))
    w_out = send(out_weight, mirror(2, "inner"))
    back3 = send(part3, inward)
    w_in_both = send(w_in, inner_across)
    w_out_both = send(w_out, outer_across)
    own_pairs, near_rows, near_pairs = [], [], []
    for q in range(per_device):
        cross3 = send(join(q, part3, back2), middle)
        near0 = join(q, part0, cross3)
        beside = send(near0, near)
        cross2 = send(join(q, part2, back3), middle)
        near1 = join(q, part1, part1_far, cross2)
        back1 = send(near1, near)
        own_pairs += [near0, back1]
        if q + 1 < per_device:
            near_rows.append(join(q, near1, beside, leveled=False))
        else:
            near_pairs += [near1, beside]
    weights = (out_weight, w_across0, w_across1, w_in, w_in_both, w_out, w_out_both)
    far_sums = project_call(near_rows, near_pairs, weights, None)
    return project_call([], own_pairs, weights, far_sums)


MESH = pl.DeviceIdType.MESH


def at_home():
    return lax.axis_index("head") % 2 == lax.axis_index("pass") // 2 % 2


def project_kernel(done, pieces, far, *refs):
    rows_refs = refs[:pieces]
    own_ref, a0_ref, a1_ref, in_ref, in2_ref, out1_ref, out2_ref = refs[pieces : pieces + 7]
    refs = refs[pieces + 7 :]
    if not far:
        far_ref, *refs = refs
    out_ref, context_ref, w_ref, part_ref, core_ref, pair_ref, y_ref, ysend_ref = refs[:8]
    row_sem, w_sem, send_sem, recv_sem = refs[8:]
    me, head = lax.axis_index("pass"), lax.axis_index("head")
    z, x, y = me // 2, me % 2, head // 2
    wide = w_ref.shape[3]
    inner = is_inner()
    core_peer, y_peer, z_peer = (me, head ^ 1), (me, head ^ 2), (me ^ 2, head ^ 1)
    home = at_home()
    sums = jnp.logical_not(home) if far else home

    row_loads = [
        pltpu.make_async_copy(ref, pair_ref.at[i // 2, i % 2], row_sem.at[done + i])
        for i, ref in enumerate(rows_refs[done:])
    ]
    row_loads += [
        pltpu.make_async_copy(ref, context_ref.at[pl.ds(i * LQ, LQ)], row_sem.at[i])
        for i, ref in enumerate(rows_refs[:done])
    ]
    for load in row_loads:
        load.start()

    def load_here():
        pltpu.make_async_copy(own_ref, w_ref.at[0, x], w_sem.at[0, x]).start()
        first, rest = a0_ref.shape[0], a1_ref.shape[0]
        low, high = w_ref.at[0, 1 - x, pl.ds(0, first)], w_ref.at[0, 1 - x, pl.ds(first, rest)]
        pltpu.make_async_copy(a0_ref, low, w_sem.at[0, 1 - x]).start()
        pltpu.make_async_copy(a1_ref, high, w_sem.at[0, 1 - x]).start()

    def load_there():
        for which, (one, two) in (
            (inner, (in_ref, in2_ref)),
            (jnp.logical_not(inner), (out1_ref, out2_ref)),
        ):

            @pl.when(which)
            def _():
                pltpu.make_async_copy(one, w_ref.at[1, x], w_sem.at[1, x]).start()
                pltpu.make_async_copy(two, w_ref.at[1, 1 - x], w_sem.at[1, 1 - x]).start()

    here_first = y != z // 2

    @pl.when(here_first)
    def _():
        load_here()
        load_there()

    @pl.when(jnp.logical_not(here_first))
    def _():
        load_there()
        load_here()

    barrier = pltpu.get_barrier_semaphore()
    peers = (core_peer, y_peer) if far else (core_peer, y_peer, z_peer)
    for peer in peers:
        pl.semaphore_signal(barrier, inc=1, device_id=peer, device_id_type=MESH)
    pl.semaphore_wait(barrier, len(peers))

    def remote(src, dst, i, peer):
        return pltpu.make_async_remote_copy(
            src_ref=src,
            dst_ref=dst,
            send_sem=send_sem.at[i],
            recv_sem=recv_sem.at[i],
            device_id=peer,
            device_id_type=MESH,
        )

    def columns(j):
        return pl.ds(j * wide, wide)

    core_copies = [
        [remote(part_ref.at[s, j], core_ref.at[s, j], s * 2 + j, core_peer) for j in range(2)]
        for s in range(2)
    ]
    y_copies = [remote(ysend_ref.at[j], y_ref.at[j], 4 + j, y_peer) for j in range(2)]
    if not far:
        z_copies = [
            remote(far_ref.at[j], out_ref.at[:, columns(j)], 6 + j, z_peer) for j in range(2)
        ]

        @pl.when(jnp.logical_not(home))
        def _():
            for copy in z_copies:
                copy.start()

    for load in row_loads:
        load.wait()
    for i in range((pieces - done) // 2):
        pair = (pair_ref.at[i, 0], pair_ref.at[i, 1])
        blend(pair, context_ref.at[pl.ds((done + i) * LQ, LQ)], False)

    def multiply(s, to_y, j):
        here = jnp.where(to_y == z // 2, 0, 1)
        block = w_ref.at[here, j]
        pltpu.make_async_copy(block, block, w_sem.at[here, j]).wait()
        part_ref[s, j] = jnp.dot(
            context_ref[...], w_ref[here, j], preferred_element_type=jnp.float32
        ).astype(part_ref.dtype)

        @pl.when(jnp.logical_not(sums))
        def _():
            core_copies[s][j].start()

    def add_up(s, j):
        @pl.when(sums)
        def _():
            core_copies[s][j].wait_recv()
            value = part_ref[s, j].astype(jnp.float32) + core_ref[s, j].astype(jnp.float32)
            if s == 0:
                ysend_ref[j] = value.astype(ysend_ref.dtype)
                y_copies[j].start()
                return
            y_copies[j].wait_recv()
            total = (value + y_ref[j].astype(jnp.float32)).astype(out_ref.dtype)
            if far:
                out_ref[j] = total
            else:
                out_ref[:, columns(j)] = total

    late = None
    for s, to_y in enumerate((1 - y, y)):
        for j in range(2):
            multiply(s, to_y, j)
            if late is not None:
                add_up(*late)
            late = (s, j)
    add_up(*late)

    @pl.when(jnp.logical_not(sums))
    def _():
        for copies in core_copies:
            for copy in copies:
                copy.wait_send()

    @pl.when(sums)
    def _():
        for copy in y_copies:
            copy.wait_send()

    if not far:

        @pl.when(jnp.logical_not(home))
        def _():
            for copy in z_copies:
                copy.wait()


def project_call(finished, pairs, weights, far_sums):
    own = weights[0]
    pieces = finished + pairs
    rows, (depth, wide) = (len(finished) + len(pairs) // 2) * LQ, own.shape
    dtype = own.dtype
    far = far_sums is None
    vmem = pl.BlockSpec(memory_space=pltpu.VMEM)
    blocks = (2, rows, wide)
    scratch = [
        pltpu.VMEM((rows, depth), dtype),
        pltpu.VMEM((2, 2, depth, wide), dtype),
        pltpu.VMEM((2,) + blocks, dtype),
        pltpu.VMEM((2,) + blocks, dtype),
        pltpu.VMEM((len(pairs) // 2, 2) + pairs[0].shape, dtype),
        pltpu.VMEM(blocks, dtype),
        pltpu.VMEM(blocks, dtype),
        pltpu.SemaphoreType.DMA((len(pieces),)),
        pltpu.SemaphoreType.DMA((2, 2)),
        pltpu.SemaphoreType.DMA((8,)),
        pltpu.SemaphoreType.DMA((8,)),
    ]
    shape = blocks if far else (rows, 2 * wide)
    return pl.pallas_call(
        functools.partial(project_kernel, len(finished), len(pieces), far),
        out_shape=jax.ShapeDtypeStruct(shape, dtype),
        in_specs=[pl.BlockSpec(memory_space=pl.ANY)] * (len(pieces) + len(weights))
        + [vmem] * (0 if far else 1),
        out_specs=vmem,
        scratch_shapes=scratch,
        compiler_params=pltpu.CompilerParams(
            collective_id=int(far), has_side_effects=True, vmem_limit_bytes=VMEM_BYTES
        ),
        name="project_far" if far else "project_home",
        cost_estimate=pl.CostEstimate(
            flops=2 * 4 * rows * depth * wide,
            bytes_accessed=4 * depth * wide * 2,
            transcendentals=0,
        ),
    )(*pieces, *weights, *([] if far else [far_sums]))


def suits_line(mesh, queries, lists):
    passes, heads = mesh.shape["pass"], mesh.shape["head"]
    entries = queries.shape[0] // LQ // passes * lists.shape[1]
    several = queries.shape[0] // LQ >= 2 * passes
    return passes == 2 * LINE and heads == LINE and several and entries % passes == 0


def solution(mesh):
    in_specs = (
        P("pass", "head"),
        P("pass", "head", None),
        P("pass", None, "head", None),
        P("head", "pass"),
        P(),
        P(),
        P(),
    )
    out_specs = P("pass", "head")

    def run(*args):
        if not suits_line(mesh, args[0], args[4]):
            return jax.shard_map(
                body, mesh=mesh, in_specs=in_specs, out_specs=out_specs, check_vma=False
            )(*args)
        step = jax.shard_map(
            line_steps, mesh=mesh, in_specs=in_specs, out_specs=out_specs, check_vma=False
        )
        return step(*args)

    return run
```

```python
import functools
import math

import jax
import jax.numpy as jnp
from jax import lax
from jax.experimental import pallas as pl
from jax.experimental.pallas import tpu as pltpu
from jax.sharding import PartitionSpec as P


H = 64
KVH = 8
HD = 128
LQ = 128
GROUP = H // KVH
COEF = HD ** (-0.5) * math.log2(math.e)
NEG = -1e30
ROWS = 256


def round_of(a, b, n):
    if n & (n - 1) == 0:
        return a ^ b
    return lax.rem(b - a + n, n)


def pairs_of(k, n):
    if n & (n - 1) == 0:
        return [(p, p ^ k) for p in range(n)]
    return [(p, (p + k) % n) for p in range(n)]


def order_of(n):
    rest = range(1, n)
    return sorted(rest, key=lambda k: (bin(k).count("1"), k))


def gather_kernel(n, most, per_device, order, lists_ref, pslot_ref, qslot_ref, cache_ref, *refs):
    recv_ref, own_row_ref = refs[0], refs[1]
    outs = refs[2 : 2 + len(order)]
    send_row, send_cnt, recv_cnt, buf, in_sem, out_sem = refs[2 + len(order) :]
    me = lax.axis_index("pass")
    pass_dev = cache_ref.shape[0]
    topp, nq = lists_ref.shape
    for k in range(n):
        send_cnt[k] = 0
        recv_cnt[k] = 0
    for i in range(n * most):
        recv_ref[i] = -1
        send_row[i] = 0

    def question(q, carry):
        slot = qslot_ref[q]
        dest = slot // per_device
        local = slot - dest * per_device
        k_send = round_of(me, dest, n)
        for t in range(topp):
            row = pslot_ref[lists_ref[t, q]]
            owner = row // pass_dev

            @pl.when(owner == me)
            def _():
                count = send_cnt[k_send]
                send_row[k_send * most + count] = row - owner * pass_dev
                send_cnt[k_send] = count + 1

            @pl.when(dest == me)
            def _():
                k = round_of(owner, me, n)
                count = recv_cnt[k]
                recv_ref[k * most + count] = local
                recv_cnt[k] = count + 1

        return carry

    lax.fori_loop(0, nq, question, 0)
    for r in range(most):
        own_row_ref[r] = send_row[r]
    copies = []
    for j, k in enumerate(order):
        for r in range(most):
            i = j * most + r
            get = pltpu.make_async_copy(
                cache_ref.at[send_row[k * most + r]], buf.at[i], in_sem.at[i]
            )
            get.start()
            copies.append((get, pltpu.make_async_copy(buf.at[i], outs[j].at[r], out_sem.at[i])))
    for get, put in copies:
        get.wait()
        put.start()
    for get, put in copies:
        put.wait()


def gather(lists, passage_slot, question_slot, cache, n, most, per_device, order):
    item = cache.shape[1:]
    slots = (n - 1) * most
    smem = pl.BlockSpec(memory_space=pltpu.SMEM)
    anyspace = pl.BlockSpec(memory_space=pl.ANY)
    return pl.pallas_call(
        functools.partial(gather_kernel, n, most, per_device, order),
        out_shape=[
            jax.ShapeDtypeStruct((n * most,), jnp.int32),
            jax.ShapeDtypeStruct((most,), jnp.int32),
        ]
        + [jax.ShapeDtypeStruct((most,) + item, cache.dtype)] * len(order),
        in_specs=[smem, smem, smem, anyspace],
        out_specs=[smem, smem] + [anyspace] * len(order),
        scratch_shapes=[
            pltpu.SMEM((n * most,), jnp.int32),
            pltpu.SMEM((n,), jnp.int32),
            pltpu.SMEM((n,), jnp.int32),
            pltpu.VMEM((slots,) + item, cache.dtype),
            pltpu.SemaphoreType.DMA((slots,)),
            pltpu.SemaphoreType.DMA((slots,)),
        ],
        name="gather_it",
        cost_estimate=pl.CostEstimate(
            flops=0, bytes_accessed=2 * slots * math.prod(item) * 2, transcendentals=0
        ),
    )(lists.T, passage_slot, question_slot, cache)


def block_step(q_ref, m_ref, l_ref, acc_ref, question, head, keys, values, causal):
    rows = q_ref.shape[2]
    step = min(ROWS, rows)
    width = keys.shape[0]
    ones = jnp.ones(values.shape, values.dtype)
    extended = jnp.concatenate([values, ones], axis=1)
    for start in range(0, rows, step):
        part = pl.ds(start, step)
        q = q_ref[question, head, part, :]
        scores = (
            lax.dot_general(q, keys, (((1,), (1,)), ((), ())), preferred_element_type=jnp.float32)
            * COEF
        )
        if causal:
            token = lax.broadcasted_iota(jnp.int32, scores.shape, 0) % LQ
            column = lax.broadcasted_iota(jnp.int32, scores.shape, 1)
            scores = jnp.where(column <= token, scores, NEG)
        old = m_ref[question, head, part, :]
        new = jnp.maximum(old, jnp.max(scores, axis=1, keepdims=True))
        weights = jnp.exp2(scores - jnp.concatenate([new] * (width // HD), axis=1))
        mixed = jnp.dot(
            weights.astype(jnp.bfloat16), extended, preferred_element_type=jnp.float32
        )
        alpha = jnp.exp2(old - new)
        m_ref[question, head, part, :] = new
        l_ref[question, head, part, :] = l_ref[question, head, part, :] * alpha + mixed[:, HD:]
        acc_ref[question, head, part, :] = (
            acc_ref[question, head, part, :] * alpha + mixed[:, :HD]
        )


def attend_kernel(first, last, rounds, most, *refs):
    refs = list(refs)
    recv_ref, q_ref = refs.pop(0), refs.pop(0)
    if first:
        row_ref, own_ref, cache_ref = refs.pop(0), refs.pop(0), refs.pop(0)
        sources = None
        entries = most
    else:
        state_in = [refs.pop(0) for _ in range(3)]
        sources = [refs.pop(0) for _ in rounds]
        entries = len(rounds) * most
    if last:
        out_ref = refs.pop(0)
        m_ref, l_ref, acc_ref = [refs.pop(0) for _ in range(3)]
    else:
        m_ref, l_ref, acc_ref = [refs.pop(0) for _ in range(3)]
    buf, sem = refs
    per_device, heads = q_ref.shape[0], q_ref.shape[1]

    def fetch(i, slot):
        if first:
            pltpu.make_async_copy(cache_ref.at[row_ref[i]], buf.at[slot], sem.at[slot]).start()
            return
        for j in range(len(rounds)):

            @pl.when(i // most == j)
            def _():
                pltpu.make_async_copy(
                    sources[j].at[i - j * most], buf.at[slot], sem.at[slot]
                ).start()

    def tag_of(i):
        if first:
            return recv_ref[i]
        k = jnp.int32(0)
        for j, value in enumerate(rounds):
            k = jnp.where(i // most == j, value, k)
        return recv_ref[k * most + lax.rem(i, most)]

    fetch(jnp.int32(0), 0)
    if first:
        m_ref[...] = jnp.full(m_ref.shape, NEG, jnp.float32)
        l_ref[...] = jnp.zeros(l_ref.shape, jnp.float32)
        acc_ref[...] = jnp.zeros(acc_ref.shape, jnp.float32)

        def own_block(question, carry):
            for head in range(heads):
                block = own_ref[question, head]
                block_step(
                    q_ref, m_ref, l_ref, acc_ref, question, head, block[:, :HD], block[:, HD:], True
                )
            return carry

        lax.fori_loop(0, per_device, own_block, 0)
    else:
        m_ref[...] = state_in[0][...]
        l_ref[...] = state_in[1][...]
        acc_ref[...] = state_in[2][...]

    def item(i, carry):
        slot = lax.rem(i, 2)
        pltpu.make_async_copy(buf.at[slot], buf.at[slot], sem.at[slot]).wait()

        @pl.when(i + 1 < entries)
        def _():
            fetch(i + 1, lax.rem(i + 1, 2))

        tag = tag_of(i)

        @pl.when(tag >= 0)
        def _():
            for head in range(heads):
                block_step(
                    q_ref,
                    m_ref,
                    l_ref,
                    acc_ref,
                    tag,
                    head,
                    buf[slot, head, :, :HD],
                    buf[slot, head, :, HD:],
                    False,
                )

        return carry

    lax.fori_loop(0, entries, item, 0)
    if last:
        for question in range(per_device):
            for head in range(heads):
                for g in range(GROUP):
                    part = pl.ds(g * LQ, LQ)
                    column = (head * GROUP + g) * HD
                    out_ref[pl.ds(question * LQ, LQ), pl.ds(column, HD)] = (
                        acc_ref[question, head, part, :] / l_ref[question, head, part, :]
                    ).astype(out_ref.dtype)


def attend_call(first, last, rounds, most, recv, q, rest, item):
    per_device, heads, rows, _ = q.shape
    state = jax.ShapeDtypeStruct(q.shape, jnp.float32)
    smem = pl.BlockSpec(memory_space=pltpu.SMEM)
    vmem = pl.BlockSpec(memory_space=pltpu.VMEM)
    anyspace = pl.BlockSpec(memory_space=pl.ANY)
    if first:
        in_specs = [smem, vmem, smem, vmem, anyspace]
        entries = most
    else:
        in_specs = [smem, vmem] + [vmem] * 3 + [anyspace] * len(rounds)
        entries = most * len(rounds)
    scratch = [pltpu.VMEM((2,) + item, q.dtype), pltpu.SemaphoreType.DMA((2,))]
    if last:
        out_shape = jax.ShapeDtypeStruct((per_device * LQ, heads * GROUP * HD), q.dtype)
        out_specs = vmem
        scratch = [pltpu.VMEM(q.shape, jnp.float32)] * 3 + scratch
    else:
        out_shape = [state] * 3
        out_specs = [vmem] * 3
    weights = entries * heads * rows * item[1]
    return pl.pallas_call(
        functools.partial(attend_kernel, first, last, rounds, most),
        out_shape=out_shape,
        in_specs=in_specs,
        out_specs=out_specs,
        scratch_shapes=scratch,
        name="a1" if first else ("a3" if last else "a2"),
        cost_estimate=pl.CostEstimate(
            flops=weights * HD * 4,
            bytes_accessed=entries * math.prod(item) * 2,
            transcendentals=weights,
        ),
    )(recv, q, *rest)


def weight_blocks(own, n):
    if n & (n - 1):
        return [lax.all_gather(own, "pass", axis=1, tiled=True)]
    have = {0: own}
    bit = n // 2
    while bit:
        for k in list(have):
            have[k ^ bit] = lax.ppermute(have[k], "pass", pairs_of(bit, n))
        bit //= 2
    return [have[k] for k in range(n)]


def project(context, weights):
    parts = [
        jnp.dot(context, weight, preferred_element_type=jnp.float32).astype(jnp.bfloat16)
        for weight in weights
    ]
    me = lax.axis_index("pass")
    bit = len(parts) // 2
    while bit:
        swap = (me & bit) != 0
        parts = [jnp.where(swap, parts[k ^ bit], parts[k]) for k in range(len(parts))]
        bit //= 2
    return jnp.concatenate(parts, axis=1)


def body(queries, own_kv, passage_cache, out_weight, lists, passage_slot, question_slot):
    n = lax.axis_size("pass")
    per_device = queries.shape[0] // LQ
    heads = own_kv.shape[1]
    entries = per_device * lists.shape[1]
    most = (entries + n - 1) // n
    order = order_of(n)
    cache = jnp.transpose(passage_cache, (0, 2, 1, 3))
    recv, own_row, *items = gather(
        lists, passage_slot, question_slot, cache, n, most, per_device, order
    )
    arrived = [
        lax.ppermute(item, "pass", pairs_of(k, n)) for k, item in zip(order, items)
    ]
    weights = weight_blocks(out_weight, n)
    q = (
        queries.reshape(per_device, LQ, heads, GROUP, HD)
        .transpose(0, 2, 3, 1, 4)
        .reshape(per_device, heads, GROUP * LQ, HD)
    )
    own = own_kv.reshape(per_device, LQ, heads, 2 * HD).transpose(0, 2, 1, 3)
    item = cache.shape[1:]
    state = attend_call(True, False, (0,), most, recv, q, (own_row, own, cache), item)
    calls = 3
    bounds = [len(order) * i // calls for i in range(calls + 1)]
    for i in range(calls):
        rounds = tuple(order[bounds[i] : bounds[i + 1]])
        rest = tuple(state) + tuple(arrived[bounds[i] : bounds[i + 1]])
        state = attend_call(False, i == calls - 1, rounds, most, recv, q, rest, item)
    context = state
    return lax.psum_scatter(project(context, weights), "head", scatter_dimension=1, tiled=True)


LINE = 4
EXTRA = 8
ITEM_ORDER = (2, 0, 3, 1)
VMEM_BYTES = 67043328


def mirror(k, ends=None):
    pairs = [(p, p ^ int(2 * k)) for p in range(2 * LINE)]
    if ends is None:
        return pairs
    return [(p, d) for p, d in pairs if (p // 2 in (0, LINE - 1)) == (ends == "outer")]


def is_inner():
    z = lax.axis_index("pass") // 2
    return jnp.logical_and(z > 0, z < LINE - 1)


def sort_kernel(most, per_device, lists_ref, pslot_ref, qslot_ref, cache_ref, *refs):
    row_ref, tag_ref, far_tag_ref = refs[:3]
    outs = refs[3 : 3 + LINE]
    send_row, near_cnt, send_cnt, far_cnt, buf, in_sem, out_sem = refs[3 + LINE :]
    me = lax.axis_index("pass")
    z, x = me // 2, me % 2
    pass_dev = cache_ref.shape[0]
    topp, nq = lists_ref.shape
    for k in range(LINE):
        near_cnt[k] = 0
        send_cnt[k] = 0
        far_cnt[k] = 0

    def take(i):
        return pltpu.make_async_copy(cache_ref.at[send_row[i]], buf.at[i], in_sem.at[i])

    def question(q, carry):
        slot = qslot_ref[q]
        dest = slot // per_device
        local = slot - dest * per_device
        k = (dest // 2) ^ z

        @pl.when(dest % 2 == x)
        def _():
            for t in range(topp):
                row = pslot_ref[lists_ref[t, q]]
                owner = row // pass_dev

                @pl.when(owner == me)
                def _():
                    at = k * most + near_cnt[k]
                    row_ref[at] = row - owner * pass_dev
                    tag_ref[at] = local
                    near_cnt[k] = near_cnt[k] + 1

                @pl.when(owner == (me ^ 1))
                def _():
                    far_tag_ref[k * most + far_cnt[k]] = local
                    far_cnt[k] = far_cnt[k] + 1

        @pl.when(dest % 2 != x)
        def _():
            for t in range(topp):
                row = pslot_ref[lists_ref[t, q]]
                owner = row // pass_dev

                @pl.when(owner == me)
                def _():
                    at = k * most + send_cnt[k]
                    send_row[at] = row - owner * pass_dev
                    send_cnt[k] = send_cnt[k] + 1
                    take(at).start()

        return carry

    lax.fori_loop(0, nq, question, 0)
    slots = [k * most + r for k in ITEM_ORDER for r in range(most)]
    puts = [pltpu.make_async_copy(buf.at[i], outs[i // most].at[i % most], out_sem.at[i]) for i in slots]
    for i, put in zip(slots, puts):
        take(i).wait()
        put.start()
    for put in puts:
        put.wait()


def sort_items(lists, passage_slot, question_slot, cache, most, per_device):
    item = cache.shape[1:]
    slots = LINE * most
    smem = pl.BlockSpec(memory_space=pltpu.SMEM)
    anyspace = pl.BlockSpec(memory_space=pl.ANY)
    return pl.pallas_call(
        functools.partial(sort_kernel, most, per_device),
        out_shape=[jax.ShapeDtypeStruct((slots,), jnp.int32)] * 3
        + [jax.ShapeDtypeStruct((most,) + item, cache.dtype)] * LINE,
        in_specs=[smem, smem, smem, anyspace],
        out_specs=[smem] * 3 + [anyspace] * LINE,
        scratch_shapes=[
            pltpu.SMEM((slots,), jnp.int32),
            pltpu.SMEM((LINE,), jnp.int32),
            pltpu.SMEM((LINE,), jnp.int32),
            pltpu.SMEM((LINE,), jnp.int32),
            pltpu.VMEM((slots,) + item, cache.dtype),
            pltpu.SemaphoreType.DMA((slots,)),
            pltpu.SemaphoreType.DMA((slots,)),
        ],
        compiler_params=pltpu.CompilerParams(vmem_limit_bytes=VMEM_BYTES),
        name="sort_it",
        cost_estimate=pl.CostEstimate(
            flops=0, bytes_accessed=2 * slots * math.prod(item) * 2, transcendentals=0
        ),
    )(lists.T, passage_slot, question_slot, cache)


def unit():
    r = lax.broadcasted_iota(jnp.int32, (LQ, LQ), 0)
    c = lax.broadcasted_iota(jnp.int32, (LQ, LQ), 1)
    return r == c


def part_step(q_ref, m_ref, l_ref, acc_ref, question, head, keys, values, causal):
    rows = GROUP * LQ
    width = keys.shape[0]
    ones = jnp.ones(values.shape, values.dtype)
    extended = jnp.concatenate([values, ones], axis=1)
    tokens = pl.ds(pl.multiple_of(question * LQ, LQ), LQ)
    for start in range(0, rows, ROWS):
        part = pl.ds(start, ROWS)
        q = jnp.concatenate(
            [
                q_ref[tokens, pl.ds(pl.multiple_of((head * GROUP + g) * HD, HD), HD)]
                for g in range(start // LQ, (start + ROWS) // LQ)
            ],
            axis=0,
        )
        scores = (
            lax.dot_general(q, keys, (((1,), (1,)), ((), ())), preferred_element_type=jnp.float32)
            * COEF
        )
        if causal:
            token = lax.broadcasted_iota(jnp.int32, scores.shape, 0) % LQ
            column = lax.broadcasted_iota(jnp.int32, scores.shape, 1)
            scores = jnp.where(column <= token, scores, NEG)
        old = m_ref[question, head, part, :]
        new = jnp.maximum(old, jnp.max(scores, axis=1, keepdims=True))
        weights = jnp.exp2(scores - jnp.concatenate([new] * (width // HD), axis=1))
        mixed = jnp.dot(
            weights.astype(jnp.bfloat16), extended, preferred_element_type=jnp.float32
        )
        alpha = jnp.exp2(old - new)
        m_ref[question, head, part, :] = new
        l_ref[question, head, part, :] = l_ref[question, head, part, :] * alpha + mixed[:, HD:]
        acc_ref[question, head, part, :] = (
            acc_ref[question, head, part, :] * alpha + mixed[:, :HD]
        )


def part_kernel(k, most, first, last, heads, *refs):
    refs = list(refs)
    row_ref, tag_ref, far_tag_ref = refs.pop(0), refs.pop(0), refs.pop(0)
    own_ref = refs.pop(0) if k == 0 else None
    questions = [refs.pop(0) for _ in range(2 if k > 1 else 1)]
    cache_ref = refs.pop(0)
    items_ref = refs.pop(0) if last > most else None
    out_ref, q_ref, m_ref, l_ref, acc_ref, buf, sem, q_sem = refs
    per_device = q_ref.shape[0] // LQ

    def fetch(i, slot):
        if first < most:

            @pl.when(i < most)
            def _():
                row = row_ref[k * most + jnp.minimum(i, most - 1)]
                pltpu.make_async_copy(cache_ref.at[row], buf.at[slot], sem.at[slot]).start()

        if last > most:

            @pl.when(i >= most)
            def _():
                pltpu.make_async_copy(
                    items_ref.at[jnp.maximum(i - most, 0)], buf.at[slot], sem.at[slot]
                ).start()

    if len(questions) == 1:
        pltpu.make_async_copy(questions[0], q_ref, q_sem).start()
    else:
        inner = is_inner()

        @pl.when(inner)
        def _():
            pltpu.make_async_copy(questions[0], q_ref, q_sem).start()

        @pl.when(jnp.logical_not(inner))
        def _():
            pltpu.make_async_copy(questions[1], q_ref, q_sem).start()

    fetch(jnp.int32(first), first % 2)
    m_ref[...] = jnp.full(m_ref.shape, NEG, jnp.float32)
    l_ref[...] = jnp.zeros(l_ref.shape, jnp.float32)
    acc_ref[...] = jnp.zeros(acc_ref.shape, jnp.float32)
    pltpu.make_async_copy(q_ref, q_ref, q_sem).wait()
    if k == 0:

        def own_block(i, carry):
            question, head = i // heads, lax.rem(i, heads)
            part_step(
                q_ref,
                m_ref,
                l_ref,
                acc_ref,
                question,
                head,
                own_ref[question, head, :, :HD],
                own_ref[question, head, :, HD:],
                True,
            )
            return carry

        lax.fori_loop(0, per_device * heads, own_block, 0)

    def item(i, carry):
        slot = lax.rem(i, 2)
        pltpu.make_async_copy(buf.at[slot], buf.at[slot], sem.at[slot]).wait()

        @pl.when(i + 1 < last)
        def _():
            fetch(i + 1, lax.rem(i + 1, 2))

        at = k * most + lax.rem(i, most)
        tag = jnp.where(i < most, tag_ref[at], far_tag_ref[at])

        for head in range(heads):
            part_step(
                q_ref,
                m_ref,
                l_ref,
                acc_ref,
                tag,
                head,
                buf[slot, head, :, :HD],
                buf[slot, head, :, HD:],
                False,
            )
        return carry

    lax.fori_loop(first, last, item, 0)
    eye = unit()

    def close(c, carry):
        head, g = c // GROUP, lax.rem(c, GROUP)
        columns = pl.ds(pl.multiple_of(c * HD, HD), HD)
        part = pl.ds(pl.multiple_of(g * LQ, LQ), LQ)
        for question in range(per_device):
            total = l_ref[question, head, part, :]
            some = total > 0.0
            safe = jnp.where(some, total, 1.0)
            out_ref[question, :LQ, columns] = (
                acc_ref[question, head, part, :] / safe
            ).astype(out_ref.dtype)
            level = jnp.where(some, m_ref[question, head, part, :] + jnp.log2(safe), NEG)
            line = jnp.sum(jnp.where(eye, level, 0.0), axis=0, keepdims=True)
            store_level(out_ref, question, columns, line)
        return carry

    lax.fori_loop(0, heads * GROUP, close, 0)


def store_level(out_ref, question, columns, line):
    row_of = lax.broadcasted_iota(jnp.int32, (EXTRA, line.shape[1]), 0)
    high = line.astype(jnp.bfloat16).astype(jnp.float32)
    both = jnp.where(row_of == 0, high, jnp.where(row_of == 1, line - high, 0.0))
    out_ref[question, LQ:, columns] = both.astype(out_ref.dtype)


def part_call(k, most, tables, own, questions, cache, items, local=True):
    tokens, columns = questions[0].shape
    heads, item = cache.shape[1], cache.shape[1:]
    state = (tokens // LQ, heads, GROUP * LQ, HD)
    smem = pl.BlockSpec(memory_space=pltpu.SMEM)
    vmem = pl.BlockSpec(memory_space=pltpu.VMEM)
    anyspace = pl.BlockSpec(memory_space=pl.ANY)
    owned = [own] if k == 0 else []
    received = [items] if items is not None else []
    first, last = 0 if local else most, 2 * most if received else most
    weights = (last - first) * heads * GROUP * LQ * item[1]
    return pl.pallas_call(
        functools.partial(part_kernel, k, most, first, last, heads),
        out_shape=jax.ShapeDtypeStruct((tokens // LQ, LQ + EXTRA, columns), cache.dtype),
        in_specs=[smem] * 3
        + [vmem] * len(owned)
        + [anyspace] * (len(questions) + 1 + len(received)),
        out_specs=vmem,
        scratch_shapes=[
            pltpu.VMEM((tokens, columns), cache.dtype),
            pltpu.VMEM(state, jnp.float32),
            pltpu.VMEM(state, jnp.float32),
            pltpu.VMEM(state, jnp.float32),
            pltpu.VMEM((2,) + item, cache.dtype),
            pltpu.SemaphoreType.DMA((2,)),
            pltpu.SemaphoreType.DMA,
        ],
        compiler_params=pltpu.CompilerParams(vmem_limit_bytes=VMEM_BYTES),
        cost_estimate=pl.CostEstimate(
            flops=weights * HD * 4,
            bytes_accessed=(last - first) * math.prod(item) * 2,
            transcendentals=weights,
        ),
    )(*tables, *owned, *questions, cache, *received)


def blend(refs, out_ref, leveled):
    eye = unit()
    ones = jnp.ones((2 * LQ, LQ), jnp.bfloat16)

    def level_of(ref):
        both = ref[0, LQ:, :].astype(jnp.float32)
        return both[:1] + both[1:2]

    levels = [level_of(ref) for ref in refs]
    top = functools.reduce(jnp.maximum, levels)
    weights = [jnp.exp2(level - top) for level in levels]
    total = functools.reduce(jnp.add, weights)
    shares = []
    for weight in weights[1:]:
        share = weight / total
        high = share.astype(jnp.bfloat16).astype(jnp.float32)
        shares.append((high, share - high))
    for c in range(total.shape[1] // HD):
        columns = slice(c * HD, (c + 1) * HD)
        base = refs[0][0, :LQ, columns].astype(jnp.float32)
        value = base
        for ref, pair in zip(refs[1:], shares):
            spread = jnp.concatenate(
                [
                    jnp.where(eye, jnp.broadcast_to(v[:, columns], (LQ, LQ)), 0.0).astype(
                        jnp.bfloat16
                    )
                    for v in pair
                ],
                axis=1,
            )
            column = jnp.dot(spread, ones, preferred_element_type=jnp.float32)
            value = value + (ref[0, :LQ, columns].astype(jnp.float32) - base) * column
        value = value.astype(out_ref.dtype)
        if leveled:
            out_ref[0, :LQ, columns] = value
        else:
            out_ref[:, columns] = value
    if leveled:
        store_level(out_ref, 0, slice(None), top + jnp.log2(total))


def merge_kernel(*refs):
    *parts, out_ref = refs
    inner = is_inner()

    @pl.when(inner)
    def _():
        blend(parts, out_ref, True)

    @pl.when(jnp.logical_not(inner))
    def _():
        if len(parts) > 2:
            blend(parts[:-1], out_ref, True)
        else:
            out_ref[...] = parts[0][...]


def finish_kernel(a_ref, b_ref, out_ref):
    blend((a_ref, b_ref), out_ref, False)


def question_spec(value, at):
    shape = (1,) + value.shape[1:]
    if value.shape[0] == 1:
        return pl.BlockSpec(shape, lambda q: (0, 0, 0))
    return pl.BlockSpec(shape, lambda q: (at, 0, 0))


def join_call(parts, at, leveled):
    columns = parts[0].shape[2]
    if leveled:
        shape = (1,) + parts[0].shape[1:]
        out_spec = pl.BlockSpec(shape, lambda q: (0, 0, 0))
    else:
        shape = (LQ, columns)
        out_spec = pl.BlockSpec(shape, lambda q: (0, 0))
    size = LQ * columns
    return pl.pallas_call(
        merge_kernel if leveled else finish_kernel,
        out_shape=jax.ShapeDtypeStruct(shape, parts[0].dtype),
        grid=(1,),
        in_specs=[question_spec(part, at) for part in parts],
        out_specs=out_spec,
        compiler_params=pltpu.CompilerParams(vmem_limit_bytes=VMEM_BYTES),
        cost_estimate=pl.CostEstimate(flops=size * 8, bytes_accessed=size * 6, transcendentals=0),
    )(*parts)


def line_steps(queries, own_kv, passage_cache, out_weight, lists, passage_slot, question_slot):
    per_device = queries.shape[0] // LQ
    heads = own_kv.shape[1]
    most = per_device * lists.shape[1] // (2 * LINE)

    def send(value, pairs):
        return lax.ppermute(value, "pass", pairs)

    def part(k, *args, local=True):
        return part_call(k, most, tables, own if k == 0 else None, *args, local=local)

    def join(at, *parts, leveled=True):
        return join_call(parts, at, leveled)

    across = [(p, p ^ 1) for p in range(2 * LINE)]
    inner_across = [(p, d) for p, d in across if p // 2 in (1, 2)]
    outer_across = [(p, d) for p, d in across if p // 2 not in (1, 2)]
    near, middle = mirror(1), mirror(3, "inner")
    inward, outward = mirror(1, "outer"), mirror(1, "inner")
    q_near = send(queries, near)
    q_mid = send(queries, middle)
    quarter = out_weight.shape[0] // 4
    w_across0 = send(out_weight[:quarter], across)
    cache = jnp.transpose(passage_cache, (0, 2, 1, 3))
    row, tag, far_tag, *items = sort_items(
        lists, passage_slot, question_slot, cache, most, per_device
    )
    tables = (row, tag, far_tag)
    later, _ = lax.optimization_barrier((out_weight, row))
    w_across1 = send(later[quarter:], across)
    q_out = send(q_mid, outward)
    q_cross = send(q_near, middle)
    q_end = send(q_cross, outward)
    far = [send(items[k], across) for k in range(LINE)]
    own = own_kv.reshape(per_device, LQ, heads, 2 * HD).transpose(0, 2, 1, 3)
    part2 = part(2, [q_cross, q_out], cache, far[2])
    part3 = part(3, [q_mid, q_end], cache, far[3])
    part0 = part(0, [queries], cache, far[0])
    part1 = part(1, [q_near], cache, None)
    part1_far = part(1, [q_near], cache, far[1], local=False)
    back2 = send(part2, inward)
    w_in = send(out_weight, mirror(2, "outer"))
    w_out = send(out_weight, mirror(2, "inner"))
    back3 = send(part3, inward)
    w_in_both = send(w_in, inner_across)
    w_out_both = send(w_out, outer_across)
    own_pairs, near_rows, near_pairs = [], [], []
    for q in range(per_device):
        cross3 = send(join(q, part3, back2), middle)
        near0 = join(q, part0, cross3)
        beside = send(near0, near)
        cross2 = send(join(q, part2, back3), middle)
        near1 = join(q, part1, part1_far, cross2)
        back1 = send(near1, near)
        own_pairs += [near0, back1]
        if q + 1 < per_device:
            near_rows.append(join(q, near1, beside, leveled=False))
        else:
            near_pairs += [near1, beside]
    weights = (out_weight, w_across0, w_across1, w_in, w_in_both, w_out, w_out_both)
    far_sums = project_call(near_rows, near_pairs, weights, None)
    return project_call([], own_pairs, weights, far_sums)


MESH = pl.DeviceIdType.MESH


def at_home():
    return lax.axis_index("head") % 2 == lax.axis_index("pass") // 2 % 2


def project_kernel(done, pieces, far, *refs):
    rows_refs = refs[:pieces]
    own_ref, a0_ref, a1_ref, in_ref, in2_ref, out1_ref, out2_ref = refs[pieces : pieces + 7]
    refs = refs[pieces + 7 :]
    if not far:
        far_ref, *refs = refs
    out_ref, context_ref, w_ref, part_ref, core_ref, pair_ref, y_ref, ysend_ref = refs[:8]
    row_sem, w_sem, send_sem, recv_sem = refs[8:]
    me, head = lax.axis_index("pass"), lax.axis_index("head")
    z, x, y = me // 2, me % 2, head // 2
    wide = w_ref.shape[3]
    inner = is_inner()
    core_peer, y_peer, z_peer = (me, head ^ 1), (me, head ^ 2), (me ^ 2, head ^ 1)
    home = at_home()
    sums = jnp.logical_not(home) if far else home

    row_loads = [
        pltpu.make_async_copy(ref, pair_ref.at[i // 2, i % 2], row_sem.at[done + i])
        for i, ref in enumerate(rows_refs[done:])
    ]
    row_loads += [
        pltpu.make_async_copy(ref, context_ref.at[pl.ds(i * LQ, LQ)], row_sem.at[i])
        for i, ref in enumerate(rows_refs[:done])
    ]
    for load in row_loads:
        load.start()

    def load_here():
        pltpu.make_async_copy(own_ref, w_ref.at[0, x], w_sem.at[0, x]).start()
        first, rest = a0_ref.shape[0], a1_ref.shape[0]
        low, high = w_ref.at[0, 1 - x, pl.ds(0, first)], w_ref.at[0, 1 - x, pl.ds(first, rest)]
        pltpu.make_async_copy(a0_ref, low, w_sem.at[0, 1 - x]).start()
        pltpu.make_async_copy(a1_ref, high, w_sem.at[0, 1 - x]).start()

    def load_there():
        for which, (one, two) in (
            (inner, (in_ref, in2_ref)),
            (jnp.logical_not(inner), (out1_ref, out2_ref)),
        ):

            @pl.when(which)
            def _():
                pltpu.make_async_copy(one, w_ref.at[1, x], w_sem.at[1, x]).start()
                pltpu.make_async_copy(two, w_ref.at[1, 1 - x], w_sem.at[1, 1 - x]).start()

    here_first = y != z // 2

    @pl.when(here_first)
    def _():
        load_here()
        load_there()

    @pl.when(jnp.logical_not(here_first))
    def _():
        load_there()
        load_here()

    barrier = pltpu.get_barrier_semaphore()
    peers = (core_peer, y_peer) if far else (core_peer, y_peer, z_peer)
    for peer in peers:
        pl.semaphore_signal(barrier, inc=1, device_id=peer, device_id_type=MESH)
    pl.semaphore_wait(barrier, len(peers))

    def remote(src, dst, i, peer):
        return pltpu.make_async_remote_copy(
            src_ref=src,
            dst_ref=dst,
            send_sem=send_sem.at[i],
            recv_sem=recv_sem.at[i],
            device_id=peer,
            device_id_type=MESH,
        )

    def columns(j):
        return pl.ds(j * wide, wide)

    core_copies = [
        [remote(part_ref.at[s, j], core_ref.at[s, j], s * 2 + j, core_peer) for j in range(2)]
        for s in range(2)
    ]
    y_copies = [remote(ysend_ref.at[j], y_ref.at[j], 4 + j, y_peer) for j in range(2)]
    if not far:
        z_copies = [
            remote(far_ref.at[j], out_ref.at[:, columns(j)], 6 + j, z_peer) for j in range(2)
        ]

        @pl.when(jnp.logical_not(home))
        def _():
            for copy in z_copies:
                copy.start()

    for load in row_loads:
        load.wait()
    for i in range((pieces - done) // 2):
        pair = (pair_ref.at[i, 0], pair_ref.at[i, 1])
        blend(pair, context_ref.at[pl.ds((done + i) * LQ, LQ)], False)

    def multiply(s, to_y, j):
        here = jnp.where(to_y == z // 2, 0, 1)
        block = w_ref.at[here, j]
        pltpu.make_async_copy(block, block, w_sem.at[here, j]).wait()
        part_ref[s, j] = jnp.dot(
            context_ref[...], w_ref[here, j], preferred_element_type=jnp.float32
        ).astype(part_ref.dtype)

        @pl.when(jnp.logical_not(sums))
        def _():
            core_copies[s][j].start()

    def add_up(s, j):
        @pl.when(sums)
        def _():
            core_copies[s][j].wait_recv()
            value = part_ref[s, j].astype(jnp.float32) + core_ref[s, j].astype(jnp.float32)
            if s == 0:
                ysend_ref[j] = value.astype(ysend_ref.dtype)
                y_copies[j].start()
                return
            y_copies[j].wait_recv()
            total = (value + y_ref[j].astype(jnp.float32)).astype(out_ref.dtype)
            if far:
                out_ref[j] = total
            else:
                out_ref[:, columns(j)] = total

    late = None
    for s, to_y in enumerate((1 - y, y)):
        for j in range(2):
            multiply(s, to_y, j)
            if late is not None:
                add_up(*late)
            late = (s, j)
    add_up(*late)

    @pl.when(jnp.logical_not(sums))
    def _():
        for copies in core_copies:
            for copy in copies:
                copy.wait_send()

    @pl.when(sums)
    def _():
        for copy in y_copies:
            copy.wait_send()

    if not far:

        @pl.when(jnp.logical_not(home))
        def _():
            for copy in z_copies:
                copy.wait()


def project_call(finished, pairs, weights, far_sums):
    own = weights[0]
    pieces = finished + pairs
    rows, (depth, wide) = (len(finished) + len(pairs) // 2) * LQ, own.shape
    dtype = own.dtype
    far = far_sums is None
    vmem = pl.BlockSpec(memory_space=pltpu.VMEM)
    blocks = (2, rows, wide)
    scratch = [
        pltpu.VMEM((rows, depth), dtype),
        pltpu.VMEM((2, 2, depth, wide), dtype),
        pltpu.VMEM((2,) + blocks, dtype),
        pltpu.VMEM((2,) + blocks, dtype),
        pltpu.VMEM((len(pairs) // 2, 2) + pairs[0].shape, dtype),
        pltpu.VMEM(blocks, dtype),
        pltpu.VMEM(blocks, dtype),
        pltpu.SemaphoreType.DMA((len(pieces),)),
        pltpu.SemaphoreType.DMA((2, 2)),
        pltpu.SemaphoreType.DMA((8,)),
        pltpu.SemaphoreType.DMA((8,)),
    ]
    shape = blocks if far else (rows, 2 * wide)
    return pl.pallas_call(
        functools.partial(project_kernel, len(finished), len(pieces), far),
        out_shape=jax.ShapeDtypeStruct(shape, dtype),
        in_specs=[pl.BlockSpec(memory_space=pl.ANY)] * (len(pieces) + len(weights))
        + [vmem] * (0 if far else 1),
        out_specs=vmem,
        scratch_shapes=scratch,
        compiler_params=pltpu.CompilerParams(
            collective_id=int(far), has_side_effects=True, vmem_limit_bytes=VMEM_BYTES
        ),
        name="pf" if far else "ph",
        cost_estimate=pl.CostEstimate(
            flops=2 * 4 * rows * depth * wide,
            bytes_accessed=4 * depth * wide * 2,
            transcendentals=0,
        ),
    )(*pieces, *weights, *([] if far else [far_sums]))


def suits_line(mesh, queries, lists):
    passes, heads = mesh.shape["pass"], mesh.shape["head"]
    entries = queries.shape[0] // LQ // passes * lists.shape[1]
    several = queries.shape[0] // LQ >= 2 * passes
    return passes == 2 * LINE and heads == LINE and several and entries % passes == 0


def solution(mesh):
    in_specs = (
        P("pass", "head"),
        P("pass", "head", None),
        P("pass", None, "head", None),
        P("head", "pass"),
        P(),
        P(),
        P(),
    )
    out_specs = P("pass", "head")

    def run(*args):
        if not suits_line(mesh, args[0], args[4]):
            return jax.shard_map(
                body, mesh=mesh, in_specs=in_specs, out_specs=out_specs, check_vma=False
            )(*args)
        step = jax.shard_map(
            line_steps, mesh=mesh, in_specs=in_specs, out_specs=out_specs, check_vma=False
        )
        return step(*args)

    return run
```
